32 devices in a mesh: ctx: 16 (over z, y, x), fsdp: 2 (over core).
Axes of the slice: x: 2, y: 2, z: 4, core: 2. Of those that a mesh axis runs over, the one named last changes fastest.
Arguments:
- post_stream: float32 [2, 8192, 512], P('fsdp', 'ctx'), may hold values from -6 to 6
- sum_stream: float32 [2, 8192, 512], P('fsdp', 'ctx'), may hold values from -6 to 6
- cotangent: float32 [2, 8192, 512], P('fsdp', 'ctx'), may hold values from -6 to 6
- block_order: int32 [2, 32], P('fsdp'), may hold values from 0 to 31, as said below
- block_sequence: int32 [2, 32], P('fsdp'), may hold values from 0 to 5, never falling along the last dimension, each value on 1 to 8 neighbouring positions
- query_weight: bfloat16 [512, 512], P(None, 'fsdp'), may hold values from -0.5 to 0.5
- key_weight: bfloat16 [512, 512], P(None, 'fsdp'), may hold values from -0.25 to 0.25
- value_weight: bfloat16 [512, 512], P(None, 'fsdp'), may hold values from -0.25 to 0.25
- output_weight: bfloat16 [512, 512], P('fsdp'), may hold values from -1.5 to 1.5
- query_bias: bfloat16 [512], P('fsdp'), may hold values from -3 to 3
- value_bias: bfloat16 [512], P('fsdp'), may hold values from -1.796875 to 1.796875
- output_bias: bfloat16 [512], P('fsdp'), may hold values from -1.796875 to 1.796875
- attend_gain: bfloat16 [512], P('fsdp'), may hold values from 0.5 to 1.5
- attend_shift: bfloat16 [512], P('fsdp'), may hold values from -1.796875 to 1.796875
- expand_weight: bfloat16 [512, 2048], P(None, 'fsdp'), may hold values from -0.25 to 0.25
- expand_bias: bfloat16 [2048], P('fsdp'), may hold values from -1.796875 to 1.796875
- shrink_weight: bfloat16 [2048, 512], P('fsdp'), may hold values from -0.1875 to 0.1875
- shrink_bias: bfloat16 [512], P('fsdp'), may hold values from -1.796875 to 1.796875
- middle_gain: bfloat16 [512], P('fsdp'), may hold values from 0.5 to 1.5
- middle_shift: bfloat16 [512], P('fsdp'), may hold values from -1.796875 to 1.796875
- final_gain: bfloat16 [512], P('fsdp'), may hold values from 0.5 to 1.5
- final_shift: bfloat16 [512], P('fsdp'), may hold values from -1.796875 to 1.796875
Outputs:
- layer_output: float32 [2, 8192, 512], P('fsdp', 'ctx')
- post_tangent: float32 [2, 8192, 512], P('fsdp', 'ctx')
- sum_tangent: float32 [2, 8192, 512], P('fsdp', 'ctx')
- query_slope: float32 [512, 512], P(None, 'fsdp')
- key_slope: float32 [512, 512], P(None, 'fsdp')
- value_slope: float32 [512, 512], P(None, 'fsdp')
- output_slope: float32 [512, 512], P('fsdp')
- query_drift: float32 [512], P('fsdp')
- value_drift: float32 [512], P('fsdp')
- output_drift: float32 [512], P('fsdp')
- attend_stretch: float32 [512], P('fsdp')
- attend_nudge: float32 [512], P('fsdp')
- expand_slope: float32 [512, 2048], P(None, 'fsdp')
- expand_drift: float32 [2048], P('fsdp')
- shrink_slope: float32 [2048, 512], P('fsdp')
- shrink_drift: float32 [512], P('fsdp')
- middle_stretch: float32 [512], P('fsdp')
- middle_nudge: float32 [512], P('fsdp')
- final_stretch: float32 [512], P('fsdp')
- final_nudge: float32 [512], P('fsdp')
The draws below stay inside these ranges and needn't reach their ends.
Inputs may be any that keep to these rules, and one draw needn't show every extreme that they name: `block_order`: in each group, ctx device c holds layout blocks 2 c and 2 c + 1, and these hold blocks b and 31 - b of the group for some b, in either order; every block is held once. `block_sequence`: never falls along a group's blocks; every sequence has 1 to 8 blocks and one has exactly 8.
All inputs are finite; a program needn't handle non-finite values.
Results may differ from the reference program's by a relative error of at most 0.02.
The reference program's roundings to bfloat16 on the way count: a program that leaves them out, or rounds other values in their place, can miss the bound.
Values may be sent and summed in bfloat16 or wider, within the bound.
A program may use at most 448 MiB of HBM per device.

```python
import math
import jax
import jax.numpy as jnp
import numpy as np
from jax import lax

D = 512
H = 8
HD = 64
FF = 2048
BLK = 256
SEQ_GROUP = 6
TOK_DEV = 512
NBLK = 32
GROUP_TOK = 8192
GROUPS = 2
LONG_BLK = 8
N_CTX = 16


def draw_block_order(key, part):
    pair_count = NBLK // 2

    def one_group(group_key):
        owner_key, flip_key = jax.random.split(group_key)
        owners = jax.random.permutation(owner_key, pair_count).astype(jnp.int32)
        flip_bits = jax.random.randint(flip_key, (pair_count,), 0, 2, dtype=jnp.int32)
        early_block = jnp.arange(pair_count, dtype=jnp.int32)
        late_block = NBLK - 1 - early_block
        first_slot = jnp.where(flip_bits == 1, late_block, early_block)
        second_slot = jnp.where(flip_bits == 1, early_block, late_block)
        layout = jnp.zeros((NBLK,), jnp.int32)
        layout = layout.at[2 * owners].set(first_slot)
        return layout.at[2 * owners + 1].set(second_slot)
    return jax.vmap(one_group)(jax.random.split(key, GROUPS))


def levels(key, shape, cuts, low, largest):
    factor_of, own = 1.0, jax.random.fold_in(key, 6)
    for axis_at, blocks in cuts:
        steps = jnp.exp(jax.random.uniform(jax.random.fold_in(own, axis_at), (blocks,), jnp.float32, low / len(cuts), largest / len(cuts)))
        factor_of = factor_of * jnp.repeat(steps, shape[axis_at] // blocks).reshape([-1 if axis == axis_at else 1 for axis in range(len(shape))])
    return factor_of


def profile(amount, total, reach, slope):
    loads = [(1 << 20) // math.isqrt(rank ** slope) + 1 for rank in range(2, amount + 1)]
    surplus, holding = total - reach - (amount - 1), [1] * (amount - 1)
    while surplus > 0:
        candidates = [i for i in range(amount - 1) if holding[i] < reach]
        mass, budget = sum([loads[i] for i in candidates]), surplus
        for i in candidates:
            addition = min(reach - holding[i], max(1, budget * loads[i] // mass), surplus)
            holding[i] = holding[i] + addition
            surplus = surplus - addition
    return np.array([reach] + holding)


def uneven_parts(key, number_of, total, reach, lean):
    if number_of == 2:
        one = jax.random.randint(key, (), max(1, total - reach), min(reach, total - 1) + 1)
        return jnp.stack([one, total - one])
    sizes = jnp.asarray(profile(number_of, total, reach, lean), jnp.int32)
    couples = (number_of - 1) // 2
    giver, taker = sizes[1:1 + 2 * couples:2], sizes[2:2 + 2 * couples:2]
    slack = jnp.minimum(giver - 1, reach - taker)
    moved = jax.random.randint(jax.random.fold_in(key, 1), (couples,), 0, 1 << 20) % (slack + 1)
    sizes = sizes.at[1:1 + 2 * couples:2].set(giver - moved).at[2:2 + 2 * couples:2].set(taker + moved)
    return sizes[jax.random.permutation(jax.random.fold_in(key, 2), number_of)]


def bell_draw(stream_key, extent, scale, bound, shards=(), kind=jnp.bfloat16):
    loudness = levels(stream_key, extent, shards, -0.22, 0.18) if shards else 1.0
    entries = jax.random.normal(stream_key, extent, jnp.float32) * scale * loudness
    return jnp.minimum(jnp.maximum(entries, -bound), bound).astype(kind)


def setup_inputs(seed: int = 0) -> dict:
    arg_keys = jax.random.split(jax.random.key(seed), 23)
    post_stream = bell_draw(arg_keys[0], (GROUPS, GROUP_TOK, D), 1.0, 6.0, ((0, 2), (1, 16)), jnp.float32)
    sum_stream = bell_draw(arg_keys[1], (GROUPS, GROUP_TOK, D), 1.0, 6.0, ((0, 2), (1, 16)), jnp.float32)
    cotangent = bell_draw(arg_keys[2], (GROUPS, GROUP_TOK, D), 1.0, 6.0, ((0, 2), (1, 16)), jnp.float32)
    block_order = draw_block_order(jax.random.fold_in(arg_keys[22], 71), 0)
    block_sequence = jax.vmap(lambda own: jnp.searchsorted(jnp.cumsum(uneven_parts(own, SEQ_GROUP, NBLK, LONG_BLK, 2)), jnp.arange(NBLK), side="right"))(jax.random.split(arg_keys[4], GROUPS)).reshape((GROUPS, NBLK)).astype(jnp.int32)
    query_weight = bell_draw(arg_keys[5], (D, D), (D // 4) ** -0.5, 0.5, ((1, 2),))
    key_weight = bell_draw(arg_keys[6], (D, D), D ** -0.5, 0.25, ((1, 2),))
    value_weight = bell_draw(arg_keys[7], (D, D), D ** -0.5, 0.25, ((1, 2),))
    output_weight = bell_draw(arg_keys[8], (D, D), (D // 32) ** -0.5, 1.5, ((0, 2),))
    query_bias = bell_draw(arg_keys[9], (D,), 0.5, 3.0, ((0, 2),))
    value_bias = bell_draw(arg_keys[10], (D,), 0.3, 1.796875, ((0, 2),))
    output_bias = bell_draw(arg_keys[11], (D,), 0.3, 1.796875, ((0, 2),))
    attend_gain = jnp.clip(1.0 + 0.1 * jax.random.normal(arg_keys[12], (D,), jnp.float32), 0.5, 1.5).astype(jnp.bfloat16)
    attend_shift = bell_draw(arg_keys[13], (D,), 0.3, 1.796875, ((0, 2),))
    expand_weight = bell_draw(arg_keys[14], (D, FF), D ** -0.5, 0.25, ((1, 2),))
    expand_bias = bell_draw(arg_keys[15], (FF,), 0.3, 1.796875, ((0, 2),))
    shrink_weight = bell_draw(arg_keys[16], (FF, D), (FF // 2) ** -0.5, 0.1875, ((0, 2),))
    shrink_bias = bell_draw(arg_keys[17], (D,), 0.3, 1.796875, ((0, 2),))
    middle_gain = jnp.clip(1.0 + 0.1 * jax.random.normal(arg_keys[18], (D,), jnp.float32), 0.5, 1.5).astype(jnp.bfloat16)
    middle_shift = bell_draw(arg_keys[19], (D,), 0.3, 1.796875, ((0, 2),))
    final_gain = jnp.clip(1.0 + 0.1 * jax.random.normal(arg_keys[20], (D,), jnp.float32), 0.5, 1.5).astype(jnp.bfloat16)
    final_shift = bell_draw(arg_keys[21], (D,), 0.3, 1.796875, ((0, 2),))
    return dict(post_stream=post_stream, sum_stream=sum_stream, cotangent=cotangent, block_order=block_order, block_sequence=block_sequence, query_weight=query_weight, key_weight=key_weight, value_weight=value_weight, output_weight=output_weight, query_bias=query_bias, value_bias=value_bias, output_bias=output_bias, attend_gain=attend_gain, attend_shift=attend_shift, expand_weight=expand_weight, expand_bias=expand_bias, shrink_weight=shrink_weight, shrink_bias=shrink_bias, middle_gain=middle_gain, middle_shift=middle_shift, final_gain=final_gain, final_shift=final_shift)


norm_eps = 1e-05
masked_value = -1e+30
gelu_coeff = 0.7978845608
gelu_cubic = 0.044715

@jax.custom_vjp
def low(v):
    return lax.optimization_barrier(v.astype(jnp.bfloat16)).astype(jnp.float32)

@jax.custom_vjp
def low_back(v):
    return v

def low_keep(v):
    return (low(v), None)

def low_pass(kept, grad):
    return (grad,)

def back_keep(v):
    return (v, None)

def back_low(kept, grad):
    return (low(grad),)
low.defvjp(low_keep, low_pass)
low_back.defvjp(back_keep, back_low)

def smooth_gate(values):
    return 0.5 * values * (1.0 + jnp.tanh(gelu_coeff * (values + gelu_cubic * values * values * values)))

def matmul(left_side, right_side):
    return jnp.dot(left_side, right_side, precision=lax.Precision.HIGHEST, preferred_element_type=jnp.float32)

def layer_norm(inputs, gain_row, shift_row):
    centre = inputs - lax.optimization_barrier(jnp.mean(inputs, axis=-1, keepdims=True))
    spread = lax.optimization_barrier(jnp.mean(centre * centre, axis=-1, keepdims=True))
    return centre * lax.rsqrt(spread + norm_eps) * gain_row + shift_row

def visibility(order_row, seq_row):
    slot_seq = seq_row[order_row]
    same_seq = slot_seq[:, None] == slot_seq[None, :]
    return same_seq & (order_row[None, :] <= order_row[:, None])

def attend_group(queries, key_rows, value_rows, seen):
    score_scale = HD ** (-0.5)
    query_blocks = queries.reshape(N_CTX, TOK_DEV, D)
    seen_blocks = seen.reshape(N_CTX, TOK_DEV // BLK, NBLK)

    def one_block(paired):
        query_block, seen_block = paired
        row_mask = jnp.repeat(jnp.repeat(seen_block, BLK, axis=0), BLK, axis=1)
        results = []
        for head_index in range(H):
            columns = slice(head_index * HD, (head_index + 1) * HD)
            scores = low_back(matmul(query_block[:, columns], key_rows[:, columns].T) * score_scale)
            masked = jnp.where(row_mask, scores, masked_value)
            log_mass = jax.nn.logsumexp(masked, axis=1, keepdims=True)
            weights = low(jnp.exp(masked - log_mass))
            results.append(matmul(weights, value_rows[:, columns]))
        return jnp.concatenate(results, axis=1)
    return lax.map(jax.checkpoint(one_block), (query_blocks, seen_blocks)).reshape(GROUP_TOK, D)

def forward(post_rows, summed, params, seen_all):
    query_weight, key_weight, value_weight, output_weight, query_bias, value_bias, output_bias, attend_gain, attend_shift, expand_weight, expand_bias, shrink_weight, shrink_bias, middle_gain, middle_shift, final_gain, final_shift = params
    results = []
    for group_index in range(GROUPS):
        inputs = post_rows[group_index]
        inputs_low = low(inputs)
        queries = low(low_back(matmul(inputs_low, query_weight) + query_bias))
        key_rows = low(low_back(matmul(inputs_low, key_weight)))
        value_rows = low(low_back(matmul(inputs_low, value_weight) + value_bias))
        mixed_low = low(low_back(attend_group(queries, key_rows, value_rows, seen_all[group_index])))
        branch = low_back(matmul(mixed_low, output_weight) + output_bias)
        normed_one = layer_norm(inputs + branch, attend_gain, attend_shift)
        stream_one = summed[group_index] + branch
        before = low_back(matmul(low(normed_one), expand_weight) + expand_bias)
        hidden = low(smooth_gate(before))
        feed_out = low_back(matmul(hidden, shrink_weight) + shrink_bias)
        normed_two = layer_norm(normed_one + feed_out, middle_gain, middle_shift)
        stream_two = stream_one + feed_out
        results.append(normed_two + layer_norm(stream_two, final_gain, final_shift))
    return jnp.stack(results)

def reference(post_stream, sum_stream, cotangent, block_order, block_sequence, query_weight, key_weight, value_weight, output_weight, query_bias, value_bias, output_bias, attend_gain, attend_shift, expand_weight, expand_bias, shrink_weight, shrink_bias, middle_gain, middle_shift, final_gain, final_shift):
    params = tuple((argument.astype(jnp.float32) for argument in (query_weight, key_weight, value_weight, output_weight, query_bias, value_bias, output_bias, attend_gain, attend_shift, expand_weight, expand_bias, shrink_weight, shrink_bias, middle_gain, middle_shift, final_gain, final_shift)))
    seen_all = jnp.stack([visibility(block_order[group_index], block_sequence[group_index]) for group_index in range(GROUPS)])

    def run(post_rows, summed, weights_all):
        return forward(post_rows, summed, weights_all, seen_all)
    output, pullback = jax.vjp(run, post_stream, sum_stream, params)
    gradients = pullback(cotangent)
    weight_grads = gradients[2]
    return (output, gradients[0], gradients[1], weight_grads[0], weight_grads[1], weight_grads[2], weight_grads[3], weight_grads[4], weight_grads[5], weight_grads[6], weight_grads[7], weight_grads[8], weight_grads[9], weight_grads[10], weight_grads[11], weight_grads[12], weight_grads[13], weight_grads[14], weight_grads[15], weight_grads[16])
```

```python
import functools

import jax
import jax.numpy as jnp
from jax import lax
from jax.experimental import pallas as pl
from jax.experimental.pallas import tpu as pltpu
from jax.sharding import PartitionSpec as P

D = 512
H = 8
HD = 64
BLK = 256
HALF = BLK // 2
LONG = 8
F32 = jnp.float32
BF16 = jnp.bfloat16
MESH = pl.DeviceIdType.MESH
VMEM = pl.BlockSpec(memory_space=pltpu.VMEM)
SMEM = pl.BlockSpec(memory_space=pltpu.SMEM)
ANY = pl.BlockSpec(memory_space=pl.ANY)


norm_eps = 1e-05
masked_value = -1e30
gelu_coeff = 0.7978845608
gelu_cubic = 0.044715


def smooth_gate(values):
    return (
        0.5
        * values
        * (1.0 + jnp.tanh(gelu_coeff * (values + gelu_cubic * values * values * values)))
    )


def layer_norm(inputs, gain_row, shift_row):
    centre = inputs - jnp.mean(inputs, axis=-1, keepdims=True)
    spread = jnp.mean(centre * centre, axis=-1, keepdims=True)
    return centre * lax.rsqrt(spread + norm_eps) * gain_row + shift_row


def product(left_side, right_side):
    return jnp.dot(left_side, right_side, preferred_element_type=jnp.float32)


def cross_rows(left_side, right_side):
    return lax.dot_general(
        left_side, right_side, (((0,), (0,)), ((), ())), preferred_element_type=jnp.float32
    )


def cross_cols(left_side, right_side):
    return lax.dot_general(
        left_side, right_side, (((1,), (1,)), ((), ())), preferred_element_type=jnp.float32
    )


def column_total(values):
    return jnp.sum(values, axis=0, dtype=jnp.float32)


def lookup(table_row, indices):
    places = jnp.arange(table_row.shape[0], dtype=jnp.int32)
    return jnp.sum(jnp.where(indices[:, None] == places[None, :], table_row[None, :], 0), axis=1)


def block_mask(query_blocks, query_seqs, key_blocks, key_seqs):
    same_seq = query_seqs[:, None] == key_seqs[None, :]
    return same_seq & (key_blocks[None, :] <= query_blocks[:, None])


def token_mask(visible):
    return jnp.repeat(jnp.repeat(visible, BLK, axis=0), BLK, axis=1)


def fold_units(carried, members, unit_step):
    unit_count = members[0].shape[0] // BLK
    inner_count = max((divisor for divisor in range(1, 17) if unit_count % divisor == 0))
    outer_count = unit_count // inner_count

    def outer_turn(outer_index, current):

        def inner_turn(inner_index, inner_state):
            offset = (outer_index * inner_count + inner_index) * BLK
            pieces = tuple((lax.dynamic_slice_in_dim(member, offset, BLK, 0) for member in members))
            return unit_step(inner_state, pieces, offset)

        return lax.fori_loop(0, inner_count, inner_turn, current)

    return lax.fori_loop(0, outer_count, outer_turn, carried)


def general_shards(
    post_stream,
    sum_stream,
    cotangent,
    block_order,
    block_sequence,
    query_weight,
    key_weight,
    value_weight,
    output_weight,
    query_bias,
    value_bias,
    output_bias,
    attend_gain,
    attend_shift,
    expand_weight,
    expand_bias,
    shrink_weight,
    shrink_bias,
    middle_gain,
    middle_shift,
    final_gain,
    final_shift,
):
    (
        query_whole,
        key_whole,
        value_whole,
        output_whole,
        query_add,
        value_add,
        output_add,
        gain_one,
        shift_one,
        expand_whole,
        expand_add,
        shrink_whole,
        shrink_add,
        gain_two,
        shift_two,
        gain_last,
        shift_last,
    ) = (
        lax.all_gather(query_weight, "fsdp", axis=1, tiled=True),
        lax.all_gather(key_weight, "fsdp", axis=1, tiled=True),
        lax.all_gather(value_weight, "fsdp", axis=1, tiled=True),
        lax.all_gather(output_weight, "fsdp", axis=0, tiled=True),
        lax.all_gather(query_bias, "fsdp", axis=0, tiled=True),
        lax.all_gather(value_bias, "fsdp", axis=0, tiled=True),
        lax.all_gather(output_bias, "fsdp", axis=0, tiled=True),
        lax.all_gather(attend_gain, "fsdp", axis=0, tiled=True),
        lax.all_gather(attend_shift, "fsdp", axis=0, tiled=True),
        lax.all_gather(expand_weight, "fsdp", axis=1, tiled=True),
        lax.all_gather(expand_bias, "fsdp", axis=0, tiled=True),
        lax.all_gather(shrink_weight, "fsdp", axis=0, tiled=True),
        lax.all_gather(shrink_bias, "fsdp", axis=0, tiled=True),
        lax.all_gather(middle_gain, "fsdp", axis=0, tiled=True),
        lax.all_gather(middle_shift, "fsdp", axis=0, tiled=True),
        lax.all_gather(final_gain, "fsdp", axis=0, tiled=True),
        lax.all_gather(final_shift, "fsdp", axis=0, tiled=True),
    )
    post_rows = post_stream[0]
    summed = sum_stream[0]
    tangent = cotangent[0]
    order_row = block_order[0]
    seq_row = block_sequence[0]
    token_count = post_rows.shape[0]
    score_scale = HD ** (-0.5)
    own_blocks = lax.dynamic_slice_in_dim(
        order_row, lax.axis_index("ctx") * (token_count // BLK), token_count // BLK
    )
    own_seqs = lookup(seq_row, own_blocks)
    post_low = post_rows.astype(jnp.bfloat16)
    queries = (product(post_low, query_whole) + query_add).astype(jnp.bfloat16)
    key_rows = product(post_low, key_whole).astype(jnp.bfloat16)
    value_rows = (product(post_low, value_whole) + value_add).astype(jnp.bfloat16)
    query_heads = queries.reshape(token_count, H, HD)

    def keys_visible(first_row):
        key_block = lax.dynamic_slice_in_dim(order_row, first_row // BLK, 1)
        return block_mask(own_blocks, own_seqs, key_block, lookup(seq_row, key_block))

    def masked_fold(block_step):

        def unit_step(current, pieces, first_row):
            visible = keys_visible(first_row)
            return lax.cond(
                jnp.any(visible),
                lambda inner_state: block_step(inner_state, pieces, visible),
                lambda inner_state: inner_state,
                current,
            )

        def folded(current, pieces, first_row):
            return fold_units(current, pieces, unit_step)

        return folded

    def stats_block(current, pieces, visible):
        row_peaks, masses = current
        key_heads = pieces[0].reshape(BLK, H, HD)
        row_mask = token_mask(visible)[None]
        scores = (
            jnp.einsum("qhd,khd->hqk", query_heads, key_heads, preferred_element_type=jnp.float32)
            * score_scale
        )
        new_peaks = jnp.maximum(
            row_peaks, jnp.max(jnp.where(row_mask, scores, masked_value), axis=2)
        )
        weights = jnp.where(row_mask, jnp.exp(scores - new_peaks[:, :, None]), 0.0)
        return (new_peaks, masses * jnp.exp(row_peaks - new_peaks) + jnp.sum(weights, axis=2))

    stats_fold = masked_fold(stats_block)
    stats_start = (
        jnp.full((H, token_count), masked_value, jnp.float32),
        jnp.zeros((H, token_count), jnp.float32),
    )
    row_peaks, masses = stats_fold(
        stats_start, (lax.all_gather(key_rows, "ctx", axis=0, tiled=True),), jnp.int32(0)
    )
    log_mass = row_peaks + jnp.log(masses)

    def forward_block(current, pieces, visible):
        key_heads = pieces[0].reshape(BLK, H, HD)
        value_heads = pieces[1].reshape(BLK, H, HD)
        row_mask = token_mask(visible)[None]
        scores = (
            jnp.einsum("qhd,khd->hqk", query_heads, key_heads, preferred_element_type=jnp.float32)
            * score_scale
        )
        weights = jnp.where(row_mask, jnp.exp(scores - log_mass[:, :, None]), 0.0).astype(
            jnp.bfloat16
        )
        addition = jnp.einsum(
            "hqk,khd->qhd", weights, value_heads, preferred_element_type=jnp.float32
        )
        return current + addition.reshape(token_count, D)

    forward_fold = masked_fold(forward_block)
    zero_rows = jnp.zeros((token_count, D), jnp.float32)
    attended = forward_fold(
        zero_rows,
        (
            lax.all_gather(key_rows, "ctx", axis=0, tiled=True),
            lax.all_gather(value_rows, "ctx", axis=0, tiled=True),
        ),
        jnp.int32(0),
    )
    mixed_low = attended.astype(jnp.bfloat16)
    branch = product(mixed_low, output_whole) + output_add
    normed_one, first_pull = jax.vjp(
        layer_norm, post_rows + branch, gain_one.astype(jnp.float32), shift_one.astype(jnp.float32)
    )
    stream_one = summed + branch
    normed_low = normed_one.astype(jnp.bfloat16)
    before = product(normed_low, expand_whole) + expand_add
    gated, gate_pull = jax.vjp(smooth_gate, before)
    hidden = gated.astype(jnp.bfloat16)
    feed_out = product(hidden, shrink_whole) + shrink_add
    normed_two, middle_pull = jax.vjp(
        layer_norm,
        normed_one + feed_out,
        gain_two.astype(jnp.float32),
        shift_two.astype(jnp.float32),
    )
    stream_two = stream_one + feed_out
    last_norm, last_pull = jax.vjp(
        layer_norm, stream_two, gain_last.astype(jnp.float32), shift_last.astype(jnp.float32)
    )
    layer_output = normed_two + last_norm
    stream_tan, stretch_last, nudge_last = last_pull(tangent)
    inflow_tan, stretch_two, nudge_two = middle_pull(tangent)
    feed_tan = (stream_tan + inflow_tan).astype(jnp.bfloat16)
    slope_shrink = cross_rows(hidden, feed_tan)
    drift_shrink = column_total(feed_tan)
    before_tan = gate_pull(cross_cols(feed_tan, shrink_whole))[0].astype(jnp.bfloat16)
    slope_expand = cross_rows(normed_low, before_tan)
    drift_expand = column_total(before_tan)
    normed_tan = inflow_tan + cross_cols(before_tan, expand_whole)
    feed_parts = lax.psum(
        (
            slope_expand,
            drift_expand,
            slope_shrink,
            drift_shrink,
            stretch_two,
            nudge_two,
            stretch_last,
            nudge_last,
        ),
        "ctx",
    )
    feed_sums = (
        lax.psum_scatter(feed_parts[0], "fsdp", scatter_dimension=1, tiled=True),
        lax.psum_scatter(feed_parts[1], "fsdp", scatter_dimension=0, tiled=True),
        lax.psum_scatter(feed_parts[2], "fsdp", scatter_dimension=0, tiled=True),
        lax.psum_scatter(feed_parts[3], "fsdp", scatter_dimension=0, tiled=True),
        lax.psum_scatter(feed_parts[4], "fsdp", scatter_dimension=0, tiled=True),
        lax.psum_scatter(feed_parts[5], "fsdp", scatter_dimension=0, tiled=True),
        lax.psum_scatter(feed_parts[6], "fsdp", scatter_dimension=0, tiled=True),
        lax.psum_scatter(feed_parts[7], "fsdp", scatter_dimension=0, tiled=True),
    )
    entry_tan, stretch_one, nudge_one = first_pull(normed_tan)
    branch_tan = (stream_tan + entry_tan).astype(jnp.bfloat16)
    slope_output = cross_rows(mixed_low, branch_tan)
    drift_output = column_total(branch_tan)
    mixed_tan = cross_cols(branch_tan, output_whole).astype(jnp.bfloat16)
    tangent_heads = mixed_tan.reshape(token_count, H, HD)
    deltas = jnp.sum((mixed_tan * attended).reshape(token_count, H, HD), axis=2).T

    def query_block(current, pieces, visible):
        key_heads = pieces[0].reshape(BLK, H, HD)
        value_heads = pieces[1].reshape(BLK, H, HD)
        row_mask = token_mask(visible)[None]
        scores = (
            jnp.einsum("qhd,khd->hqk", query_heads, key_heads, preferred_element_type=jnp.float32)
            * score_scale
        )
        probability = jnp.where(row_mask, jnp.exp(scores - log_mass[:, :, None]), 0.0)
        prob_tan = jnp.einsum(
            "qhd,khd->hqk", tangent_heads, value_heads, preferred_element_type=jnp.float32
        )
        score_tan = (probability * (prob_tan - deltas[:, :, None])).astype(jnp.bfloat16)
        addition = jnp.einsum(
            "hqk,khd->qhd", score_tan, key_heads, preferred_element_type=jnp.float32
        )
        return current + addition.reshape(token_count, D) * score_scale

    query_fold = masked_fold(query_block)
    query_sum = query_fold(
        zero_rows,
        (
            lax.all_gather(key_rows, "ctx", axis=0, tiled=True),
            lax.all_gather(value_rows, "ctx", axis=0, tiled=True),
        ),
        jnp.int32(0),
    )
    gathered_mass, gathered_delta = (
        lax.all_gather(log_mass.T, "ctx", axis=0, tiled=True),
        lax.all_gather(deltas.T, "ctx", axis=0, tiled=True),
    )
    own_keys = key_rows.reshape(token_count, H, HD)
    own_values = value_rows.reshape(token_count, H, HD)

    def owner_block(current, pieces, first_row, visible):
        key_acc, value_acc = current
        part_queries = pieces[0].reshape(BLK, H, HD)
        part_tangent = pieces[1].reshape(BLK, H, HD)
        part_mass = lax.dynamic_slice_in_dim(gathered_mass, first_row, BLK, 0).T
        part_delta = lax.dynamic_slice_in_dim(gathered_delta, first_row, BLK, 0).T
        row_mask = token_mask(visible)[None]
        scores = (
            jnp.einsum("qhd,khd->hqk", part_queries, own_keys, preferred_element_type=jnp.float32)
            * score_scale
        )
        probability = jnp.where(row_mask, jnp.exp(scores - part_mass[:, :, None]), 0.0)
        value_add_rows = jnp.einsum(
            "hqk,qhd->khd",
            probability.astype(jnp.bfloat16),
            part_tangent,
            preferred_element_type=jnp.float32,
        )
        prob_tan = jnp.einsum(
            "qhd,khd->hqk", part_tangent, own_values, preferred_element_type=jnp.float32
        )
        score_tan = (probability * (prob_tan - part_delta[:, :, None])).astype(jnp.bfloat16)
        key_add_rows = jnp.einsum(
            "hqk,qhd->khd", score_tan, part_queries, preferred_element_type=jnp.float32
        )
        return (
            key_acc + key_add_rows.reshape(token_count, D) * score_scale,
            value_acc + value_add_rows.reshape(token_count, D),
        )

    def owner_unit(current, pieces, first_row):
        query_blocks = lax.dynamic_slice_in_dim(order_row, first_row // BLK, 1)
        visible = block_mask(query_blocks, lookup(seq_row, query_blocks), own_blocks, own_seqs)
        return lax.cond(
            jnp.any(visible),
            lambda inner_state: owner_block(inner_state, pieces, first_row, visible),
            lambda inner_state: inner_state,
            current,
        )

    key_sum, value_sum = fold_units(
        (zero_rows, zero_rows),
        (
            lax.all_gather(queries, "ctx", axis=0, tiled=True),
            lax.all_gather(mixed_tan, "ctx", axis=0, tiled=True),
        ),
        owner_unit,
    )
    query_tan = query_sum.astype(jnp.bfloat16)
    key_tan = key_sum.astype(jnp.bfloat16)
    value_tan = value_sum.astype(jnp.bfloat16)
    slope_query = cross_rows(post_low, query_tan)
    slope_key = cross_rows(post_low, key_tan)
    slope_value = cross_rows(post_low, value_tan)
    drift_query = column_total(query_tan)
    drift_value = column_total(value_tan)
    post_tangent = (
        entry_tan
        + cross_cols(query_tan, query_whole)
        + cross_cols(key_tan, key_whole)
        + cross_cols(value_tan, value_whole)
    )
    heads_parts = lax.psum(
        (
            slope_query,
            slope_key,
            slope_value,
            slope_output,
            drift_query,
            drift_value,
            drift_output,
            stretch_one,
            nudge_one,
        ),
        "ctx",
    )
    heads_sums = (
        lax.psum_scatter(heads_parts[0], "fsdp", scatter_dimension=1, tiled=True),
        lax.psum_scatter(heads_parts[1], "fsdp", scatter_dimension=1, tiled=True),
        lax.psum_scatter(heads_parts[2], "fsdp", scatter_dimension=1, tiled=True),
        lax.psum_scatter(heads_parts[3], "fsdp", scatter_dimension=0, tiled=True),
        lax.psum_scatter(heads_parts[4], "fsdp", scatter_dimension=0, tiled=True),
        lax.psum_scatter(heads_parts[5], "fsdp", scatter_dimension=0, tiled=True),
        lax.psum_scatter(heads_parts[6], "fsdp", scatter_dimension=0, tiled=True),
        lax.psum_scatter(heads_parts[7], "fsdp", scatter_dimension=0, tiled=True),
        lax.psum_scatter(heads_parts[8], "fsdp", scatter_dimension=0, tiled=True),
    )
    return (
        layer_output[None],
        post_tangent[None],
        stream_tan[None],
        heads_sums[0],
        heads_sums[1],
        heads_sums[2],
        heads_sums[3],
        heads_sums[4],
        heads_sums[5],
        heads_sums[6],
        heads_sums[7],
        heads_sums[8],
        feed_sums[0],
        feed_sums[1],
        feed_sums[2],
        feed_sums[3],
        feed_sums[4],
        feed_sums[5],
        feed_sums[6],
        feed_sums[7],
    )


def low_lanes(values):
    return lax.broadcasted_iota(jnp.int32, values.shape, 1) < HD


def swap_lanes(values):
    return pltpu.roll(values, HD, 1)


def low_pair(first, second):
    return jnp.where(low_lanes(first), first, swap_lanes(second))


def high_pair(first, second):
    return jnp.where(low_lanes(first), swap_lanes(first), second)


def side_pair(side, first, second):
    return low_pair(first, second) if side == 0 else high_pair(first, second)


def dot_nn(left, right):
    return jnp.dot(left, right, preferred_element_type=F32)


def dot_nt(left, right):
    return lax.dot_general(left, right, (((1,), (1,)), ((), ())), preferred_element_type=F32)


def dot_tn(left, right):
    return lax.dot_general(left, right, (((0,), (0,)), ((), ())), preferred_element_type=F32)


class Place:
    def __init__(self):
        self.c = lax.axis_index("ctx")
        self.f = lax.axis_index("fsdp")
        self.group = self.c // H
        self.head = self.c % H
        self.inside = jnp.where(self.group == self.f, 1, 0)

    def is_me(self, tc, tf):
        return jnp.logical_and(self.c == tc, self.f == tf)

    def signal(self, barrier, tc, tf):
        @pl.when(jnp.logical_not(self.is_me(tc, tf)))
        def _():
            pl.semaphore_signal(barrier, 1, device_id=(tc, tf), device_id_type=MESH)

    def greet_sources(self, n_ctx, partner):
        barrier = pltpu.get_barrier_semaphore()
        for tc in range(n_ctx):
            self.signal(barrier, tc, self.group)
        if partner:
            pl.semaphore_signal(
                barrier, 1, device_id=(self.c, 1 - self.f), device_id_type=MESH
            )
        pl.semaphore_wait(barrier, 2 * H + (1 if partner else 0) - self.inside)

    def greet_owners(self, n_ctx, partner):
        barrier = pltpu.get_barrier_semaphore()
        for head in range(H):
            for core in range(2):
                self.signal(barrier, self.f * H + head, core)
        if partner:
            pl.semaphore_signal(
                barrier, 1, device_id=(self.c, 1 - self.f), device_id_type=MESH
            )
        pl.semaphore_wait(barrier, n_ctx + (1 if partner else 0) - self.inside)

    def send(self, src, dst, send_sem, recv_sem, tc, tf):
        me = self.is_me(tc, tf)

        @pl.when(me)
        def _():
            pltpu.make_async_copy(src, dst, recv_sem).start()

        @pl.when(jnp.logical_not(me))
        def _():
            self.remote(src, dst, send_sem, recv_sem, tc, tf).start()

    def remote(self, src, dst, send_sem, recv_sem, tc, tf):
        return pltpu.make_async_remote_copy(
            src_ref=src,
            dst_ref=dst,
            send_sem=send_sem,
            recv_sem=recv_sem,
            device_id=(tc, tf),
            device_id_type=MESH,
        )

    def wait_sent(self, src, dst, send_sem, recv_sem, tc, tf):
        @pl.when(jnp.logical_not(self.is_me(tc, tf)))
        def _():
            self.remote(src, dst, send_sem, recv_sem, tc, tf).wait_send()


def project_kernel(
    n_ctx,
    x_ref,
    wq_ref,
    wk_ref,
    wv_ref,
    bias_ref,
    q_out,
    kv_out,
    w_other,
    x_low,
    w_in,
    bias_in,
    q_send,
    kv_send,
    w_ss,
    w_rs,
    q_ss,
    q_rs,
    kv_ss,
    kv_rs,
    relay_ss,
    relay_rs,
):
    at = Place()
    other = 1 - at.f
    at.greet_sources(n_ctx, True)
    swaps = [
        at.remote(src, dst, w_ss.at[i], w_rs.at[i], at.c, other)
        for i, (src, dst) in enumerate(
            (
                (bias_ref, bias_in),
                (wq_ref, w_in.at[0]),
                (wk_ref, w_in.at[1]),
                (wv_ref, w_in.at[2]),
            )
        )
    ]
    for swap in swaps:
        swap.start()
    x_low[...] = x_ref[...].astype(BF16)

    def targets(half):
        for pair in range(2):
            for side in range(2):
                head = half * (H // 2) + 2 * pair + side
                for core in range(2):
                    slot = head * 2 + core
                    yield pair, side, head, core, (
                        kv_send.at[head, pl.ds(core * BLK, BLK)],
                        kv_out.at[2 * at.c + core],
                        kv_ss.at[slot],
                        kv_rs.at[at.c],
                        at.f * H + head,
                        core,
                    ), (
                        q_send.at[head, core],
                        q_out.at[at.c],
                        q_ss.at[slot],
                        q_rs.at[at.c],
                        at.f * H + head,
                        core,
                    )

    def one_half(half, wq, wk, wv, bias):
        low = x_low[...]
        q = dot_nn(low, wq[...]) + bias[0:1, :]
        k = dot_nn(low, wk[...])
        v = dot_nn(low, wv[...]) + bias[1:2, :]
        for pair, side, head, core, kv_move, q_move in targets(half):
            columns = slice(pair * 128, pair * 128 + 128)
            if core == 0:
                kv_send[head] = side_pair(side, k[:, columns], v[:, columns]).astype(BF16)
            rows = slice(core * HALF, core * HALF + HALF)
            late = slice(BLK + core * HALF, BLK + core * HALF + HALF)
            q_send[head, core] = side_pair(side, q[rows, columns], q[late, columns]).astype(BF16)
            at.send(*kv_move)
            at.send(*q_move)

    one_half(at.f, wq_ref, wk_ref, wv_ref, bias_ref)
    for swap in swaps:
        swap.wait()
    one_half(other, w_in.at[0], w_in.at[1], w_in.at[2], bias_in)
    w_other[...] = w_in[...]

    def relay(source):
        mine = kv_out.at[2 * source + at.f]
        return at.remote(mine, mine, relay_ss.at[source], relay_rs.at[source], at.c, other)

    def relay_in(source):
        theirs = kv_out.at[2 * source + other]
        return at.remote(theirs, theirs, relay_ss.at[source], relay_rs.at[source], at.c, other)

    for source in range(n_ctx):
        arrived = kv_out.at[2 * source + at.f]
        at.remote(arrived, arrived, kv_ss.at[0], kv_rs.at[source], at.c, other).wait_recv()
        relay(source).start()
    for source in range(n_ctx):
        arrived = q_out.at[source]
        at.remote(arrived, arrived, q_ss.at[0], q_rs.at[source], at.c, other).wait_recv()
        relay_in(source).wait_recv()
    for source in range(n_ctx):
        relay(source).wait_send()
    for half in (at.f, other):
        for _, _, _, _, kv_move, q_move in targets(half):
            at.wait_sent(*kv_move)
            at.wait_sent(*q_move)


def project_and_scatter(n_ctx, x, wq, wk, wv, bias):
    wide = wq.shape[1]
    return pl.pallas_call(
        functools.partial(project_kernel, n_ctx),
        out_shape=(
            jax.ShapeDtypeStruct((n_ctx, HALF, 128), BF16),
            jax.ShapeDtypeStruct((2 * n_ctx, BLK, 128), BF16),
            jax.ShapeDtypeStruct((3, D, wide), BF16),
        ),
        in_specs=[VMEM] * 5,
        out_specs=(ANY, ANY, VMEM),
        scratch_shapes=[
            pltpu.VMEM((2 * BLK, D), BF16),
            pltpu.VMEM((3, D, wide), BF16),
            pltpu.VMEM((8, wide), F32),
            pltpu.VMEM((H, 2, HALF, 128), BF16),
            pltpu.VMEM((H, 2 * BLK, 128), BF16),
            pltpu.SemaphoreType.DMA((4,)),
            pltpu.SemaphoreType.DMA((4,)),
            pltpu.SemaphoreType.DMA((2 * H,)),
            pltpu.SemaphoreType.DMA((n_ctx,)),
            pltpu.SemaphoreType.DMA((2 * H,)),
            pltpu.SemaphoreType.DMA((n_ctx,)),
            pltpu.SemaphoreType.DMA((n_ctx,)),
            pltpu.SemaphoreType.DMA((n_ctx,)),
        ],
        compiler_params=pltpu.CompilerParams(
            collective_id=0, has_side_effects=True, vmem_limit_bytes=48 << 20
        ),
        name="project_scatter",
    )(x, wq, wk, wv, bias)


def forward_kernel(
    blocks,
    order_ref,
    seq_ref,
    q_ref,
    kv_ref,
    o_ref,
    keep_ref,
    lse_ref,
    pairs_ref,
    place,
    q_low,
    peaks,
    masses,
    total,
):
    def place_block(slot, _):
        place[order_ref[slot]] = slot
        return 0

    lax.fori_loop(0, blocks, place_block, 0)

    def unpack(source, _):
        packed = q_ref[source].astype(F32) * (HD**-0.5)
        q_low[2 * source] = jnp.where(low_lanes(packed), packed, 0.0).astype(BF16)
        q_low[2 * source + 1] = jnp.where(low_lanes(packed), swap_lanes(packed), 0.0).astype(BF16)
        return 0

    lax.fori_loop(0, blocks // 2, unpack, 0)
    q_low[blocks] = jnp.zeros((HALF, 128), BF16)
    peaks[blocks] = jnp.zeros((HALF, 128), F32)
    masses[blocks] = jnp.zeros((HALF, 128), F32)
    total[blocks] = jnp.zeros((HALF, 128), F32)

    count = jnp.int32(0)
    for gap in range(1, LONG):

        def look(late, found):
            pairs_ref[0, found] = place[late]
            pairs_ref[1, found] = place[late - gap]
            return found + jnp.where(seq_ref[late] == seq_ref[late - gap], 1, 0)

        count = lax.fori_loop(gap, blocks, look, count)
    for spare in range(4):
        pairs_ref[0, count + spare] = blocks
        pairs_ref[1, count + spare] = 0
    turns = (count + 3) // 4
    pairs_ref[2, 0] = turns

    def own_blocks(step, _):
        for part in range(4):
            slot = step * 4 + part
            scores = dot_nt(q_low[slot], kv_ref[slot])
            peak = jnp.broadcast_to(jnp.max(scores, axis=1, keepdims=True), (HALF, 128))
            left = jnp.exp(scores[:, :128] - peak)
            right = jnp.exp(scores[:, 128:] - peak)
            peaks[slot] = peak
            masses[slot] = left + right
            weights = jnp.concatenate([left, right], axis=1).astype(BF16)
            total[slot] = dot_nn(weights, kv_ref[slot])
        return 0

    lax.fori_loop(0, blocks // 4, own_blocks, 0)

    def other_blocks(step, _):
        for part in range(4):
            q_slot = pairs_ref[0, step * 4 + part]
            k_slot = pairs_ref[1, step * 4 + part]
            scores = dot_nt(q_low[q_slot], kv_ref[k_slot])
            before = peaks[q_slot]
            peak = jnp.maximum(
                before, jnp.broadcast_to(jnp.max(scores, axis=1, keepdims=True), (HALF, 128))
            )
            fade = jnp.exp(before - peak)
            left = jnp.exp(scores[:, :128] - peak)
            right = jnp.exp(scores[:, 128:] - peak)
            peaks[q_slot] = peak
            masses[q_slot] = masses[q_slot] * fade + (left + right)
            weights = jnp.concatenate([left, right], axis=1).astype(BF16)
            total[q_slot] = total[q_slot] * fade + dot_nn(weights, kv_ref[k_slot])
        return 0

    lax.fori_loop(0, turns, other_blocks, 0)

    def finish(source, _):
        results = []
        for side in range(2):
            slot = 2 * source + side
            mass = jnp.broadcast_to(
                jnp.sum(masses[slot], axis=1, keepdims=True), (HALF, 128)
            )
            results.append(total[slot] / mass)
            lse_ref[slot] = jnp.transpose(peaks[slot] + jnp.log(mass))[0:8]
        packed = high_pair(results[0], results[1])
        keep_ref[source] = packed
        o_ref[source] = packed.astype(BF16)
        return 0

    lax.fori_loop(0, blocks // 2, finish, 0)


def attend(order, seqs, q, kv):
    blocks = kv.shape[0]
    pair_room = blocks * LONG
    return pl.pallas_call(
        functools.partial(forward_kernel, blocks),
        out_shape=(
            jax.ShapeDtypeStruct((blocks // 2, HALF, 128), BF16),
            jax.ShapeDtypeStruct((blocks // 2, HALF, 128), F32),
            jax.ShapeDtypeStruct((blocks, 8, HALF), F32),
            jax.ShapeDtypeStruct((3, pair_room), jnp.int32),
        ),
        in_specs=[SMEM, SMEM, VMEM, VMEM],
        out_specs=(VMEM, VMEM, VMEM, SMEM),
        scratch_shapes=[
            pltpu.SMEM((blocks,), jnp.int32),
            pltpu.VMEM((blocks + 1, HALF, 128), BF16),
            pltpu.VMEM((blocks + 1, HALF, 128), F32),
            pltpu.VMEM((blocks + 1, HALF, 128), F32),
            pltpu.VMEM((blocks + 1, HALF, 128), F32),
        ],
        compiler_params=pltpu.CompilerParams(vmem_limit_bytes=48 << 20),
        name="attend",
    )(order, seqs, q, kv)


def backward_kernel(
    blocks,
    pairs_ref,
    q_ref,
    tan_ref,
    keep_ref,
    lse_ref,
    kv_ref,
    dq_ref,
    dkv_ref,
    both,
    mass_rows,
    delta_rows,
    dq_sum,
):
    def unpack(source, _):
        packed = q_ref[source].astype(F32) * (HD**-0.5)
        tangent = tan_ref[source].astype(F32)
        low = low_lanes(packed)
        both[2 * source, 0:HALF] = jnp.where(low, packed, 0.0).astype(BF16)
        both[2 * source + 1, 0:HALF] = jnp.where(low, swap_lanes(packed), 0.0).astype(BF16)
        both[2 * source, HALF:BLK] = jnp.where(low, 0.0, swap_lanes(tangent)).astype(BF16)
        both[2 * source + 1, HALF:BLK] = jnp.where(low, 0.0, tangent).astype(BF16)
        across = jnp.transpose(tangent * keep_ref[source])
        for side in range(2):
            delta = jnp.sum(across[side * HD : side * HD + HD], axis=0, keepdims=True)
            delta_rows[2 * source + side] = jnp.broadcast_to(delta, (8, HALF))
            mass_rows[2 * source + side] = lse_ref[2 * source + side]
        return 0

    lax.fori_loop(0, blocks // 2, unpack, 0)
    both[blocks] = jnp.zeros((BLK, 128), BF16)
    mass_rows[blocks] = jnp.zeros((8, HALF), F32)
    delta_rows[blocks] = jnp.zeros((8, HALF), F32)
    dq_sum[blocks] = jnp.zeros((HALF, 128), F32)

    def one_pair(q_slot, k_slot):
        stacked = both[q_slot]
        kv = kv_ref[k_slot]
        products = dot_nt(kv, stacked)
        weights = jnp.exp(products[:, :HALF] - mass_rows[q_slot, 0:1, :])
        score_tan = (weights * (products[:, HALF:] - delta_rows[q_slot, 0:1, :])).astype(BF16)
        sides = jnp.concatenate([score_tan, weights.astype(BF16)], axis=1)
        return dot_nn(sides, stacked), dot_tn(score_tan, kv)

    def own_blocks(step, _):
        for part in range(4):
            slot = step * 4 + part
            dkv, dq = one_pair(slot, slot)
            dkv_ref[slot] = dkv
            dq_sum[slot] = dq
        return 0

    lax.fori_loop(0, blocks // 4, own_blocks, 0)

    def other_blocks(step, _):
        slots = [(pairs_ref[0, step * 4 + part], pairs_ref[1, step * 4 + part]) for part in range(4)]
        results = [one_pair(*slot) for slot in slots]
        for (q_slot, k_slot), (dkv, dq) in zip(slots, results):
            dkv_ref[k_slot] = dkv_ref[k_slot] + dkv
            dq_sum[q_slot] = dq_sum[q_slot] + dq
        return 0

    lax.fori_loop(0, pairs_ref[2, 0], other_blocks, 0)

    def finish(source, _):
        packed = low_pair(dq_sum[2 * source], dq_sum[2 * source + 1]) * (HD**-0.5)
        dq_ref[source] = packed.astype(BF16)
        return 0

    lax.fori_loop(0, blocks // 2, finish, 0)


def attend_back(pairs, q, tangent, keep, lse, kv):
    blocks = kv.shape[0]
    return pl.pallas_call(
        functools.partial(backward_kernel, blocks),
        out_shape=(
            jax.ShapeDtypeStruct((blocks // 2, HALF, 128), BF16),
            jax.ShapeDtypeStruct((blocks, BLK, 128), F32),
        ),
        in_specs=[SMEM, VMEM, VMEM, VMEM, VMEM, VMEM],
        out_specs=(VMEM, VMEM),
        scratch_shapes=[
            pltpu.VMEM((blocks + 1, BLK, 128), BF16),
            pltpu.VMEM((blocks + 1, 8, HALF), F32),
            pltpu.VMEM((blocks + 1, 8, HALF), F32),
            pltpu.VMEM((blocks + 1, HALF, 128), F32),
        ],
        compiler_params=pltpu.CompilerParams(vmem_limit_bytes=48 << 20),
        name="attend_back",
    )(pairs, q, tangent, keep, lse, kv)


def return_kernel(n_ctx, rows_ref, out_ref, ss, rs):
    at = Place()
    at.greet_owners(n_ctx, False)

    def move(target):
        return (
            rows_ref.at[target],
            out_ref.at[at.head, at.f],
            ss.at[target],
            rs.at[at.head * 2 + at.f],
            target,
            at.group,
        )

    for target in range(n_ctx):
        at.send(*move(target))
    for head in range(H):
        for core in range(2):
            arrived = out_ref.at[head, core]
            at.remote(
                arrived, arrived, ss.at[0], rs.at[head * 2 + core], at.c, 1 - at.f
            ).wait_recv()
    for target in range(n_ctx):
        at.wait_sent(*move(target))


def return_rows(n_ctx, rows):
    return pl.pallas_call(
        functools.partial(return_kernel, n_ctx),
        out_shape=jax.ShapeDtypeStruct((H, 2, HALF, 128), BF16),
        in_specs=[ANY],
        out_specs=ANY,
        scratch_shapes=[
            pltpu.SemaphoreType.DMA((n_ctx,)),
            pltpu.SemaphoreType.DMA((2 * H,)),
        ],
        compiler_params=pltpu.CompilerParams(collective_id=1, has_side_effects=True),
        name="return_rows",
    )(rows)


def scatter_kernel(n_ctx, rows_ref, out_ref, ss, rs):
    at = Place()
    at.greet_sources(n_ctx, False)

    def moves():
        for head in range(H):
            for core in range(2):
                yield (
                    rows_ref.at[head, core],
                    out_ref.at[at.c],
                    ss.at[head * 2 + core],
                    rs.at[at.c],
                    at.f * H + head,
                    core,
                )

    for move in moves():
        at.send(*move)
    for source in range(n_ctx):
        arrived = out_ref.at[source]
        at.remote(arrived, arrived, ss.at[0], rs.at[source], at.c, 1 - at.f).wait_recv()
    for move in moves():
        at.wait_sent(*move)


def scatter_rows(n_ctx, rows):
    return pl.pallas_call(
        functools.partial(scatter_kernel, n_ctx),
        out_shape=jax.ShapeDtypeStruct((n_ctx, HALF, 128), BF16),
        in_specs=[ANY],
        out_specs=ANY,
        scratch_shapes=[
            pltpu.SemaphoreType.DMA((2 * H,)),
            pltpu.SemaphoreType.DMA((n_ctx,)),
        ],
        compiler_params=pltpu.CompilerParams(collective_id=2, has_side_effects=True),
        name="scatter_rows",
    )(rows)


def return_grads_kernel(
    n_ctx, dq_ref, dkv_ref, dq_out, dkv_out, own, part, ready,
    q_ss, q_rs, kv_ss, kv_rs, part_ss, part_rs, own_sem,
):
    at = Place()
    other = 1 - at.f
    at.greet_owners(n_ctx, True)

    def partial_move(source):
        return at.remote(
            dkv_ref.at[2 * source + other],
            part.at[source],
            part_ss.at[source],
            part_rs.at[source],
            at.c,
            other,
        )

    def own_move(source):
        return pltpu.make_async_copy(
            dkv_ref.at[2 * source + at.f], own.at[source], own_sem.at[source]
        )

    def q_move(target):
        return (
            dq_ref.at[target],
            dq_out.at[at.head, at.f],
            q_ss.at[target],
            q_rs.at[at.head * 2 + at.f],
            target,
            at.group,
        )

    def kv_move(target):
        return (
            ready.at[target],
            dkv_out.at[at.head, pl.ds(pl.multiple_of(at.f * BLK, BLK), BLK)],
            kv_ss.at[target],
            kv_rs.at[at.head * 2 + at.f],
            target,
            at.group,
        )

    for source in range(n_ctx):
        partial_move(source).start()
        own_move(source).start()
    for target in range(n_ctx):
        at.send(*q_move(target))
    for source in range(n_ctx):
        own_move(source).wait()
        partial_move(source).wait_recv()
        ready[source] = (own[source] + part[source]).astype(BF16)
        at.send(*kv_move(source))
    for head in range(H):
        for core in range(2):
            slot = head * 2 + core
            arrived = dq_out.at[head, core]
            at.remote(arrived, arrived, q_ss.at[0], q_rs.at[slot], at.c, other).wait_recv()
            arrived = dkv_out.at[head, pl.ds(core * BLK, BLK)]
            at.remote(arrived, arrived, kv_ss.at[0], kv_rs.at[slot], at.c, other).wait_recv()
    for target in range(n_ctx):
        partial_move(target).wait_send()
        at.wait_sent(*q_move(target))
        at.wait_sent(*kv_move(target))


def return_grads(n_ctx, dq, dkv):
    return pl.pallas_call(
        functools.partial(return_grads_kernel, n_ctx),
        out_shape=(
            jax.ShapeDtypeStruct((H, 2, HALF, 128), BF16),
            jax.ShapeDtypeStruct((H, 2 * BLK, 128), BF16),
        ),
        in_specs=[ANY, ANY],
        out_specs=(ANY, ANY),
        scratch_shapes=[
            pltpu.VMEM((n_ctx, BLK, 128), F32),
            pltpu.VMEM((n_ctx, BLK, 128), F32),
            pltpu.VMEM((n_ctx, BLK, 128), BF16),
            pltpu.SemaphoreType.DMA((n_ctx,)),
            pltpu.SemaphoreType.DMA((2 * H,)),
            pltpu.SemaphoreType.DMA((n_ctx,)),
            pltpu.SemaphoreType.DMA((2 * H,)),
            pltpu.SemaphoreType.DMA((n_ctx,)),
            pltpu.SemaphoreType.DMA((n_ctx,)),
            pltpu.SemaphoreType.DMA((n_ctx,)),
        ],
        compiler_params=pltpu.CompilerParams(
            collective_id=3, has_side_effects=True, vmem_limit_bytes=32 << 20
        ),
        name="return_grads",
    )(dq, dkv)


COLS = 512


def whole_rows(own, other, first):
    return jnp.where(
        first,
        jnp.concatenate([own, other], axis=1),
        jnp.concatenate([other, own], axis=1),
    )


def row_mean(values):
    return jnp.mean(values, axis=1, keepdims=True)


def normalize(values):
    centre = values - row_mean(values)
    scale = lax.rsqrt(row_mean(centre * centre) + norm_eps)
    return centre * scale, scale


def norm_back(tangent, normed, scale, gain):
    pushed = tangent * gain
    return scale * (pushed - row_mean(pushed) - normed * row_mean(pushed * normed))


def column_sum(values):
    return jnp.sum(values, axis=0, keepdims=True)


def dense_kernel(
    x_ref, sum_ref, cot_ref, o_ref,
    wo_a, wo_b, we_a, we_b, ws_a, ws_b, be_a, be_b, vec_a, vec_b,
    out_ref, sum_tan_ref, entry_ref, tan_ref, own_ref, send_ref, vec_ref,
    mixed, low, hidden, slope, before_tan, feed_tan, branch_tan, mixed_tan,
):
    f = lax.axis_index("fsdp")
    first = f == 0
    wo, we, ws, be = (wo_a, wo_b), (we_a, we_b), (ws_a, ws_b), (be_a, be_b)
    halves = (f, 1 - f)
    vectors = whole_rows(vec_a[...], vec_b[...], first)
    (out_bias, gain_one, shift_one, shrink_bias, gain_two, shift_two, gain_last, shift_last) = (
        vectors[i : i + 1] for i in range(8)
    )
    for kind in range(2):
        for pair in range(2):
            head = halves[kind] * (H // 2) + 2 * pair
            for core in range(2):
                early = o_ref[head, core].astype(F32)
                late = o_ref[head + 1, core].astype(F32)
                columns = slice(pair * 128, pair * 128 + 128)
                for side in range(2):
                    start = side * BLK + core * HALF
                    mixed[kind, start : start + HALF, columns] = side_pair(
                        side, early, late
                    ).astype(BF16)
    vec_ref[...] = jnp.zeros_like(vec_ref)

    def tile(step, _):
        rows = pl.ds(pl.multiple_of(step * BLK, BLK), BLK)
        branch = (
            dot_nn(mixed[0, rows, :], wo[0][...]) + dot_nn(mixed[1, rows, :], wo[1][...]) + out_bias
        )
        n_one, scale_one = normalize(x_ref[rows, :] + branch)
        normed_one = n_one * gain_one + shift_one
        stream_one = sum_ref[rows, :] + branch
        normed_low = normed_one.astype(BF16)
        low[rows, :] = normed_low
        feed = jnp.zeros((BLK, D), F32)
        for kind in range(2):

            def expand(chunk, carried):
                columns = pl.ds(pl.multiple_of(chunk * COLS, COLS), COLS)
                v = dot_nn(normed_low, we[kind][:, columns]) + be[kind][:, columns]
                square = v * v
                t = jnp.tanh(gelu_coeff * (v + gelu_cubic * square * v))
                half_up = 0.5 + 0.5 * t
                hidden_part = (v * half_up).astype(BF16)
                hidden[kind, rows, columns] = hidden_part
                slope[kind, :, columns] = half_up + v * half_up * (1.0 - t) * (
                    gelu_coeff + (3.0 * gelu_coeff * gelu_cubic) * square
                )
                return carried + dot_nn(hidden_part, ws[kind][columns, :])

            feed = lax.fori_loop(0, ws[kind].shape[0] // COLS, expand, feed)
        feed_out = feed + shrink_bias
        n_two, scale_two = normalize(normed_one + feed_out)
        n_last, scale_last = normalize(stream_one + feed_out)
        out_ref[rows, :] = (n_two * gain_two + shift_two) + (n_last * gain_last + shift_last)
        u = cot_ref[rows, :]
        nudge = column_sum(u)
        sum_tan = norm_back(u, n_last, scale_last, gain_last)
        inflow = norm_back(u, n_two, scale_two, gain_two)
        sum_tan_ref[rows, :] = sum_tan
        feed_low = (sum_tan + inflow).astype(BF16)
        feed_tan[rows, :] = feed_low
        vec_ref[0:1, :] += column_sum(feed_low.astype(F32))
        vec_ref[1:2, :] += column_sum(u * n_two)
        vec_ref[2:3, :] += nudge
        vec_ref[3:4, :] += column_sum(u * n_last)
        vec_ref[4:5, :] += nudge
        normed_tan = inflow
        for kind in range(2):

            def expand_back(chunk, carried):
                columns = pl.ds(pl.multiple_of(chunk * COLS, COLS), COLS)
                pushed = dot_nt(feed_low, ws[kind][columns, :])
                tan_part = (pushed * slope[kind, :, columns]).astype(BF16)
                before_tan[kind, rows, columns] = tan_part
                vec_row = pl.ds(8 + 2 * halves[kind] + chunk, 1)
                vec_ref[vec_row, :] += column_sum(tan_part.astype(F32))
                return carried + dot_nt(tan_part, we[kind][:, columns])

            normed_tan = lax.fori_loop(0, ws[kind].shape[0] // COLS, expand_back, normed_tan)
        vec_ref[5:6, :] += column_sum(normed_tan * n_one)
        vec_ref[6:7, :] += column_sum(normed_tan)
        entry = norm_back(normed_tan, n_one, scale_one, gain_one)
        entry_ref[rows, :] = entry
        branch_low = (sum_tan + entry).astype(BF16)
        branch_tan[rows, :] = branch_low
        vec_ref[7:8, :] += column_sum(branch_low.astype(F32))
        for kind in range(2):
            mixed_tan[kind, rows, :] = dot_nt(branch_low, wo[kind][...])
        return 0

    lax.fori_loop(0, 2, tile, 0)

    for kind in range(2):
        for pair in range(2):
            columns = slice(pair * 128, pair * 128 + 128)
            for side in range(2):
                head = halves[kind] * (H // 2) + 2 * pair + side
                for core in range(2):
                    early = mixed_tan[kind, core * HALF : core * HALF + HALF, columns]
                    late = mixed_tan[kind, BLK + core * HALF : BLK + core * HALF + HALF, columns]
                    tan_ref[head, core] = side_pair(side, early, late).astype(BF16)

    for kind, grad_ref in enumerate((own_ref, send_ref)):
        unit_count = ws[kind].shape[0] // COLS

        def slopes(chunk, _):
            columns = pl.ds(pl.multiple_of(chunk * COLS, COLS), COLS)
            grad_ref[columns, :] = dot_tn(hidden[kind, :, columns], feed_tan[...]).astype(BF16)
            below = pl.ds(pl.multiple_of((unit_count + chunk) * COLS, COLS), COLS)
            grad_ref[below, :] = dot_tn(low[...], before_tan[kind, :, columns]).astype(BF16)
            return 0

        lax.fori_loop(0, unit_count, slopes, 0)
        grad_ref[2 * unit_count * COLS : 2 * unit_count * COLS + D // 2, :] = dot_tn(
            mixed[kind], branch_tan[...]
        ).astype(BF16)


def dense(x, summed, cotangent, o, wo, we, ws, be, vec):
    tokens = x.shape[0]
    units = ws[0].shape[0]
    grad_rows = units + units + D // 2
    return pl.pallas_call(
        dense_kernel,
        out_shape=(
            jax.ShapeDtypeStruct((tokens, D), F32),
            jax.ShapeDtypeStruct((tokens, D), F32),
            jax.ShapeDtypeStruct((tokens, D), F32),
            jax.ShapeDtypeStruct((H, 2, HALF, 128), BF16),
            jax.ShapeDtypeStruct((grad_rows, D), BF16),
            jax.ShapeDtypeStruct((grad_rows, D), BF16),
            jax.ShapeDtypeStruct((16, D), F32),
        ),
        in_specs=[VMEM] * 14,
        out_specs=(VMEM,) * 7,
        scratch_shapes=[
            pltpu.VMEM((2, tokens, D // 2), BF16),
            pltpu.VMEM((tokens, D), BF16),
            pltpu.VMEM((2, tokens, units), BF16),
            pltpu.VMEM((2, BLK, units), F32),
            pltpu.VMEM((2, tokens, units), BF16),
            pltpu.VMEM((tokens, D), BF16),
            pltpu.VMEM((tokens, D), BF16),
            pltpu.VMEM((2, tokens, D // 2), F32),
        ],
        compiler_params=pltpu.CompilerParams(vmem_limit_bytes=56 << 20),
        name="dense",
    )(x, summed, cotangent, o, *wo, *we, *ws, *be, *vec)


def last_kernel(
    x_ref, entry_ref, dq_ref, dkv_ref, wq, wk, wv, w_other,
    out_ref, own_ref, send_ref, vec_ref, tangents,
):
    f = lax.axis_index("fsdp")
    halves = (f, 1 - f)
    wide = D // 2
    vec_ref[...] = jnp.zeros_like(vec_ref)
    for kind in range(2):
        for pair in range(2):
            head = halves[kind] * (H // 2) + 2 * pair
            columns = slice(pair * 128, pair * 128 + 128)
            for core in range(2):
                early = dq_ref[head, core].astype(F32)
                late = dq_ref[head + 1, core].astype(F32)
                for side in range(2):
                    start = side * BLK + core * HALF
                    tangents[kind, 0, start : start + HALF, columns] = side_pair(
                        side, early, late
                    ).astype(BF16)
            early = dkv_ref[head].astype(F32)
            late = dkv_ref[head + 1].astype(F32)
            tangents[kind, 1, :, columns] = low_pair(early, late).astype(BF16)
            tangents[kind, 2, :, columns] = high_pair(early, late).astype(BF16)
    weights = ((wq, wk, wv), (w_other.at[0], w_other.at[1], w_other.at[2]))
    total = entry_ref[...]
    for kind in range(2):
        for which in range(3):
            total = total + dot_nt(tangents[kind, which], weights[kind][which][...])
    out_ref[...] = total
    low = x_ref[...].astype(BF16)
    for kind, grad_ref in enumerate((own_ref, send_ref)):
        grad_ref[0:D, 0:wide] = dot_tn(low, tangents[kind, 0]).astype(BF16)
        grad_ref[0:D, wide:D] = dot_tn(low, tangents[kind, 1]).astype(BF16)
        value_grad = dot_tn(low, tangents[kind, 2]).astype(BF16)
        grad_ref[D : D + wide, 0:wide] = value_grad[0:wide]
        grad_ref[D : D + wide, wide:D] = value_grad[wide:D]
        columns = pl.ds(pl.multiple_of(halves[kind] * wide, wide), wide)
        vec_ref[0:1, columns] = column_sum(tangents[kind, 0].astype(F32))
        vec_ref[1:2, columns] = column_sum(tangents[kind, 2].astype(F32))


def last_dense(x, entry, dq, dkv, wq, wk, wv, w_other):
    tokens = x.shape[0]
    grad_rows = D + D // 2
    return pl.pallas_call(
        last_kernel,
        out_shape=(
            jax.ShapeDtypeStruct((tokens, D), F32),
            jax.ShapeDtypeStruct((grad_rows, D), BF16),
            jax.ShapeDtypeStruct((grad_rows, D), BF16),
            jax.ShapeDtypeStruct((8, D), F32),
        ),
        in_specs=[VMEM] * 8,
        out_specs=(VMEM,) * 4,
        scratch_shapes=[pltpu.VMEM((2, 3, tokens, D // 2), BF16)],
        compiler_params=pltpu.CompilerParams(vmem_limit_bytes=48 << 20),
        name="last_dense",
    )(x, entry, dq, dkv, wq, wk, wv, w_other)


def reduce_kernel(rows, own_ref, send_ref, out_ref, *scratch):
    first_in, acc, stage = scratch[:3]
    landing = scratch[3:7]
    core_ss, core_rs, down_ss, down_rs, up_ss, up_rs = scratch[7:]
    at = Place()
    c, f = at.c, at.f

    def step_of(stride):
        bit = (c // stride) % 2
        return bit, c + stride * (1 - 2 * bit)

    x_step, y_step, near_z, far_z = step_of(1), step_of(2), step_of(4), step_of(8)
    plans = ((x_step, y_step, far_z, near_z), (y_step, x_step, far_z, near_z))

    barrier = pltpu.get_barrier_semaphore()
    pl.semaphore_signal(barrier, 1, device_id=(c, 1 - f), device_id_type=MESH)
    for _, peer in (x_step, y_step, near_z, far_z):
        pl.semaphore_signal(barrier, 1, device_id=(peer, f), device_id_type=MESH)
    pl.semaphore_wait(barrier, 5)

    def span(start, size):
        return pl.ds(pl.multiple_of(start, 32), size)

    def each(start, size, body):
        piece = 96 if size % 96 == 0 else 80
        lax.fori_loop(0, size // piece, lambda i, _: (body(span(start + i * piece, piece)), 0)[1], 0)

    ranges = []
    for region, plan in enumerate(plans):
        start, size, listed = region * (rows // 2), rows // 2, []
        for bit, peer in plan:
            size = size // 2
            listed.append((start + bit * size, start + (1 - bit) * size, size, peer))
            start = start + bit * size
        ranges.append(listed)

    pieces = [(0, 1), (1, 1), (0, 0), (1, 0)]

    def core_move(index):
        region, give = pieces[index]
        kept, given, size, _ = ranges[region][0]
        where = span(given if give else kept, size)
        return at.remote(
            send_ref.at[where], first_in.at[where], core_ss.at[index], core_rs.at[index], c, 1 - f
        )

    def down_move(region, step):
        _, given, size, peer = ranges[region][step]
        where = span(given, size)
        slot = region * 4 + step
        return at.remote(
            stage.at[where], landing[step].at[where], down_ss.at[slot], down_rs.at[slot], peer, f
        )

    def down_wait(region, step):
        kept, _, size, peer = ranges[region][step]
        where = span(kept, size)
        slot = region * 4 + step
        at.remote(
            stage.at[where], landing[step].at[where], down_ss.at[slot], down_rs.at[slot], peer, f
        ).wait_recv()

    def up_move(region, step):
        kept, _, size, peer = ranges[region][step]
        where = span(kept, size)
        slot = region * 4 + step
        return at.remote(
            out_ref.at[where], out_ref.at[where], up_ss.at[slot], up_rs.at[slot], peer, f
        )

    def up_wait(region, step):
        _, given, size, peer = ranges[region][step]
        where = span(given, size)
        slot = region * 4 + step
        at.remote(
            out_ref.at[where], out_ref.at[where], up_ss.at[slot], up_rs.at[slot], peer, f
        ).wait_recv()

    for index in range(4):
        core_move(index).start()
    for index, (region, give) in enumerate(pieces):
        core_move(index).wait_recv()
        kept, given, size, _ = ranges[region][0]

        def join(where, target):
            total = own_ref[where, :].astype(F32) + first_in[where, :].astype(F32)
            target[where, :] = total.astype(target.dtype)

        if give:
            each(given, size, lambda where: join(where, stage))
            down_move(region, 0).start()
        else:
            each(kept, size, lambda where: join(where, acc))
    for step in range(1, 5):
        for region in range(2):
            down_wait(region, step - 1)
            arrived = landing[step - 1]

            def join(where, target):
                total = acc[where, :] + arrived[where, :].astype(F32)
                target[where, :] = total.astype(target.dtype)

            if step < 4:
                kept, given, size, _ = ranges[region][step]
                each(given, size, lambda where: join(where, stage))
                down_move(region, step).start()
                each(kept, size, lambda where: join(where, acc))
            else:
                kept, _, size, _ = ranges[region][3]
                each(kept, size, lambda where: join(where, out_ref))
                up_move(region, 3).start()
    for step in (3, 2, 1, 0):
        for region in range(2):
            up_wait(region, step)
            if step > 0:
                up_move(region, step - 1).start()
    for index in range(4):
        core_move(index).wait_send()
    for region in range(2):
        for step in range(4):
            down_move(region, step).wait_send()
            up_move(region, step).wait_send()


def reduce_grads(own, send, ident):
    rows = own.shape[0]
    wide = (rows, D)
    return pl.pallas_call(
        functools.partial(reduce_kernel, rows),
        out_shape=jax.ShapeDtypeStruct(wide, BF16),
        in_specs=[VMEM, VMEM],
        out_specs=VMEM,
        scratch_shapes=[pltpu.VMEM(wide, BF16), pltpu.VMEM(wide, F32), pltpu.VMEM(wide, BF16)]
        + [pltpu.VMEM(wide, BF16)] * 4
        + [pltpu.SemaphoreType.DMA((4,))] * 2
        + [pltpu.SemaphoreType.DMA((8,))] * 4,
        compiler_params=pltpu.CompilerParams(
            collective_id=ident, has_side_effects=True, vmem_limit_bytes=56 << 20
        ),
        name="reduce_grads",
    )(own, send)


def head_shards(
    n_ctx,
    post_stream,
    sum_stream,
    cotangent,
    block_order,
    block_sequence,
    query_weight,
    key_weight,
    value_weight,
    output_weight,
    query_bias,
    value_bias,
    output_bias,
    attend_gain,
    attend_shift,
    expand_weight,
    expand_bias,
    shrink_weight,
    shrink_bias,
    middle_gain,
    middle_shift,
    final_gain,
    final_shift,
):
    x, summed, tangent = post_stream[0], sum_stream[0], cotangent[0]
    f = lax.axis_index("fsdp")
    swap = [(0, 1), (1, 0)]

    def from_other(values):
        return lax.ppermute(values, "fsdp", swap)

    order_both = lax.all_gather(block_order, "fsdp", axis=0, tiled=True)
    seqs_both = lax.all_gather(block_sequence, "fsdp", axis=0, tiled=True)
    group = lax.axis_index("ctx") // H
    order = lax.dynamic_slice_in_dim(order_both, group, 1, 0)[0]
    seqs = lax.dynamic_slice_in_dim(seqs_both, group, 1, 0)[0]

    bias = jnp.concatenate(
        [query_bias[None], value_bias[None], jnp.zeros((6, D // 2), BF16)], axis=0
    ).astype(F32)
    q, kv, w_other = project_and_scatter(n_ctx, x, query_weight, key_weight, value_weight, bias)
    o, keep, lse, pairs = attend(order, seqs, q, kv)
    o_rows = return_rows(n_ctx, o)
    vec = jnp.stack(
        [
            output_bias,
            attend_gain,
            attend_shift,
            shrink_bias,
            middle_gain,
            middle_shift,
            final_gain,
            final_shift,
        ]
    ).astype(F32)
    own_bias = expand_bias[None].astype(F32)
    layer_output, sum_tan, entry, tan_rows, own_feed, send_feed, vec_feed = dense(
        x,
        summed,
        tangent,
        o_rows,
        (output_weight, from_other(output_weight)),
        (expand_weight, from_other(expand_weight)),
        (shrink_weight, from_other(shrink_weight)),
        (own_bias, from_other(own_bias)),
        (vec, from_other(vec)),
    )
    tan = scatter_rows(n_ctx, tan_rows)
    dq, dkv = attend_back(pairs, q, tan, keep, lse, kv)
    dq_rows, dkv_rows = return_grads(n_ctx, dq, dkv)
    post_tangent, own_last, send_last, vec_last = last_dense(
        x, entry, dq_rows, dkv_rows, query_weight, key_weight, value_weight, w_other
    )
    grads = reduce_grads(
        jnp.concatenate([own_feed, own_last]), jnp.concatenate([send_feed, send_last]), 4
    )
    vecs = lax.psum(jnp.concatenate([vec_feed, vec_last]), ("ctx", "fsdp"))
    wide = D // 2
    units = shrink_weight.shape[0]

    def mine(row):
        return lax.dynamic_slice_in_dim(vecs[row], f * wide, wide)

    shrink_slope = grads[0:units].astype(F32)
    expand_slope = jnp.concatenate(
        [grads[units + i * D : units + i * D + D] for i in range(units // D)], axis=1
    ).astype(F32)
    after = 2 * units
    output_slope = grads[after : after + wide].astype(F32)
    after = after + wide
    query_slope = grads[after : after + D, 0:wide].astype(F32)
    key_slope = grads[after : after + D, wide:D].astype(F32)
    value_slope = jnp.concatenate(
        [grads[after + D : after + D + wide, 0:wide], grads[after + D : after + D + wide, wide:D]]
    ).astype(F32)
    expand_drift = lax.dynamic_slice_in_dim(vecs[8:12].reshape(4 * D), f * units, units)
    return (
        layer_output[None],
        post_tangent[None],
        sum_tan[None],
        query_slope,
        key_slope,
        value_slope,
        output_slope,
        mine(16),
        mine(17),
        mine(7),
        mine(5),
        mine(6),
        expand_slope,
        expand_drift,
        shrink_slope,
        mine(0),
        mine(1),
        mine(2),
        mine(3),
        mine(4),
    )


def solution(mesh):
    n_ctx, n_fsdp = mesh.shape["ctx"], mesh.shape["fsdp"]
    if n_fsdp == 2 and n_ctx == n_fsdp * H:
        body = functools.partial(head_shards, n_ctx)
    else:
        body = general_shards
    return jax.shard_map(
        body,
        mesh=mesh,
        in_specs=(
            P("fsdp", "ctx", None),
            P("fsdp", "ctx", None),
            P("fsdp", "ctx", None),
            P("fsdp", None),
            P("fsdp", None),
            P(None, "fsdp"),
            P(None, "fsdp"),
            P(None, "fsdp"),
            P("fsdp", None),
            P("fsdp"),
            P("fsdp"),
            P("fsdp"),
            P("fsdp"),
            P("fsdp"),
            P(None, "fsdp"),
            P("fsdp"),
            P("fsdp", None),
            P("fsdp"),
            P("fsdp"),
            P("fsdp"),
            P("fsdp"),
            P("fsdp"),
        ),
        out_specs=(
            P("fsdp", "ctx", None),
            P("fsdp", "ctx", None),
            P("fsdp", "ctx", None),
            P(None, "fsdp"),
            P(None, "fsdp"),
            P(None, "fsdp"),
            P("fsdp", None),
            P("fsdp"),
            P("fsdp"),
            P("fsdp"),
            P("fsdp"),
            P("fsdp"),
            P(None, "fsdp"),
            P("fsdp"),
            P("fsdp", None),
            P("fsdp"),
            P("fsdp"),
            P("fsdp"),
            P("fsdp"),
            P("fsdp"),
        ),
        check_vma=False,
    )
```

```python
import functools

import jax
import jax.numpy as jnp
from jax import lax
from jax.experimental import pallas as pl
from jax.experimental.pallas import tpu as pltpu
from jax.sharding import PartitionSpec as P

D = 512
H = 8
HD = 64
BLK = 256
HALF = BLK // 2
LONG = 8
TOGETHER = 16
BACK_TOGETHER = 8
MOST = LONG + 1
F32 = jnp.float32
BF16 = jnp.bfloat16
MESH = pl.DeviceIdType.MESH
VMEM = pl.BlockSpec(memory_space=pltpu.VMEM)
SMEM = pl.BlockSpec(memory_space=pltpu.SMEM)
ANY = pl.BlockSpec(memory_space=pl.ANY)


norm_eps = 1e-05
masked_value = -1e30
gelu_coeff = 0.7978845608
gelu_cubic = 0.044715


def smooth_gate(values):
    return (
        0.5
        * values
        * (1.0 + jnp.tanh(gelu_coeff * (values + gelu_cubic * values * values * values)))
    )


def layer_norm(inputs, gain_row, shift_row):
    centre = inputs - jnp.mean(inputs, axis=-1, keepdims=True)
    spread = jnp.mean(centre * centre, axis=-1, keepdims=True)
    return centre * lax.rsqrt(spread + norm_eps) * gain_row + shift_row


def product(left_side, right_side):
    return jnp.dot(left_side, right_side, preferred_element_type=jnp.float32)


def cross_rows(left_side, right_side):
    return lax.dot_general(
        left_side, right_side, (((0,), (0,)), ((), ())), preferred_element_type=jnp.float32
    )


def cross_cols(left_side, right_side):
    return lax.dot_general(
        left_side, right_side, (((1,), (1,)), ((), ())), preferred_element_type=jnp.float32
    )


def column_total(values):
    return jnp.sum(values, axis=0, dtype=jnp.float32)


def lookup(table_row, indices):
    places = jnp.arange(table_row.shape[0], dtype=jnp.int32)
    return jnp.sum(jnp.where(indices[:, None] == places[None, :], table_row[None, :], 0), axis=1)


def block_mask(query_blocks, query_seqs, key_blocks, key_seqs):
    same_seq = query_seqs[:, None] == key_seqs[None, :]
    return same_seq & (key_blocks[None, :] <= query_blocks[:, None])


def token_mask(visible):
    return jnp.repeat(jnp.repeat(visible, BLK, axis=0), BLK, axis=1)


def fold_units(carried, members, unit_step):
    unit_count = members[0].shape[0] // BLK
    inner_count = max((divisor for divisor in range(1, 17) if unit_count % divisor == 0))
    outer_count = unit_count // inner_count

    def outer_turn(outer_index, current):

        def inner_turn(inner_index, inner_state):
            offset = (outer_index * inner_count + inner_index) * BLK
            pieces = tuple((lax.dynamic_slice_in_dim(member, offset, BLK, 0) for member in members))
            return unit_step(inner_state, pieces, offset)

        return lax.fori_loop(0, inner_count, inner_turn, current)

    return lax.fori_loop(0, outer_count, outer_turn, carried)


def general_shards(
    post_stream,
    sum_stream,
    cotangent,
    block_order,
    block_sequence,
    query_weight,
    key_weight,
    value_weight,
    output_weight,
    query_bias,
    value_bias,
    output_bias,
    attend_gain,
    attend_shift,
    expand_weight,
    expand_bias,
    shrink_weight,
    shrink_bias,
    middle_gain,
    middle_shift,
    final_gain,
    final_shift,
):
    (
        query_whole,
        key_whole,
        value_whole,
        output_whole,
        query_add,
        value_add,
        output_add,
        gain_one,
        shift_one,
        expand_whole,
        expand_add,
        shrink_whole,
        shrink_add,
        gain_two,
        shift_two,
        gain_last,
        shift_last,
    ) = (
        lax.all_gather(query_weight, "fsdp", axis=1, tiled=True),
        lax.all_gather(key_weight, "fsdp", axis=1, tiled=True),
        lax.all_gather(value_weight, "fsdp", axis=1, tiled=True),
        lax.all_gather(output_weight, "fsdp", axis=0, tiled=True),
        lax.all_gather(query_bias, "fsdp", axis=0, tiled=True),
        lax.all_gather(value_bias, "fsdp", axis=0, tiled=True),
        lax.all_gather(output_bias, "fsdp", axis=0, tiled=True),
        lax.all_gather(attend_gain, "fsdp", axis=0, tiled=True),
        lax.all_gather(attend_shift, "fsdp", axis=0, tiled=True),
        lax.all_gather(expand_weight, "fsdp", axis=1, tiled=True),
        lax.all_gather(expand_bias, "fsdp", axis=0, tiled=True),
        lax.all_gather(shrink_weight, "fsdp", axis=0, tiled=True),
        lax.all_gather(shrink_bias, "fsdp", axis=0, tiled=True),
        lax.all_gather(middle_gain, "fsdp", axis=0, tiled=True),
        lax.all_gather(middle_shift, "fsdp", axis=0, tiled=True),
        lax.all_gather(final_gain, "fsdp", axis=0, tiled=True),
        lax.all_gather(final_shift, "fsdp", axis=0, tiled=True),
    )
    post_rows = post_stream[0]
    summed = sum_stream[0]
    tangent = cotangent[0]
    order_row = block_order[0]
    seq_row = block_sequence[0]
    token_count = post_rows.shape[0]
    score_scale = HD ** (-0.5)
    own_blocks = lax.dynamic_slice_in_dim(
        order_row, lax.axis_index("ctx") * (token_count // BLK), token_count // BLK
    )
    own_seqs = lookup(seq_row, own_blocks)
    post_low = post_rows.astype(jnp.bfloat16)
    queries = (product(post_low, query_whole) + query_add).astype(jnp.bfloat16)
    key_rows = product(post_low, key_whole).astype(jnp.bfloat16)
    value_rows = (product(post_low, value_whole) + value_add).astype(jnp.bfloat16)
    query_heads = queries.reshape(token_count, H, HD)

    def keys_visible(first_row):
        key_block = lax.dynamic_slice_in_dim(order_row, first_row // BLK, 1)
        return block_mask(own_blocks, own_seqs, key_block, lookup(seq_row, key_block))

    def masked_fold(block_step):

        def unit_step(current, pieces, first_row):
            visible = keys_visible(first_row)
            return lax.cond(
                jnp.any(visible),
                lambda inner_state: block_step(inner_state, pieces, visible),
                lambda inner_state: inner_state,
                current,
            )

        def folded(current, pieces, first_row):
            return fold_units(current, pieces, unit_step)

        return folded

    def stats_block(current, pieces, visible):
        row_peaks, masses = current
        key_heads = pieces[0].reshape(BLK, H, HD)
        row_mask = token_mask(visible)[None]
        scores = (
            jnp.einsum("qhd,khd->hqk", query_heads, key_heads, preferred_element_type=jnp.float32)
            * score_scale
        )
        new_peaks = jnp.maximum(
            row_peaks, jnp.max(jnp.where(row_mask, scores, masked_value), axis=2)
        )
        weights = jnp.where(row_mask, jnp.exp(scores - new_peaks[:, :, None]), 0.0)
        return (new_peaks, masses * jnp.exp(row_peaks - new_peaks) + jnp.sum(weights, axis=2))

    stats_fold = masked_fold(stats_block)
    stats_start = (
        jnp.full((H, token_count), masked_value, jnp.float32),
        jnp.zeros((H, token_count), jnp.float32),
    )
    row_peaks, masses = stats_fold(
        stats_start, (lax.all_gather(key_rows, "ctx", axis=0, tiled=True),), jnp.int32(0)
    )
    log_mass = row_peaks + jnp.log(masses)

    def forward_block(current, pieces, visible):
        key_heads = pieces[0].reshape(BLK, H, HD)
        value_heads = pieces[1].reshape(BLK, H, HD)
        row_mask = token_mask(visible)[None]
        scores = (
            jnp.einsum("qhd,khd->hqk", query_heads, key_heads, preferred_element_type=jnp.float32)
            * score_scale
        )
        weights = jnp.where(row_mask, jnp.exp(scores - log_mass[:, :, None]), 0.0).astype(
            jnp.bfloat16
        )
        addition = jnp.einsum(
            "hqk,khd->qhd", weights, value_heads, preferred_element_type=jnp.float32
        )
        return current + addition.reshape(token_count, D)

    forward_fold = masked_fold(forward_block)
    zero_rows = jnp.zeros((token_count, D), jnp.float32)
    attended = forward_fold(
        zero_rows,
        (
            lax.all_gather(key_rows, "ctx", axis=0, tiled=True),
            lax.all_gather(value_rows, "ctx", axis=0, tiled=True),
        ),
        jnp.int32(0),
    )
    mixed_low = attended.astype(jnp.bfloat16)
    branch = product(mixed_low, output_whole) + output_add
    normed_one, first_pull = jax.vjp(
        layer_norm, post_rows + branch, gain_one.astype(jnp.float32), shift_one.astype(jnp.float32)
    )
    stream_one = summed + branch
    normed_low = normed_one.astype(jnp.bfloat16)
    before = product(normed_low, expand_whole) + expand_add
    gated, gate_pull = jax.vjp(smooth_gate, before)
    hidden = gated.astype(jnp.bfloat16)
    feed_out = product(hidden, shrink_whole) + shrink_add
    normed_two, middle_pull = jax.vjp(
        layer_norm,
        normed_one + feed_out,
        gain_two.astype(jnp.float32),
        shift_two.astype(jnp.float32),
    )
    stream_two = stream_one + feed_out
    last_norm, last_pull = jax.vjp(
        layer_norm, stream_two, gain_last.astype(jnp.float32), shift_last.astype(jnp.float32)
    )
    layer_output = normed_two + last_norm
    stream_tan, stretch_last, nudge_last = last_pull(tangent)
    inflow_tan, stretch_two, nudge_two = middle_pull(tangent)
    feed_tan = (stream_tan + inflow_tan).astype(jnp.bfloat16)
    slope_shrink = cross_rows(hidden, feed_tan)
    drift_shrink = column_total(feed_tan)
    before_tan = gate_pull(cross_cols(feed_tan, shrink_whole))[0].astype(jnp.bfloat16)
    slope_expand = cross_rows(normed_low, before_tan)
    drift_expand = column_total(before_tan)
    normed_tan = inflow_tan + cross_cols(before_tan, expand_whole)
    feed_parts = lax.psum(
        (
            slope_expand,
            drift_expand,
            slope_shrink,
            drift_shrink,
            stretch_two,
            nudge_two,
            stretch_last,
            nudge_last,
        ),
        "ctx",
    )
    feed_sums = (
        lax.psum_scatter(feed_parts[0], "fsdp", scatter_dimension=1, tiled=True),
        lax.psum_scatter(feed_parts[1], "fsdp", scatter_dimension=0, tiled=True),
        lax.psum_scatter(feed_parts[2], "fsdp", scatter_dimension=0, tiled=True),
        lax.psum_scatter(feed_parts[3], "fsdp", scatter_dimension=0, tiled=True),
        lax.psum_scatter(feed_parts[4], "fsdp", scatter_dimension=0, tiled=True),
        lax.psum_scatter(feed_parts[5], "fsdp", scatter_dimension=0, tiled=True),
        lax.psum_scatter(feed_parts[6], "fsdp", scatter_dimension=0, tiled=True),
        lax.psum_scatter(feed_parts[7], "fsdp", scatter_dimension=0, tiled=True),
    )
    entry_tan, stretch_one, nudge_one = first_pull(normed_tan)
    branch_tan = (stream_tan + entry_tan).astype(jnp.bfloat16)
    slope_output = cross_rows(mixed_low, branch_tan)
    drift_output = column_total(branch_tan)
    mixed_tan = cross_cols(branch_tan, output_whole).astype(jnp.bfloat16)
    tangent_heads = mixed_tan.reshape(token_count, H, HD)
    deltas = jnp.sum((mixed_tan * attended).reshape(token_count, H, HD), axis=2).T

    def query_block(current, pieces, visible):
        key_heads = pieces[0].reshape(BLK, H, HD)
        value_heads = pieces[1].reshape(BLK, H, HD)
        row_mask = token_mask(visible)[None]
        scores = (
            jnp.einsum("qhd,khd->hqk", query_heads, key_heads, preferred_element_type=jnp.float32)
            * score_scale
        )
        probability = jnp.where(row_mask, jnp.exp(scores - log_mass[:, :, None]), 0.0)
        prob_tan = jnp.einsum(
            "qhd,khd->hqk", tangent_heads, value_heads, preferred_element_type=jnp.float32
        )
        score_tan = (probability * (prob_tan - deltas[:, :, None])).astype(jnp.bfloat16)
        addition = jnp.einsum(
            "hqk,khd->qhd", score_tan, key_heads, preferred_element_type=jnp.float32
        )
        return current + addition.reshape(token_count, D) * score_scale

    query_fold = masked_fold(query_block)
    query_sum = query_fold(
        zero_rows,
        (
            lax.all_gather(key_rows, "ctx", axis=0, tiled=True),
            lax.all_gather(value_rows, "ctx", axis=0, tiled=True),
        ),
        jnp.int32(0),
    )
    gathered_mass, gathered_delta = (
        lax.all_gather(log_mass.T, "ctx", axis=0, tiled=True),
        lax.all_gather(deltas.T, "ctx", axis=0, tiled=True),
    )
    own_keys = key_rows.reshape(token_count, H, HD)
    own_values = value_rows.reshape(token_count, H, HD)

    def owner_block(current, pieces, first_row, visible):
        key_acc, value_acc = current
        part_queries = pieces[0].reshape(BLK, H, HD)
        part_tangent = pieces[1].reshape(BLK, H, HD)
        part_mass = lax.dynamic_slice_in_dim(gathered_mass, first_row, BLK, 0).T
        part_delta = lax.dynamic_slice_in_dim(gathered_delta, first_row, BLK, 0).T
        row_mask = token_mask(visible)[None]
        scores = (
            jnp.einsum("qhd,khd->hqk", part_queries, own_keys, preferred_element_type=jnp.float32)
            * score_scale
        )
        probability = jnp.where(row_mask, jnp.exp(scores - part_mass[:, :, None]), 0.0)
        value_add_rows = jnp.einsum(
            "hqk,qhd->khd",
            probability.astype(jnp.bfloat16),
            part_tangent,
            preferred_element_type=jnp.float32,
        )
        prob_tan = jnp.einsum(
            "qhd,khd->hqk", part_tangent, own_values, preferred_element_type=jnp.float32
        )
        score_tan = (probability * (prob_tan - part_delta[:, :, None])).astype(jnp.bfloat16)
        key_add_rows = jnp.einsum(
            "hqk,qhd->khd", score_tan, part_queries, preferred_element_type=jnp.float32
        )
        return (
            key_acc + key_add_rows.reshape(token_count, D) * score_scale,
            value_acc + value_add_rows.reshape(token_count, D),
        )

    def owner_unit(current, pieces, first_row):
        query_blocks = lax.dynamic_slice_in_dim(order_row, first_row // BLK, 1)
        visible = block_mask(query_blocks, lookup(seq_row, query_blocks), own_blocks, own_seqs)
        return lax.cond(
            jnp.any(visible),
            lambda inner_state: owner_block(inner_state, pieces, first_row, visible),
            lambda inner_state: inner_state,
            current,
        )

    key_sum, value_sum = fold_units(
        (zero_rows, zero_rows),
        (
            lax.all_gather(queries, "ctx", axis=0, tiled=True),
            lax.all_gather(mixed_tan, "ctx", axis=0, tiled=True),
        ),
        owner_unit,
    )
    query_tan = query_sum.astype(jnp.bfloat16)
    key_tan = key_sum.astype(jnp.bfloat16)
    value_tan = value_sum.astype(jnp.bfloat16)
    slope_query = cross_rows(post_low, query_tan)
    slope_key = cross_rows(post_low, key_tan)
    slope_value = cross_rows(post_low, value_tan)
    drift_query = column_total(query_tan)
    drift_value = column_total(value_tan)
    post_tangent = (
        entry_tan
        + cross_cols(query_tan, query_whole)
        + cross_cols(key_tan, key_whole)
        + cross_cols(value_tan, value_whole)
    )
    heads_parts = lax.psum(
        (
            slope_query,
            slope_key,
            slope_value,
            slope_output,
            drift_query,
            drift_value,
            drift_output,
            stretch_one,
            nudge_one,
        ),
        "ctx",
    )
    heads_sums = (
        lax.psum_scatter(heads_parts[0], "fsdp", scatter_dimension=1, tiled=True),
        lax.psum_scatter(heads_parts[1], "fsdp", scatter_dimension=1, tiled=True),
        lax.psum_scatter(heads_parts[2], "fsdp", scatter_dimension=1, tiled=True),
        lax.psum_scatter(heads_parts[3], "fsdp", scatter_dimension=0, tiled=True),
        lax.psum_scatter(heads_parts[4], "fsdp", scatter_dimension=0, tiled=True),
        lax.psum_scatter(heads_parts[5], "fsdp", scatter_dimension=0, tiled=True),
        lax.psum_scatter(heads_parts[6], "fsdp", scatter_dimension=0, tiled=True),
        lax.psum_scatter(heads_parts[7], "fsdp", scatter_dimension=0, tiled=True),
        lax.psum_scatter(heads_parts[8], "fsdp", scatter_dimension=0, tiled=True),
    )
    return (
        layer_output[None],
        post_tangent[None],
        stream_tan[None],
        heads_sums[0],
        heads_sums[1],
        heads_sums[2],
        heads_sums[3],
        heads_sums[4],
        heads_sums[5],
        heads_sums[6],
        heads_sums[7],
        heads_sums[8],
        feed_sums[0],
        feed_sums[1],
        feed_sums[2],
        feed_sums[3],
        feed_sums[4],
        feed_sums[5],
        feed_sums[6],
        feed_sums[7],
    )


def low_lanes(values):
    return lax.broadcasted_iota(jnp.int32, values.shape, 1) < HD


def swap_lanes(values):
    return pltpu.roll(values, HD, 1)


def low_pair(first, second):
    return jnp.where(low_lanes(first), first, swap_lanes(second))


def high_pair(first, second):
    return jnp.where(low_lanes(first), swap_lanes(first), second)


def side_pair(side, first, second):
    return low_pair(first, second) if side == 0 else high_pair(first, second)


def dot_nn(left, right):
    return jnp.dot(left, right, preferred_element_type=F32)


def dot_nt(left, right):
    return lax.dot_general(left, right, (((1,), (1,)), ((), ())), preferred_element_type=F32)


def dot_tn(left, right):
    return lax.dot_general(left, right, (((0,), (0,)), ((), ())), preferred_element_type=F32)


class Place:
    def __init__(self):
        self.c = lax.axis_index("ctx")
        self.f = lax.axis_index("fsdp")
        self.group = self.c // H
        self.head = self.c % H
        self.inside = jnp.where(self.group == self.f, 1, 0)

    def is_me(self, tc, tf):
        return jnp.logical_and(self.c == tc, self.f == tf)

    def signal(self, barrier, tc, tf):
        @pl.when(jnp.logical_not(self.is_me(tc, tf)))
        def _():
            pl.semaphore_signal(barrier, 1, device_id=(tc, tf), device_id_type=MESH)

    def greet_sources(self, n_ctx, partner):
        barrier = pltpu.get_barrier_semaphore()
        for tc in range(n_ctx):
            self.signal(barrier, tc, self.group)
        if partner:
            pl.semaphore_signal(
                barrier, 1, device_id=(self.c, 1 - self.f), device_id_type=MESH
            )
        pl.semaphore_wait(barrier, 2 * H + (1 if partner else 0) - self.inside)

    def greet_owners(self, n_ctx, partner, more=0):
        barrier = pltpu.get_barrier_semaphore()
        for head in range(H):
            for core in range(2):
                self.signal(barrier, self.f * H + head, core)
        if partner:
            pl.semaphore_signal(
                barrier, 1, device_id=(self.c, 1 - self.f), device_id_type=MESH
            )
        pl.semaphore_wait(barrier, n_ctx + (1 if partner else 0) + more - self.inside)

    def send(self, src, dst, send_sem, recv_sem, tc, tf):
        me = self.is_me(tc, tf)

        @pl.when(me)
        def _():
            pltpu.make_async_copy(src, dst, recv_sem).start()

        @pl.when(jnp.logical_not(me))
        def _():
            self.remote(src, dst, send_sem, recv_sem, tc, tf).start()

    def remote(self, src, dst, send_sem, recv_sem, tc, tf):
        return pltpu.make_async_remote_copy(
            src_ref=src,
            dst_ref=dst,
            send_sem=send_sem,
            recv_sem=recv_sem,
            device_id=(tc, tf),
            device_id_type=MESH,
        )

    def wait_sent(self, src, dst, send_sem, recv_sem, tc, tf):
        @pl.when(jnp.logical_not(self.is_me(tc, tf)))
        def _():
            self.remote(src, dst, send_sem, recv_sem, tc, tf).wait_send()


BIAS_ROWS = 16


def project_kernel(
    n_ctx,
    x_ref,
    wq_ref,
    wk_ref,
    wv_ref,
    order_ref,
    seq_ref,
    expand_ref,
    *rest,
):
    vector_refs, rest = rest[:10], rest[10:]
    (
        q_out,
        kv_out,
        w_other,
        order_out,
        seq_out,
        vec_out,
        expand_out,
        x_low,
        w_in,
        bias_own,
        bias_in,
        order_in,
        seq_in,
        q_send,
        kv_send,
        w_ss,
        w_rs,
        q_ss,
        q_rs,
        kv_ss,
        kv_rs,
        relay_ss,
        relay_rs,
    ) = rest
    at = Place()
    other = 1 - at.f
    wide = wq_ref.shape[1]
    for row, ref in enumerate(vector_refs):
        bias_own[row : row + 1, :] = ref[...].astype(F32)
    for part in range(expand_ref.shape[1] // wide):
        row = len(vector_refs) + part
        bias_own[row : row + 1, :] = expand_ref[:, part * wide : part * wide + wide].astype(F32)
    at.greet_sources(n_ctx, True)
    swaps = [
        at.remote(src, dst, w_ss.at[i], w_rs.at[i], at.c, other)
        for i, (src, dst) in enumerate(
            (
                (bias_own, bias_in),
                (wq_ref, w_in.at[0]),
                (wk_ref, w_in.at[1]),
                (wv_ref, w_in.at[2]),
                (order_ref, order_in),
                (seq_ref, seq_in),
            )
        )
    ]
    for swap in swaps:
        swap.start()
    x_low[...] = x_ref[...].astype(BF16)

    def targets(half):
        for pair in range(2):
            for side in range(2):
                head = half * (H // 2) + 2 * pair + side
                for core in range(2):
                    slot = head * 2 + core
                    yield pair, side, head, core, (
                        kv_send.at[head, pl.ds(core * BLK, BLK)],
                        kv_out.at[2 * at.c + core],
                        kv_ss.at[slot],
                        kv_rs.at[at.c],
                        at.f * H + head,
                        core,
                    ), (
                        q_send.at[head, core],
                        q_out.at[at.c],
                        q_ss.at[slot],
                        q_rs.at[at.c],
                        at.f * H + head,
                        core,
                    )

    def one_half(half, wq, wk, wv, bias):
        low = x_low[...]
        q = dot_nn(low, wq[...]) + bias[0:1, :]
        k = dot_nn(low, wk[...])
        v = dot_nn(low, wv[...]) + bias[1:2, :]
        for pair, side, head, core, kv_move, q_move in targets(half):
            columns = slice(pair * 128, pair * 128 + 128)
            if core == 0:
                kv_send[head] = side_pair(side, k[:, columns], v[:, columns]).astype(BF16)
            rows = slice(core * HALF, core * HALF + HALF)
            late = slice(BLK + core * HALF, BLK + core * HALF + HALF)
            q_send[head, core] = side_pair(side, q[rows, columns], q[late, columns]).astype(BF16)
            at.send(*kv_move)
            at.send(*q_move)

    one_half(at.f, wq_ref, wk_ref, wv_ref, bias_own)
    for swap in swaps:
        swap.wait()
    one_half(other, w_in.at[0], w_in.at[1], w_in.at[2], bias_in)
    w_other[...] = w_in[...]
    inside = at.inside == 1
    order_out[...] = jnp.where(inside, order_ref[...], order_in[...])
    seq_out[...] = jnp.where(inside, seq_ref[...], seq_in[...])
    vec_out[...] = whole_rows(bias_own[...], bias_in[...], at.f == 0)
    for row, source in enumerate((bias_own, bias_in)):
        for part in range(expand_ref.shape[1] // wide):
            at_row = len(vector_refs) + part
            expand_out[row : row + 1, part * wide : part * wide + wide] = source[
                at_row : at_row + 1, :
            ]

    def relay(source):
        mine = kv_out.at[2 * source + at.f]
        return at.remote(mine, mine, relay_ss.at[source], relay_rs.at[source], at.c, other)

    def relay_in(source):
        theirs = kv_out.at[2 * source + other]
        return at.remote(theirs, theirs, relay_ss.at[source], relay_rs.at[source], at.c, other)

    for source in range(n_ctx):
        arrived = kv_out.at[2 * source + at.f]
        at.remote(arrived, arrived, kv_ss.at[0], kv_rs.at[source], at.c, other).wait_recv()
        relay(source).start()
    for source in range(n_ctx):
        arrived = q_out.at[source]
        at.remote(arrived, arrived, q_ss.at[0], q_rs.at[source], at.c, other).wait_recv()
        relay_in(source).wait_recv()
    for source in range(n_ctx):
        relay(source).wait_send()
    for half in (at.f, other):
        for _, _, _, _, kv_move, q_move in targets(half):
            at.wait_sent(*kv_move)
            at.wait_sent(*q_move)


def project_and_scatter(n_ctx, x, wq, wk, wv, order, seqs, expand, vectors):
    wide = wq.shape[1]
    blocks = order.shape[1]
    return pl.pallas_call(
        functools.partial(project_kernel, n_ctx),
        out_shape=(
            jax.ShapeDtypeStruct((n_ctx, HALF, 128), BF16),
            jax.ShapeDtypeStruct((2 * n_ctx, BLK, 128), BF16),
            jax.ShapeDtypeStruct((3, D, wide), BF16),
            jax.ShapeDtypeStruct((1, blocks), jnp.int32),
            jax.ShapeDtypeStruct((1, blocks), jnp.int32),
            jax.ShapeDtypeStruct((BIAS_ROWS, D), F32),
            jax.ShapeDtypeStruct((2, expand.shape[1]), F32),
        ),
        in_specs=[VMEM] * 17,
        out_specs=(ANY, ANY) + (VMEM,) * 5,
        scratch_shapes=[
            pltpu.VMEM((2 * BLK, D), BF16),
            pltpu.VMEM((3, D, wide), BF16),
            pltpu.VMEM((BIAS_ROWS, wide), F32),
            pltpu.VMEM((BIAS_ROWS, wide), F32),
            pltpu.VMEM((1, blocks), jnp.int32),
            pltpu.VMEM((1, blocks), jnp.int32),
            pltpu.VMEM((H, 2, HALF, 128), BF16),
            pltpu.VMEM((H, 2 * BLK, 128), BF16),
            pltpu.SemaphoreType.DMA((6,)),
            pltpu.SemaphoreType.DMA((6,)),
            pltpu.SemaphoreType.DMA((2 * H,)),
            pltpu.SemaphoreType.DMA((n_ctx,)),
            pltpu.SemaphoreType.DMA((2 * H,)),
            pltpu.SemaphoreType.DMA((n_ctx,)),
            pltpu.SemaphoreType.DMA((n_ctx,)),
            pltpu.SemaphoreType.DMA((n_ctx,)),
        ],
        compiler_params=pltpu.CompilerParams(
            collective_id=0, has_side_effects=True, vmem_limit_bytes=48 << 20
        ),
        name="project_scatter",
    )(x, wq, wk, wv, order, seqs, expand, *vectors)


def forward_kernel(
    blocks,
    order_ref,
    seq_ref,
    q_ref,
    kv_ref,
    o_ref,
    keep_ref,
    lse_ref,
    pairs_ref,
    place,
    q_low,
    peaks,
    masses,
    total,
    scores,
):
    def place_block(slot, _):
        place[order_ref[0, slot]] = slot
        return 0

    lax.fori_loop(0, blocks, place_block, 0)

    count = jnp.int32(0)
    for gap in range(LONG):

        def look(late, found):
            pairs_ref[0, found] = place[late]
            pairs_ref[1, found] = place[late - gap]
            return found + jnp.where(seq_ref[0, late] == seq_ref[0, late - gap], 1, 0)

        count = lax.fori_loop(gap, blocks, look, count)
    for spare in range(TOGETHER):
        pairs_ref[0, count + spare] = blocks
        pairs_ref[1, count + spare] = 0
    turns = (count + TOGETHER - 1) // TOGETHER
    pairs_ref[2, 1] = (count + BACK_TOGETHER - 1) // BACK_TOGETHER

    def unpack(step, _):
        for part in range(4):
            source = step * 4 + part
            packed = q_ref[source].astype(F32) * (HD**-0.5)
            low = low_lanes(packed)
            q_low[2 * source] = jnp.where(low, packed, 0.0).astype(BF16)
            q_low[2 * source + 1] = jnp.where(low, swap_lanes(packed), 0.0).astype(BF16)
        return 0

    lax.fori_loop(0, blocks // 8, unpack, 0)
    q_low[blocks] = jnp.zeros((HALF, 128), BF16)

    def clear(slot, _):
        peaks[slot] = jnp.full((HALF, 128), masked_value, F32)
        masses[slot] = jnp.zeros((HALF, 128), F32)
        total[slot] = jnp.zeros((HALF, 128), F32)
        return 0

    lax.fori_loop(0, blocks + 1, clear, 0)

    def score(step, _):
        slots, results = [], []
        for part in range(TOGETHER):
            index = step * TOGETHER + part
            q_slot = pairs_ref[0, index]
            result = dot_nt(q_low[q_slot], kv_ref[pairs_ref[1, index]])
            scores[index] = result
            slots.append(q_slot)
            results.append(jnp.maximum(result[:, :128], result[:, 128:]))
        for q_slot, result in zip(slots, results):
            peaks[q_slot] = jnp.maximum(peaks[q_slot], result)
        return 0

    lax.fori_loop(0, turns, score, 0)

    def level(step, _):
        for part in range(4):
            slot = step * 4 + part
            peaks[slot] = jnp.broadcast_to(
                jnp.max(peaks[slot], axis=1, keepdims=True), (HALF, 128)
            )
        return 0

    lax.fori_loop(0, blocks // 4, level, 0)

    def weigh(step, _):
        slots, results = [], []
        for part in range(TOGETHER):
            index = step * TOGETHER + part
            q_slot = pairs_ref[0, index]
            peak = peaks[q_slot]
            left = jnp.exp(scores[index, :, :128] - peak)
            right = jnp.exp(scores[index, :, 128:] - peak)
            weights = jnp.concatenate([left, right], axis=1).astype(BF16)
            slots.append(q_slot)
            results.append((left + right, dot_nn(weights, kv_ref[pairs_ref[1, index]])))
        for q_slot, (mass, part_total) in zip(slots, results):
            masses[q_slot] = masses[q_slot] + mass
            total[q_slot] = total[q_slot] + part_total
        return 0

    lax.fori_loop(0, turns, weigh, 0)

    def finish(step, _):
        for part in range(4):
            source = step * 4 + part
            results = []
            for side in range(2):
                slot = 2 * source + side
                mass = jnp.broadcast_to(
                    jnp.sum(masses[slot], axis=1, keepdims=True), (HALF, 128)
                )
                results.append(total[slot] / mass)
                lse_ref[slot] = jnp.transpose(peaks[slot] + jnp.log(mass))[0:8]
            packed = high_pair(results[0], results[1])
            keep_ref[source] = packed
            o_ref[source] = packed.astype(BF16)
        return 0

    lax.fori_loop(0, blocks // 8, finish, 0)


def pair_room(blocks):
    return blocks * MOST // 2 + TOGETHER


def attend(order, seqs, q, kv):
    blocks = kv.shape[0]
    room = pair_room(blocks)
    return pl.pallas_call(
        functools.partial(forward_kernel, blocks),
        out_shape=(
            jax.ShapeDtypeStruct((blocks // 2, HALF, 128), BF16),
            jax.ShapeDtypeStruct((blocks // 2, HALF, 128), F32),
            jax.ShapeDtypeStruct((blocks, 8, HALF), F32),
            jax.ShapeDtypeStruct((3, room), jnp.int32),
        ),
        in_specs=[SMEM, SMEM, VMEM, VMEM],
        out_specs=(VMEM, VMEM, VMEM, SMEM),
        scratch_shapes=[
            pltpu.SMEM((blocks,), jnp.int32),
            pltpu.VMEM((blocks + 1, HALF, 128), BF16),
            pltpu.VMEM((blocks + 1, HALF, 128), F32),
            pltpu.VMEM((blocks + 1, HALF, 128), F32),
            pltpu.VMEM((blocks + 1, HALF, 128), F32),
            pltpu.VMEM((room, HALF, BLK), F32),
        ],
        compiler_params=pltpu.CompilerParams(vmem_limit_bytes=48 << 20),
        name="attend",
    )(order, seqs, q, kv)


def backward_kernel(
    blocks,
    pairs_ref,
    q_ref,
    tan_ref,
    keep_ref,
    lse_ref,
    kv_ref,
    dq_ref,
    dkv_ref,
    both,
    mass_rows,
    delta_rows,
    dq_sum,
):
    def unpack(step, _):
        for part in range(4):
            source = step * 4 + part
            packed = q_ref[source].astype(F32) * (HD**-0.5)
            tangent = tan_ref[source].astype(F32)
            low = low_lanes(packed)
            both[2 * source, 0:HALF] = jnp.where(low, packed, 0.0).astype(BF16)
            both[2 * source + 1, 0:HALF] = jnp.where(low, swap_lanes(packed), 0.0).astype(BF16)
            both[2 * source, HALF:BLK] = jnp.where(low, 0.0, swap_lanes(tangent)).astype(BF16)
            both[2 * source + 1, HALF:BLK] = jnp.where(low, 0.0, tangent).astype(BF16)
            across = jnp.transpose(tangent * keep_ref[source])
            for side in range(2):
                delta = jnp.sum(across[side * HD : side * HD + HD], axis=0, keepdims=True)
                delta_rows[2 * source + side] = jnp.broadcast_to(delta, (8, HALF))
                mass_rows[2 * source + side] = lse_ref[2 * source + side]
        return 0

    lax.fori_loop(0, blocks // 8, unpack, 0)
    both[blocks] = jnp.zeros((BLK, 128), BF16)
    mass_rows[blocks] = jnp.zeros((8, HALF), F32)
    delta_rows[blocks] = jnp.zeros((8, HALF), F32)

    def clear(slot, _):
        dq_sum[slot] = jnp.zeros((HALF, 128), F32)
        dkv_ref[slot] = jnp.zeros((BLK, 128), F32)
        return 0

    lax.fori_loop(0, blocks, clear, 0)
    dq_sum[blocks] = jnp.zeros((HALF, 128), F32)

    def one_pair(q_slot, k_slot):
        stacked = both[q_slot]
        kv = kv_ref[k_slot]
        products = dot_nt(kv, stacked)
        weights = jnp.exp(products[:, :HALF] - mass_rows[q_slot, 0:1, :])
        score_tan = (weights * (products[:, HALF:] - delta_rows[q_slot, 0:1, :])).astype(BF16)
        sides = jnp.concatenate([score_tan, weights.astype(BF16)], axis=1)
        return dot_nn(sides, stacked), dot_tn(score_tan, kv)

    def pair_turn(step, _):
        slots = [
            (pairs_ref[0, step * BACK_TOGETHER + part], pairs_ref[1, step * BACK_TOGETHER + part])
            for part in range(BACK_TOGETHER)
        ]
        results = [one_pair(*slot) for slot in slots]
        for (q_slot, k_slot), (dkv, dq) in zip(slots, results):
            dkv_ref[k_slot] = dkv_ref[k_slot] + dkv
            dq_sum[q_slot] = dq_sum[q_slot] + dq
        return 0

    lax.fori_loop(0, pairs_ref[2, 1], pair_turn, 0)

    def finish(step, _):
        for part in range(4):
            source = step * 4 + part
            packed = low_pair(dq_sum[2 * source], dq_sum[2 * source + 1]) * (HD**-0.5)
            dq_ref[source] = packed.astype(BF16)
        return 0

    lax.fori_loop(0, blocks // 8, finish, 0)


def attend_back(pairs, q, tangent, keep, lse, kv):
    blocks = kv.shape[0]
    return pl.pallas_call(
        functools.partial(backward_kernel, blocks),
        out_shape=(
            jax.ShapeDtypeStruct((blocks // 2, HALF, 128), BF16),
            jax.ShapeDtypeStruct((blocks, BLK, 128), F32),
        ),
        in_specs=[SMEM, VMEM, VMEM, VMEM, VMEM, VMEM],
        out_specs=(VMEM, VMEM),
        scratch_shapes=[
            pltpu.VMEM((blocks + 1, BLK, 128), BF16),
            pltpu.VMEM((blocks + 1, 8, HALF), F32),
            pltpu.VMEM((blocks + 1, 8, HALF), F32),
            pltpu.VMEM((blocks + 1, HALF, 128), F32),
        ],
        compiler_params=pltpu.CompilerParams(vmem_limit_bytes=48 << 20),
        name="attend_back",
    )(pairs, q, tangent, keep, lse, kv)


def return_kernel(n_ctx, rows_ref, out_ref, ss, rs):
    at = Place()
    at.greet_owners(n_ctx, False)

    def move(target):
        return (
            rows_ref.at[target],
            out_ref.at[at.head, at.f],
            ss.at[target],
            rs.at[at.head * 2 + at.f],
            target,
            at.group,
        )

    for target in range(n_ctx):
        at.send(*move(target))
    for head in range(H):
        for core in range(2):
            arrived = out_ref.at[head, core]
            at.remote(
                arrived, arrived, ss.at[0], rs.at[head * 2 + core], at.c, 1 - at.f
            ).wait_recv()
    for target in range(n_ctx):
        at.wait_sent(*move(target))


def return_rows(n_ctx, rows):
    return pl.pallas_call(
        functools.partial(return_kernel, n_ctx),
        out_shape=jax.ShapeDtypeStruct((H, 2, HALF, 128), BF16),
        in_specs=[ANY],
        out_specs=ANY,
        scratch_shapes=[
            pltpu.SemaphoreType.DMA((n_ctx,)),
            pltpu.SemaphoreType.DMA((2 * H,)),
        ],
        compiler_params=pltpu.CompilerParams(collective_id=1, has_side_effects=True),
        name="return_rows",
    )(rows)


def pieces_of(start, size, body):
    piece = max(n for n in range(16, 97, 16) if size % n == 0)
    lax.fori_loop(
        0,
        size // piece,
        lambda i, _: (body(i * piece, span(start + i * piece, piece), piece), 0)[1],
        0,
    )


def span(start, size):
    return pl.ds(pl.multiple_of(start, 16), size)


def step_of(c, stride):
    bit = (c // stride) % 2
    return bit, c + stride * (1 - 2 * bit)


def scatter_kernel(
    n_ctx, rows_ref, own_ref, send_ref, out_ref, stage_a, stage_b, keep_ref, first_in,
    ss, rs, core_ss, core_rs,
):
    at = Place()
    at.greet_sources(n_ctx, True)
    quarter = own_ref.shape[0] // 4
    bits = (step_of(at.c, 1)[0], step_of(at.c, 2)[0])
    stages = (stage_a, stage_b)

    def moves():
        for head in range(H):
            for core in range(2):
                yield (
                    rows_ref.at[head, core],
                    out_ref.at[at.c],
                    ss.at[head * 2 + core],
                    rs.at[at.c],
                    at.f * H + head,
                    core,
                )

    def core_move(region, give):
        bit = bits[region]
        start = region * 2 * quarter + (1 - bit if give else bit) * quarter
        where = span(start, quarter)
        slot = region + 2 * (0 if give else 1)
        return start, at.remote(
            send_ref.at[where], first_in.at[where], core_ss.at[slot], core_rs.at[slot],
            at.c, 1 - at.f,
        )

    order = [(0, True), (1, True), (0, False), (1, False)]
    for step in order:
        core_move(*step)[1].start()
    for move in moves():
        at.send(*move)
    for region, give in order:
        start, move = core_move(region, give)
        move.wait_recv()

        def join(offset, where, size):
            total = own_ref[where, :].astype(F32) + first_in[where, :].astype(F32)
            if give:
                stages[region][span(offset, size), :] = total.astype(BF16)
            else:
                keep_ref[region, span(offset, size), :] = total

        pieces_of(start, quarter, join)
    for source in range(n_ctx):
        arrived = out_ref.at[source]
        at.remote(arrived, arrived, ss.at[0], rs.at[source], at.c, 1 - at.f).wait_recv()
    for move in moves():
        at.wait_sent(*move)
    for step in order:
        core_move(*step)[1].wait_send()


def scatter_rows(n_ctx, rows, own, send):
    grad_rows = own.shape[0]
    return pl.pallas_call(
        functools.partial(scatter_kernel, n_ctx),
        out_shape=(
            jax.ShapeDtypeStruct((n_ctx, HALF, 128), BF16),
            jax.ShapeDtypeStruct((grad_rows // 4, D), BF16),
            jax.ShapeDtypeStruct((grad_rows // 4, D), BF16),
            jax.ShapeDtypeStruct((2, grad_rows // 4, D), F32),
        ),
        in_specs=[ANY, VMEM, ANY],
        out_specs=(ANY, VMEM, VMEM, VMEM),
        scratch_shapes=[
            pltpu.VMEM((grad_rows, D), BF16),
            pltpu.SemaphoreType.DMA((2 * H,)),
            pltpu.SemaphoreType.DMA((n_ctx,)),
            pltpu.SemaphoreType.DMA((4,)),
            pltpu.SemaphoreType.DMA((4,)),
        ],
        compiler_params=pltpu.CompilerParams(
            collective_id=2, has_side_effects=True, vmem_limit_bytes=32 << 20
        ),
        name="scatter_rows",
    )(rows, own, send)


class Ladder:
    def __init__(self, at, plans, starts, size, acc, stage, landing, out, sems):
        self.at, self.acc, self.stage, self.landing, self.out = at, acc, stage, landing, out
        self.down_ss, self.down_rs, self.up_ss, self.up_rs = sems
        self.ranges = []
        for plan, start in zip(plans, starts):
            listed, rows = [], size
            for bit, peer in plan[:-1]:
                rows = rows // 2
                listed.append((start + bit * rows, start + (1 - bit) * rows, rows, peer))
                start = start + bit * rows
            listed.append((start, start, rows, plan[-1][1]))
            self.ranges.append(listed)
        self.last = len(plans[0]) - 1

    def slot(self, region, step):
        return region * (self.last + 1) + step

    def down(self, region, step, sent):
        kept, given, size, peer = self.ranges[region][step]
        where, slot = span(given if sent else kept, size), self.slot(region, step)
        return self.at.remote(
            self.stage[region].at[where],
            self.landing[region][step].at[where],
            self.down_ss.at[slot],
            self.down_rs.at[slot],
            peer,
            self.at.f,
        )

    def up(self, region, step, sent):
        kept, given, size, peer = self.ranges[region][step]
        where, slot = span(kept if sent else given, size), self.slot(region, step)
        return self.at.remote(
            self.out[region].at[where],
            self.out[region].at[where],
            self.up_ss.at[slot],
            self.up_rs.at[slot],
            peer,
            self.at.f,
        )

    def join(self, region, start, size, arrived, target):
        def body(offset, where, _):
            total = self.acc[region][where, :]
            if arrived is not None:
                total = total + arrived[where, :].astype(F32)
            target[where, :] = total.astype(target.dtype)

        pieces_of(start, size, body)

    def give(self, region, step, arrived):
        kept, given, size, _ = self.ranges[region][step]
        self.join(region, given, size, arrived, self.stage[region])
        self.down(region, step, True).start()
        if step < self.last:
            self.join(region, kept, size, arrived, self.acc[region])

    def settle(self, region):
        kept, _, size, _ = self.ranges[region][self.last]
        arrived = self.landing[region][self.last]

        def body(offset, where, _):
            total = self.stage[region][where, :].astype(F32) + arrived[where, :].astype(F32)
            self.out[region][where, :] = total.astype(BF16)

        self.down(region, self.last, False).wait_recv()
        pieces_of(kept, size, body)
        self.up(region, self.last - 1, True).start()

    def wait_sent(self):
        for region in range(2):
            for step in range(self.last + 1):
                self.down(region, step, True).wait_send()
            for step in range(self.last):
                self.up(region, step, True).wait_send()


def return_grads_kernel(
    n_ctx, dq_ref, dkv_ref, keep_ref, land_a, land_b, dq_out, dkv_out, done_ref,
    own, part, ready, acc, stage, landing,
    q_ss, q_rs, kv_ss, kv_rs, part_ss, part_rs, own_sem, down_ss, down_rs, up_ss, up_rs,
):
    at = Place()
    other = 1 - at.f
    x_step, y_step, near, far = (step_of(at.c, stride) for stride in (1, 2, 4, 8))
    barrier = pltpu.get_barrier_semaphore()
    for _, peer in (x_step, y_step, near, far):
        pl.semaphore_signal(barrier, 1, device_id=(peer, at.f), device_id_type=MESH)
    at.greet_owners(n_ctx, True, 4)

    def partial_move(source):
        return at.remote(
            dkv_ref.at[2 * source + other],
            part.at[source],
            part_ss.at[source],
            part_rs.at[source],
            at.c,
            other,
        )

    def own_move(source):
        return pltpu.make_async_copy(
            dkv_ref.at[2 * source + at.f], own.at[source], own_sem.at[source]
        )

    def q_move(target):
        return (
            dq_ref.at[target],
            dq_out.at[at.head, at.f],
            q_ss.at[target],
            q_rs.at[at.head * 2 + at.f],
            target,
            at.group,
        )

    def kv_move(target):
        return (
            ready.at[target],
            dkv_out.at[at.head, pl.ds(pl.multiple_of(at.f * BLK, BLK), BLK)],
            kv_ss.at[target],
            kv_rs.at[at.head * 2 + at.f],
            target,
            at.group,
        )

    size = keep_ref.shape[1]
    ladder = Ladder(
        at,
        ((y_step, near, far), (x_step, near, far)),
        (0, 0),
        size,
        [acc.at[region] for region in range(2)],
        [stage.at[region] for region in range(2)],
        [[landing.at[region, step] for step in range(3)] for region in range(2)],
        [done_ref.at[region] for region in range(2)],
        (down_ss, down_rs, up_ss, up_rs),
    )
    for source in range(n_ctx):
        partial_move(source).start()
        own_move(source).start()
    for region, first_in in enumerate((land_a, land_b)):
        ladder.acc[region] = keep_ref.at[region]
        kept, given, half, _ = ladder.ranges[region][0]
        ladder.join(region, given, half, first_in, stage.at[region])
        ladder.down(region, 0, True).start()
        ladder.join(region, kept, half, first_in, acc.at[region])
        ladder.acc[region] = acc.at[region]
    for target in range(n_ctx):
        at.send(*q_move(target))
    for source in range(n_ctx):
        own_move(source).wait()
        partial_move(source).wait_recv()
        ready[source] = (own[source] + part[source]).astype(BF16)
        at.send(*kv_move(source))
    for step in (1, 2):
        for region in range(2):
            ladder.down(region, step - 1, False).wait_recv()
            ladder.give(region, step, ladder.landing[region][step - 1])
    for region in range(2):
        ladder.settle(region)
    for region in range(2):
        ladder.up(region, 1, False).wait_recv()
        ladder.up(region, 0, True).start()
    for region in range(2):
        ladder.up(region, 0, False).wait_recv()
    for head in range(H):
        for core in range(2):
            slot = head * 2 + core
            arrived = dq_out.at[head, core]
            at.remote(arrived, arrived, q_ss.at[0], q_rs.at[slot], at.c, other).wait_recv()
            arrived = dkv_out.at[head, pl.ds(core * BLK, BLK)]
            at.remote(arrived, arrived, kv_ss.at[0], kv_rs.at[slot], at.c, other).wait_recv()
    for target in range(n_ctx):
        partial_move(target).wait_send()
        at.wait_sent(*q_move(target))
        at.wait_sent(*kv_move(target))
    ladder.wait_sent()


def return_grads(n_ctx, dq, dkv, keep, land_a, land_b):
    size = keep.shape[1]
    return pl.pallas_call(
        functools.partial(return_grads_kernel, n_ctx),
        out_shape=(
            jax.ShapeDtypeStruct((H, 2, HALF, 128), BF16),
            jax.ShapeDtypeStruct((H, 2 * BLK, 128), BF16),
            jax.ShapeDtypeStruct((2, size, D), BF16),
        ),
        in_specs=[ANY, ANY, VMEM, VMEM, VMEM],
        out_specs=(ANY, ANY, VMEM),
        scratch_shapes=[
            pltpu.VMEM((n_ctx, BLK, 128), F32),
            pltpu.VMEM((n_ctx, BLK, 128), F32),
            pltpu.VMEM((n_ctx, BLK, 128), BF16),
            pltpu.VMEM((2, size, D), F32),
            pltpu.VMEM((2, size, D), BF16),
            pltpu.VMEM((2, 3, size, D), BF16),
            pltpu.SemaphoreType.DMA((n_ctx,)),
            pltpu.SemaphoreType.DMA((2 * H,)),
            pltpu.SemaphoreType.DMA((n_ctx,)),
            pltpu.SemaphoreType.DMA((2 * H,)),
            pltpu.SemaphoreType.DMA((n_ctx,)),
            pltpu.SemaphoreType.DMA((n_ctx,)),
            pltpu.SemaphoreType.DMA((n_ctx,)),
            pltpu.SemaphoreType.DMA((6,)),
            pltpu.SemaphoreType.DMA((6,)),
            pltpu.SemaphoreType.DMA((6,)),
            pltpu.SemaphoreType.DMA((6,)),
        ],
        compiler_params=pltpu.CompilerParams(
            collective_id=3, has_side_effects=True, vmem_limit_bytes=40 << 20
        ),
        name="return_grads",
    )(dq, dkv, keep, land_a, land_b)


COLS = 512


def whole_rows(own, other, first):
    return jnp.where(
        first,
        jnp.concatenate([own, other], axis=1),
        jnp.concatenate([other, own], axis=1),
    )


def row_mean(values):
    return jnp.mean(values, axis=1, keepdims=True)


def normalize(values):
    centre = values - row_mean(values)
    scale = lax.rsqrt(row_mean(centre * centre) + norm_eps)
    return centre * scale, scale


def norm_back(tangent, normed, scale, gain):
    pushed = tangent * gain
    return scale * (pushed - row_mean(pushed) - normed * row_mean(pushed * normed))


def column_sum(values):
    return jnp.sum(values, axis=0, keepdims=True)


def dense_kernel(
    x_ref, sum_ref, cot_ref, o_ref,
    wo_a, wo_b, we_a, we_b, ws_a, ws_b, be_ref, vec_in,
    out_ref, sum_tan_ref, entry_ref, tan_ref, own_ref, send_ref, vec_ref,
    mixed, low, hidden, slope, before_tan, feed_tan, branch_tan, mixed_tan,
):
    f = lax.axis_index("fsdp")
    wo, we, ws = (wo_a, wo_b), (we_a, we_b), (ws_a, ws_b)
    be = (be_ref.at[0:1], be_ref.at[1:2])
    halves = (f, 1 - f)
    vectors = vec_in[...]
    (out_bias, gain_one, shift_one, shrink_bias, gain_two, shift_two, gain_last, shift_last) = (
        vectors[i : i + 1] for i in range(2, 10)
    )
    for kind in range(2):
        for pair in range(2):
            head = halves[kind] * (H // 2) + 2 * pair
            for core in range(2):
                early = o_ref[head, core].astype(F32)
                late = o_ref[head + 1, core].astype(F32)
                columns = slice(pair * 128, pair * 128 + 128)
                for side in range(2):
                    start = side * BLK + core * HALF
                    mixed[kind, start : start + HALF, columns] = side_pair(
                        side, early, late
                    ).astype(BF16)
    vec_ref[...] = jnp.zeros_like(vec_ref)

    def tile(step, _):
        rows = pl.ds(pl.multiple_of(step * BLK, BLK), BLK)
        branch = (
            dot_nn(mixed[0, rows, :], wo[0][...]) + dot_nn(mixed[1, rows, :], wo[1][...]) + out_bias
        )
        n_one, scale_one = normalize(x_ref[rows, :] + branch)
        normed_one = n_one * gain_one + shift_one
        stream_one = sum_ref[rows, :] + branch
        normed_low = normed_one.astype(BF16)
        low[rows, :] = normed_low
        feed = jnp.zeros((BLK, D), F32)
        for kind in range(2):

            def expand(chunk, carried):
                columns = pl.ds(pl.multiple_of(chunk * COLS, COLS), COLS)
                v = dot_nn(normed_low, we[kind][:, columns]) + be[kind][:, columns]
                square = v * v
                t = jnp.tanh(gelu_coeff * (v + gelu_cubic * square * v))
                half_up = 0.5 + 0.5 * t
                hidden_part = (v * half_up).astype(BF16)
                hidden[kind, rows, columns] = hidden_part
                slope[kind, :, columns] = half_up + v * half_up * (1.0 - t) * (
                    gelu_coeff + (3.0 * gelu_coeff * gelu_cubic) * square
                )
                return carried + dot_nn(hidden_part, ws[kind][columns, :])

            feed = lax.fori_loop(0, ws[kind].shape[0] // COLS, expand, feed)
        feed_out = feed + shrink_bias
        n_two, scale_two = normalize(normed_one + feed_out)
        n_last, scale_last = normalize(stream_one + feed_out)
        out_ref[rows, :] = (n_two * gain_two + shift_two) + (n_last * gain_last + shift_last)
        u = cot_ref[rows, :]
        nudge = column_sum(u)
        sum_tan = norm_back(u, n_last, scale_last, gain_last)
        inflow = norm_back(u, n_two, scale_two, gain_two)
        sum_tan_ref[rows, :] = sum_tan
        feed_low = (sum_tan + inflow).astype(BF16)
        feed_tan[rows, :] = feed_low
        vec_ref[0:1, :] += column_sum(feed_low.astype(F32))
        vec_ref[1:2, :] += column_sum(u * n_two)
        vec_ref[2:3, :] += nudge
        vec_ref[3:4, :] += column_sum(u * n_last)
        vec_ref[4:5, :] += nudge
        normed_tan = inflow
        for kind in range(2):

            def expand_back(chunk, carried):
                columns = pl.ds(pl.multiple_of(chunk * COLS, COLS), COLS)
                pushed = dot_nt(feed_low, ws[kind][columns, :])
                tan_part = (pushed * slope[kind, :, columns]).astype(BF16)
                before_tan[kind, rows, columns] = tan_part
                vec_row = pl.ds(8 + 2 * halves[kind] + chunk, 1)
                vec_ref[vec_row, :] += column_sum(tan_part.astype(F32))
                return carried + dot_nt(tan_part, we[kind][:, columns])

            normed_tan = lax.fori_loop(0, ws[kind].shape[0] // COLS, expand_back, normed_tan)
        vec_ref[5:6, :] += column_sum(normed_tan * n_one)
        vec_ref[6:7, :] += column_sum(normed_tan)
        entry = norm_back(normed_tan, n_one, scale_one, gain_one)
        entry_ref[rows, :] = entry
        branch_low = (sum_tan + entry).astype(BF16)
        branch_tan[rows, :] = branch_low
        vec_ref[7:8, :] += column_sum(branch_low.astype(F32))
        for kind in range(2):
            mixed_tan[kind, rows, :] = dot_nt(branch_low, wo[kind][...])
        return 0

    lax.fori_loop(0, 2, tile, 0)

    for kind in range(2):
        for pair in range(2):
            columns = slice(pair * 128, pair * 128 + 128)
            for side in range(2):
                head = halves[kind] * (H // 2) + 2 * pair + side
                for core in range(2):
                    early = mixed_tan[kind, core * HALF : core * HALF + HALF, columns]
                    late = mixed_tan[kind, BLK + core * HALF : BLK + core * HALF + HALF, columns]
                    tan_ref[head, core] = side_pair(side, early, late).astype(BF16)

    for kind, grad_ref in enumerate((own_ref, send_ref)):
        unit_count = ws[kind].shape[0] // COLS

        def slopes(chunk, _):
            columns = pl.ds(pl.multiple_of(chunk * COLS, COLS), COLS)
            grad_ref[columns, :] = dot_tn(hidden[kind, :, columns], feed_tan[...]).astype(BF16)
            below = pl.ds(pl.multiple_of((unit_count + chunk) * COLS, COLS), COLS)
            grad_ref[below, :] = dot_tn(low[...], before_tan[kind, :, columns]).astype(BF16)
            return 0

        lax.fori_loop(0, unit_count, slopes, 0)
        grad_ref[2 * unit_count * COLS : 2 * unit_count * COLS + D // 2, :] = dot_tn(
            mixed[kind], branch_tan[...]
        ).astype(BF16)


def dense(x, summed, cotangent, o, wo, we, ws, be, vec):
    tokens = x.shape[0]
    units = ws[0].shape[0]
    grad_rows = units + units + D // 2
    return pl.pallas_call(
        dense_kernel,
        out_shape=(
            jax.ShapeDtypeStruct((tokens, D), F32),
            jax.ShapeDtypeStruct((tokens, D), F32),
            jax.ShapeDtypeStruct((tokens, D), F32),
            jax.ShapeDtypeStruct((H, 2, HALF, 128), BF16),
            jax.ShapeDtypeStruct((grad_rows, D), BF16),
            jax.ShapeDtypeStruct((grad_rows, D), BF16),
            jax.ShapeDtypeStruct((16, D), F32),
        ),
        in_specs=[VMEM] * 12,
        out_specs=(VMEM,) * 7,
        scratch_shapes=[
            pltpu.VMEM((2, tokens, D // 2), BF16),
            pltpu.VMEM((tokens, D), BF16),
            pltpu.VMEM((2, tokens, units), BF16),
            pltpu.VMEM((2, BLK, units), F32),
            pltpu.VMEM((2, tokens, units), BF16),
            pltpu.VMEM((tokens, D), BF16),
            pltpu.VMEM((tokens, D), BF16),
            pltpu.VMEM((2, tokens, D // 2), F32),
        ],
        compiler_params=pltpu.CompilerParams(vmem_limit_bytes=56 << 20),
        name="dense",
    )(x, summed, cotangent, o, *wo, *we, *ws, be, vec)


def last_kernel(
    x_ref, entry_ref, dq_ref, dkv_ref, wq, wk, wv, w_other,
    out_ref, own_ref, send_ref, vec_ref, tangents,
):
    f = lax.axis_index("fsdp")
    halves = (f, 1 - f)
    wide = D // 2
    vec_ref[...] = jnp.zeros_like(vec_ref)
    for kind in range(2):
        for pair in range(2):
            head = halves[kind] * (H // 2) + 2 * pair
            columns = slice(pair * 128, pair * 128 + 128)
            for core in range(2):
                early = dq_ref[head, core].astype(F32)
                late = dq_ref[head + 1, core].astype(F32)
                for side in range(2):
                    start = side * BLK + core * HALF
                    tangents[kind, 0, start : start + HALF, columns] = side_pair(
                        side, early, late
                    ).astype(BF16)
            early = dkv_ref[head].astype(F32)
            late = dkv_ref[head + 1].astype(F32)
            tangents[kind, 1, :, columns] = low_pair(early, late).astype(BF16)
            tangents[kind, 2, :, columns] = high_pair(early, late).astype(BF16)
    weights = ((wq, wk, wv), (w_other.at[0], w_other.at[1], w_other.at[2]))
    total = entry_ref[...]
    for kind in range(2):
        for which in range(3):
            total = total + dot_nt(tangents[kind, which], weights[kind][which][...])
    out_ref[...] = total
    low = x_ref[...].astype(BF16)
    for kind, grad_ref in enumerate((own_ref, send_ref)):
        grad_ref[0:D, 0:wide] = dot_tn(low, tangents[kind, 0]).astype(BF16)
        grad_ref[0:D, wide:D] = dot_tn(low, tangents[kind, 1]).astype(BF16)
        value_grad = dot_tn(low, tangents[kind, 2]).astype(BF16)
        grad_ref[D : D + wide, 0:wide] = value_grad[0:wide]
        grad_ref[D : D + wide, wide:D] = value_grad[wide:D]
        columns = pl.ds(pl.multiple_of(halves[kind] * wide, wide), wide)
        vec_ref[0:1, columns] = column_sum(tangents[kind, 0].astype(F32))
        vec_ref[1:2, columns] = column_sum(tangents[kind, 2].astype(F32))


def last_dense(x, entry, dq, dkv, wq, wk, wv, w_other):
    tokens = x.shape[0]
    grad_rows = D + D // 2
    return pl.pallas_call(
        last_kernel,
        out_shape=(
            jax.ShapeDtypeStruct((tokens, D), F32),
            jax.ShapeDtypeStruct((grad_rows, D), BF16),
            jax.ShapeDtypeStruct((grad_rows, D), BF16),
            jax.ShapeDtypeStruct((8, D), F32),
        ),
        in_specs=[VMEM] * 8,
        out_specs=(VMEM,) * 4,
        scratch_shapes=[pltpu.VMEM((2, 3, tokens, D // 2), BF16)],
        compiler_params=pltpu.CompilerParams(vmem_limit_bytes=48 << 20),
        name="last_dense",
    )(x, entry, dq, dkv, wq, wk, wv, w_other)


def reduce_kernel(
    own_ref, send_ref, vec_feed, vec_last, out_ref, vec_out,
    first_in, acc, stage, landing, vec_sum, vec_in,
    core_ss, core_rs, down_ss, down_rs, up_ss, up_rs, vec_ss, vec_rs,
):
    at = Place()
    c, f = at.c, at.f
    rows = own_ref.shape[0]
    quarter = rows // 4
    x_step, y_step, near, far = (step_of(c, stride) for stride in (1, 2, 4, 8))
    barrier = pltpu.get_barrier_semaphore()
    pl.semaphore_signal(barrier, 1, device_id=(c, 1 - f), device_id_type=MESH)
    for _, peer in (x_step, y_step, near, far):
        pl.semaphore_signal(barrier, 1, device_id=(peer, f), device_id_type=MESH)
    pl.semaphore_wait(barrier, 5)

    vec_peers = [(c, 1 - f)] + [(peer, f) for _, peer in (x_step, y_step, near, far)]

    def vec_move(step):
        return at.remote(
            vec_sum.at[step], vec_in.at[step], vec_ss.at[step], vec_rs.at[step], *vec_peers[step]
        )

    def vec_next(step):
        vec_move(step).wait_recv()
        target = vec_sum.at[step + 1] if step < 4 else vec_out
        target[...] = vec_sum[step] + vec_in[step]
        if step < 4:
            vec_move(step + 1).start()

    shared = [acc, acc], [stage, stage], [[landing.at[step] for step in range(4)]] * 2
    ladder = Ladder(
        at,
        ((x_step, y_step, near, far), (y_step, x_step, near, far)),
        (0, 2 * quarter),
        2 * quarter,
        shared[0],
        shared[1],
        shared[2],
        [out_ref, out_ref],
        (down_ss, down_rs, up_ss, up_rs),
    )

    def core_move(region, give):
        kept, given, size, _ = ladder.ranges[region][0]
        where = span(given if give else kept, size)
        slot = region + 2 * (0 if give else 1)
        return at.remote(
            send_ref.at[where], first_in.at[where], core_ss.at[slot], core_rs.at[slot], c, 1 - f
        )

    order = [(0, True), (1, True), (0, False), (1, False)]
    for step in order:
        core_move(*step).start()
    feed_rows = vec_feed.shape[0]
    vec_sum[0, 0:feed_rows] = vec_feed[...]
    vec_sum[0, feed_rows : feed_rows + vec_last.shape[0]] = vec_last[...]
    vec_move(0).start()
    for region, give in order:
        core_move(region, give).wait_recv()
        kept, given, size, _ = ladder.ranges[region][0]

        def join(offset, where, _):
            total = own_ref[where, :].astype(F32) + first_in[where, :].astype(F32)
            if give:
                stage[where, :] = total.astype(BF16)
            else:
                acc[where, :] = total

        pieces_of(given if give else kept, size, join)
        if give:
            ladder.down(region, 0, True).start()
    vec_next(0)
    for step in (1, 2, 3):
        for region in range(2):
            ladder.down(region, step - 1, False).wait_recv()
            ladder.give(region, step, ladder.landing[region][step - 1])
        vec_next(step)
    for region in range(2):
        ladder.settle(region)
    vec_next(4)
    for step in (2, 1, 0):
        for region in range(2):
            ladder.up(region, step, False).wait_recv()
            if step > 0:
                ladder.up(region, step - 1, True).start()
    for step in order:
        core_move(*step).wait_send()
    for step in range(5):
        vec_move(step).wait_send()
    ladder.wait_sent()


def reduce_grads(own, send, vec_feed, vec_last):
    wide = own.shape
    vec_shape = (vec_feed.shape[0] + vec_last.shape[0], D)
    return pl.pallas_call(
        reduce_kernel,
        out_shape=(jax.ShapeDtypeStruct(wide, BF16), jax.ShapeDtypeStruct(vec_shape, F32)),
        in_specs=[VMEM] * 4,
        out_specs=(VMEM, VMEM),
        scratch_shapes=[
            pltpu.VMEM(wide, BF16),
            pltpu.VMEM(wide, F32),
            pltpu.VMEM(wide, BF16),
            pltpu.VMEM((4,) + wide, BF16),
            pltpu.VMEM((5,) + vec_shape, F32),
            pltpu.VMEM((5,) + vec_shape, F32),
        ]
        + [pltpu.SemaphoreType.DMA((4,))] * 2
        + [pltpu.SemaphoreType.DMA((8,))] * 4
        + [pltpu.SemaphoreType.DMA((5,))] * 2,
        compiler_params=pltpu.CompilerParams(
            collective_id=4, has_side_effects=True, vmem_limit_bytes=32 << 20
        ),
        name="reduce_grads",
    )(own, send, vec_feed, vec_last)


def unpack_kernel(
    done_ref, rest_a, rest_b, grads_ref, vec_ref,
    query_ref, key_ref, value_ref, output_ref, expand_ref, shrink_ref, *rest,
):
    vector_outs, full = rest[:-1], rest[-1]
    c, f = lax.axis_index("ctx"), lax.axis_index("fsdp")
    size = done_ref.shape[1]
    for region, far_part in enumerate((rest_a, rest_b)):
        bit = step_of(c, 1 + region)[0]
        start = 2 * region * size
        full[span(start + bit * size, size), :] = done_ref[region]
        full[span(start + (1 - bit) * size, size), :] = far_part[...]
    units, wide = shrink_ref.shape[0], D // 2
    shrink_ref[...] = full[0:units].astype(F32)
    for part in range(units // D):
        start = units + part * D
        expand_ref[:, part * D : part * D + D] = full[start : start + D].astype(F32)
    output_ref[...] = full[2 * units : 2 * units + wide].astype(F32)
    query_ref[...] = grads_ref[0:D, 0:wide].astype(F32)
    key_ref[...] = grads_ref[0:D, wide:D].astype(F32)
    value_ref[0:wide] = grads_ref[D : D + wide, 0:wide].astype(F32)
    value_ref[wide:D] = grads_ref[D : D + wide, wide:D].astype(F32)
    vectors = vec_ref[...]
    mine = jnp.where(f == 0, vectors[:, 0:wide], vectors[:, wide:D])
    for row, ref in zip((16, 17, 7, 5, 6, 0, 1, 2, 3, 4), vector_outs):
        ref[...] = mine[row : row + 1]
    drift = jnp.where(f == 0, vectors[8:10], vectors[10:12])
    for part in range(units // D):
        vector_outs[10][:, part * D : part * D + D] = drift[part : part + 1]


def unpack_grads(units, done, rest_a, rest_b, grads, vecs):
    wide = D // 2
    shapes = [(D, wide)] * 3 + [(wide, D), (D, units), (units, D)] + [(1, wide)] * 10 + [(1, units)]
    return pl.pallas_call(
        unpack_kernel,
        out_shape=tuple(jax.ShapeDtypeStruct(shape, F32) for shape in shapes),
        in_specs=[VMEM] * 5,
        out_specs=(VMEM,) * len(shapes),
        scratch_shapes=[pltpu.VMEM((4 * done.shape[1], D), BF16)],
        compiler_params=pltpu.CompilerParams(vmem_limit_bytes=32 << 20),
        name="unpack_grads",
    )(done, rest_a, rest_b, grads, vecs)


def head_shards(
    n_ctx,
    post_stream,
    sum_stream,
    cotangent,
    block_order,
    block_sequence,
    query_weight,
    key_weight,
    value_weight,
    output_weight,
    query_bias,
    value_bias,
    output_bias,
    attend_gain,
    attend_shift,
    expand_weight,
    expand_bias,
    shrink_weight,
    shrink_bias,
    middle_gain,
    middle_shift,
    final_gain,
    final_shift,
):
    x, summed, tangent = post_stream[0], sum_stream[0], cotangent[0]
    swap = [(0, 1), (1, 0)]

    def from_other(values):
        return lax.ppermute(values, "fsdp", swap)

    def across(values, stride):
        return lax.ppermute(values, "ctx", [(c, c ^ stride) for c in range(n_ctx)])

    vectors = [
        vector[None]
        for vector in (
            query_bias,
            value_bias,
            output_bias,
            attend_gain,
            attend_shift,
            shrink_bias,
            middle_gain,
            middle_shift,
            final_gain,
            final_shift,
        )
    ]
    q, kv, w_other, order, seqs, vec, expand_add = project_and_scatter(
        n_ctx,
        x,
        query_weight,
        key_weight,
        value_weight,
        block_order,
        block_sequence,
        expand_bias[None],
        vectors,
    )
    o, keep, lse, pairs = attend(order, seqs, q, kv)
    o_rows = return_rows(n_ctx, o)
    layer_output, sum_tan, entry, tan_rows, own_feed, send_feed, vec_feed = dense(
        x,
        summed,
        tangent,
        o_rows,
        (output_weight, from_other(output_weight)),
        (expand_weight, from_other(expand_weight)),
        (shrink_weight, from_other(shrink_weight)),
        expand_add,
        vec,
    )
    tan, stage_a, stage_b, kept = scatter_rows(n_ctx, tan_rows, own_feed, send_feed)
    land_a, land_b = across(stage_a, 1), across(stage_b, 2)
    dq, dkv = attend_back(pairs, q, tan, keep, lse, kv)
    dq_rows, dkv_rows, done = return_grads(n_ctx, dq, dkv, kept, land_a, land_b)
    rest_a, rest_b = across(done[0], 1), across(done[1], 2)
    post_tangent, own_last, send_last, vec_last = last_dense(
        x, entry, dq_rows, dkv_rows, query_weight, key_weight, value_weight, w_other
    )
    grads, vecs = reduce_grads(own_last, send_last, vec_feed, vec_last)
    (
        query_slope,
        key_slope,
        value_slope,
        output_slope,
        expand_slope,
        shrink_slope,
        query_drift,
        value_drift,
        output_drift,
        attend_stretch,
        attend_nudge,
        shrink_drift,
        middle_stretch,
        middle_nudge,
        final_stretch,
        final_nudge,
        expand_drift,
    ) = unpack_grads(shrink_weight.shape[0], done, rest_a, rest_b, grads, vecs)
    return (
        layer_output[None],
        post_tangent[None],
        sum_tan[None],
        query_slope,
        key_slope,
        value_slope,
        output_slope,
        query_drift[0],
        value_drift[0],
        output_drift[0],
        attend_stretch[0],
        attend_nudge[0],
        expand_slope,
        expand_drift[0],
        shrink_slope,
        shrink_drift[0],
        middle_stretch[0],
        middle_nudge[0],
        final_stretch[0],
        final_nudge[0],
    )


def solution(mesh):
    n_ctx, n_fsdp = mesh.shape["ctx"], mesh.shape["fsdp"]
    if n_fsdp == 2 and n_ctx == n_fsdp * H:
        body = functools.partial(head_shards, n_ctx)
    else:
        body = general_shards
    return jax.shard_map(
        body,
        mesh=mesh,
        in_specs=(
            P("fsdp", "ctx", None),
            P("fsdp", "ctx", None),
            P("fsdp", "ctx", None),
            P("fsdp", None),
            P("fsdp", None),
            P(None, "fsdp"),
            P(None, "fsdp"),
            P(None, "fsdp"),
            P("fsdp", None),
            P("fsdp"),
            P("fsdp"),
            P("fsdp"),
            P("fsdp"),
            P("fsdp"),
            P(None, "fsdp"),
            P("fsdp"),
            P("fsdp", None),
            P("fsdp"),
            P("fsdp"),
            P("fsdp"),
            P("fsdp"),
            P("fsdp"),
        ),
        out_specs=(
            P("fsdp", "ctx", None),
            P("fsdp", "ctx", None),
            P("fsdp", "ctx", None),
            P(None, "fsdp"),
            P(None, "fsdp"),
            P(None, "fsdp"),
            P("fsdp", None),
            P("fsdp"),
            P("fsdp"),
            P("fsdp"),
            P("fsdp"),
            P("fsdp"),
            P(None, "fsdp"),
            P("fsdp"),
            P("fsdp", None),
            P("fsdp"),
            P("fsdp"),
            P("fsdp"),
            P("fsdp"),
            P("fsdp"),
        ),
        check_vma=False,
    )
```

```python
import functools

import jax
import jax.numpy as jnp
from jax import lax
from jax.experimental import pallas as pl
from jax.experimental.pallas import tpu as pltpu
from jax.sharding import PartitionSpec as P

D = 512
H = 8
HD = 64
BLK = 256
HALF = BLK // 2
LONG = 8
TOGETHER = 16
BACK_TOGETHER = 16
MOST = LONG + 1
F32 = jnp.float32
BF16 = jnp.bfloat16
MESH = pl.DeviceIdType.MESH
ROOM = 60 << 20
VMEM = pl.BlockSpec(memory_space=pltpu.VMEM)
SMEM = pl.BlockSpec(memory_space=pltpu.SMEM)
ANY = pl.BlockSpec(memory_space=pltpu.HBM)


norm_eps = 1e-05
masked_value = -1e30
gelu_coeff = 0.7978845608
gelu_cubic = 0.044715


def smooth_gate(values):
    return (
        0.5
        * values
        * (1.0 + jnp.tanh(gelu_coeff * (values + gelu_cubic * values * values * values)))
    )


def layer_norm(inputs, gain_row, shift_row):
    centre = inputs - jnp.mean(inputs, axis=-1, keepdims=True)
    spread = jnp.mean(centre * centre, axis=-1, keepdims=True)
    return centre * lax.rsqrt(spread + norm_eps) * gain_row + shift_row


def product(left_side, right_side):
    return jnp.dot(left_side, right_side, preferred_element_type=jnp.float32)


def cross_rows(left_side, right_side):
    return lax.dot_general(
        left_side, right_side, (((0,), (0,)), ((), ())), preferred_element_type=jnp.float32
    )


def cross_cols(left_side, right_side):
    return lax.dot_general(
        left_side, right_side, (((1,), (1,)), ((), ())), preferred_element_type=jnp.float32
    )


def column_total(values):
    return jnp.sum(values, axis=0, dtype=jnp.float32)


def lookup(table_row, indices):
    places = jnp.arange(table_row.shape[0], dtype=jnp.int32)
    return jnp.sum(jnp.where(indices[:, None] == places[None, :], table_row[None, :], 0), axis=1)


def block_mask(query_blocks, query_seqs, key_blocks, key_seqs):
    same_seq = query_seqs[:, None] == key_seqs[None, :]
    return same_seq & (key_blocks[None, :] <= query_blocks[:, None])


def token_mask(visible):
    return jnp.repeat(jnp.repeat(visible, BLK, axis=0), BLK, axis=1)


def fold_units(carried, members, unit_step):
    unit_count = members[0].shape[0] // BLK
    inner_count = max((divisor for divisor in range(1, 17) if unit_count % divisor == 0))
    outer_count = unit_count // inner_count

    def outer_turn(outer_index, current):

        def inner_turn(inner_index, inner_state):
            offset = (outer_index * inner_count + inner_index) * BLK
            pieces = tuple((lax.dynamic_slice_in_dim(member, offset, BLK, 0) for member in members))
            return unit_step(inner_state, pieces, offset)

        return lax.fori_loop(0, inner_count, inner_turn, current)

    return lax.fori_loop(0, outer_count, outer_turn, carried)


def general_shards(
    post_stream,
    sum_stream,
    cotangent,
    block_order,
    block_sequence,
    query_weight,
    key_weight,
    value_weight,
    output_weight,
    query_bias,
    value_bias,
    output_bias,
    attend_gain,
    attend_shift,
    expand_weight,
    expand_bias,
    shrink_weight,
    shrink_bias,
    middle_gain,
    middle_shift,
    final_gain,
    final_shift,
):
    (
        query_whole,
        key_whole,
        value_whole,
        output_whole,
        query_add,
        value_add,
        output_add,
        gain_one,
        shift_one,
        expand_whole,
        expand_add,
        shrink_whole,
        shrink_add,
        gain_two,
        shift_two,
        gain_last,
        shift_last,
    ) = (
        lax.all_gather(query_weight, "fsdp", axis=1, tiled=True),
        lax.all_gather(key_weight, "fsdp", axis=1, tiled=True),
        lax.all_gather(value_weight, "fsdp", axis=1, tiled=True),
        lax.all_gather(output_weight, "fsdp", axis=0, tiled=True),
        lax.all_gather(query_bias, "fsdp", axis=0, tiled=True),
        lax.all_gather(value_bias, "fsdp", axis=0, tiled=True),
        lax.all_gather(output_bias, "fsdp", axis=0, tiled=True),
        lax.all_gather(attend_gain, "fsdp", axis=0, tiled=True),
        lax.all_gather(attend_shift, "fsdp", axis=0, tiled=True),
        lax.all_gather(expand_weight, "fsdp", axis=1, tiled=True),
        lax.all_gather(expand_bias, "fsdp", axis=0, tiled=True),
        lax.all_gather(shrink_weight, "fsdp", axis=0, tiled=True),
        lax.all_gather(shrink_bias, "fsdp", axis=0, tiled=True),
        lax.all_gather(middle_gain, "fsdp", axis=0, tiled=True),
        lax.all_gather(middle_shift, "fsdp", axis=0, tiled=True),
        lax.all_gather(final_gain, "fsdp", axis=0, tiled=True),
        lax.all_gather(final_shift, "fsdp", axis=0, tiled=True),
    )
    post_rows = post_stream[0]
    summed = sum_stream[0]
    tangent = cotangent[0]
    order_row = block_order[0]
    seq_row = block_sequence[0]
    token_count = post_rows.shape[0]
    score_scale = HD ** (-0.5)
    own_blocks = lax.dynamic_slice_in_dim(
        order_row, lax.axis_index("ctx") * (token_count // BLK), token_count // BLK
    )
    own_seqs = lookup(seq_row, own_blocks)
    post_low = post_rows.astype(jnp.bfloat16)
    queries = (product(post_low, query_whole) + query_add).astype(jnp.bfloat16)
    key_rows = product(post_low, key_whole).astype(jnp.bfloat16)
    value_rows = (product(post_low, value_whole) + value_add).astype(jnp.bfloat16)
    query_heads = queries.reshape(token_count, H, HD)

    def keys_visible(first_row):
        key_block = lax.dynamic_slice_in_dim(order_row, first_row // BLK, 1)
        return block_mask(own_blocks, own_seqs, key_block, lookup(seq_row, key_block))

    def masked_fold(block_step):

        def unit_step(current, pieces, first_row):
            visible = keys_visible(first_row)
            return lax.cond(
                jnp.any(visible),
                lambda inner_state: block_step(inner_state, pieces, visible),
                lambda inner_state: inner_state,
                current,
            )

        def folded(current, pieces, first_row):
            return fold_units(current, pieces, unit_step)

        return folded

    def stats_block(current, pieces, visible):
        row_peaks, masses = current
        key_heads = pieces[0].reshape(BLK, H, HD)
        row_mask = token_mask(visible)[None]
        scores = (
            jnp.einsum("qhd,khd->hqk", query_heads, key_heads, preferred_element_type=jnp.float32)
            * score_scale
        )
        new_peaks = jnp.maximum(
            row_peaks, jnp.max(jnp.where(row_mask, scores, masked_value), axis=2)
        )
        weights = jnp.where(row_mask, jnp.exp(scores - new_peaks[:, :, None]), 0.0)
        return (new_peaks, masses * jnp.exp(row_peaks - new_peaks) + jnp.sum(weights, axis=2))

    stats_fold = masked_fold(stats_block)
    stats_start = (
        jnp.full((H, token_count), masked_value, jnp.float32),
        jnp.zeros((H, token_count), jnp.float32),
    )
    row_peaks, masses = stats_fold(
        stats_start, (lax.all_gather(key_rows, "ctx", axis=0, tiled=True),), jnp.int32(0)
    )
    log_mass = row_peaks + jnp.log(masses)

    def forward_block(current, pieces, visible):
        key_heads = pieces[0].reshape(BLK, H, HD)
        value_heads = pieces[1].reshape(BLK, H, HD)
        row_mask = token_mask(visible)[None]
        scores = (
            jnp.einsum("qhd,khd->hqk", query_heads, key_heads, preferred_element_type=jnp.float32)
            * score_scale
        )
        weights = jnp.where(row_mask, jnp.exp(scores - log_mass[:, :, None]), 0.0).astype(
            jnp.bfloat16
        )
        addition = jnp.einsum(
            "hqk,khd->qhd", weights, value_heads, preferred_element_type=jnp.float32
        )
        return current + addition.reshape(token_count, D)

    forward_fold = masked_fold(forward_block)
    zero_rows = jnp.zeros((token_count, D), jnp.float32)
    attended = forward_fold(
        zero_rows,
        (
            lax.all_gather(key_rows, "ctx", axis=0, tiled=True),
            lax.all_gather(value_rows, "ctx", axis=0, tiled=True),
        ),
        jnp.int32(0),
    )
    mixed_low = attended.astype(jnp.bfloat16)
    branch = product(mixed_low, output_whole) + output_add
    normed_one, first_pull = jax.vjp(
        layer_norm, post_rows + branch, gain_one.astype(jnp.float32), shift_one.astype(jnp.float32)
    )
    stream_one = summed + branch
    normed_low = normed_one.astype(jnp.bfloat16)
    before = product(normed_low, expand_whole) + expand_add
    gated, gate_pull = jax.vjp(smooth_gate, before)
    hidden = gated.astype(jnp.bfloat16)
    feed_out = product(hidden, shrink_whole) + shrink_add
    normed_two, middle_pull = jax.vjp(
        layer_norm,
        normed_one + feed_out,
        gain_two.astype(jnp.float32),
        shift_two.astype(jnp.float32),
    )
    stream_two = stream_one + feed_out
    last_norm, last_pull = jax.vjp(
        layer_norm, stream_two, gain_last.astype(jnp.float32), shift_last.astype(jnp.float32)
    )
    layer_output = normed_two + last_norm
    stream_tan, stretch_last, nudge_last = last_pull(tangent)
    inflow_tan, stretch_two, nudge_two = middle_pull(tangent)
    feed_tan = (stream_tan + inflow_tan).astype(jnp.bfloat16)
    slope_shrink = cross_rows(hidden, feed_tan)
    drift_shrink = column_total(feed_tan)
    before_tan = gate_pull(cross_cols(feed_tan, shrink_whole))[0].astype(jnp.bfloat16)
    slope_expand = cross_rows(normed_low, before_tan)
    drift_expand = column_total(before_tan)
    normed_tan = inflow_tan + cross_cols(before_tan, expand_whole)
    feed_parts = lax.psum(
        (
            slope_expand,
            drift_expand,
            slope_shrink,
            drift_shrink,
            stretch_two,
            nudge_two,
            stretch_last,
            nudge_last,
        ),
        "ctx",
    )
    feed_sums = (
        lax.psum_scatter(feed_parts[0], "fsdp", scatter_dimension=1, tiled=True),
        lax.psum_scatter(feed_parts[1], "fsdp", scatter_dimension=0, tiled=True),
        lax.psum_scatter(feed_parts[2], "fsdp", scatter_dimension=0, tiled=True),
        lax.psum_scatter(feed_parts[3], "fsdp", scatter_dimension=0, tiled=True),
        lax.psum_scatter(feed_parts[4], "fsdp", scatter_dimension=0, tiled=True),
        lax.psum_scatter(feed_parts[5], "fsdp", scatter_dimension=0, tiled=True),
        lax.psum_scatter(feed_parts[6], "fsdp", scatter_dimension=0, tiled=True),
        lax.psum_scatter(feed_parts[7], "fsdp", scatter_dimension=0, tiled=True),
    )
    entry_tan, stretch_one, nudge_one = first_pull(normed_tan)
    branch_tan = (stream_tan + entry_tan).astype(jnp.bfloat16)
    slope_output = cross_rows(mixed_low, branch_tan)
    drift_output = column_total(branch_tan)
    mixed_tan = cross_cols(branch_tan, output_whole).astype(jnp.bfloat16)
    tangent_heads = mixed_tan.reshape(token_count, H, HD)
    deltas = jnp.sum((mixed_tan * attended).reshape(token_count, H, HD), axis=2).T

    def query_block(current, pieces, visible):
        key_heads = pieces[0].reshape(BLK, H, HD)
        value_heads = pieces[1].reshape(BLK, H, HD)
        row_mask = token_mask(visible)[None]
        scores = (
            jnp.einsum("qhd,khd->hqk", query_heads, key_heads, preferred_element_type=jnp.float32)
            * score_scale
        )
        probability = jnp.where(row_mask, jnp.exp(scores - log_mass[:, :, None]), 0.0)
        prob_tan = jnp.einsum(
            "qhd,khd->hqk", tangent_heads, value_heads, preferred_element_type=jnp.float32
        )
        score_tan = (probability * (prob_tan - deltas[:, :, None])).astype(jnp.bfloat16)
        addition = jnp.einsum(
            "hqk,khd->qhd", score_tan, key_heads, preferred_element_type=jnp.float32
        )
        return current + addition.reshape(token_count, D) * score_scale

    query_fold = masked_fold(query_block)
    query_sum = query_fold(
        zero_rows,
        (
            lax.all_gather(key_rows, "ctx", axis=0, tiled=True),
            lax.all_gather(value_rows, "ctx", axis=0, tiled=True),
        ),
        jnp.int32(0),
    )
    gathered_mass, gathered_delta = (
        lax.all_gather(log_mass.T, "ctx", axis=0, tiled=True),
        lax.all_gather(deltas.T, "ctx", axis=0, tiled=True),
    )
    own_keys = key_rows.reshape(token_count, H, HD)
    own_values = value_rows.reshape(token_count, H, HD)

    def owner_block(current, pieces, first_row, visible):
        key_acc, value_acc = current
        part_queries = pieces[0].reshape(BLK, H, HD)
        part_tangent = pieces[1].reshape(BLK, H, HD)
        part_mass = lax.dynamic_slice_in_dim(gathered_mass, first_row, BLK, 0).T
        part_delta = lax.dynamic_slice_in_dim(gathered_delta, first_row, BLK, 0).T
        row_mask = token_mask(visible)[None]
        scores = (
            jnp.einsum("qhd,khd->hqk", part_queries, own_keys, preferred_element_type=jnp.float32)
            * score_scale
        )
        probability = jnp.where(row_mask, jnp.exp(scores - part_mass[:, :, None]), 0.0)
        value_add_rows = jnp.einsum(
            "hqk,qhd->khd",
            probability.astype(jnp.bfloat16),
            part_tangent,
            preferred_element_type=jnp.float32,
        )
        prob_tan = jnp.einsum(
            "qhd,khd->hqk", part_tangent, own_values, preferred_element_type=jnp.float32
        )
        score_tan = (probability * (prob_tan - part_delta[:, :, None])).astype(jnp.bfloat16)
        key_add_rows = jnp.einsum(
            "hqk,qhd->khd", score_tan, part_queries, preferred_element_type=jnp.float32
        )
        return (
            key_acc + key_add_rows.reshape(token_count, D) * score_scale,
            value_acc + value_add_rows.reshape(token_count, D),
        )

    def owner_unit(current, pieces, first_row):
        query_blocks = lax.dynamic_slice_in_dim(order_row, first_row // BLK, 1)
        visible = block_mask(query_blocks, lookup(seq_row, query_blocks), own_blocks, own_seqs)
        return lax.cond(
            jnp.any(visible),
            lambda inner_state: owner_block(inner_state, pieces, first_row, visible),
            lambda inner_state: inner_state,
            current,
        )

    key_sum, value_sum = fold_units(
        (zero_rows, zero_rows),
        (
            lax.all_gather(queries, "ctx", axis=0, tiled=True),
            lax.all_gather(mixed_tan, "ctx", axis=0, tiled=True),
        ),
        owner_unit,
    )
    query_tan = query_sum.astype(jnp.bfloat16)
    key_tan = key_sum.astype(jnp.bfloat16)
    value_tan = value_sum.astype(jnp.bfloat16)
    slope_query = cross_rows(post_low, query_tan)
    slope_key = cross_rows(post_low, key_tan)
    slope_value = cross_rows(post_low, value_tan)
    drift_query = column_total(query_tan)
    drift_value = column_total(value_tan)
    post_tangent = (
        entry_tan
        + cross_cols(query_tan, query_whole)
        + cross_cols(key_tan, key_whole)
        + cross_cols(value_tan, value_whole)
    )
    heads_parts = lax.psum(
        (
            slope_query,
            slope_key,
            slope_value,
            slope_output,
            drift_query,
            drift_value,
            drift_output,
            stretch_one,
            nudge_one,
        ),
        "ctx",
    )
    heads_sums = (
        lax.psum_scatter(heads_parts[0], "fsdp", scatter_dimension=1, tiled=True),
        lax.psum_scatter(heads_parts[1], "fsdp", scatter_dimension=1, tiled=True),
        lax.psum_scatter(heads_parts[2], "fsdp", scatter_dimension=1, tiled=True),
        lax.psum_scatter(heads_parts[3], "fsdp", scatter_dimension=0, tiled=True),
        lax.psum_scatter(heads_parts[4], "fsdp", scatter_dimension=0, tiled=True),
        lax.psum_scatter(heads_parts[5], "fsdp", scatter_dimension=0, tiled=True),
        lax.psum_scatter(heads_parts[6], "fsdp", scatter_dimension=0, tiled=True),
        lax.psum_scatter(heads_parts[7], "fsdp", scatter_dimension=0, tiled=True),
        lax.psum_scatter(heads_parts[8], "fsdp", scatter_dimension=0, tiled=True),
    )
    return (
        layer_output[None],
        post_tangent[None],
        stream_tan[None],
        heads_sums[0],
        heads_sums[1],
        heads_sums[2],
        heads_sums[3],
        heads_sums[4],
        heads_sums[5],
        heads_sums[6],
        heads_sums[7],
        heads_sums[8],
        feed_sums[0],
        feed_sums[1],
        feed_sums[2],
        feed_sums[3],
        feed_sums[4],
        feed_sums[5],
        feed_sums[6],
        feed_sums[7],
    )


def low_lanes(values):
    return lax.broadcasted_iota(jnp.int32, values.shape, 1) < HD


def swap_lanes(values):
    return pltpu.roll(values, HD, 1)


def low_pair(first, second):
    return jnp.where(low_lanes(first), first, swap_lanes(second))


def high_pair(first, second):
    return jnp.where(low_lanes(first), swap_lanes(first), second)


def side_pair(side, first, second):
    return low_pair(first, second) if side == 0 else high_pair(first, second)


def dot_nn(left, right):
    return jnp.dot(left, right, preferred_element_type=F32)


def dot_nt(left, right):
    return lax.dot_general(left, right, (((1,), (1,)), ((), ())), preferred_element_type=F32)


def dot_tn(left, right):
    return lax.dot_general(left, right, (((0,), (0,)), ((), ())), preferred_element_type=F32)


class Place:
    def __init__(self):
        self.c = lax.axis_index("ctx")
        self.f = lax.axis_index("fsdp")
        self.group = self.c // H
        self.head = self.c % H
        self.inside = jnp.where(self.group == self.f, 1, 0)

    def is_me(self, tc, tf):
        return jnp.logical_and(self.c == tc, self.f == tf)

    def signal(self, barrier, tc, tf):
        @pl.when(jnp.logical_not(self.is_me(tc, tf)))
        def _():
            pl.semaphore_signal(barrier, 1, device_id=(tc, tf), device_id_type=MESH)

    def greet_sources(self, n_ctx, partner):
        barrier = pltpu.get_barrier_semaphore()
        for tc in range(n_ctx):
            self.signal(barrier, tc, self.group)
        if partner:
            pl.semaphore_signal(
                barrier, 1, device_id=(self.c, 1 - self.f), device_id_type=MESH
            )
        pl.semaphore_wait(barrier, 2 * H + (1 if partner else 0) - self.inside)

    def greet_owners(self, n_ctx, partner, more=0):
        barrier = pltpu.get_barrier_semaphore()
        for head in range(H):
            for core in range(2):
                self.signal(barrier, self.f * H + head, core)
        if partner:
            pl.semaphore_signal(
                barrier, 1, device_id=(self.c, 1 - self.f), device_id_type=MESH
            )
        pl.semaphore_wait(barrier, n_ctx + (1 if partner else 0) + more - self.inside)

    def send(self, src, dst, send_sem, recv_sem, tc, tf):
        me = self.is_me(tc, tf)

        @pl.when(me)
        def _():
            pltpu.make_async_copy(src, dst, recv_sem).start()

        @pl.when(jnp.logical_not(me))
        def _():
            self.remote(src, dst, send_sem, recv_sem, tc, tf).start()

    def remote(self, src, dst, send_sem, recv_sem, tc, tf):
        return pltpu.make_async_remote_copy(
            src_ref=src,
            dst_ref=dst,
            send_sem=send_sem,
            recv_sem=recv_sem,
            device_id=(tc, tf),
            device_id_type=MESH,
        )

    def wait_sent(self, src, dst, send_sem, recv_sem, tc, tf):
        @pl.when(jnp.logical_not(self.is_me(tc, tf)))
        def _():
            self.remote(src, dst, send_sem, recv_sem, tc, tf).wait_send()


VECTORS = 10


def project_kernel(
    n_ctx,
    x_hbm,
    wq_hbm,
    wk_hbm,
    wv_hbm,
    order_hbm,
    seq_hbm,
    *rest,
):
    vector_hbm, rest = rest[: VECTORS + 1], rest[VECTORS + 1 :]
    vector_in, rest = rest[-VECTORS - 1 :], rest[: -VECTORS - 1]
    (
        q_out,
        kv_out,
        w_other,
        order_out,
        seq_out,
        vec_out,
        expand_out,
        x_in,
        w_own,
        w_in,
        bias_own,
        bias_in,
        order_own,
        seq_own,
        order_in,
        seq_in,
        q_send,
        kv_send,
        load_sem,
        w_ss,
        w_rs,
        q_ss,
        q_rs,
        kv_ss,
        kv_rs,
        relay_ss,
        relay_rs,
    ) = rest
    at = Place()
    other = 1 - at.f
    loads = [
        pltpu.make_async_copy(src, dst, load_sem.at[i])
        for i, (src, dst) in enumerate(
            (
                (x_hbm, x_in),
                (wq_hbm, w_own.at[0]),
                (wk_hbm, w_own.at[1]),
                (wv_hbm, w_own.at[2]),
                (order_hbm, order_own),
                (seq_hbm, seq_own),
                *zip(vector_hbm, vector_in),
            )
        )
    ]
    for load in loads:
        load.start()
    at.greet_sources(n_ctx, True)
    for load in loads[6:]:
        load.wait()
    wide = bias_own.shape[1]
    for row, ref in enumerate(vector_in[:VECTORS]):
        bias_own[row : row + 1, :] = ref[...].astype(F32).reshape(1, wide)
    for part in range(vector_in[VECTORS].shape[0] // wide):
        piece = vector_in[VECTORS][part * wide : part * wide + wide]
        bias_own[VECTORS + part : VECTORS + part + 1, :] = piece.astype(F32).reshape(1, wide)
    swaps = [
        at.remote(src, dst, w_ss.at[i], w_rs.at[i], at.c, other)
        for i, (src, dst) in enumerate(
            (
                (bias_own, bias_in),
                (wq_hbm, w_in.at[0]),
                (wk_hbm, w_in.at[1]),
                (wv_hbm, w_in.at[2]),
                (order_hbm, order_in),
                (seq_hbm, seq_in),
            )
        )
    ]
    for swap in swaps:
        swap.start()
    for load in loads[:6]:
        load.wait()

    def targets(half):
        for pair in range(2):
            for side in range(2):
                head = half * (H // 2) + 2 * pair + side
                for core in range(2):
                    slot = head * 2 + core
                    yield pair, side, head, core, (
                        kv_send.at[head, pl.ds(core * BLK, BLK)],
                        kv_out.at[2 * at.c + core],
                        kv_ss.at[slot],
                        kv_rs.at[at.c],
                        at.f * H + head,
                        core,
                    ), (
                        q_send.at[head, core],
                        q_out.at[at.c],
                        q_ss.at[slot],
                        q_rs.at[at.c],
                        at.f * H + head,
                        core,
                    )

    def one_half(half, wq, wk, wv, bias):
        low = x_in[...].astype(BF16)
        q = dot_nn(low, wq[...]) + bias[0:1, :]
        k = dot_nn(low, wk[...])
        v = dot_nn(low, wv[...]) + bias[1:2, :]
        for pair, side, head, core, kv_move, q_move in targets(half):
            columns = slice(pair * 128, pair * 128 + 128)
            if core == 0:
                kv_send[head] = side_pair(side, k[:, columns], v[:, columns]).astype(BF16)
            rows = slice(core * HALF, core * HALF + HALF)
            late = slice(BLK + core * HALF, BLK + core * HALF + HALF)
            q_send[head, core] = side_pair(side, q[rows, columns], q[late, columns]).astype(BF16)
            at.send(*kv_move)
            at.send(*q_move)

    one_half(at.f, w_own.at[0], w_own.at[1], w_own.at[2], bias_own)
    for swap in swaps:
        swap.wait()
    one_half(other, w_in.at[0], w_in.at[1], w_in.at[2], bias_in)
    w_other[...] = w_in[...]
    inside = at.inside == 1
    order_out[...] = jnp.where(inside, order_own[...], order_in[...])
    seq_out[...] = jnp.where(inside, seq_own[...], seq_in[...])
    vec_out[...] = whole_rows(bias_own[...], bias_in[...], at.f == 0)
    for row, source in enumerate((bias_own, bias_in)):
        for part in range(expand_out.shape[1] // wide):
            at_row = VECTORS + part
            expand_out[row : row + 1, part * wide : part * wide + wide] = source[
                at_row : at_row + 1, :
            ]

    def relay(source):
        mine = kv_out.at[2 * source + at.f]
        return at.remote(mine, mine, relay_ss.at[source], relay_rs.at[source], at.c, other)

    def relay_in(source):
        theirs = kv_out.at[2 * source + other]
        return at.remote(theirs, theirs, relay_ss.at[source], relay_rs.at[source], at.c, other)

    for source in range(n_ctx):
        arrived = kv_out.at[2 * source + at.f]
        at.remote(arrived, arrived, kv_ss.at[0], kv_rs.at[source], at.c, other).wait_recv()
        relay(source).start()
    for source in range(n_ctx):
        arrived = q_out.at[source]
        at.remote(arrived, arrived, q_ss.at[0], q_rs.at[source], at.c, other).wait_recv()
        relay_in(source).wait_recv()
    for source in range(n_ctx):
        relay(source).wait_send()
    for half in (at.f, other):
        for _, _, _, _, kv_move, q_move in targets(half):
            at.wait_sent(*kv_move)
            at.wait_sent(*q_move)


def project_and_scatter(n_ctx, x, wq, wk, wv, order, seqs, vectors):
    wide = wq.shape[1]
    blocks = order.shape[1]
    units = vectors[VECTORS].shape[0]
    bias_rows = VECTORS + units // wide
    return pl.pallas_call(
        functools.partial(project_kernel, n_ctx),
        out_shape=(
            jax.ShapeDtypeStruct((n_ctx, HALF, 128), BF16),
            jax.ShapeDtypeStruct((2 * n_ctx, BLK, 128), BF16),
            jax.ShapeDtypeStruct((3, D, wide), BF16),
            jax.ShapeDtypeStruct((1, blocks), jnp.int32),
            jax.ShapeDtypeStruct((1, blocks), jnp.int32),
            jax.ShapeDtypeStruct((bias_rows, D), F32),
            jax.ShapeDtypeStruct((2, units), F32),
        ),
        in_specs=[ANY] * (7 + VECTORS),
        out_specs=(ANY, ANY) + (VMEM,) * 5,
        scratch_shapes=[
            pltpu.VMEM((2 * BLK, D), F32),
            pltpu.VMEM((3, D, wide), BF16),
            pltpu.VMEM((3, D, wide), BF16),
            pltpu.VMEM((bias_rows, wide), F32),
            pltpu.VMEM((bias_rows, wide), F32),
            pltpu.VMEM((1, blocks), jnp.int32),
            pltpu.VMEM((1, blocks), jnp.int32),
            pltpu.VMEM((1, blocks), jnp.int32),
            pltpu.VMEM((1, blocks), jnp.int32),
            pltpu.VMEM((H, 2, HALF, 128), BF16),
            pltpu.VMEM((H, 2 * BLK, 128), BF16),
            pltpu.SemaphoreType.DMA((7 + VECTORS,)),
            pltpu.SemaphoreType.DMA((6,)),
            pltpu.SemaphoreType.DMA((6,)),
            pltpu.SemaphoreType.DMA((2 * H,)),
            pltpu.SemaphoreType.DMA((n_ctx,)),
            pltpu.SemaphoreType.DMA((2 * H,)),
            pltpu.SemaphoreType.DMA((n_ctx,)),
            pltpu.SemaphoreType.DMA((n_ctx,)),
            pltpu.SemaphoreType.DMA((n_ctx,)),
        ]
        + [pltpu.VMEM(vector.shape, BF16) for vector in vectors],
        compiler_params=pltpu.CompilerParams(
            collective_id=0, has_side_effects=True, vmem_limit_bytes=ROOM
        ),
        name="project_scatter",
    )(x, wq, wk, wv, order, seqs, *vectors)


def forward_kernel(
    blocks,
    order_ref,
    seq_ref,
    q_ref,
    kv_ref,
    o_ref,
    keep_ref,
    lse_ref,
    pairs_ref,
    place,
    q_low,
    peaks,
    masses,
    total,
    scores,
):
    def place_block(slot, _):
        place[order_ref[0, slot]] = slot
        return 0

    lax.fori_loop(0, blocks, place_block, 0)

    count = jnp.int32(0)
    for gap in range(LONG):

        def look(late, found):
            pairs_ref[0, found] = place[late]
            pairs_ref[1, found] = place[late - gap]
            return found + jnp.where(seq_ref[0, late] == seq_ref[0, late - gap], 1, 0)

        count = lax.fori_loop(gap, blocks, look, count)
    for spare in range(TOGETHER):
        pairs_ref[0, count + spare] = blocks
        pairs_ref[1, count + spare] = 0
    turns = (count + TOGETHER - 1) // TOGETHER
    pairs_ref[2, 1] = (count + BACK_TOGETHER - 1) // BACK_TOGETHER

    def unpack(step, _):
        for part in range(4):
            source = step * 4 + part
            packed = q_ref[source].astype(F32) * (HD**-0.5)
            low = low_lanes(packed)
            q_low[2 * source] = jnp.where(low, packed, 0.0).astype(BF16)
            q_low[2 * source + 1] = jnp.where(low, swap_lanes(packed), 0.0).astype(BF16)
        return 0

    lax.fori_loop(0, blocks // 8, unpack, 0)
    q_low[blocks] = jnp.zeros((HALF, 128), BF16)

    def clear(slot, _):
        peaks[slot] = jnp.full((HALF, 128), masked_value, F32)
        masses[slot] = jnp.zeros((HALF, 128), F32)
        total[slot] = jnp.zeros((HALF, 128), F32)
        return 0

    lax.fori_loop(0, blocks + 1, clear, 0)

    def score(step, _):
        slots, results = [], []
        for part in range(TOGETHER):
            index = step * TOGETHER + part
            q_slot = pairs_ref[0, index]
            result = dot_nt(q_low[q_slot], kv_ref[pairs_ref[1, index]])
            scores[index] = result
            slots.append(q_slot)
            results.append(jnp.maximum(result[:, :128], result[:, 128:]))
        for q_slot, result in zip(slots, results):
            peaks[q_slot] = jnp.maximum(peaks[q_slot], result)
        return 0

    lax.fori_loop(0, turns, score, 0)

    def level(step, _):
        for part in range(4):
            slot = step * 4 + part
            peaks[slot] = jnp.broadcast_to(
                jnp.max(peaks[slot], axis=1, keepdims=True), (HALF, 128)
            )
        return 0

    lax.fori_loop(0, blocks // 4, level, 0)

    def weigh(step, _):
        slots, results = [], []
        for part in range(TOGETHER):
            index = step * TOGETHER + part
            q_slot = pairs_ref[0, index]
            peak = peaks[q_slot]
            left = jnp.exp(scores[index, :, :128] - peak)
            right = jnp.exp(scores[index, :, 128:] - peak)
            weights = jnp.concatenate([left, right], axis=1).astype(BF16)
            slots.append(q_slot)
            results.append((left + right, dot_nn(weights, kv_ref[pairs_ref[1, index]])))
        for q_slot, (mass, part_total) in zip(slots, results):
            masses[q_slot] = masses[q_slot] + mass
            total[q_slot] = total[q_slot] + part_total
        return 0

    lax.fori_loop(0, turns, weigh, 0)

    def finish(step, _):
        for part in range(4):
            source = step * 4 + part
            results = []
            for side in range(2):
                slot = 2 * source + side
                mass = jnp.broadcast_to(
                    jnp.sum(masses[slot], axis=1, keepdims=True), (HALF, 128)
                )
                results.append(total[slot] / mass)
                lse_ref[slot] = peaks[slot] + jnp.log(mass)
            packed = high_pair(results[0], results[1])
            keep_ref[source] = packed
            o_ref[source] = packed.astype(BF16)
        return 0

    lax.fori_loop(0, blocks // 8, finish, 0)


def pair_room(blocks):
    return blocks * MOST // 2 + TOGETHER


def attend(order, seqs, q, kv):
    blocks = kv.shape[0]
    room = pair_room(blocks)
    return pl.pallas_call(
        functools.partial(forward_kernel, blocks),
        out_shape=(
            jax.ShapeDtypeStruct((blocks // 2, HALF, 128), BF16),
            jax.ShapeDtypeStruct((blocks // 2, HALF, 128), F32),
            jax.ShapeDtypeStruct((blocks, HALF, 128), F32),
            jax.ShapeDtypeStruct((3, room), jnp.int32),
        ),
        in_specs=[SMEM, SMEM, VMEM, VMEM],
        out_specs=(VMEM, VMEM, VMEM, SMEM),
        scratch_shapes=[
            pltpu.SMEM((blocks,), jnp.int32),
            pltpu.VMEM((blocks + 1, HALF, 128), BF16),
            pltpu.VMEM((blocks + 1, HALF, 128), F32),
            pltpu.VMEM((blocks + 1, HALF, 128), F32),
            pltpu.VMEM((blocks + 1, HALF, 128), F32),
            pltpu.VMEM((room, HALF, BLK), F32),
        ],
        compiler_params=pltpu.CompilerParams(vmem_limit_bytes=ROOM),
        name="attend",
    )(order, seqs, q, kv)


def backward_kernel(
    blocks,
    pairs_ref,
    q_ref,
    tan_ref,
    keep_ref,
    lse_ref,
    kv_ref,
    dq_ref,
    dkv_ref,
    both,
    turned,
    masses,
    deltas,
    dq_sum,
    dkv_sum,
):
    def unpack(step, _):
        for part in range(4):
            source = step * 4 + part
            packed = q_ref[source].astype(F32) * (HD**-0.5)
            tangent = tan_ref[source].astype(F32)
            low = low_lanes(packed)
            product = tangent * keep_ref[source]
            for side in range(2):
                slot = 2 * source + side
                q = packed if side == 0 else swap_lanes(packed)
                tan = tangent if side == 1 else swap_lanes(tangent)
                both[slot, 0:HALF] = jnp.where(low, q, 0.0).astype(BF16)
                both[slot, HALF:BLK] = jnp.where(low, 0.0, tan).astype(BF16)
                turned[slot] = jnp.transpose(both[slot])
                mine = jnp.where(low == (side == 0), product, 0.0)
                deltas[slot] = jnp.broadcast_to(
                    jnp.sum(mine, axis=1, keepdims=True), (HALF, 128)
                )
                masses[slot] = lse_ref[slot]
        return 0

    lax.fori_loop(0, blocks // 8, unpack, 0)
    both[blocks] = jnp.zeros((BLK, 128), BF16)
    turned[blocks] = jnp.zeros((128, BLK), BF16)
    masses[blocks] = jnp.zeros((HALF, 128), F32)
    deltas[blocks] = jnp.zeros((HALF, 128), F32)

    def clear(slot, _):
        dq_sum[slot] = jnp.zeros((HALF, 128), F32)
        dkv_sum[slot] = jnp.zeros((128, BLK), F32)
        return 0

    lax.fori_loop(0, blocks, clear, 0)
    dq_sum[blocks] = jnp.zeros((HALF, 128), F32)

    def one_pair(q_slot, k_slot):
        kv = kv_ref[k_slot]
        products = dot_nt(both[q_slot], kv)
        mass, delta = masses[q_slot], deltas[q_slot]
        weights = jnp.exp(products[:HALF] - jnp.concatenate([mass, mass], axis=1))
        score_tan = weights * (products[HALF:] - jnp.concatenate([delta, delta], axis=1))
        score_tan = score_tan.astype(BF16)
        sides = jnp.concatenate([score_tan, weights.astype(BF16)], axis=0)
        return dot_nn(turned[q_slot], sides), dot_nn(score_tan, kv)

    def pair_turn(step, _):
        slots = [
            (pairs_ref[0, step * BACK_TOGETHER + part], pairs_ref[1, step * BACK_TOGETHER + part])
            for part in range(BACK_TOGETHER)
        ]
        results = [one_pair(*slot) for slot in slots]
        for (q_slot, k_slot), (dkv, dq) in zip(slots, results):
            dkv_sum[k_slot] = dkv_sum[k_slot] + dkv
            dq_sum[q_slot] = dq_sum[q_slot] + dq
        return 0

    lax.fori_loop(0, pairs_ref[2, 1], pair_turn, 0)

    def finish_rows(step, _):
        for part in range(4):
            source = step * 4 + part
            packed = low_pair(dq_sum[2 * source], dq_sum[2 * source + 1]) * (HD**-0.5)
            dq_ref[source] = packed.astype(BF16)
            for slot in (2 * source, 2 * source + 1):
                dkv_ref[slot] = jnp.transpose(dkv_sum[slot])
        return 0

    lax.fori_loop(0, blocks // 8, finish_rows, 0)


def attend_back(pairs, q, tangent, keep, lse, kv):
    blocks = kv.shape[0]
    return pl.pallas_call(
        functools.partial(backward_kernel, blocks),
        out_shape=(
            jax.ShapeDtypeStruct((blocks // 2, HALF, 128), BF16),
            jax.ShapeDtypeStruct((blocks, BLK, 128), F32),
        ),
        in_specs=[SMEM, VMEM, VMEM, VMEM, VMEM, VMEM],
        out_specs=(VMEM, VMEM),
        scratch_shapes=[
            pltpu.VMEM((blocks + 1, BLK, 128), BF16),
            pltpu.VMEM((blocks + 1, 128, BLK), BF16),
            pltpu.VMEM((blocks + 1, HALF, 128), F32),
            pltpu.VMEM((blocks + 1, HALF, 128), F32),
            pltpu.VMEM((blocks + 1, HALF, 128), F32),
            pltpu.VMEM((blocks, 128, BLK), F32),
        ],
        compiler_params=pltpu.CompilerParams(vmem_limit_bytes=ROOM),
        name="attend_back",
    )(pairs, q, tangent, keep, lse, kv)


def return_kernel(n_ctx, rows_ref, out_ref, ss, rs):
    at = Place()
    at.greet_owners(n_ctx, False)

    def move(target):
        return (
            rows_ref.at[target],
            out_ref.at[at.head, at.f],
            ss.at[target],
            rs.at[at.head * 2 + at.f],
            target,
            at.group,
        )

    for target in range(n_ctx):
        at.send(*move(target))
    for head in range(H):
        for core in range(2):
            arrived = out_ref.at[head, core]
            at.remote(
                arrived, arrived, ss.at[0], rs.at[head * 2 + core], at.c, 1 - at.f
            ).wait_recv()
    for target in range(n_ctx):
        at.wait_sent(*move(target))


def return_rows(n_ctx, rows):
    return pl.pallas_call(
        functools.partial(return_kernel, n_ctx),
        out_shape=jax.ShapeDtypeStruct((H, 2, HALF, 128), BF16),
        in_specs=[ANY],
        out_specs=ANY,
        scratch_shapes=[
            pltpu.SemaphoreType.DMA((n_ctx,)),
            pltpu.SemaphoreType.DMA((2 * H,)),
        ],
        compiler_params=pltpu.CompilerParams(
            collective_id=1, has_side_effects=True, vmem_limit_bytes=ROOM
        ),
        name="return_rows",
    )(rows)


def pieces_of(start, size, body):
    piece = max(n for n in range(16, 97, 16) if size % n == 0)
    lax.fori_loop(
        0,
        size // piece,
        lambda i, _: (body(i * piece, span(start + i * piece, piece), piece), 0)[1],
        0,
    )


def span(start, size):
    return pl.ds(pl.multiple_of(start, 16), size)


def step_of(c, stride):
    bit = (c // stride) % 2
    return bit, c + stride * (1 - 2 * bit)


def feed_slopes(kind, target, mixed, low_turned, hidden, before_tan, feed_tan, branch_tan):
    unit_count = hidden.shape[2] // COLS

    def chunk_slopes(chunk, _):
        columns = pl.ds(pl.multiple_of(chunk * COLS, COLS), COLS)
        target[columns, :] = dot_tn(hidden[kind, :, columns], feed_tan[...]).astype(target.dtype)
        below = pl.ds(pl.multiple_of((unit_count + chunk) * COLS, COLS), COLS)
        target[below, :] = dot_nn(low_turned[...], before_tan[kind, :, columns]).astype(
            target.dtype
        )
        return 0

    lax.fori_loop(0, unit_count, chunk_slopes, 0)
    start = 2 * unit_count * COLS
    target[start : start + D // 2, :] = dot_tn(mixed[kind], branch_tan[...]).astype(target.dtype)


def scatter_kernel(
    n_ctx, rows_ref, mixed, low, hidden, before_tan, feed_tan, branch_tan,
    out_ref, stage_a, stage_b, keep_ref, own_grads, send_grads, first_in, low_turned,
    ss, rs, core_ss, core_rs,
):
    at = Place()
    at.greet_sources(n_ctx, True)
    quarter = first_in.shape[0] // 4
    bits = (step_of(at.c, 1)[0], step_of(at.c, 2)[0])
    stages = (stage_a, stage_b)

    def moves():
        for head in range(H):
            for core in range(2):
                yield (
                    rows_ref.at[head, core],
                    out_ref.at[at.c],
                    ss.at[head * 2 + core],
                    rs.at[at.c],
                    at.f * H + head,
                    core,
                )

    def core_move(region, give):
        bit = bits[region]
        start = region * 2 * quarter + (1 - bit if give else bit) * quarter
        where = span(start, quarter)
        slot = region + 2 * (0 if give else 1)
        return start, at.remote(
            send_grads.at[where], first_in.at[where], core_ss.at[slot], core_rs.at[slot],
            at.c, 1 - at.f,
        )

    order = [(0, True), (1, True), (0, False), (1, False)]
    for move in moves():
        at.send(*move)
    low_turned[...] = jnp.transpose(low[...])
    operands = (mixed, low_turned, hidden, before_tan, feed_tan, branch_tan)
    feed_slopes(1, send_grads, *operands)
    for step in order:
        core_move(*step)[1].start()
    feed_slopes(0, own_grads, *operands)
    for region, give in order:
        start, move = core_move(region, give)
        move.wait_recv()

        def join(offset, where, size):
            total = own_grads[where, :] + first_in[where, :].astype(F32)
            if give:
                stages[region][span(offset, size), :] = total.astype(BF16)
            else:
                keep_ref[region, span(offset, size), :] = total

        pieces_of(start, quarter, join)
    for source in range(n_ctx):
        arrived = out_ref.at[source]
        at.remote(arrived, arrived, ss.at[0], rs.at[source], at.c, 1 - at.f).wait_recv()
    for move in moves():
        at.wait_sent(*move)
    for step in order:
        core_move(*step)[1].wait_send()


def scatter_rows(n_ctx, rows, operands):
    mixed, low, hidden = operands[:3]
    grad_rows = 2 * hidden.shape[2] + D // 2
    return pl.pallas_call(
        functools.partial(scatter_kernel, n_ctx),
        out_shape=(
            jax.ShapeDtypeStruct((n_ctx, HALF, 128), BF16),
            jax.ShapeDtypeStruct((grad_rows // 4, D), BF16),
            jax.ShapeDtypeStruct((grad_rows // 4, D), BF16),
            jax.ShapeDtypeStruct((2, grad_rows // 4, D), F32),
        ),
        in_specs=[ANY] + [VMEM] * 6,
        out_specs=(ANY, VMEM, VMEM, VMEM),
        scratch_shapes=[
            pltpu.VMEM((grad_rows, D), F32),
            pltpu.VMEM((grad_rows, D), BF16),
            pltpu.VMEM((grad_rows, D), BF16),
            pltpu.VMEM((D, low.shape[0]), BF16),
            pltpu.SemaphoreType.DMA((2 * H,)),
            pltpu.SemaphoreType.DMA((n_ctx,)),
            pltpu.SemaphoreType.DMA((4,)),
            pltpu.SemaphoreType.DMA((4,)),
        ],
        compiler_params=pltpu.CompilerParams(
            collective_id=2, has_side_effects=True, vmem_limit_bytes=ROOM
        ),
        name="scatter_rows",
    )(rows, *operands)


class Ladder:
    def __init__(self, at, plans, starts, size, acc, stage, landing, out, sems, bases=(0, 0)):
        self.bases = bases
        self.at, self.acc, self.stage, self.landing, self.out = at, acc, stage, landing, out
        self.down_ss, self.down_rs, self.up_ss, self.up_rs = sems
        self.ranges = []
        for plan, start in zip(plans, starts):
            listed, rows = [], size
            for bit, peer in plan[:-1]:
                rows = rows // 2
                listed.append((start + bit * rows, start + (1 - bit) * rows, rows, peer))
                start = start + bit * rows
            listed.append((start, start, rows, plan[-1][1]))
            self.ranges.append(listed)
        self.last = len(plans[0]) - 1

    def slot(self, region, step):
        return region * (self.last + 1) + step

    def down(self, region, step, sent):
        kept, given, size, peer = self.ranges[region][step]
        where, slot = span(given if sent else kept, size), self.slot(region, step)
        return self.at.remote(
            self.stage[region].at[where],
            self.landing[region][step].at[where],
            self.down_ss.at[slot],
            self.down_rs.at[slot],
            peer,
            self.at.f,
        )

    def up(self, region, step, sent):
        kept, given, size, peer = self.ranges[region][step]
        start = self.bases[region] + (kept if sent else given)
        where, slot = span(start, size), self.slot(region, step)
        return self.at.remote(
            self.out[region].at[where],
            self.out[region].at[where],
            self.up_ss.at[slot],
            self.up_rs.at[slot],
            peer,
            self.at.f,
        )

    def join(self, region, start, size, arrived, target):
        def body(offset, where, _):
            total = self.acc[region][where, :]
            if arrived is not None:
                total = total + arrived[where, :].astype(F32)
            target[where, :] = total.astype(target.dtype)

        pieces_of(start, size, body)

    def give(self, region, step, arrived):
        kept, given, size, _ = self.ranges[region][step]
        self.join(region, given, size, arrived, self.stage[region])
        self.down(region, step, True).start()
        if step < self.last:
            self.join(region, kept, size, arrived, self.acc[region])

    def settle(self, region):
        kept, _, size, _ = self.ranges[region][self.last]
        arrived = self.landing[region][self.last]

        def body(offset, where, rows):
            total = self.stage[region][where, :].astype(F32) + arrived[where, :].astype(F32)
            self.out[region][span(self.bases[region] + kept + offset, rows), :] = total.astype(BF16)

        self.down(region, self.last, False).wait_recv()
        pieces_of(kept, size, body)
        self.up(region, self.last - 1, True).start()

    def wait_sent(self):
        for region in range(2):
            for step in range(self.last + 1):
                self.down(region, step, True).wait_send()
            for step in range(self.last):
                self.up(region, step, True).wait_send()


COLS = 512


def whole_rows(own, other, first):
    return jnp.where(
        first,
        jnp.concatenate([own, other], axis=1),
        jnp.concatenate([other, own], axis=1),
    )


def row_mean(values):
    return jnp.mean(values, axis=1, keepdims=True)


def normalize(values):
    centre = values - row_mean(values)
    scale = lax.rsqrt(row_mean(centre * centre) + norm_eps)
    return centre * scale, scale


def norm_back(tangent, normed, scale, gain):
    pushed = tangent * gain
    return scale * (pushed - row_mean(pushed) - normed * row_mean(pushed * normed))


def column_sum(values):
    return jnp.sum(values, axis=0, keepdims=True)


def dense_kernel(
    x_ref, sum_ref, cot_ref, o_ref,
    wo_a, wo_b, we_a, we_b, ws_a, ws_b, be_ref, vec_in,
    out_ref, sum_tan_ref, entry_ref, tan_ref, vec_ref,
    mixed, low, hidden, before_tan, feed_tan, branch_tan, slope, mixed_tan,
):
    f = lax.axis_index("fsdp")
    wo, we, ws = (wo_a, wo_b), (we_a, we_b), (ws_a, ws_b)
    be = (be_ref.at[0:1], be_ref.at[1:2])
    halves = (f, 1 - f)
    vectors = vec_in[...]
    (out_bias, gain_one, shift_one, shrink_bias, gain_two, shift_two, gain_last, shift_last) = (
        vectors[i : i + 1] for i in range(2, 10)
    )
    for kind in range(2):
        for pair in range(2):
            head = halves[kind] * (H // 2) + 2 * pair
            for core in range(2):
                early = o_ref[head, core].astype(F32)
                late = o_ref[head + 1, core].astype(F32)
                columns = slice(pair * 128, pair * 128 + 128)
                for side in range(2):
                    start = side * BLK + core * HALF
                    mixed[kind, start : start + HALF, columns] = side_pair(
                        side, early, late
                    ).astype(BF16)
    vec_ref[...] = jnp.zeros_like(vec_ref)

    def tile(step, _):
        rows = pl.ds(pl.multiple_of(step * BLK, BLK), BLK)
        branch = (
            dot_nn(mixed[0, rows, :], wo[0][...]) + dot_nn(mixed[1, rows, :], wo[1][...]) + out_bias
        )
        n_one, scale_one = normalize(x_ref[rows, :] + branch)
        normed_one = n_one * gain_one + shift_one
        stream_one = sum_ref[rows, :] + branch
        normed_low = normed_one.astype(BF16)
        low[rows, :] = normed_low
        feed = jnp.zeros((BLK, D), F32)
        for kind in range(2):

            def expand(chunk, carried):
                columns = pl.ds(pl.multiple_of(chunk * COLS, COLS), COLS)
                v = dot_nn(normed_low, we[kind][:, columns]) + be[kind][:, columns]
                square = v * v
                t = jnp.tanh(gelu_coeff * (v + gelu_cubic * square * v))
                half_up = 0.5 + 0.5 * t
                hidden_part = (v * half_up).astype(BF16)
                hidden[kind, rows, columns] = hidden_part
                slope[kind, :, columns] = half_up + v * half_up * (1.0 - t) * (
                    gelu_coeff + (3.0 * gelu_coeff * gelu_cubic) * square
                )
                return carried + dot_nn(hidden_part, ws[kind][columns, :])

            feed = lax.fori_loop(0, ws[kind].shape[0] // COLS, expand, feed)
        feed_out = feed + shrink_bias
        n_two, scale_two = normalize(normed_one + feed_out)
        n_last, scale_last = normalize(stream_one + feed_out)
        out_ref[rows, :] = (n_two * gain_two + shift_two) + (n_last * gain_last + shift_last)
        u = cot_ref[rows, :]
        nudge = column_sum(u)
        sum_tan = norm_back(u, n_last, scale_last, gain_last)
        inflow = norm_back(u, n_two, scale_two, gain_two)
        sum_tan_ref[rows, :] = sum_tan
        feed_low = (sum_tan + inflow).astype(BF16)
        feed_tan[rows, :] = feed_low
        vec_ref[0:1, :] += column_sum(feed_low.astype(F32))
        vec_ref[1:2, :] += column_sum(u * n_two)
        vec_ref[2:3, :] += nudge
        vec_ref[3:4, :] += column_sum(u * n_last)
        vec_ref[4:5, :] += nudge
        normed_tan = inflow
        for kind in range(2):

            def expand_back(chunk, carried):
                columns = pl.ds(pl.multiple_of(chunk * COLS, COLS), COLS)
                pushed = dot_nt(feed_low, ws[kind][columns, :])
                tan_part = (pushed * slope[kind, :, columns]).astype(BF16)
                before_tan[kind, rows, columns] = tan_part
                vec_row = pl.ds(8 + 2 * halves[kind] + chunk, 1)
                vec_ref[vec_row, :] += column_sum(tan_part.astype(F32))
                return carried + dot_nt(tan_part, we[kind][:, columns])

            normed_tan = lax.fori_loop(0, ws[kind].shape[0] // COLS, expand_back, normed_tan)
        vec_ref[5:6, :] += column_sum(normed_tan * n_one)
        vec_ref[6:7, :] += column_sum(normed_tan)
        entry = norm_back(normed_tan, n_one, scale_one, gain_one)
        entry_ref[rows, :] = entry
        branch_low = (sum_tan + entry).astype(BF16)
        branch_tan[rows, :] = branch_low
        vec_ref[7:8, :] += column_sum(branch_low.astype(F32))
        for kind in range(2):
            mixed_tan[kind, rows, :] = dot_nt(branch_low, wo[kind][...])
        return 0

    lax.fori_loop(0, 2, tile, 0)

    for kind in range(2):
        for pair in range(2):
            columns = slice(pair * 128, pair * 128 + 128)
            for side in range(2):
                head = halves[kind] * (H // 2) + 2 * pair + side
                for core in range(2):
                    early = mixed_tan[kind, core * HALF : core * HALF + HALF, columns]
                    late = mixed_tan[kind, BLK + core * HALF : BLK + core * HALF + HALF, columns]
                    tan_ref[head, core] = side_pair(side, early, late).astype(BF16)


def dense(x, summed, cotangent, o, wo, we, ws, be, vec):
    tokens = x.shape[0]
    units = ws[0].shape[0]
    return pl.pallas_call(
        dense_kernel,
        out_shape=(
            jax.ShapeDtypeStruct((tokens, D), F32),
            jax.ShapeDtypeStruct((tokens, D), F32),
            jax.ShapeDtypeStruct((tokens, D), F32),
            jax.ShapeDtypeStruct((H, 2, HALF, 128), BF16),
            jax.ShapeDtypeStruct((16, D), F32),
            jax.ShapeDtypeStruct((2, tokens, D // 2), BF16),
            jax.ShapeDtypeStruct((tokens, D), BF16),
            jax.ShapeDtypeStruct((2, tokens, units), BF16),
            jax.ShapeDtypeStruct((2, tokens, units), BF16),
            jax.ShapeDtypeStruct((tokens, D), BF16),
            jax.ShapeDtypeStruct((tokens, D), BF16),
        ),
        in_specs=[VMEM] * 12,
        out_specs=(VMEM,) * 11,
        scratch_shapes=[
            pltpu.VMEM((2, BLK, units), F32),
            pltpu.VMEM((2, tokens, D // 2), F32),
        ],
        compiler_params=pltpu.CompilerParams(vmem_limit_bytes=ROOM),
        name="dense",
    )(x, summed, cotangent, o, *wo, *we, *ws, be, vec)


def finish_kernel(
    n_ctx,
    dq_ref, dkv_ref, keep_hbm, land_a, land_b, x_hbm, entry_hbm, wq_hbm, wk_hbm, wv_hbm,
    w_other_hbm, vec_feed,
    post_ref, feed_ref, grads_ref, vec_out,
    own, part, ready, dq_in, dkv_in, keep, acc, stage, landing,
    x_in, entry_in, w_in, w_far, low_turned, tangents,
    own_grads, send_grads, first_in, acc_last, stage_last, landing_last, vec_sum, vec_in,
    load_sem, q_ss, q_rs, kv_ss, kv_rs, part_ss, part_rs, own_sem,
    down_ss, down_rs, up_ss, up_rs, top_ss, top_rs,
    core_ss, core_rs, down_ss2, down_rs2, up_ss2, up_rs2, vec_ss, vec_rs,
):
    at = Place()
    c, f = at.c, at.f
    other = 1 - f
    halves = (f, other)
    wide = D // 2
    loads = [
        pltpu.make_async_copy(src, dst, load_sem.at[i])
        for i, (src, dst) in enumerate(
            (
                (keep_hbm, keep),
                (x_hbm, x_in),
                (entry_hbm, entry_in),
                (wq_hbm, w_in.at[0]),
                (wk_hbm, w_in.at[1]),
                (wv_hbm, w_in.at[2]),
                (w_other_hbm, w_far),
            )
        )
    ]
    for load in loads:
        load.start()
    x_step, y_step, near, far = (step_of(c, stride) for stride in (1, 2, 4, 8))
    barrier = pltpu.get_barrier_semaphore()
    for _, peer in (x_step, y_step, near, far):
        pl.semaphore_signal(barrier, 1, device_id=(peer, f), device_id_type=MESH)
    at.greet_owners(n_ctx, True, 4)

    def partial_move(source):
        return at.remote(
            dkv_ref.at[2 * source + other],
            part.at[source],
            part_ss.at[source],
            part_rs.at[source],
            c,
            other,
        )

    def own_move(source):
        return pltpu.make_async_copy(
            dkv_ref.at[2 * source + f], own.at[source], own_sem.at[source]
        )

    def q_move(target):
        return (
            dq_ref.at[target],
            dq_in.at[at.head, f],
            q_ss.at[target],
            q_rs.at[at.head * 2 + f],
            target,
            at.group,
        )

    def kv_move(target):
        return (
            ready.at[target],
            dkv_in.at[at.head, pl.ds(pl.multiple_of(f * BLK, BLK), BLK)],
            kv_ss.at[target],
            kv_rs.at[at.head * 2 + f],
            target,
            at.group,
        )

    for source in range(n_ctx):
        partial_move(source).start()
        own_move(source).start()
    for target in range(n_ctx):
        at.send(*q_move(target))

    size = keep.shape[1]
    firsts = (x_step, y_step)
    bases = [2 * size * region + firsts[region][0] * size for region in range(2)]
    feed = Ladder(
        at,
        ((y_step, near, far), (x_step, near, far)),
        (0, 0),
        size,
        [keep.at[region] for region in range(2)],
        [stage.at[region] for region in range(2)],
        [[landing.at[region, step] for step in range(3)] for region in range(2)],
        [feed_ref, feed_ref],
        (down_ss, down_rs, up_ss, up_rs),
        bases,
    )

    def top_move(region, sent):
        kept = bases[region]
        given = 2 * size * region + (1 - firsts[region][0]) * size
        where = span(kept if sent else given, size)
        return at.remote(
            feed_ref.at[where],
            feed_ref.at[where],
            top_ss.at[region],
            top_rs.at[region],
            firsts[region][1],
            f,
        )

    loads[0].wait()
    for region, first in enumerate((land_a, land_b)):
        kept, given, half, _ = feed.ranges[region][0]
        feed.join(region, given, half, first, stage.at[region])
        feed.down(region, 0, True).start()
        feed.join(region, kept, half, first, acc.at[region])
        feed.acc[region] = acc.at[region]
    for source in range(n_ctx):
        own_move(source).wait()
        partial_move(source).wait_recv()
        ready[source] = (own[source] + part[source]).astype(BF16)
        at.send(*kv_move(source))
    for load in loads[1:]:
        load.wait()
    low_turned[...] = jnp.transpose(x_in[...]).astype(BF16)
    for step in (1, 2):
        for region in range(2):
            feed.down(region, step - 1, False).wait_recv()
            feed.give(region, step, feed.landing[region][step - 1])

    for head in range(H):
        for core in range(2):
            slot = head * 2 + core
            arrived = dq_in.at[head, core]
            at.remote(arrived, arrived, q_ss.at[0], q_rs.at[slot], c, other).wait_recv()
            arrived = dkv_in.at[head, pl.ds(core * BLK, BLK)]
            at.remote(arrived, arrived, kv_ss.at[0], kv_rs.at[slot], c, other).wait_recv()
    feed_rows = vec_feed.shape[0]
    vec_sum[0, 0:feed_rows] = vec_feed[...]
    vec_sum[0, feed_rows:] = jnp.zeros_like(vec_sum[0, feed_rows:])

    plans = ((x_step, y_step, near, far), (y_step, x_step, near, far))
    quarter = first_in.shape[0] // 4
    last = Ladder(
        at,
        plans,
        (0, 2 * quarter),
        2 * quarter,
        [acc_last, acc_last],
        [stage_last, stage_last],
        [[landing_last.at[step] for step in range(4)]] * 2,
        [grads_ref, grads_ref],
        (down_ss2, down_rs2, up_ss2, up_rs2),
    )

    def core_move(region, give):
        kept, given, rows, _ = last.ranges[region][0]
        where = span(given if give else kept, rows)
        slot = region + 2 * (0 if give else 1)
        return at.remote(
            send_grads.at[where], first_in.at[where], core_ss.at[slot], core_rs.at[slot], c, other
        )

    order = [(0, True), (1, True), (0, False), (1, False)]
    vec_peers = [(c, other)] + [(peer, f) for _, peer in (x_step, y_step, near, far)]

    def vec_move(step):
        return at.remote(
            vec_sum.at[step], vec_in.at[step], vec_ss.at[step], vec_rs.at[step], *vec_peers[step]
        )

    def vec_next(step):
        vec_move(step).wait_recv()
        target = vec_sum.at[step + 1] if step < 4 else vec_out
        target[...] = vec_sum[step] + vec_in[step]
        if step < 4:
            vec_move(step + 1).start()

    for kind, grad_ref in ((1, send_grads), (0, own_grads)):
        for pair in range(2):
            head = halves[kind] * (H // 2) + 2 * pair
            columns = slice(pair * 128, pair * 128 + 128)
            for core in range(2):
                early = dq_in[head, core].astype(F32)
                late = dq_in[head + 1, core].astype(F32)
                for side in range(2):
                    start = side * BLK + core * HALF
                    tangents[kind, 0, start : start + HALF, columns] = side_pair(
                        side, early, late
                    ).astype(BF16)
            early = dkv_in[head].astype(F32)
            late = dkv_in[head + 1].astype(F32)
            tangents[kind, 1, :, columns] = low_pair(early, late).astype(BF16)
            tangents[kind, 2, :, columns] = high_pair(early, late).astype(BF16)
        turned = low_turned[...]
        grad_ref[0:D, 0:wide] = dot_nn(turned, tangents[kind, 0]).astype(grad_ref.dtype)
        grad_ref[0:D, wide:D] = dot_nn(turned, tangents[kind, 1]).astype(grad_ref.dtype)
        value_grad = dot_nn(turned, tangents[kind, 2]).astype(grad_ref.dtype)
        grad_ref[D : D + wide, 0:wide] = value_grad[0:wide]
        grad_ref[D : D + wide, wide:D] = value_grad[wide:D]
        columns = pl.ds(pl.multiple_of(halves[kind] * wide, wide), wide)
        vec_sum[0, feed_rows : feed_rows + 1, columns] = column_sum(tangents[kind, 0].astype(F32))
        vec_sum[0, feed_rows + 1 : feed_rows + 2, columns] = column_sum(
            tangents[kind, 2].astype(F32)
        )
        if kind == 1:
            for step in order:
                core_move(*step).start()
    vec_move(0).start()
    for region in range(2):
        feed.settle(region)
    for region, give in order:
        core_move(region, give).wait_recv()
        kept, given, rows, _ = last.ranges[region][0]

        def join(offset, where, _):
            total = own_grads[where, :] + first_in[where, :].astype(F32)
            if give:
                stage_last[where, :] = total.astype(BF16)
            else:
                acc_last[where, :] = total

        pieces_of(given if give else kept, rows, join)
        if give:
            last.down(region, 0, True).start()
    vec_next(0)
    total = entry_in[...]
    for which in range(3):
        total = total + dot_nt(tangents[0, which], w_in[which])
        total = total + dot_nt(tangents[1, which], w_far[which])
    post_ref[...] = total
    for region in range(2):
        feed.up(region, 1, False).wait_recv()
        feed.up(region, 0, True).start()
    for step in (1, 2):
        for region in range(2):
            last.down(region, step - 1, False).wait_recv()
            last.give(region, step, last.landing[region][step - 1])
        vec_next(step)
    for region in range(2):
        feed.up(region, 0, False).wait_recv()
        top_move(region, True).start()
    for region in range(2):
        last.down(region, 2, False).wait_recv()
        last.give(region, 3, last.landing[region][2])
    vec_next(3)
    for region in range(2):
        last.settle(region)
    vec_next(4)
    for step in (2, 1, 0):
        for region in range(2):
            last.up(region, step, False).wait_recv()
            if step > 0:
                last.up(region, step - 1, True).start()
    for region in range(2):
        top_move(region, False).wait_recv()

    for target in range(n_ctx):
        partial_move(target).wait_send()
        at.wait_sent(*q_move(target))
        at.wait_sent(*kv_move(target))
    for step in order:
        core_move(*step).wait_send()
    for step in range(5):
        vec_move(step).wait_send()
    for region in range(2):
        top_move(region, True).wait_send()
    feed.wait_sent()
    last.wait_sent()


def finish(n_ctx, dq, dkv, keep, land_a, land_b, x, entry, wq, wk, wv, w_other, vec_feed):
    size, tokens, wide = keep.shape[1], x.shape[0], D // 2
    last_shape = (D + wide, D)
    vec_shape = (vec_feed.shape[0] + 8, D)

    def sems(*counts):
        return [pltpu.SemaphoreType.DMA((count,)) for count in counts]

    return pl.pallas_call(
        functools.partial(finish_kernel, n_ctx),
        out_shape=(
            jax.ShapeDtypeStruct((tokens, D), F32),
            jax.ShapeDtypeStruct((4 * size, D), BF16),
            jax.ShapeDtypeStruct(last_shape, BF16),
            jax.ShapeDtypeStruct(vec_shape, F32),
        ),
        in_specs=[ANY, ANY, ANY, VMEM, VMEM] + [ANY] * 6 + [VMEM],
        out_specs=(VMEM,) * 4,
        scratch_shapes=[
            pltpu.VMEM((n_ctx, BLK, 128), F32),
            pltpu.VMEM((n_ctx, BLK, 128), F32),
            pltpu.VMEM((n_ctx, BLK, 128), BF16),
            pltpu.VMEM((H, 2, HALF, 128), BF16),
            pltpu.VMEM((H, 2 * BLK, 128), BF16),
            pltpu.VMEM((2, size, D), F32),
            pltpu.VMEM((2, size, D), F32),
            pltpu.VMEM((2, size, D), BF16),
            pltpu.VMEM((2, 3, size, D), BF16),
            pltpu.VMEM((tokens, D), F32),
            pltpu.VMEM((tokens, D), F32),
            pltpu.VMEM((3, D, wide), BF16),
            pltpu.VMEM((3, D, wide), BF16),
            pltpu.VMEM((D, tokens), BF16),
            pltpu.VMEM((2, 3, tokens, wide), BF16),
            pltpu.VMEM(last_shape, F32),
            pltpu.VMEM(last_shape, BF16),
            pltpu.VMEM(last_shape, BF16),
            pltpu.VMEM(last_shape, F32),
            pltpu.VMEM(last_shape, BF16),
            pltpu.VMEM((4,) + last_shape, BF16),
            pltpu.VMEM((5,) + vec_shape, F32),
            pltpu.VMEM((5,) + vec_shape, F32),
        ]
        + sems(7, n_ctx, 2 * H, n_ctx, 2 * H, n_ctx, n_ctx, n_ctx)
        + sems(6, 6, 6, 6, 2, 2, 4, 4, 8, 8, 8, 8, 5, 5),
        compiler_params=pltpu.CompilerParams(
            collective_id=3, has_side_effects=True, vmem_limit_bytes=ROOM
        ),
        name="finish",
    )(dq, dkv, keep, land_a, land_b, x, entry, wq, wk, wv, w_other, vec_feed)


def unpack_kernel(
    full, grads_ref, vec_ref,
    query_ref, key_ref, value_ref, output_ref, expand_ref, shrink_ref, *vector_outs,
):
    f = lax.axis_index("fsdp")
    units, wide = shrink_ref.shape[0], D // 2
    shrink_ref[...] = full[0:units].astype(F32)
    for part in range(units // D):
        start = units + part * D
        expand_ref[:, part * D : part * D + D] = full[start : start + D].astype(F32)
    output_ref[...] = full[2 * units : 2 * units + wide].astype(F32)
    query_ref[...] = grads_ref[0:D, 0:wide].astype(F32)
    key_ref[...] = grads_ref[0:D, wide:D].astype(F32)
    value_ref[0:wide] = grads_ref[D : D + wide, 0:wide].astype(F32)
    value_ref[wide:D] = grads_ref[D : D + wide, wide:D].astype(F32)
    vectors = vec_ref[...]
    mine = jnp.where(f == 0, vectors[:, 0:wide], vectors[:, wide:D])
    for row, ref in zip((16, 17, 7, 5, 6, 0, 1, 2, 3, 4), vector_outs):
        ref[...] = mine[row : row + 1]
    drift = jnp.where(f == 0, vectors[8:10], vectors[10:12])
    for part in range(units // D):
        vector_outs[10][:, part * D : part * D + D] = drift[part : part + 1]


def unpack_grads(units, full, grads, vecs):
    wide = D // 2
    shapes = [(D, wide)] * 3 + [(wide, D), (D, units), (units, D)] + [(1, wide)] * 10 + [(1, units)]
    return pl.pallas_call(
        unpack_kernel,
        out_shape=tuple(jax.ShapeDtypeStruct(shape, F32) for shape in shapes),
        in_specs=[VMEM] * 3,
        out_specs=(VMEM,) * len(shapes),
        compiler_params=pltpu.CompilerParams(vmem_limit_bytes=ROOM),
        name="unpack_grads",
    )(full, grads, vecs)


def head_shards(
    n_ctx,
    post_stream,
    sum_stream,
    cotangent,
    block_order,
    block_sequence,
    query_weight,
    key_weight,
    value_weight,
    output_weight,
    query_bias,
    value_bias,
    output_bias,
    attend_gain,
    attend_shift,
    expand_weight,
    expand_bias,
    shrink_weight,
    shrink_bias,
    middle_gain,
    middle_shift,
    final_gain,
    final_shift,
):
    x, summed, tangent = post_stream[0], sum_stream[0], cotangent[0]
    swap = [(0, 1), (1, 0)]

    def from_other(values):
        return lax.ppermute(values, "fsdp", swap)

    def across(values, stride):
        return lax.ppermute(values, "ctx", [(c, c ^ stride) for c in range(n_ctx)])

    vectors = [
        query_bias,
        value_bias,
        output_bias,
        attend_gain,
        attend_shift,
        shrink_bias,
        middle_gain,
        middle_shift,
        final_gain,
        final_shift,
        expand_bias,
    ]
    q, kv, w_other, order, seqs, vec, expand_add = project_and_scatter(
        n_ctx, x, query_weight, key_weight, value_weight, block_order, block_sequence, vectors
    )
    o, keep, lse, pairs = attend(order, seqs, q, kv)
    o_rows = return_rows(n_ctx, o)
    layer_output, sum_tan, entry, tan_rows, vec_feed, *operands = dense(
        x,
        summed,
        tangent,
        o_rows,
        (output_weight, from_other(output_weight)),
        (expand_weight, from_other(expand_weight)),
        (shrink_weight, from_other(shrink_weight)),
        expand_add,
        vec,
    )
    tan, stage_a, stage_b, kept = scatter_rows(n_ctx, tan_rows, operands)
    land_a, land_b = across(stage_a, 1), across(stage_b, 2)
    dq, dkv = attend_back(pairs, q, tan, keep, lse, kv)
    post_tangent, feed_sums, last_sums, vecs = finish(
        n_ctx,
        dq,
        dkv,
        kept,
        land_a,
        land_b,
        x,
        entry,
        query_weight,
        key_weight,
        value_weight,
        w_other,
        vec_feed,
    )
    (
        query_slope,
        key_slope,
        value_slope,
        output_slope,
        expand_slope,
        shrink_slope,
        query_drift,
        value_drift,
        output_drift,
        attend_stretch,
        attend_nudge,
        shrink_drift,
        middle_stretch,
        middle_nudge,
        final_stretch,
        final_nudge,
        expand_drift,
    ) = unpack_grads(shrink_weight.shape[0], feed_sums, last_sums, vecs)
    return (
        layer_output[None],
        post_tangent[None],
        sum_tan[None],
        query_slope,
        key_slope,
        value_slope,
        output_slope,
        query_drift[0],
        value_drift[0],
        output_drift[0],
        attend_stretch[0],
        attend_nudge[0],
        expand_slope,
        expand_drift[0],
        shrink_slope,
        shrink_drift[0],
        middle_stretch[0],
        middle_nudge[0],
        final_stretch[0],
        final_nudge[0],
    )


def solution(mesh):
    n_ctx, n_fsdp = mesh.shape["ctx"], mesh.shape["fsdp"]
    if n_fsdp == 2 and n_ctx == n_fsdp * H:
        body = functools.partial(head_shards, n_ctx)
    else:
        body = general_shards
    return jax.shard_map(
        body,
        mesh=mesh,
        in_specs=(
            P("fsdp", "ctx", None),
            P("fsdp", "ctx", None),
            P("fsdp", "ctx", None),
            P("fsdp", None),
            P("fsdp", None),
            P(None, "fsdp"),
            P(None, "fsdp"),
            P(None, "fsdp"),
            P("fsdp", None),
            P("fsdp"),
            P("fsdp"),
            P("fsdp"),
            P("fsdp"),
            P("fsdp"),
            P(None, "fsdp"),
            P("fsdp"),
            P("fsdp", None),
            P("fsdp"),
            P("fsdp"),
            P("fsdp"),
            P("fsdp"),
            P("fsdp"),
        ),
        out_specs=(
            P("fsdp", "ctx", None),
            P("fsdp", "ctx", None),
            P("fsdp", "ctx", None),
            P(None, "fsdp"),
            P(None, "fsdp"),
            P(None, "fsdp"),
            P("fsdp", None),
            P("fsdp"),
            P("fsdp"),
            P("fsdp"),
            P("fsdp"),
            P("fsdp"),
            P(None, "fsdp"),
            P("fsdp"),
            P("fsdp", None),
            P("fsdp"),
            P("fsdp"),
            P("fsdp"),
            P("fsdp"),
            P("fsdp"),
        ),
        check_vma=False,
    )
```

```python
import functools

import jax
import jax.numpy as jnp
from jax import lax
from jax.experimental import pallas as pl
from jax.experimental.pallas import tpu as pltpu
from jax.sharding import PartitionSpec as P

D = 512
H = 8
HD = 64
BLK = 256
HALF = BLK // 2
LONG = 8
TOGETHER = 16
BACK_TOGETHER = 16
MOST = LONG + 1
F32 = jnp.float32
BF16 = jnp.bfloat16
MESH = pl.DeviceIdType.MESH
ROOM = 60 << 20
VMEM = pl.BlockSpec(memory_space=pltpu.VMEM)
SMEM = pl.BlockSpec(memory_space=pltpu.SMEM)
ANY = pl.BlockSpec(memory_space=pltpu.HBM)


norm_eps = 1e-05
masked_value = -1e30
gelu_coeff = 0.7978845608
gelu_cubic = 0.044715


def smooth_gate(values):
    return (
        0.5
        * values
        * (1.0 + jnp.tanh(gelu_coeff * (values + gelu_cubic * values * values * values)))
    )


def layer_norm(inputs, gain_row, shift_row):
    centre = inputs - jnp.mean(inputs, axis=-1, keepdims=True)
    spread = jnp.mean(centre * centre, axis=-1, keepdims=True)
    return centre * lax.rsqrt(spread + norm_eps) * gain_row + shift_row


def product(left_side, right_side):
    return jnp.dot(left_side, right_side, preferred_element_type=jnp.float32)


def cross_rows(left_side, right_side):
    return lax.dot_general(
        left_side, right_side, (((0,), (0,)), ((), ())), preferred_element_type=jnp.float32
    )


def cross_cols(left_side, right_side):
    return lax.dot_general(
        left_side, right_side, (((1,), (1,)), ((), ())), preferred_element_type=jnp.float32
    )


def column_total(values):
    return jnp.sum(values, axis=0, dtype=jnp.float32)


def lookup(table_row, indices):
    places = jnp.arange(table_row.shape[0], dtype=jnp.int32)
    return jnp.sum(jnp.where(indices[:, None] == places[None, :], table_row[None, :], 0), axis=1)


def block_mask(query_blocks, query_seqs, key_blocks, key_seqs):
    same_seq = query_seqs[:, None] == key_seqs[None, :]
    return same_seq & (key_blocks[None, :] <= query_blocks[:, None])


def token_mask(visible):
    return jnp.repeat(jnp.repeat(visible, BLK, axis=0), BLK, axis=1)


def fold_units(carried, members, unit_step):
    unit_count = members[0].shape[0] // BLK
    inner_count = max((divisor for divisor in range(1, 17) if unit_count % divisor == 0))
    outer_count = unit_count // inner_count

    def outer_turn(outer_index, current):

        def inner_turn(inner_index, inner_state):
            offset = (outer_index * inner_count + inner_index) * BLK
            pieces = tuple((lax.dynamic_slice_in_dim(member, offset, BLK, 0) for member in members))
            return unit_step(inner_state, pieces, offset)

        return lax.fori_loop(0, inner_count, inner_turn, current)

    return lax.fori_loop(0, outer_count, outer_turn, carried)


def general_shards(
    post_stream,
    sum_stream,
    cotangent,
    block_order,
    block_sequence,
    query_weight,
    key_weight,
    value_weight,
    output_weight,
    query_bias,
    value_bias,
    output_bias,
    attend_gain,
    attend_shift,
    expand_weight,
    expand_bias,
    shrink_weight,
    shrink_bias,
    middle_gain,
    middle_shift,
    final_gain,
    final_shift,
):
    (
        query_whole,
        key_whole,
        value_whole,
        output_whole,
        query_add,
        value_add,
        output_add,
        gain_one,
        shift_one,
        expand_whole,
        expand_add,
        shrink_whole,
        shrink_add,
        gain_two,
        shift_two,
        gain_last,
        shift_last,
    ) = (
        lax.all_gather(query_weight, "fsdp", axis=1, tiled=True),
        lax.all_gather(key_weight, "fsdp", axis=1, tiled=True),
        lax.all_gather(value_weight, "fsdp", axis=1, tiled=True),
        lax.all_gather(output_weight, "fsdp", axis=0, tiled=True),
        lax.all_gather(query_bias, "fsdp", axis=0, tiled=True),
        lax.all_gather(value_bias, "fsdp", axis=0, tiled=True),
        lax.all_gather(output_bias, "fsdp", axis=0, tiled=True),
        lax.all_gather(attend_gain, "fsdp", axis=0, tiled=True),
        lax.all_gather(attend_shift, "fsdp", axis=0, tiled=True),
        lax.all_gather(expand_weight, "fsdp", axis=1, tiled=True),
        lax.all_gather(expand_bias, "fsdp", axis=0, tiled=True),
        lax.all_gather(shrink_weight, "fsdp", axis=0, tiled=True),
        lax.all_gather(shrink_bias, "fsdp", axis=0, tiled=True),
        lax.all_gather(middle_gain, "fsdp", axis=0, tiled=True),
        lax.all_gather(middle_shift, "fsdp", axis=0, tiled=True),
        lax.all_gather(final_gain, "fsdp", axis=0, tiled=True),
        lax.all_gather(final_shift, "fsdp", axis=0, tiled=True),
    )
    post_rows = post_stream[0]
    summed = sum_stream[0]
    tangent = cotangent[0]
    order_row = block_order[0]
    seq_row = block_sequence[0]
    token_count = post_rows.shape[0]
    score_scale = HD ** (-0.5)
    own_blocks = lax.dynamic_slice_in_dim(
        order_row, lax.axis_index("ctx") * (token_count // BLK), token_count // BLK
    )
    own_seqs = lookup(seq_row, own_blocks)
    post_low = post_rows.astype(jnp.bfloat16)
    queries = (product(post_low, query_whole) + query_add).astype(jnp.bfloat16)
    key_rows = product(post_low, key_whole).astype(jnp.bfloat16)
    value_rows = (product(post_low, value_whole) + value_add).astype(jnp.bfloat16)
    query_heads = queries.reshape(token_count, H, HD)

    def keys_visible(first_row):
        key_block = lax.dynamic_slice_in_dim(order_row, first_row // BLK, 1)
        return block_mask(own_blocks, own_seqs, key_block, lookup(seq_row, key_block))

    def masked_fold(block_step):

        def unit_step(current, pieces, first_row):
            visible = keys_visible(first_row)
            return lax.cond(
                jnp.any(visible),
                lambda inner_state: block_step(inner_state, pieces, visible),
                lambda inner_state: inner_state,
                current,
            )

        def folded(current, pieces, first_row):
            return fold_units(current, pieces, unit_step)

        return folded

    def stats_block(current, pieces, visible):
        row_peaks, masses = current
        key_heads = pieces[0].reshape(BLK, H, HD)
        row_mask = token_mask(visible)[None]
        scores = (
            jnp.einsum("qhd,khd->hqk", query_heads, key_heads, preferred_element_type=jnp.float32)
            * score_scale
        )
        new_peaks = jnp.maximum(
            row_peaks, jnp.max(jnp.where(row_mask, scores, masked_value), axis=2)
        )
        weights = jnp.where(row_mask, jnp.exp(scores - new_peaks[:, :, None]), 0.0)
        return (new_peaks, masses * jnp.exp(row_peaks - new_peaks) + jnp.sum(weights, axis=2))

    stats_fold = masked_fold(stats_block)
    stats_start = (
        jnp.full((H, token_count), masked_value, jnp.float32),
        jnp.zeros((H, token_count), jnp.float32),
    )
    row_peaks, masses = stats_fold(
        stats_start, (lax.all_gather(key_rows, "ctx", axis=0, tiled=True),), jnp.int32(0)
    )
    log_mass = row_peaks + jnp.log(masses)

    def forward_block(current, pieces, visible):
        key_heads = pieces[0].reshape(BLK, H, HD)
        value_heads = pieces[1].reshape(BLK, H, HD)
        row_mask = token_mask(visible)[None]
        scores = (
            jnp.einsum("qhd,khd->hqk", query_heads, key_heads, preferred_element_type=jnp.float32)
            * score_scale
        )
        weights = jnp.where(row_mask, jnp.exp(scores - log_mass[:, :, None]), 0.0).astype(
            jnp.bfloat16
        )
        addition = jnp.einsum(
            "hqk,khd->qhd", weights, value_heads, preferred_element_type=jnp.float32
        )
        return current + addition.reshape(token_count, D)

    forward_fold = masked_fold(forward_block)
    zero_rows = jnp.zeros((token_count, D), jnp.float32)
    attended = forward_fold(
        zero_rows,
        (
            lax.all_gather(key_rows, "ctx", axis=0, tiled=True),
            lax.all_gather(value_rows, "ctx", axis=0, tiled=True),
        ),
        jnp.int32(0),
    )
    mixed_low = attended.astype(jnp.bfloat16)
    branch = product(mixed_low, output_whole) + output_add
    normed_one, first_pull = jax.vjp(
        layer_norm, post_rows + branch, gain_one.astype(jnp.float32), shift_one.astype(jnp.float32)
    )
    stream_one = summed + branch
    normed_low = normed_one.astype(jnp.bfloat16)
    before = product(normed_low, expand_whole) + expand_add
    gated, gate_pull = jax.vjp(smooth_gate, before)
    hidden = gated.astype(jnp.bfloat16)
    feed_out = product(hidden, shrink_whole) + shrink_add
    normed_two, middle_pull = jax.vjp(
        layer_norm,
        normed_one + feed_out,
        gain_two.astype(jnp.float32),
        shift_two.astype(jnp.float32),
    )
    stream_two = stream_one + feed_out
    last_norm, last_pull = jax.vjp(
        layer_norm, stream_two, gain_last.astype(jnp.float32), shift_last.astype(jnp.float32)
    )
    layer_output = normed_two + last_norm
    stream_tan, stretch_last, nudge_last = last_pull(tangent)
    inflow_tan, stretch_two, nudge_two = middle_pull(tangent)
    feed_tan = (stream_tan + inflow_tan).astype(jnp.bfloat16)
    slope_shrink = cross_rows(hidden, feed_tan)
    drift_shrink = column_total(feed_tan)
    before_tan = gate_pull(cross_cols(feed_tan, shrink_whole))[0].astype(jnp.bfloat16)
    slope_expand = cross_rows(normed_low, before_tan)
    drift_expand = column_total(before_tan)
    normed_tan = inflow_tan + cross_cols(before_tan, expand_whole)
    feed_parts = lax.psum(
        (
            slope_expand,
            drift_expand,
            slope_shrink,
            drift_shrink,
            stretch_two,
            nudge_two,
            stretch_last,
            nudge_last,
        ),
        "ctx",
    )
    feed_sums = (
        lax.psum_scatter(feed_parts[0], "fsdp", scatter_dimension=1, tiled=True),
        lax.psum_scatter(feed_parts[1], "fsdp", scatter_dimension=0, tiled=True),
        lax.psum_scatter(feed_parts[2], "fsdp", scatter_dimension=0, tiled=True),
        lax.psum_scatter(feed_parts[3], "fsdp", scatter_dimension=0, tiled=True),
        lax.psum_scatter(feed_parts[4], "fsdp", scatter_dimension=0, tiled=True),
        lax.psum_scatter(feed_parts[5], "fsdp", scatter_dimension=0, tiled=True),
        lax.psum_scatter(feed_parts[6], "fsdp", scatter_dimension=0, tiled=True),
        lax.psum_scatter(feed_parts[7], "fsdp", scatter_dimension=0, tiled=True),
    )
    entry_tan, stretch_one, nudge_one = first_pull(normed_tan)
    branch_tan = (stream_tan + entry_tan).astype(jnp.bfloat16)
    slope_output = cross_rows(mixed_low, branch_tan)
    drift_output = column_total(branch_tan)
    mixed_tan = cross_cols(branch_tan, output_whole).astype(jnp.bfloat16)
    tangent_heads = mixed_tan.reshape(token_count, H, HD)
    deltas = jnp.sum((mixed_tan * attended).reshape(token_count, H, HD), axis=2).T

    def query_block(current, pieces, visible):
        key_heads = pieces[0].reshape(BLK, H, HD)
        value_heads = pieces[1].reshape(BLK, H, HD)
        row_mask = token_mask(visible)[None]
        scores = (
            jnp.einsum("qhd,khd->hqk", query_heads, key_heads, preferred_element_type=jnp.float32)
            * score_scale
        )
        probability = jnp.where(row_mask, jnp.exp(scores - log_mass[:, :, None]), 0.0)
        prob_tan = jnp.einsum(
            "qhd,khd->hqk", tangent_heads, value_heads, preferred_element_type=jnp.float32
        )
        score_tan = (probability * (prob_tan - deltas[:, :, None])).astype(jnp.bfloat16)
        addition = jnp.einsum(
            "hqk,khd->qhd", score_tan, key_heads, preferred_element_type=jnp.float32
        )
        return current + addition.reshape(token_count, D) * score_scale

    query_fold = masked_fold(query_block)
    query_sum = query_fold(
        zero_rows,
        (
            lax.all_gather(key_rows, "ctx", axis=0, tiled=True),
            lax.all_gather(value_rows, "ctx", axis=0, tiled=True),
        ),
        jnp.int32(0),
    )
    gathered_mass, gathered_delta = (
        lax.all_gather(log_mass.T, "ctx", axis=0, tiled=True),
        lax.all_gather(deltas.T, "ctx", axis=0, tiled=True),
    )
    own_keys = key_rows.reshape(token_count, H, HD)
    own_values = value_rows.reshape(token_count, H, HD)

    def owner_block(current, pieces, first_row, visible):
        key_acc, value_acc = current
        part_queries = pieces[0].reshape(BLK, H, HD)
        part_tangent = pieces[1].reshape(BLK, H, HD)
        part_mass = lax.dynamic_slice_in_dim(gathered_mass, first_row, BLK, 0).T
        part_delta = lax.dynamic_slice_in_dim(gathered_delta, first_row, BLK, 0).T
        row_mask = token_mask(visible)[None]
        scores = (
            jnp.einsum("qhd,khd->hqk", part_queries, own_keys, preferred_element_type=jnp.float32)
            * score_scale
        )
        probability = jnp.where(row_mask, jnp.exp(scores - part_mass[:, :, None]), 0.0)
        value_add_rows = jnp.einsum(
            "hqk,qhd->khd",
            probability.astype(jnp.bfloat16),
            part_tangent,
            preferred_element_type=jnp.float32,
        )
        prob_tan = jnp.einsum(
            "qhd,khd->hqk", part_tangent, own_values, preferred_element_type=jnp.float32
        )
        score_tan = (probability * (prob_tan - part_delta[:, :, None])).astype(jnp.bfloat16)
        key_add_rows = jnp.einsum(
            "hqk,qhd->khd", score_tan, part_queries, preferred_element_type=jnp.float32
        )
        return (
            key_acc + key_add_rows.reshape(token_count, D) * score_scale,
            value_acc + value_add_rows.reshape(token_count, D),
        )

    def owner_unit(current, pieces, first_row):
        query_blocks = lax.dynamic_slice_in_dim(order_row, first_row // BLK, 1)
        visible = block_mask(query_blocks, lookup(seq_row, query_blocks), own_blocks, own_seqs)
        return lax.cond(
            jnp.any(visible),
            lambda inner_state: owner_block(inner_state, pieces, first_row, visible),
            lambda inner_state: inner_state,
            current,
        )

    key_sum, value_sum = fold_units(
        (zero_rows, zero_rows),
        (
            lax.all_gather(queries, "ctx", axis=0, tiled=True),
            lax.all_gather(mixed_tan, "ctx", axis=0, tiled=True),
        ),
        owner_unit,
    )
    query_tan = query_sum.astype(jnp.bfloat16)
    key_tan = key_sum.astype(jnp.bfloat16)
    value_tan = value_sum.astype(jnp.bfloat16)
    slope_query = cross_rows(post_low, query_tan)
    slope_key = cross_rows(post_low, key_tan)
    slope_value = cross_rows(post_low, value_tan)
    drift_query = column_total(query_tan)
    drift_value = column_total(value_tan)
    post_tangent = (
        entry_tan
        + cross_cols(query_tan, query_whole)
        + cross_cols(key_tan, key_whole)
        + cross_cols(value_tan, value_whole)
    )
    heads_parts = lax.psum(
        (
            slope_query,
            slope_key,
            slope_value,
            slope_output,
            drift_query,
            drift_value,
            drift_output,
            stretch_one,
            nudge_one,
        ),
        "ctx",
    )
    heads_sums = (
        lax.psum_scatter(heads_parts[0], "fsdp", scatter_dimension=1, tiled=True),
        lax.psum_scatter(heads_parts[1], "fsdp", scatter_dimension=1, tiled=True),
        lax.psum_scatter(heads_parts[2], "fsdp", scatter_dimension=1, tiled=True),
        lax.psum_scatter(heads_parts[3], "fsdp", scatter_dimension=0, tiled=True),
        lax.psum_scatter(heads_parts[4], "fsdp", scatter_dimension=0, tiled=True),
        lax.psum_scatter(heads_parts[5], "fsdp", scatter_dimension=0, tiled=True),
        lax.psum_scatter(heads_parts[6], "fsdp", scatter_dimension=0, tiled=True),
        lax.psum_scatter(heads_parts[7], "fsdp", scatter_dimension=0, tiled=True),
        lax.psum_scatter(heads_parts[8], "fsdp", scatter_dimension=0, tiled=True),
    )
    return (
        layer_output[None],
        post_tangent[None],
        stream_tan[None],
        heads_sums[0],
        heads_sums[1],
        heads_sums[2],
        heads_sums[3],
        heads_sums[4],
        heads_sums[5],
        heads_sums[6],
        heads_sums[7],
        heads_sums[8],
        feed_sums[0],
        feed_sums[1],
        feed_sums[2],
        feed_sums[3],
        feed_sums[4],
        feed_sums[5],
        feed_sums[6],
        feed_sums[7],
    )


def low_lanes(values):
    return lax.broadcasted_iota(jnp.int32, values.shape, 1) < HD


def swap_lanes(values):
    return pltpu.roll(values, HD, 1)


def low_pair(first, second):
    return jnp.where(low_lanes(first), first, swap_lanes(second))


def high_pair(first, second):
    return jnp.where(low_lanes(first), swap_lanes(first), second)


def side_pair(side, first, second):
    return low_pair(first, second) if side == 0 else high_pair(first, second)


def dot_nn(left, right):
    return jnp.dot(left, right, preferred_element_type=F32)


def dot_nt(left, right):
    return lax.dot_general(left, right, (((1,), (1,)), ((), ())), preferred_element_type=F32)


def dot_tn(left, right):
    return lax.dot_general(left, right, (((0,), (0,)), ((), ())), preferred_element_type=F32)


class Place:
    def __init__(self):
        self.c = lax.axis_index("ctx")
        self.f = lax.axis_index("fsdp")
        self.group = self.c // H
        self.head = self.c % H
        self.inside = jnp.where(self.group == self.f, 1, 0)

    def is_me(self, tc, tf):
        return jnp.logical_and(self.c == tc, self.f == tf)

    def signal(self, barrier, tc, tf):
        @pl.when(jnp.logical_not(self.is_me(tc, tf)))
        def _():
            pl.semaphore_signal(barrier, 1, device_id=(tc, tf), device_id_type=MESH)

    def greet_sources(self, n_ctx, partner):
        barrier = pltpu.get_barrier_semaphore()
        for tc in range(n_ctx):
            self.signal(barrier, tc, self.group)
        if partner:
            pl.semaphore_signal(
                barrier, 1, device_id=(self.c, 1 - self.f), device_id_type=MESH
            )
        pl.semaphore_wait(barrier, 2 * H + (1 if partner else 0) - self.inside)

    def greet_owners(self, n_ctx, partner, more=0):
        barrier = pltpu.get_barrier_semaphore()
        for head in range(H):
            for core in range(2):
                self.signal(barrier, self.f * H + head, core)
        if partner:
            pl.semaphore_signal(
                barrier, 1, device_id=(self.c, 1 - self.f), device_id_type=MESH
            )
        pl.semaphore_wait(barrier, n_ctx + (1 if partner else 0) + more - self.inside)

    def send(self, src, dst, send_sem, recv_sem, tc, tf):
        me = self.is_me(tc, tf)

        @pl.when(me)
        def _():
            pltpu.make_async_copy(src, dst, recv_sem).start()

        @pl.when(jnp.logical_not(me))
        def _():
            self.remote(src, dst, send_sem, recv_sem, tc, tf).start()

    def remote(self, src, dst, send_sem, recv_sem, tc, tf):
        return pltpu.make_async_remote_copy(
            src_ref=src,
            dst_ref=dst,
            send_sem=send_sem,
            recv_sem=recv_sem,
            device_id=(tc, tf),
            device_id_type=MESH,
        )

    def wait_sent(self, src, dst, send_sem, recv_sem, tc, tf):
        @pl.when(jnp.logical_not(self.is_me(tc, tf)))
        def _():
            self.remote(src, dst, send_sem, recv_sem, tc, tf).wait_send()


VECTORS = 10


def project_kernel(
    n_ctx,
    x_hbm,
    wq_hbm,
    wk_hbm,
    wv_hbm,
    order_hbm,
    seq_hbm,
    *rest,
):
    vector_hbm, rest = rest[: VECTORS + 1], rest[VECTORS + 1 :]
    vector_in, rest = rest[-VECTORS - 1 :], rest[: -VECTORS - 1]
    (
        q_out,
        kv_out,
        w_other,
        order_out,
        seq_out,
        vec_out,
        expand_out,
        x_in,
        w_own,
        w_in,
        bias_own,
        bias_in,
        order_own,
        seq_own,
        order_in,
        seq_in,
        q_send,
        kv_send,
        load_sem,
        w_ss,
        w_rs,
        q_ss,
        q_rs,
        kv_ss,
        kv_rs,
        relay_ss,
        relay_rs,
    ) = rest
    at = Place()
    other = 1 - at.f
    loads = [
        pltpu.make_async_copy(src, dst, load_sem.at[i])
        for i, (src, dst) in enumerate(
            (
                (x_hbm, x_in),
                (wq_hbm, w_own.at[0]),
                (wk_hbm, w_own.at[1]),
                (wv_hbm, w_own.at[2]),
                (order_hbm, order_own),
                (seq_hbm, seq_own),
                *zip(vector_hbm, vector_in),
            )
        )
    ]
    for load in loads:
        load.start()
    at.greet_sources(n_ctx, True)
    for load in loads[6:]:
        load.wait()
    wide = bias_own.shape[1]
    for row, ref in enumerate(vector_in[:VECTORS]):
        bias_own[row : row + 1, :] = ref[...].astype(F32).reshape(1, wide)
    for part in range(vector_in[VECTORS].shape[0] // wide):
        piece = vector_in[VECTORS][part * wide : part * wide + wide]
        bias_own[VECTORS + part : VECTORS + part + 1, :] = piece.astype(F32).reshape(1, wide)
    swaps = [
        at.remote(src, dst, w_ss.at[i], w_rs.at[i], at.c, other)
        for i, (src, dst) in enumerate(
            (
                (bias_own, bias_in),
                (wq_hbm, w_in.at[0]),
                (wk_hbm, w_in.at[1]),
                (wv_hbm, w_in.at[2]),
                (order_hbm, order_in),
                (seq_hbm, seq_in),
            )
        )
    ]
    for swap in swaps:
        swap.start()
    for load in loads[:6]:
        load.wait()

    def targets(half):
        for pair in range(2):
            for side in range(2):
                head = half * (H // 2) + 2 * pair + side
                for core in range(2):
                    slot = head * 2 + core
                    yield pair, side, head, core, (
                        kv_send.at[head, pl.ds(core * BLK, BLK)],
                        kv_out.at[2 * at.c + core],
                        kv_ss.at[slot],
                        kv_rs.at[at.c],
                        at.f * H + head,
                        core,
                    ), (
                        q_send.at[head, core],
                        q_out.at[at.c],
                        q_ss.at[slot],
                        q_rs.at[at.c],
                        at.f * H + head,
                        core,
                    )

    def one_half(half, wq, wk, wv, bias):
        low = x_in[...].astype(BF16)
        q = dot_nn(low, wq[...]) + bias[0:1, :]
        k = dot_nn(low, wk[...])
        v = dot_nn(low, wv[...]) + bias[1:2, :]
        for pair, side, head, core, kv_move, q_move in targets(half):
            columns = slice(pair * 128, pair * 128 + 128)
            if core == 0:
                kv_send[head] = side_pair(side, k[:, columns], v[:, columns]).astype(BF16)
            rows = slice(core * HALF, core * HALF + HALF)
            late = slice(BLK + core * HALF, BLK + core * HALF + HALF)
            q_send[head, core] = side_pair(side, q[rows, columns], q[late, columns]).astype(BF16)
            at.send(*kv_move)
            at.send(*q_move)

    one_half(at.f, w_own.at[0], w_own.at[1], w_own.at[2], bias_own)
    for swap in swaps:
        swap.wait()
    one_half(other, w_in.at[0], w_in.at[1], w_in.at[2], bias_in)
    w_other[...] = w_in[...]
    inside = at.inside == 1
    order_out[...] = jnp.where(inside, order_own[...], order_in[...])
    seq_out[...] = jnp.where(inside, seq_own[...], seq_in[...])
    vec_out[...] = whole_rows(bias_own[...], bias_in[...], at.f == 0)
    for row, source in enumerate((bias_own, bias_in)):
        for part in range(expand_out.shape[1] // wide):
            at_row = VECTORS + part
            expand_out[row : row + 1, part * wide : part * wide + wide] = source[
                at_row : at_row + 1, :
            ]

    def relay(source):
        mine = kv_out.at[2 * source + at.f]
        return at.remote(mine, mine, relay_ss.at[source], relay_rs.at[source], at.c, other)

    def relay_in(source):
        theirs = kv_out.at[2 * source + other]
        return at.remote(theirs, theirs, relay_ss.at[source], relay_rs.at[source], at.c, other)

    for source in range(n_ctx):
        arrived = kv_out.at[2 * source + at.f]
        at.remote(arrived, arrived, kv_ss.at[0], kv_rs.at[source], at.c, other).wait_recv()
        relay(source).start()
    for source in range(n_ctx):
        arrived = q_out.at[source]
        at.remote(arrived, arrived, q_ss.at[0], q_rs.at[source], at.c, other).wait_recv()
        relay_in(source).wait_recv()
    for source in range(n_ctx):
        relay(source).wait_send()
    for half in (at.f, other):
        for _, _, _, _, kv_move, q_move in targets(half):
            at.wait_sent(*kv_move)
            at.wait_sent(*q_move)


def project_and_scatter(n_ctx, x, wq, wk, wv, order, seqs, vectors):
    wide = wq.shape[1]
    blocks = order.shape[1]
    units = vectors[VECTORS].shape[0]
    bias_rows = VECTORS + units // wide
    return pl.pallas_call(
        functools.partial(project_kernel, n_ctx),
        out_shape=(
            jax.ShapeDtypeStruct((n_ctx, HALF, 128), BF16),
            jax.ShapeDtypeStruct((2 * n_ctx, BLK, 128), BF16),
            jax.ShapeDtypeStruct((3, D, wide), BF16),
            jax.ShapeDtypeStruct((1, blocks), jnp.int32),
            jax.ShapeDtypeStruct((1, blocks), jnp.int32),
            jax.ShapeDtypeStruct((bias_rows, D), F32),
            jax.ShapeDtypeStruct((2, units), F32),
        ),
        in_specs=[ANY] * (7 + VECTORS),
        out_specs=(ANY, ANY) + (VMEM,) * 5,
        scratch_shapes=[
            pltpu.VMEM((2 * BLK, D), F32),
            pltpu.VMEM((3, D, wide), BF16),
            pltpu.VMEM((3, D, wide), BF16),
            pltpu.VMEM((bias_rows, wide), F32),
            pltpu.VMEM((bias_rows, wide), F32),
            pltpu.VMEM((1, blocks), jnp.int32),
            pltpu.VMEM((1, blocks), jnp.int32),
            pltpu.VMEM((1, blocks), jnp.int32),
            pltpu.VMEM((1, blocks), jnp.int32),
            pltpu.VMEM((H, 2, HALF, 128), BF16),
            pltpu.VMEM((H, 2 * BLK, 128), BF16),
            pltpu.SemaphoreType.DMA((7 + VECTORS,)),
            pltpu.SemaphoreType.DMA((6,)),
            pltpu.SemaphoreType.DMA((6,)),
            pltpu.SemaphoreType.DMA((2 * H,)),
            pltpu.SemaphoreType.DMA((n_ctx,)),
            pltpu.SemaphoreType.DMA((2 * H,)),
            pltpu.SemaphoreType.DMA((n_ctx,)),
            pltpu.SemaphoreType.DMA((n_ctx,)),
            pltpu.SemaphoreType.DMA((n_ctx,)),
        ]
        + [pltpu.VMEM(vector.shape, BF16) for vector in vectors],
        compiler_params=pltpu.CompilerParams(
            collective_id=0, has_side_effects=True, vmem_limit_bytes=ROOM
        ),
        name="project_scatter",
    )(x, wq, wk, wv, order, seqs, *vectors)


def forward_kernel(
    blocks,
    order_ref,
    seq_ref,
    q_ref,
    kv_ref,
    o_ref,
    keep_ref,
    lse_ref,
    pairs_ref,
    place,
    q_low,
    peaks,
    masses,
    total,
    scores,
):
    def place_block(slot, _):
        place[order_ref[0, slot]] = slot
        return 0

    lax.fori_loop(0, blocks, place_block, 0)

    count = jnp.int32(0)
    for gap in range(LONG):

        def look(late, found):
            pairs_ref[0, found] = place[late]
            pairs_ref[1, found] = place[late - gap]
            return found + jnp.where(seq_ref[0, late] == seq_ref[0, late - gap], 1, 0)

        count = lax.fori_loop(gap, blocks, look, count)
    for spare in range(TOGETHER):
        pairs_ref[0, count + spare] = blocks
        pairs_ref[1, count + spare] = 0
    turns = (count + TOGETHER - 1) // TOGETHER
    pairs_ref[2, 1] = (count + BACK_TOGETHER - 1) // BACK_TOGETHER

    def unpack(step, _):
        for part in range(4):
            source = step * 4 + part
            packed = q_ref[source].astype(F32) * (HD**-0.5)
            low = low_lanes(packed)
            q_low[2 * source] = jnp.where(low, packed, 0.0).astype(BF16)
            q_low[2 * source + 1] = jnp.where(low, swap_lanes(packed), 0.0).astype(BF16)
        return 0

    lax.fori_loop(0, blocks // 8, unpack, 0)
    q_low[blocks] = jnp.zeros((HALF, 128), BF16)

    def clear(slot, _):
        peaks[slot] = jnp.full((HALF, 128), masked_value, F32)
        masses[slot] = jnp.zeros((HALF, 128), F32)
        total[slot] = jnp.zeros((HALF, 128), F32)
        return 0

    lax.fori_loop(0, blocks + 1, clear, 0)

    def score(step, _):
        slots, results = [], []
        for part in range(TOGETHER):
            index = step * TOGETHER + part
            q_slot = pairs_ref[0, index]
            result = dot_nt(q_low[q_slot], kv_ref[pairs_ref[1, index]])
            scores[index] = result
            slots.append(q_slot)
            results.append(jnp.maximum(result[:, :128], result[:, 128:]))
        for q_slot, result in zip(slots, results):
            peaks[q_slot] = jnp.maximum(peaks[q_slot], result)
        return 0

    lax.fori_loop(0, turns, score, 0)

    def level(step, _):
        for part in range(4):
            slot = step * 4 + part
            peaks[slot] = jnp.broadcast_to(
                jnp.max(peaks[slot], axis=1, keepdims=True), (HALF, 128)
            )
        return 0

    lax.fori_loop(0, blocks // 4, level, 0)

    def weigh(step, _):
        slots, results = [], []
        for part in range(TOGETHER):
            index = step * TOGETHER + part
            q_slot = pairs_ref[0, index]
            peak = peaks[q_slot]
            left = jnp.exp(scores[index, :, :128] - peak)
            right = jnp.exp(scores[index, :, 128:] - peak)
            weights = jnp.concatenate([left, right], axis=1).astype(BF16)
            slots.append(q_slot)
            results.append((left + right, dot_nn(weights, kv_ref[pairs_ref[1, index]])))
        for q_slot, (mass, part_total) in zip(slots, results):
            masses[q_slot] = masses[q_slot] + mass
            total[q_slot] = total[q_slot] + part_total
        return 0

    lax.fori_loop(0, turns, weigh, 0)

    def finish(step, _):
        for part in range(4):
            source = step * 4 + part
            for side in range(2):
                slot = 2 * source + side
                mass = jnp.broadcast_to(
                    jnp.sum(masses[slot], axis=1, keepdims=True), (HALF, 128)
                )
                result = total[slot] / mass
                lse_ref[slot] = peaks[slot] + jnp.log(mass)
                packed = high_pair(result[: HALF // 2], result[HALF // 2 :])
                keep_ref[source, side] = packed
                o_ref[source, side] = packed.astype(BF16)
        return 0

    lax.fori_loop(0, blocks // 8, finish, 0)


def pair_room(blocks):
    return blocks * MOST // 2 + TOGETHER


def attend(order, seqs, q, kv):
    blocks = kv.shape[0]
    room = pair_room(blocks)
    return pl.pallas_call(
        functools.partial(forward_kernel, blocks),
        out_shape=(
            jax.ShapeDtypeStruct((blocks // 2, 2, HALF // 2, 128), BF16),
            jax.ShapeDtypeStruct((blocks // 2, 2, HALF // 2, 128), F32),
            jax.ShapeDtypeStruct((blocks, HALF, 128), F32),
            jax.ShapeDtypeStruct((3, room), jnp.int32),
        ),
        in_specs=[SMEM, SMEM, VMEM, VMEM],
        out_specs=(VMEM, VMEM, VMEM, SMEM),
        scratch_shapes=[
            pltpu.SMEM((blocks,), jnp.int32),
            pltpu.VMEM((blocks + 1, HALF, 128), BF16),
            pltpu.VMEM((blocks + 1, HALF, 128), F32),
            pltpu.VMEM((blocks + 1, HALF, 128), F32),
            pltpu.VMEM((blocks + 1, HALF, 128), F32),
            pltpu.VMEM((room, HALF, BLK), F32),
        ],
        compiler_params=pltpu.CompilerParams(vmem_limit_bytes=ROOM),
        name="attend",
    )(order, seqs, q, kv)


def backward_kernel(
    blocks,
    pairs_ref,
    q_ref,
    tan_ref,
    keep_ref,
    lse_ref,
    kv_ref,
    dq_ref,
    dkv_ref,
    both,
    turned,
    masses,
    deltas,
    dq_sum,
    dkv_sum,
):
    def unpack(step, _):
        for part in range(4):
            source = step * 4 + part
            packed = q_ref[source].astype(F32) * (HD**-0.5)
            low = low_lanes(packed)
            for side in range(2):
                slot = 2 * source + side
                q = packed if side == 0 else swap_lanes(packed)
                both[slot, 0:HALF] = jnp.where(low, q, 0.0).astype(BF16)
                tangent = tan_ref[source, side].astype(F32)
                first = low_lanes(tangent)
                both[slot, HALF : HALF + HALF // 2] = jnp.where(
                    first, 0.0, swap_lanes(tangent)
                ).astype(BF16)
                both[slot, HALF + HALF // 2 : BLK] = jnp.where(first, 0.0, tangent).astype(BF16)
                turned[slot] = jnp.transpose(both[slot])
                product = tangent * keep_ref[source, side]
                delta = jnp.concatenate(
                    [
                        jnp.sum(jnp.where(first, product, 0.0), axis=1, keepdims=True),
                        jnp.sum(jnp.where(first, 0.0, product), axis=1, keepdims=True),
                    ],
                    axis=0,
                )
                deltas[slot] = jnp.broadcast_to(delta, (HALF, 128))
                masses[slot] = lse_ref[slot]
        return 0

    lax.fori_loop(0, blocks // 8, unpack, 0)
    both[blocks] = jnp.zeros((BLK, 128), BF16)
    turned[blocks] = jnp.zeros((128, BLK), BF16)
    masses[blocks] = jnp.zeros((HALF, 128), F32)
    deltas[blocks] = jnp.zeros((HALF, 128), F32)

    def clear(slot, _):
        dq_sum[slot] = jnp.zeros((HALF, 128), F32)
        dkv_sum[slot] = jnp.zeros((128, BLK), F32)
        return 0

    lax.fori_loop(0, blocks, clear, 0)
    dq_sum[blocks] = jnp.zeros((HALF, 128), F32)

    def one_pair(q_slot, k_slot):
        kv = kv_ref[k_slot]
        products = dot_nt(both[q_slot], kv)
        mass, delta = masses[q_slot], deltas[q_slot]
        weights = jnp.exp(products[:HALF] - jnp.concatenate([mass, mass], axis=1))
        score_tan = weights * (products[HALF:] - jnp.concatenate([delta, delta], axis=1))
        score_tan = score_tan.astype(BF16)
        sides = jnp.concatenate([score_tan, weights.astype(BF16)], axis=0)
        return dot_nn(turned[q_slot], sides), dot_nn(score_tan, kv)

    def pair_turn(step, _):
        slots = [
            (pairs_ref[0, step * BACK_TOGETHER + part], pairs_ref[1, step * BACK_TOGETHER + part])
            for part in range(BACK_TOGETHER)
        ]
        results = [one_pair(*slot) for slot in slots]
        for (q_slot, k_slot), (dkv, dq) in zip(slots, results):
            dkv_sum[k_slot] = dkv_sum[k_slot] + dkv
            dq_sum[q_slot] = dq_sum[q_slot] + dq
        return 0

    lax.fori_loop(0, pairs_ref[2, 1], pair_turn, 0)

    def finish_rows(step, _):
        for part in range(4):
            source = step * 4 + part
            packed = low_pair(dq_sum[2 * source], dq_sum[2 * source + 1]) * (HD**-0.5)
            dq_ref[source] = packed.astype(BF16)
            for slot in (2 * source, 2 * source + 1):
                dkv_ref[slot] = jnp.transpose(dkv_sum[slot])
        return 0

    lax.fori_loop(0, blocks // 8, finish_rows, 0)


def attend_back(pairs, q, tangent, keep, lse, kv):
    blocks = kv.shape[0]
    return pl.pallas_call(
        functools.partial(backward_kernel, blocks),
        out_shape=(
            jax.ShapeDtypeStruct((blocks // 2, HALF, 128), BF16),
            jax.ShapeDtypeStruct((blocks, BLK, 128), F32),
        ),
        in_specs=[SMEM, VMEM, VMEM, VMEM, VMEM, VMEM],
        out_specs=(VMEM, VMEM),
        scratch_shapes=[
            pltpu.VMEM((blocks + 1, BLK, 128), BF16),
            pltpu.VMEM((blocks + 1, 128, BLK), BF16),
            pltpu.VMEM((blocks + 1, HALF, 128), F32),
            pltpu.VMEM((blocks + 1, HALF, 128), F32),
            pltpu.VMEM((blocks + 1, HALF, 128), F32),
            pltpu.VMEM((blocks, 128, BLK), F32),
        ],
        compiler_params=pltpu.CompilerParams(vmem_limit_bytes=ROOM),
        name="attend_back",
    )(pairs, q, tangent, keep, lse, kv)


def pieces_of(start, size, body):
    piece = max(n for n in range(16, 97, 16) if size % n == 0)
    lax.fori_loop(
        0,
        size // piece,
        lambda i, _: (body(i * piece, span(start + i * piece, piece), piece), 0)[1],
        0,
    )


def span(start, size):
    return pl.ds(pl.multiple_of(start, 16), size)


def step_of(c, stride):
    bit = (c // stride) % 2
    return bit, c + stride * (1 - 2 * bit)


class Ladder:
    def __init__(self, at, plans, starts, size, acc, stage, landing, out, sems, bases=(0, 0)):
        self.bases = bases
        self.at, self.acc, self.stage, self.landing, self.out = at, acc, stage, landing, out
        self.down_ss, self.down_rs, self.up_ss, self.up_rs = sems
        self.ranges = []
        for plan, start in zip(plans, starts):
            listed, rows = [], size
            for bit, peer in plan[:-1]:
                rows = rows // 2
                listed.append((start + bit * rows, start + (1 - bit) * rows, rows, peer))
                start = start + bit * rows
            listed.append((start, start, rows, plan[-1][1]))
            self.ranges.append(listed)
        self.last = len(plans[0]) - 1

    def slot(self, region, step):
        return region * (self.last + 1) + step

    def down(self, region, step, sent):
        kept, given, size, peer = self.ranges[region][step]
        where, slot = span(given if sent else kept, size), self.slot(region, step)
        return self.at.remote(
            self.stage[region].at[where],
            self.landing[region][step].at[where],
            self.down_ss.at[slot],
            self.down_rs.at[slot],
            peer,
            self.at.f,
        )

    def up(self, region, step, sent):
        kept, given, size, peer = self.ranges[region][step]
        start = self.bases[region] + (kept if sent else given)
        where, slot = span(start, size), self.slot(region, step)
        return self.at.remote(
            self.out[region].at[where],
            self.out[region].at[where],
            self.up_ss.at[slot],
            self.up_rs.at[slot],
            peer,
            self.at.f,
        )

    def join(self, region, start, size, arrived, target):
        def body(offset, where, _):
            total = self.acc[region][where, :]
            if arrived is not None:
                total = total + arrived[where, :].astype(F32)
            target[where, :] = total.astype(target.dtype)

        pieces_of(start, size, body)

    def give(self, region, step, arrived):
        kept, given, size, _ = self.ranges[region][step]
        self.join(region, given, size, arrived, self.stage[region])
        self.down(region, step, True).start()
        if step < self.last:
            self.join(region, kept, size, arrived, self.acc[region])

    def settle(self, region):
        kept, _, size, _ = self.ranges[region][self.last]
        arrived = self.landing[region][self.last]

        def body(offset, where, rows):
            total = self.stage[region][where, :].astype(F32) + arrived[where, :].astype(F32)
            self.out[region][span(self.bases[region] + kept + offset, rows), :] = total.astype(BF16)

        self.down(region, self.last, False).wait_recv()
        pieces_of(kept, size, body)
        self.up(region, self.last - 1, True).start()

    def wait_sent(self):
        for region in range(2):
            for step in range(self.last + 1):
                self.down(region, step, True).wait_send()
            for step in range(self.last):
                self.up(region, step, True).wait_send()


COLS = 512


def whole_rows(own, other, first):
    return jnp.where(
        first,
        jnp.concatenate([own, other], axis=1),
        jnp.concatenate([other, own], axis=1),
    )


def row_mean(values):
    return jnp.mean(values, axis=1, keepdims=True)


def normalize(values):
    centre = values - row_mean(values)
    scale = lax.rsqrt(row_mean(centre * centre) + norm_eps)
    return centre * scale, scale


def norm_back(tangent, normed, scale, gain):
    pushed = tangent * gain
    return scale * (pushed - row_mean(pushed) - normed * row_mean(pushed * normed))


def column_sum(values):
    return jnp.sum(values, axis=0, keepdims=True)


def feed_slopes(kind, target, mixed, low_turned, hidden, before_tan, feed_tan, branch_tan):
    unit_count = hidden.shape[2] // COLS

    def chunk_slopes(chunk, _):
        columns = pl.ds(pl.multiple_of(chunk * COLS, COLS), COLS)
        target[columns, :] = dot_tn(hidden[kind, :, columns], feed_tan[...]).astype(target.dtype)
        below = pl.ds(pl.multiple_of((unit_count + chunk) * COLS, COLS), COLS)
        target[below, :] = dot_nn(low_turned[...], before_tan[kind, :, columns]).astype(
            target.dtype
        )
        return 0

    lax.fori_loop(0, unit_count, chunk_slopes, 0)
    start = 2 * unit_count * COLS
    target[start : start + D // 2, :] = dot_tn(mixed[kind], branch_tan[...]).astype(target.dtype)


def middle_kernel(
    n_ctx,
    o_hbm, x_hbm, sum_hbm, cot_hbm, wo_a, wo_b, we_a, we_b, ws_a, ws_b, be_ref, vec_in,
    out_hbm, sum_tan_hbm, entry_hbm, tan_out, vec_ref, stage_a, stage_b, keep_ref,
    o_in, x_ref, sum_ref, cot_ref, wo, we, ws, out_ref, sum_tan_ref, entry_ref,
    mixed, low, hidden, before_tan, feed_tan, branch_tan, slope, mixed_tan, tan_send,
    own_grads, send_grads, first_in, low_turned,
    load_sem, store_sem, o_ss, o_rs, tan_ss, tan_rs, core_ss, core_rs,
):
    at = Place()
    f = at.f
    other = 1 - f
    halves = (f, other)
    piece = HALF // 2
    loads = [
        pltpu.make_async_copy(src, dst, load_sem.at[i])
        for i, (src, dst) in enumerate(
            (
                (x_hbm, x_ref),
                (wo_a, wo.at[0]),
                (wo_b, wo.at[1]),
                (we_a, we.at[0]),
                (we_b, we.at[1]),
                (ws_a, ws.at[0]),
                (ws_b, ws.at[1]),
                (sum_hbm, sum_ref),
                (cot_hbm, cot_ref),
            )
        )
    ]
    for load in loads:
        load.start()
    barrier = pltpu.get_barrier_semaphore()
    for target in range(n_ctx):
        at.signal(barrier, target, at.group)
    at.greet_owners(n_ctx, True, 2 * H - at.inside)

    def o_move(target, side):
        return (
            o_hbm.at[target, side],
            o_in.at[side, at.head, f],
            o_ss.at[2 * target + side],
            o_rs.at[side * 2 * H + at.head * 2 + f],
            target,
            at.group,
        )

    def tan_move(side, head, core):
        return (
            tan_send.at[side, head, core],
            tan_out.at[at.c, side],
            tan_ss.at[side * 2 * H + head * 2 + core],
            tan_rs.at[at.c * 2 + side],
            f * H + head,
            core,
        )

    for side in range(2):
        for target in range(n_ctx):
            at.send(*o_move(target, side))
    vec_ref[...] = jnp.zeros_like(vec_ref)
    vectors = vec_in[...]
    (out_bias, gain_one, shift_one, shrink_bias, gain_two, shift_two, gain_last, shift_last) = (
        vectors[i : i + 1] for i in range(2, 10)
    )
    be = (be_ref.at[0:1], be_ref.at[1:2])
    for load in loads:
        load.wait()

    def stores(step):
        rows = pl.ds(pl.multiple_of(step * BLK, BLK), BLK)
        return [
            pltpu.make_async_copy(src.at[rows], dst.at[rows], store_sem.at[3 * step + i])
            for i, (src, dst) in enumerate(
                ((out_ref, out_hbm), (sum_tan_ref, sum_tan_hbm), (entry_ref, entry_hbm))
            )
        ]

    def tile(step, _):
        first_row = pl.multiple_of(step * BLK, BLK)
        rows = pl.ds(first_row, BLK)
        for head in range(H):
            for core in range(2):
                arrived = o_in.at[step, head, core]
                at.remote(
                    arrived, arrived, o_ss.at[0], o_rs.at[step * 2 * H + head * 2 + core],
                    at.c, other,
                ).wait_recv()
        for kind in range(2):
            for pair in range(2):
                head = halves[kind] * (H // 2) + 2 * pair
                columns = slice(pair * 128, pair * 128 + 128)
                for core in range(2):
                    early = o_in[step, head, core].astype(F32)
                    late = o_in[step, head + 1, core].astype(F32)
                    for part in range(2):
                        start = pl.multiple_of(first_row + core * HALF + part * piece, piece)
                        mixed[kind, pl.ds(start, piece), columns] = side_pair(
                            part, early, late
                        ).astype(BF16)
        branch = dot_nn(mixed[0, rows, :], wo[0]) + dot_nn(mixed[1, rows, :], wo[1]) + out_bias
        n_one, scale_one = normalize(x_ref[rows, :] + branch)
        normed_one = n_one * gain_one + shift_one
        stream_one = sum_ref[rows, :] + branch
        normed_low = normed_one.astype(BF16)
        low[rows, :] = normed_low
        feed = jnp.zeros((BLK, D), F32)
        for kind in range(2):

            def expand(chunk, carried):
                columns = pl.ds(pl.multiple_of(chunk * COLS, COLS), COLS)
                v = dot_nn(normed_low, we[kind, :, columns]) + be[kind][:, columns]
                square = v * v
                t = jnp.tanh(gelu_coeff * (v + gelu_cubic * square * v))
                half_up = 0.5 + 0.5 * t
                hidden_part = (v * half_up).astype(BF16)
                hidden[kind, rows, columns] = hidden_part
                slope[kind, :, columns] = half_up + v * half_up * (1.0 - t) * (
                    gelu_coeff + (3.0 * gelu_coeff * gelu_cubic) * square
                )
                return carried + dot_nn(hidden_part, ws[kind, columns, :])

            feed = lax.fori_loop(0, ws.shape[1] // COLS, expand, feed)
        feed_out = feed + shrink_bias
        n_two, scale_two = normalize(normed_one + feed_out)
        n_last, scale_last = normalize(stream_one + feed_out)
        out_ref[rows, :] = (n_two * gain_two + shift_two) + (n_last * gain_last + shift_last)
        u = cot_ref[rows, :]
        nudge = column_sum(u)
        sum_tan = norm_back(u, n_last, scale_last, gain_last)
        inflow = norm_back(u, n_two, scale_two, gain_two)
        sum_tan_ref[rows, :] = sum_tan
        feed_low = (sum_tan + inflow).astype(BF16)
        feed_tan[rows, :] = feed_low
        vec_ref[0:1, :] += column_sum(feed_low.astype(F32))
        vec_ref[1:2, :] += column_sum(u * n_two)
        vec_ref[2:3, :] += nudge
        vec_ref[3:4, :] += column_sum(u * n_last)
        vec_ref[4:5, :] += nudge
        normed_tan = inflow
        for kind in range(2):

            def expand_back(chunk, carried):
                columns = pl.ds(pl.multiple_of(chunk * COLS, COLS), COLS)
                pushed = dot_nt(feed_low, ws[kind, columns, :])
                tan_part = (pushed * slope[kind, :, columns]).astype(BF16)
                before_tan[kind, rows, columns] = tan_part
                vec_row = pl.ds(8 + 2 * halves[kind] + chunk, 1)
                vec_ref[vec_row, :] += column_sum(tan_part.astype(F32))
                return carried + dot_nt(tan_part, we[kind, :, columns])

            normed_tan = lax.fori_loop(0, ws.shape[1] // COLS, expand_back, normed_tan)
        vec_ref[5:6, :] += column_sum(normed_tan * n_one)
        vec_ref[6:7, :] += column_sum(normed_tan)
        entry = norm_back(normed_tan, n_one, scale_one, gain_one)
        entry_ref[rows, :] = entry
        branch_low = (sum_tan + entry).astype(BF16)
        branch_tan[rows, :] = branch_low
        vec_ref[7:8, :] += column_sum(branch_low.astype(F32))
        for kind in range(2):
            mixed_tan[kind] = dot_nt(branch_low, wo[kind])
        for kind in range(2):
            for pair in range(2):
                columns = slice(pair * 128, pair * 128 + 128)
                for side in range(2):
                    head = halves[kind] * (H // 2) + 2 * pair + side
                    for core in range(2):
                        start = core * HALF
                        early = mixed_tan[kind, start : start + piece, columns]
                        late = mixed_tan[kind, start + piece : start + HALF, columns]
                        tan_send[step, head, core] = side_pair(side, early, late).astype(BF16)
                        at.send(*tan_move(step, head, core))
        for store in stores(step):
            store.start()
        return 0

    lax.fori_loop(0, 2, tile, 0)

    quarter = first_in.shape[0] // 4
    bits = (step_of(at.c, 1)[0], step_of(at.c, 2)[0])
    stages = (stage_a, stage_b)

    def core_move(region, give):
        bit = bits[region]
        start = region * 2 * quarter + (1 - bit if give else bit) * quarter
        where = span(start, quarter)
        slot = region + 2 * (0 if give else 1)
        return start, at.remote(
            send_grads.at[where], first_in.at[where], core_ss.at[slot], core_rs.at[slot],
            at.c, other,
        )

    order = [(0, True), (1, True), (0, False), (1, False)]
    low_turned[...] = jnp.transpose(low[...])
    operands = (mixed, low_turned, hidden, before_tan, feed_tan, branch_tan)
    feed_slopes(1, send_grads, *operands)
    for step in order:
        core_move(*step)[1].start()
    feed_slopes(0, own_grads, *operands)
    for region, give in order:
        start, move = core_move(region, give)
        move.wait_recv()

        def join(offset, where, size):
            total = own_grads[where, :] + first_in[where, :].astype(F32)
            if give:
                stages[region][span(offset, size), :] = total.astype(BF16)
            else:
                keep_ref[region, span(offset, size), :] = total

        pieces_of(start, quarter, join)
    for source in range(n_ctx):
        for side in range(2):
            arrived = tan_out.at[source, side]
            at.remote(
                arrived, arrived, tan_ss.at[0], tan_rs.at[source * 2 + side], at.c, other
            ).wait_recv()
    for step in range(2):
        for store in stores(step):
            store.wait()
    for side in range(2):
        for target in range(n_ctx):
            at.wait_sent(*o_move(target, side))
        for head in range(H):
            for core in range(2):
                at.wait_sent(*tan_move(side, head, core))
    for step in order:
        core_move(*step)[1].wait_send()


def middle(n_ctx, o, x, summed, cotangent, wo, we, ws, be, vec):
    tokens, wide, units = x.shape[0], D // 2, ws[0].shape[0]
    grad_rows = 2 * units + wide
    rows = jax.ShapeDtypeStruct((tokens, D), F32)

    def sems(*counts):
        return [pltpu.SemaphoreType.DMA((count,)) for count in counts]

    return pl.pallas_call(
        functools.partial(middle_kernel, n_ctx),
        out_shape=(
            rows,
            rows,
            rows,
            jax.ShapeDtypeStruct((n_ctx, 2, HALF // 2, 128), BF16),
            jax.ShapeDtypeStruct((16, D), F32),
            jax.ShapeDtypeStruct((grad_rows // 4, D), BF16),
            jax.ShapeDtypeStruct((grad_rows // 4, D), BF16),
            jax.ShapeDtypeStruct((2, grad_rows // 4, D), F32),
        ),
        in_specs=[ANY] * 10 + [VMEM] * 2,
        out_specs=(ANY,) * 4 + (VMEM,) * 4,
        scratch_shapes=[
            pltpu.VMEM((2, H, 2, HALF // 2, 128), BF16),
            pltpu.VMEM((tokens, D), F32),
            pltpu.VMEM((tokens, D), F32),
            pltpu.VMEM((tokens, D), F32),
            pltpu.VMEM((2, wide, D), BF16),
            pltpu.VMEM((2, D, units), BF16),
            pltpu.VMEM((2, units, D), BF16),
            pltpu.VMEM((tokens, D), F32),
            pltpu.VMEM((tokens, D), F32),
            pltpu.VMEM((tokens, D), F32),
            pltpu.VMEM((2, tokens, wide), BF16),
            pltpu.VMEM((tokens, D), BF16),
            pltpu.VMEM((2, tokens, units), BF16),
            pltpu.VMEM((2, tokens, units), BF16),
            pltpu.VMEM((tokens, D), BF16),
            pltpu.VMEM((tokens, D), BF16),
            pltpu.VMEM((2, BLK, units), F32),
            pltpu.VMEM((2, BLK, wide), F32),
            pltpu.VMEM((2, H, 2, HALF // 2, 128), BF16),
            pltpu.VMEM((grad_rows, D), F32),
            pltpu.VMEM((grad_rows, D), BF16),
            pltpu.VMEM((grad_rows, D), BF16),
            pltpu.VMEM((D, tokens), BF16),
        ]
        + sems(9, 6, 2 * n_ctx, 4 * H, 4 * H, 2 * n_ctx, 4, 4),
        compiler_params=pltpu.CompilerParams(
            collective_id=1, has_side_effects=True, vmem_limit_bytes=ROOM
        ),
        name="middle",
    )(o, x, summed, cotangent, *wo, *we, *ws, be, vec)


def finish_kernel(
    n_ctx,
    dq_ref, dkv_ref, keep_hbm, land_a, land_b, x_hbm, entry_hbm, wq_hbm, wk_hbm, wv_hbm,
    w_other_hbm, vec_feed,
    post_ref, feed_ref, grads_ref, vec_out,
    own, part, ready, dq_in, dkv_in, keep, acc, stage, landing,
    x_in, entry_in, w_in, w_far, low_turned, tangents,
    own_grads, send_grads, first_in, acc_last, stage_last, landing_last, vec_sum, vec_in,
    load_sem, q_ss, q_rs, kv_ss, kv_rs, part_ss, part_rs, own_sem,
    down_ss, down_rs, up_ss, up_rs, top_ss, top_rs,
    core_ss, core_rs, down_ss2, down_rs2, up_ss2, up_rs2, vec_ss, vec_rs,
):
    at = Place()
    c, f = at.c, at.f
    other = 1 - f
    halves = (f, other)
    wide = D // 2
    loads = [
        pltpu.make_async_copy(src, dst, load_sem.at[i])
        for i, (src, dst) in enumerate(
            (
                (keep_hbm, keep),
                (x_hbm, x_in),
                (entry_hbm, entry_in),
                (wq_hbm, w_in.at[0]),
                (wk_hbm, w_in.at[1]),
                (wv_hbm, w_in.at[2]),
                (w_other_hbm, w_far),
            )
        )
    ]
    for load in loads:
        load.start()
    x_step, y_step, near, far = (step_of(c, stride) for stride in (1, 2, 4, 8))
    barrier = pltpu.get_barrier_semaphore()
    for _, peer in (x_step, y_step, near, far):
        pl.semaphore_signal(barrier, 1, device_id=(peer, f), device_id_type=MESH)
    at.greet_owners(n_ctx, True, 4)

    def partial_move(source):
        return at.remote(
            dkv_ref.at[2 * source + other],
            part.at[source],
            part_ss.at[source],
            part_rs.at[source],
            c,
            other,
        )

    def own_move(source):
        return pltpu.make_async_copy(
            dkv_ref.at[2 * source + f], own.at[source], own_sem.at[source]
        )

    def q_move(target):
        return (
            dq_ref.at[target],
            dq_in.at[at.head, f],
            q_ss.at[target],
            q_rs.at[at.head * 2 + f],
            target,
            at.group,
        )

    def kv_move(target):
        return (
            ready.at[target],
            dkv_in.at[at.head, pl.ds(pl.multiple_of(f * BLK, BLK), BLK)],
            kv_ss.at[target],
            kv_rs.at[at.head * 2 + f],
            target,
            at.group,
        )

    for source in range(n_ctx):
        partial_move(source).start()
        own_move(source).start()
    for target in range(n_ctx):
        at.send(*q_move(target))

    size = keep.shape[1]
    firsts = (x_step, y_step)
    bases = [2 * size * region + firsts[region][0] * size for region in range(2)]
    feed = Ladder(
        at,
        ((y_step, near, far), (x_step, near, far)),
        (0, 0),
        size,
        [keep.at[region] for region in range(2)],
        [stage.at[region] for region in range(2)],
        [[landing.at[region, step] for step in range(3)] for region in range(2)],
        [feed_ref, feed_ref],
        (down_ss, down_rs, up_ss, up_rs),
        bases,
    )

    def top_move(region, sent):
        kept = bases[region]
        given = 2 * size * region + (1 - firsts[region][0]) * size
        where = span(kept if sent else given, size)
        return at.remote(
            feed_ref.at[where],
            feed_ref.at[where],
            top_ss.at[region],
            top_rs.at[region],
            firsts[region][1],
            f,
        )

    loads[0].wait()
    for region, first in enumerate((land_a, land_b)):
        kept, given, half, _ = feed.ranges[region][0]
        feed.join(region, given, half, first, stage.at[region])
        feed.down(region, 0, True).start()
        feed.join(region, kept, half, first, acc.at[region])
        feed.acc[region] = acc.at[region]
    for source in range(n_ctx):
        own_move(source).wait()
        partial_move(source).wait_recv()
        ready[source] = (own[source] + part[source]).astype(BF16)
        at.send(*kv_move(source))
    for load in loads[1:]:
        load.wait()
    low_turned[...] = jnp.transpose(x_in[...]).astype(BF16)
    for step in (1, 2):
        for region in range(2):
            feed.down(region, step - 1, False).wait_recv()
            feed.give(region, step, feed.landing[region][step - 1])

    for head in range(H):
        for core in range(2):
            slot = head * 2 + core
            arrived = dq_in.at[head, core]
            at.remote(arrived, arrived, q_ss.at[0], q_rs.at[slot], c, other).wait_recv()
            arrived = dkv_in.at[head, pl.ds(core * BLK, BLK)]
            at.remote(arrived, arrived, kv_ss.at[0], kv_rs.at[slot], c, other).wait_recv()
    feed_rows = vec_feed.shape[0]
    vec_sum[0, 0:feed_rows] = vec_feed[...]
    vec_sum[0, feed_rows:] = jnp.zeros_like(vec_sum[0, feed_rows:])

    plans = ((x_step, y_step, near, far), (y_step, x_step, near, far))
    quarter = first_in.shape[0] // 4
    last = Ladder(
        at,
        plans,
        (0, 2 * quarter),
        2 * quarter,
        [acc_last, acc_last],
        [stage_last, stage_last],
        [[landing_last.at[step] for step in range(4)]] * 2,
        [grads_ref, grads_ref],
        (down_ss2, down_rs2, up_ss2, up_rs2),
    )

    def core_move(region, give):
        kept, given, rows, _ = last.ranges[region][0]
        where = span(given if give else kept, rows)
        slot = region + 2 * (0 if give else 1)
        return at.remote(
            send_grads.at[where], first_in.at[where], core_ss.at[slot], core_rs.at[slot], c, other
        )

    order = [(0, True), (1, True), (0, False), (1, False)]
    vec_peers = [(c, other)] + [(peer, f) for _, peer in (x_step, y_step, near, far)]

    def vec_move(step):
        return at.remote(
            vec_sum.at[step], vec_in.at[step], vec_ss.at[step], vec_rs.at[step], *vec_peers[step]
        )

    def vec_next(step):
        vec_move(step).wait_recv()
        target = vec_sum.at[step + 1] if step < 4 else vec_out
        target[...] = vec_sum[step] + vec_in[step]
        if step < 4:
            vec_move(step + 1).start()

    for kind, grad_ref in ((1, send_grads), (0, own_grads)):
        for pair in range(2):
            head = halves[kind] * (H // 2) + 2 * pair
            columns = slice(pair * 128, pair * 128 + 128)
            for core in range(2):
                early = dq_in[head, core].astype(F32)
                late = dq_in[head + 1, core].astype(F32)
                for side in range(2):
                    start = side * BLK + core * HALF
                    tangents[kind, 0, start : start + HALF, columns] = side_pair(
                        side, early, late
                    ).astype(BF16)
            early = dkv_in[head].astype(F32)
            late = dkv_in[head + 1].astype(F32)
            tangents[kind, 1, :, columns] = low_pair(early, late).astype(BF16)
            tangents[kind, 2, :, columns] = high_pair(early, late).astype(BF16)
        turned = low_turned[...]
        grad_ref[0:D, 0:wide] = dot_nn(turned, tangents[kind, 0]).astype(grad_ref.dtype)
        grad_ref[0:D, wide:D] = dot_nn(turned, tangents[kind, 1]).astype(grad_ref.dtype)
        value_grad = dot_nn(turned, tangents[kind, 2]).astype(grad_ref.dtype)
        grad_ref[D : D + wide, 0:wide] = value_grad[0:wide]
        grad_ref[D : D + wide, wide:D] = value_grad[wide:D]
        columns = pl.ds(pl.multiple_of(halves[kind] * wide, wide), wide)
        vec_sum[0, feed_rows : feed_rows + 1, columns] = column_sum(tangents[kind, 0].astype(F32))
        vec_sum[0, feed_rows + 1 : feed_rows + 2, columns] = column_sum(
            tangents[kind, 2].astype(F32)
        )
        if kind == 1:
            for step in order:
                core_move(*step).start()
    vec_move(0).start()
    for region in range(2):
        feed.settle(region)
    for region, give in order:
        core_move(region, give).wait_recv()
        kept, given, rows, _ = last.ranges[region][0]

        def join(offset, where, _):
            total = own_grads[where, :] + first_in[where, :].astype(F32)
            if give:
                stage_last[where, :] = total.astype(BF16)
            else:
                acc_last[where, :] = total

        pieces_of(given if give else kept, rows, join)
        if give:
            last.down(region, 0, True).start()
    vec_next(0)
    total = entry_in[...]
    for which in range(3):
        total = total + dot_nt(tangents[0, which], w_in[which])
        total = total + dot_nt(tangents[1, which], w_far[which])
    post_ref[...] = total
    for region in range(2):
        feed.up(region, 1, False).wait_recv()
        feed.up(region, 0, True).start()
    for step in (1, 2):
        for region in range(2):
            last.down(region, step - 1, False).wait_recv()
            last.give(region, step, last.landing[region][step - 1])
        vec_next(step)
    for region in range(2):
        feed.up(region, 0, False).wait_recv()
        top_move(region, True).start()
    for region in range(2):
        last.down(region, 2, False).wait_recv()
        last.give(region, 3, last.landing[region][2])
    vec_next(3)
    for region in range(2):
        last.settle(region)
    vec_next(4)
    for step in (2, 1, 0):
        for region in range(2):
            last.up(region, step, False).wait_recv()
            if step > 0:
                last.up(region, step - 1, True).start()
    for region in range(2):
        top_move(region, False).wait_recv()

    for target in range(n_ctx):
        partial_move(target).wait_send()
        at.wait_sent(*q_move(target))
        at.wait_sent(*kv_move(target))
    for step in order:
        core_move(*step).wait_send()
    for step in range(5):
        vec_move(step).wait_send()
    for region in range(2):
        top_move(region, True).wait_send()
    feed.wait_sent()
    last.wait_sent()


def finish(n_ctx, dq, dkv, keep, land_a, land_b, x, entry, wq, wk, wv, w_other, vec_feed):
    size, tokens, wide = keep.shape[1], x.shape[0], D // 2
    last_shape = (D + wide, D)
    vec_shape = (vec_feed.shape[0] + 8, D)

    def sems(*counts):
        return [pltpu.SemaphoreType.DMA((count,)) for count in counts]

    return pl.pallas_call(
        functools.partial(finish_kernel, n_ctx),
        out_shape=(
            jax.ShapeDtypeStruct((tokens, D), F32),
            jax.ShapeDtypeStruct((4 * size, D), BF16),
            jax.ShapeDtypeStruct(last_shape, BF16),
            jax.ShapeDtypeStruct(vec_shape, F32),
        ),
        in_specs=[ANY, ANY, ANY, VMEM, VMEM] + [ANY] * 6 + [VMEM],
        out_specs=(VMEM,) * 4,
        scratch_shapes=[
            pltpu.VMEM((n_ctx, BLK, 128), F32),
            pltpu.VMEM((n_ctx, BLK, 128), F32),
            pltpu.VMEM((n_ctx, BLK, 128), BF16),
            pltpu.VMEM((H, 2, HALF, 128), BF16),
            pltpu.VMEM((H, 2 * BLK, 128), BF16),
            pltpu.VMEM((2, size, D), F32),
            pltpu.VMEM((2, size, D), F32),
            pltpu.VMEM((2, size, D), BF16),
            pltpu.VMEM((2, 3, size, D), BF16),
            pltpu.VMEM((tokens, D), F32),
            pltpu.VMEM((tokens, D), F32),
            pltpu.VMEM((3, D, wide), BF16),
            pltpu.VMEM((3, D, wide), BF16),
            pltpu.VMEM((D, tokens), BF16),
            pltpu.VMEM((2, 3, tokens, wide), BF16),
            pltpu.VMEM(last_shape, F32),
            pltpu.VMEM(last_shape, BF16),
            pltpu.VMEM(last_shape, BF16),
            pltpu.VMEM(last_shape, F32),
            pltpu.VMEM(last_shape, BF16),
            pltpu.VMEM((4,) + last_shape, BF16),
            pltpu.VMEM((5,) + vec_shape, F32),
            pltpu.VMEM((5,) + vec_shape, F32),
        ]
        + sems(7, n_ctx, 2 * H, n_ctx, 2 * H, n_ctx, n_ctx, n_ctx)
        + sems(6, 6, 6, 6, 2, 2, 4, 4, 8, 8, 8, 8, 5, 5),
        compiler_params=pltpu.CompilerParams(
            collective_id=3, has_side_effects=True, vmem_limit_bytes=ROOM
        ),
        name="finish",
    )(dq, dkv, keep, land_a, land_b, x, entry, wq, wk, wv, w_other, vec_feed)


def unpack_kernel(
    full, grads_ref, vec_ref,
    query_ref, key_ref, value_ref, output_ref, expand_ref, shrink_ref, *vector_outs,
):
    f = lax.axis_index("fsdp")
    units, wide = shrink_ref.shape[0], D // 2
    shrink_ref[...] = full[0:units].astype(F32)
    for part in range(units // D):
        start = units + part * D
        expand_ref[:, part * D : part * D + D] = full[start : start + D].astype(F32)
    output_ref[...] = full[2 * units : 2 * units + wide].astype(F32)
    query_ref[...] = grads_ref[0:D, 0:wide].astype(F32)
    key_ref[...] = grads_ref[0:D, wide:D].astype(F32)
    value_ref[0:wide] = grads_ref[D : D + wide, 0:wide].astype(F32)
    value_ref[wide:D] = grads_ref[D : D + wide, wide:D].astype(F32)
    vectors = vec_ref[...]
    mine = jnp.where(f == 0, vectors[:, 0:wide], vectors[:, wide:D])
    for row, ref in zip((16, 17, 7, 5, 6, 0, 1, 2, 3, 4), vector_outs):
        ref[...] = mine[row : row + 1]
    drift = jnp.where(f == 0, vectors[8:10], vectors[10:12])
    for part in range(units // D):
        vector_outs[10][:, part * D : part * D + D] = drift[part : part + 1]


def unpack_grads(units, full, grads, vecs):
    wide = D // 2
    shapes = [(D, wide)] * 3 + [(wide, D), (D, units), (units, D)] + [(1, wide)] * 10 + [(1, units)]
    return pl.pallas_call(
        unpack_kernel,
        out_shape=tuple(jax.ShapeDtypeStruct(shape, F32) for shape in shapes),
        in_specs=[VMEM] * 3,
        out_specs=(VMEM,) * len(shapes),
        compiler_params=pltpu.CompilerParams(vmem_limit_bytes=ROOM),
        name="unpack_grads",
    )(full, grads, vecs)


def head_shards(
    n_ctx,
    post_stream,
    sum_stream,
    cotangent,
    block_order,
    block_sequence,
    query_weight,
    key_weight,
    value_weight,
    output_weight,
    query_bias,
    value_bias,
    output_bias,
    attend_gain,
    attend_shift,
    expand_weight,
    expand_bias,
    shrink_weight,
    shrink_bias,
    middle_gain,
    middle_shift,
    final_gain,
    final_shift,
):
    x, summed, tangent = post_stream[0], sum_stream[0], cotangent[0]
    swap = [(0, 1), (1, 0)]

    def from_other(values):
        return lax.ppermute(values, "fsdp", swap)

    def across(values, stride):
        return lax.ppermute(values, "ctx", [(c, c ^ stride) for c in range(n_ctx)])

    vectors = [
        query_bias,
        value_bias,
        output_bias,
        attend_gain,
        attend_shift,
        shrink_bias,
        middle_gain,
        middle_shift,
        final_gain,
        final_shift,
        expand_bias,
    ]
    q, kv, w_other, order, seqs, vec, expand_add = project_and_scatter(
        n_ctx, x, query_weight, key_weight, value_weight, block_order, block_sequence, vectors
    )
    o, keep, lse, pairs = attend(order, seqs, q, kv)
    layer_output, sum_tan, entry, tan, vec_feed, stage_a, stage_b, kept = middle(
        n_ctx,
        o,
        x,
        summed,
        tangent,
        (output_weight, from_other(output_weight)),
        (expand_weight, from_other(expand_weight)),
        (shrink_weight, from_other(shrink_weight)),
        expand_add,
        vec,
    )
    land_a, land_b = across(stage_a, 1), across(stage_b, 2)
    dq, dkv = attend_back(pairs, q, tan, keep, lse, kv)
    post_tangent, feed_sums, last_sums, vecs = finish(
        n_ctx,
        dq,
        dkv,
        kept,
        land_a,
        land_b,
        x,
        entry,
        query_weight,
        key_weight,
        value_weight,
        w_other,
        vec_feed,
    )
    (
        query_slope,
        key_slope,
        value_slope,
        output_slope,
        expand_slope,
        shrink_slope,
        query_drift,
        value_drift,
        output_drift,
        attend_stretch,
        attend_nudge,
        shrink_drift,
        middle_stretch,
        middle_nudge,
        final_stretch,
        final_nudge,
        expand_drift,
    ) = unpack_grads(shrink_weight.shape[0], feed_sums, last_sums, vecs)
    return (
        layer_output[None],
        post_tangent[None],
        sum_tan[None],
        query_slope,
        key_slope,
        value_slope,
        output_slope,
        query_drift[0],
        value_drift[0],
        output_drift[0],
        attend_stretch[0],
        attend_nudge[0],
        expand_slope,
        expand_drift[0],
        shrink_slope,
        shrink_drift[0],
        middle_stretch[0],
        middle_nudge[0],
        final_stretch[0],
        final_nudge[0],
    )


def solution(mesh):
    n_ctx, n_fsdp = mesh.shape["ctx"], mesh.shape["fsdp"]
    if n_fsdp == 2 and n_ctx == n_fsdp * H:
        body = functools.partial(head_shards, n_ctx)
    else:
        body = general_shards
    return jax.shard_map(
        body,
        mesh=mesh,
        in_specs=(
            P("fsdp", "ctx", None),
            P("fsdp", "ctx", None),
            P("fsdp", "ctx", None),
            P("fsdp", None),
            P("fsdp", None),
            P(None, "fsdp"),
            P(None, "fsdp"),
            P(None, "fsdp"),
            P("fsdp", None),
            P("fsdp"),
            P("fsdp"),
            P("fsdp"),
            P("fsdp"),
            P("fsdp"),
            P(None, "fsdp"),
            P("fsdp"),
            P("fsdp", None),
            P("fsdp"),
            P("fsdp"),
            P("fsdp"),
            P("fsdp"),
            P("fsdp"),
        ),
        out_specs=(
            P("fsdp", "ctx", None),
            P("fsdp", "ctx", None),
            P("fsdp", "ctx", None),
            P(None, "fsdp"),
            P(None, "fsdp"),
            P(None, "fsdp"),
            P("fsdp", None),
            P("fsdp"),
            P("fsdp"),
            P("fsdp"),
            P("fsdp"),
            P("fsdp"),
            P(None, "fsdp"),
            P("fsdp"),
            P("fsdp", None),
            P("fsdp"),
            P("fsdp"),
            P("fsdp"),
            P("fsdp"),
            P("fsdp"),
        ),
        check_vma=False,
    )
```

```python
import functools

import jax
import jax.numpy as jnp
from jax import lax
from jax.experimental import pallas as pl
from jax.experimental.pallas import tpu as pltpu
from jax.sharding import PartitionSpec as P

D = 512
H = 8
HD = 64
BLK = 256
HALF = BLK // 2
LONG = 8
TOGETHER = 16
MOST = LONG + 1
F32 = jnp.float32
BF16 = jnp.bfloat16
MESH = pl.DeviceIdType.MESH
ROOM = 60 << 20
VMEM = pl.BlockSpec(memory_space=pltpu.VMEM)
SMEM = pl.BlockSpec(memory_space=pltpu.SMEM)
ANY = pl.BlockSpec(memory_space=pltpu.HBM)


norm_eps = 1e-05
masked_value = -1e30
gelu_coeff = 0.7978845608
gelu_cubic = 0.044715


def smooth_gate(values):
    return (
        0.5
        * values
        * (1.0 + jnp.tanh(gelu_coeff * (values + gelu_cubic * values * values * values)))
    )


def layer_norm(inputs, gain_row, shift_row):
    centre = inputs - jnp.mean(inputs, axis=-1, keepdims=True)
    spread = jnp.mean(centre * centre, axis=-1, keepdims=True)
    return centre * lax.rsqrt(spread + norm_eps) * gain_row + shift_row


def product(left_side, right_side):
    return jnp.dot(left_side, right_side, preferred_element_type=jnp.float32)


def cross_rows(left_side, right_side):
    return lax.dot_general(
        left_side, right_side, (((0,), (0,)), ((), ())), preferred_element_type=jnp.float32
    )


def cross_cols(left_side, right_side):
    return lax.dot_general(
        left_side, right_side, (((1,), (1,)), ((), ())), preferred_element_type=jnp.float32
    )


def column_total(values):
    return jnp.sum(values, axis=0, dtype=jnp.float32)


def lookup(table_row, indices):
    places = jnp.arange(table_row.shape[0], dtype=jnp.int32)
    return jnp.sum(jnp.where(indices[:, None] == places[None, :], table_row[None, :], 0), axis=1)


def block_mask(query_blocks, query_seqs, key_blocks, key_seqs):
    same_seq = query_seqs[:, None] == key_seqs[None, :]
    return same_seq & (key_blocks[None, :] <= query_blocks[:, None])


def token_mask(visible):
    return jnp.repeat(jnp.repeat(visible, BLK, axis=0), BLK, axis=1)


def fold_units(carried, members, unit_step):
    unit_count = members[0].shape[0] // BLK
    inner_count = max((divisor for divisor in range(1, 17) if unit_count % divisor == 0))
    outer_count = unit_count // inner_count

    def outer_turn(outer_index, current):

        def inner_turn(inner_index, inner_state):
            offset = (outer_index * inner_count + inner_index) * BLK
            pieces = tuple((lax.dynamic_slice_in_dim(member, offset, BLK, 0) for member in members))
            return unit_step(inner_state, pieces, offset)

        return lax.fori_loop(0, inner_count, inner_turn, current)

    return lax.fori_loop(0, outer_count, outer_turn, carried)


def general_shards(
    post_stream,
    sum_stream,
    cotangent,
    block_order,
    block_sequence,
    query_weight,
    key_weight,
    value_weight,
    output_weight,
    query_bias,
    value_bias,
    output_bias,
    attend_gain,
    attend_shift,
    expand_weight,
    expand_bias,
    shrink_weight,
    shrink_bias,
    middle_gain,
    middle_shift,
    final_gain,
    final_shift,
):
    (
        query_whole,
        key_whole,
        value_whole,
        output_whole,
        query_add,
        value_add,
        output_add,
        gain_one,
        shift_one,
        expand_whole,
        expand_add,
        shrink_whole,
        shrink_add,
        gain_two,
        shift_two,
        gain_last,
        shift_last,
    ) = (
        lax.all_gather(query_weight, "fsdp", axis=1, tiled=True),
        lax.all_gather(key_weight, "fsdp", axis=1, tiled=True),
        lax.all_gather(value_weight, "fsdp", axis=1, tiled=True),
        lax.all_gather(output_weight, "fsdp", axis=0, tiled=True),
        lax.all_gather(query_bias, "fsdp", axis=0, tiled=True),
        lax.all_gather(value_bias, "fsdp", axis=0, tiled=True),
        lax.all_gather(output_bias, "fsdp", axis=0, tiled=True),
        lax.all_gather(attend_gain, "fsdp", axis=0, tiled=True),
        lax.all_gather(attend_shift, "fsdp", axis=0, tiled=True),
        lax.all_gather(expand_weight, "fsdp", axis=1, tiled=True),
        lax.all_gather(expand_bias, "fsdp", axis=0, tiled=True),
        lax.all_gather(shrink_weight, "fsdp", axis=0, tiled=True),
        lax.all_gather(shrink_bias, "fsdp", axis=0, tiled=True),
        lax.all_gather(middle_gain, "fsdp", axis=0, tiled=True),
        lax.all_gather(middle_shift, "fsdp", axis=0, tiled=True),
        lax.all_gather(final_gain, "fsdp", axis=0, tiled=True),
        lax.all_gather(final_shift, "fsdp", axis=0, tiled=True),
    )
    post_rows = post_stream[0]
    summed = sum_stream[0]
    tangent = cotangent[0]
    order_row = block_order[0]
    seq_row = block_sequence[0]
    token_count = post_rows.shape[0]
    score_scale = HD ** (-0.5)
    own_blocks = lax.dynamic_slice_in_dim(
        order_row, lax.axis_index("ctx") * (token_count // BLK), token_count // BLK
    )
    own_seqs = lookup(seq_row, own_blocks)
    post_low = post_rows.astype(jnp.bfloat16)
    queries = (product(post_low, query_whole) + query_add).astype(jnp.bfloat16)
    key_rows = product(post_low, key_whole).astype(jnp.bfloat16)
    value_rows = (product(post_low, value_whole) + value_add).astype(jnp.bfloat16)
    query_heads = queries.reshape(token_count, H, HD)

    def keys_visible(first_row):
        key_block = lax.dynamic_slice_in_dim(order_row, first_row // BLK, 1)
        return block_mask(own_blocks, own_seqs, key_block, lookup(seq_row, key_block))

    def masked_fold(block_step):

        def unit_step(current, pieces, first_row):
            visible = keys_visible(first_row)
            return lax.cond(
                jnp.any(visible),
                lambda inner_state: block_step(inner_state, pieces, visible),
                lambda inner_state: inner_state,
                current,
            )

        def folded(current, pieces, first_row):
            return fold_units(current, pieces, unit_step)

        return folded

    def stats_block(current, pieces, visible):
        row_peaks, masses = current
        key_heads = pieces[0].reshape(BLK, H, HD)
        row_mask = token_mask(visible)[None]
        scores = (
            jnp.einsum("qhd,khd->hqk", query_heads, key_heads, preferred_element_type=jnp.float32)
            * score_scale
        )
        new_peaks = jnp.maximum(
            row_peaks, jnp.max(jnp.where(row_mask, scores, masked_value), axis=2)
        )
        weights = jnp.where(row_mask, jnp.exp(scores - new_peaks[:, :, None]), 0.0)
        return (new_peaks, masses * jnp.exp(row_peaks - new_peaks) + jnp.sum(weights, axis=2))

    stats_fold = masked_fold(stats_block)
    stats_start = (
        jnp.full((H, token_count), masked_value, jnp.float32),
        jnp.zeros((H, token_count), jnp.float32),
    )
    row_peaks, masses = stats_fold(
        stats_start, (lax.all_gather(key_rows, "ctx", axis=0, tiled=True),), jnp.int32(0)
    )
    log_mass = row_peaks + jnp.log(masses)

    def forward_block(current, pieces, visible):
        key_heads = pieces[0].reshape(BLK, H, HD)
        value_heads = pieces[1].reshape(BLK, H, HD)
        row_mask = token_mask(visible)[None]
        scores = (
            jnp.einsum("qhd,khd->hqk", query_heads, key_heads, preferred_element_type=jnp.float32)
            * score_scale
        )
        weights = jnp.where(row_mask, jnp.exp(scores - log_mass[:, :, None]), 0.0).astype(
            jnp.bfloat16
        )
        addition = jnp.einsum(
            "hqk,khd->qhd", weights, value_heads, preferred_element_type=jnp.float32
        )
        return current + addition.reshape(token_count, D)

    forward_fold = masked_fold(forward_block)
    zero_rows = jnp.zeros((token_count, D), jnp.float32)
    attended = forward_fold(
        zero_rows,
        (
            lax.all_gather(key_rows, "ctx", axis=0, tiled=True),
            lax.all_gather(value_rows, "ctx", axis=0, tiled=True),
        ),
        jnp.int32(0),
    )
    mixed_low = attended.astype(jnp.bfloat16)
    branch = product(mixed_low, output_whole) + output_add
    normed_one, first_pull = jax.vjp(
        layer_norm, post_rows + branch, gain_one.astype(jnp.float32), shift_one.astype(jnp.float32)
    )
    stream_one = summed + branch
    normed_low = normed_one.astype(jnp.bfloat16)
    before = product(normed_low, expand_whole) + expand_add
    gated, gate_pull = jax.vjp(smooth_gate, before)
    hidden = gated.astype(jnp.bfloat16)
    feed_out = product(hidden, shrink_whole) + shrink_add
    normed_two, middle_pull = jax.vjp(
        layer_norm,
        normed_one + feed_out,
        gain_two.astype(jnp.float32),
        shift_two.astype(jnp.float32),
    )
    stream_two = stream_one + feed_out
    last_norm, last_pull = jax.vjp(
        layer_norm, stream_two, gain_last.astype(jnp.float32), shift_last.astype(jnp.float32)
    )
    layer_output = normed_two + last_norm
    stream_tan, stretch_last, nudge_last = last_pull(tangent)
    inflow_tan, stretch_two, nudge_two = middle_pull(tangent)
    feed_tan = (stream_tan + inflow_tan).astype(jnp.bfloat16)
    slope_shrink = cross_rows(hidden, feed_tan)
    drift_shrink = column_total(feed_tan)
    before_tan = gate_pull(cross_cols(feed_tan, shrink_whole))[0].astype(jnp.bfloat16)
    slope_expand = cross_rows(normed_low, before_tan)
    drift_expand = column_total(before_tan)
    normed_tan = inflow_tan + cross_cols(before_tan, expand_whole)
    feed_parts = lax.psum(
        (
            slope_expand,
            drift_expand,
            slope_shrink,
            drift_shrink,
            stretch_two,
            nudge_two,
            stretch_last,
            nudge_last,
        ),
        "ctx",
    )
    feed_sums = (
        lax.psum_scatter(feed_parts[0], "fsdp", scatter_dimension=1, tiled=True),
        lax.psum_scatter(feed_parts[1], "fsdp", scatter_dimension=0, tiled=True),
        lax.psum_scatter(feed_parts[2], "fsdp", scatter_dimension=0, tiled=True),
        lax.psum_scatter(feed_parts[3], "fsdp", scatter_dimension=0, tiled=True),
        lax.psum_scatter(feed_parts[4], "fsdp", scatter_dimension=0, tiled=True),
        lax.psum_scatter(feed_parts[5], "fsdp", scatter_dimension=0, tiled=True),
        lax.psum_scatter(feed_parts[6], "fsdp", scatter_dimension=0, tiled=True),
        lax.psum_scatter(feed_parts[7], "fsdp", scatter_dimension=0, tiled=True),
    )
    entry_tan, stretch_one, nudge_one = first_pull(normed_tan)
    branch_tan = (stream_tan + entry_tan).astype(jnp.bfloat16)
    slope_output = cross_rows(mixed_low, branch_tan)
    drift_output = column_total(branch_tan)
    mixed_tan = cross_cols(branch_tan, output_whole).astype(jnp.bfloat16)
    tangent_heads = mixed_tan.reshape(token_count, H, HD)
    deltas = jnp.sum((mixed_tan * attended).reshape(token_count, H, HD), axis=2).T

    def query_block(current, pieces, visible):
        key_heads = pieces[0].reshape(BLK, H, HD)
        value_heads = pieces[1].reshape(BLK, H, HD)
        row_mask = token_mask(visible)[None]
        scores = (
            jnp.einsum("qhd,khd->hqk", query_heads, key_heads, preferred_element_type=jnp.float32)
            * score_scale
        )
        probability = jnp.where(row_mask, jnp.exp(scores - log_mass[:, :, None]), 0.0)
        prob_tan = jnp.einsum(
            "qhd,khd->hqk", tangent_heads, value_heads, preferred_element_type=jnp.float32
        )
        score_tan = (probability * (prob_tan - deltas[:, :, None])).astype(jnp.bfloat16)
        addition = jnp.einsum(
            "hqk,khd->qhd", score_tan, key_heads, preferred_element_type=jnp.float32
        )
        return current + addition.reshape(token_count, D) * score_scale

    query_fold = masked_fold(query_block)
    query_sum = query_fold(
        zero_rows,
        (
            lax.all_gather(key_rows, "ctx", axis=0, tiled=True),
            lax.all_gather(value_rows, "ctx", axis=0, tiled=True),
        ),
        jnp.int32(0),
    )
    gathered_mass, gathered_delta = (
        lax.all_gather(log_mass.T, "ctx", axis=0, tiled=True),
        lax.all_gather(deltas.T, "ctx", axis=0, tiled=True),
    )
    own_keys = key_rows.reshape(token_count, H, HD)
    own_values = value_rows.reshape(token_count, H, HD)

    def owner_block(current, pieces, first_row, visible):
        key_acc, value_acc = current
        part_queries = pieces[0].reshape(BLK, H, HD)
        part_tangent = pieces[1].reshape(BLK, H, HD)
        part_mass = lax.dynamic_slice_in_dim(gathered_mass, first_row, BLK, 0).T
        part_delta = lax.dynamic_slice_in_dim(gathered_delta, first_row, BLK, 0).T
        row_mask = token_mask(visible)[None]
        scores = (
            jnp.einsum("qhd,khd->hqk", part_queries, own_keys, preferred_element_type=jnp.float32)
            * score_scale
        )
        probability = jnp.where(row_mask, jnp.exp(scores - part_mass[:, :, None]), 0.0)
        value_add_rows = jnp.einsum(
            "hqk,qhd->khd",
            probability.astype(jnp.bfloat16),
            part_tangent,
            preferred_element_type=jnp.float32,
        )
        prob_tan = jnp.einsum(
            "qhd,khd->hqk", part_tangent, own_values, preferred_element_type=jnp.float32
        )
        score_tan = (probability * (prob_tan - part_delta[:, :, None])).astype(jnp.bfloat16)
        key_add_rows = jnp.einsum(
            "hqk,qhd->khd", score_tan, part_queries, preferred_element_type=jnp.float32
        )
        return (
            key_acc + key_add_rows.reshape(token_count, D) * score_scale,
            value_acc + value_add_rows.reshape(token_count, D),
        )

    def owner_unit(current, pieces, first_row):
        query_blocks = lax.dynamic_slice_in_dim(order_row, first_row // BLK, 1)
        visible = block_mask(query_blocks, lookup(seq_row, query_blocks), own_blocks, own_seqs)
        return lax.cond(
            jnp.any(visible),
            lambda inner_state: owner_block(inner_state, pieces, first_row, visible),
            lambda inner_state: inner_state,
            current,
        )

    key_sum, value_sum = fold_units(
        (zero_rows, zero_rows),
        (
            lax.all_gather(queries, "ctx", axis=0, tiled=True),
            lax.all_gather(mixed_tan, "ctx", axis=0, tiled=True),
        ),
        owner_unit,
    )
    query_tan = query_sum.astype(jnp.bfloat16)
    key_tan = key_sum.astype(jnp.bfloat16)
    value_tan = value_sum.astype(jnp.bfloat16)
    slope_query = cross_rows(post_low, query_tan)
    slope_key = cross_rows(post_low, key_tan)
    slope_value = cross_rows(post_low, value_tan)
    drift_query = column_total(query_tan)
    drift_value = column_total(value_tan)
    post_tangent = (
        entry_tan
        + cross_cols(query_tan, query_whole)
        + cross_cols(key_tan, key_whole)
        + cross_cols(value_tan, value_whole)
    )
    heads_parts = lax.psum(
        (
            slope_query,
            slope_key,
            slope_value,
            slope_output,
            drift_query,
            drift_value,
            drift_output,
            stretch_one,
            nudge_one,
        ),
        "ctx",
    )
    heads_sums = (
        lax.psum_scatter(heads_parts[0], "fsdp", scatter_dimension=1, tiled=True),
        lax.psum_scatter(heads_parts[1], "fsdp", scatter_dimension=1, tiled=True),
        lax.psum_scatter(heads_parts[2], "fsdp", scatter_dimension=1, tiled=True),
        lax.psum_scatter(heads_parts[3], "fsdp", scatter_dimension=0, tiled=True),
        lax.psum_scatter(heads_parts[4], "fsdp", scatter_dimension=0, tiled=True),
        lax.psum_scatter(heads_parts[5], "fsdp", scatter_dimension=0, tiled=True),
        lax.psum_scatter(heads_parts[6], "fsdp", scatter_dimension=0, tiled=True),
        lax.psum_scatter(heads_parts[7], "fsdp", scatter_dimension=0, tiled=True),
        lax.psum_scatter(heads_parts[8], "fsdp", scatter_dimension=0, tiled=True),
    )
    return (
        layer_output[None],
        post_tangent[None],
        stream_tan[None],
        heads_sums[0],
        heads_sums[1],
        heads_sums[2],
        heads_sums[3],
        heads_sums[4],
        heads_sums[5],
        heads_sums[6],
        heads_sums[7],
        heads_sums[8],
        feed_sums[0],
        feed_sums[1],
        feed_sums[2],
        feed_sums[3],
        feed_sums[4],
        feed_sums[5],
        feed_sums[6],
        feed_sums[7],
    )


def low_lanes(values):
    return lax.broadcasted_iota(jnp.int32, values.shape, 1) < HD


def swap_lanes(values):
    return pltpu.roll(values, HD, 1)


def low_pair(first, second):
    return jnp.where(low_lanes(first), first, swap_lanes(second))


def high_pair(first, second):
    return jnp.where(low_lanes(first), swap_lanes(first), second)


def side_pair(side, first, second):
    return low_pair(first, second) if side == 0 else high_pair(first, second)


def dot_nn(left, right):
    return jnp.dot(left, right, preferred_element_type=F32)


def dot_nt(left, right):
    return lax.dot_general(left, right, (((1,), (1,)), ((), ())), preferred_element_type=F32)


def dot_tn(left, right):
    return lax.dot_general(left, right, (((0,), (0,)), ((), ())), preferred_element_type=F32)


class Place:
    def __init__(self):
        self.c = lax.axis_index("ctx")
        self.f = lax.axis_index("fsdp")
        self.group = self.c // H
        self.head = self.c % H
        self.inside = jnp.where(self.group == self.f, 1, 0)

    def is_me(self, tc, tf):
        return jnp.logical_and(self.c == tc, self.f == tf)

    def signal(self, barrier, tc, tf):
        @pl.when(jnp.logical_not(self.is_me(tc, tf)))
        def _():
            pl.semaphore_signal(barrier, 1, device_id=(tc, tf), device_id_type=MESH)

    def greet_sources(self, n_ctx, partner):
        barrier = pltpu.get_barrier_semaphore()
        for tc in range(n_ctx):
            self.signal(barrier, tc, self.group)
        if partner:
            pl.semaphore_signal(
                barrier, 1, device_id=(self.c, 1 - self.f), device_id_type=MESH
            )
        pl.semaphore_wait(barrier, 2 * H + (1 if partner else 0) - self.inside)

    def greet_owners(self, n_ctx, partner, more=0):
        barrier = pltpu.get_barrier_semaphore()
        for head in range(H):
            for core in range(2):
                self.signal(barrier, self.f * H + head, core)
        if partner:
            pl.semaphore_signal(
                barrier, 1, device_id=(self.c, 1 - self.f), device_id_type=MESH
            )
        pl.semaphore_wait(barrier, n_ctx + (1 if partner else 0) + more - self.inside)

    def send(self, src, dst, send_sem, recv_sem, tc, tf):
        me = self.is_me(tc, tf)

        @pl.when(me)
        def _():
            pltpu.make_async_copy(src, dst, recv_sem).start()

        @pl.when(jnp.logical_not(me))
        def _():
            self.remote(src, dst, send_sem, recv_sem, tc, tf).start()

    def remote(self, src, dst, send_sem, recv_sem, tc, tf):
        return pltpu.make_async_remote_copy(
            src_ref=src,
            dst_ref=dst,
            send_sem=send_sem,
            recv_sem=recv_sem,
            device_id=(tc, tf),
            device_id_type=MESH,
        )

    def wait_sent(self, src, dst, send_sem, recv_sem, tc, tf):
        @pl.when(jnp.logical_not(self.is_me(tc, tf)))
        def _():
            self.remote(src, dst, send_sem, recv_sem, tc, tf).wait_send()


VECTORS = 10


def project_kernel(
    n_ctx,
    x_hbm,
    wq_hbm,
    wk_hbm,
    wv_hbm,
    order_hbm,
    seq_hbm,
    *rest,
):
    vector_hbm, rest = rest[: VECTORS + 1], rest[VECTORS + 1 :]
    vector_in, rest = rest[-VECTORS - 1 :], rest[: -VECTORS - 1]
    (
        q_out,
        kv_out,
        w_other,
        order_out,
        seq_out,
        vec_out,
        expand_out,
        x_in,
        w_own,
        w_in,
        bias_own,
        bias_in,
        order_own,
        seq_own,
        order_in,
        seq_in,
        q_send,
        kv_send,
        load_sem,
        w_ss,
        w_rs,
        q_ss,
        q_rs,
        kv_ss,
        kv_rs,
        relay_ss,
        relay_rs,
    ) = rest
    at = Place()
    other = 1 - at.f
    loads = [
        pltpu.make_async_copy(src, dst, load_sem.at[i])
        for i, (src, dst) in enumerate(
            (
                (x_hbm, x_in),
                (wq_hbm, w_own.at[0]),
                (wk_hbm, w_own.at[1]),
                (wv_hbm, w_own.at[2]),
                (order_hbm, order_own),
                (seq_hbm, seq_own),
                *zip(vector_hbm, vector_in),
            )
        )
    ]
    for load in loads:
        load.start()
    at.greet_sources(n_ctx, True)
    for load in loads[6:]:
        load.wait()
    wide = bias_own.shape[1]
    for row, ref in enumerate(vector_in[:VECTORS]):
        bias_own[row : row + 1, :] = ref[...].astype(F32).reshape(1, wide)
    for part in range(vector_in[VECTORS].shape[0] // wide):
        piece = vector_in[VECTORS][part * wide : part * wide + wide]
        bias_own[VECTORS + part : VECTORS + part + 1, :] = piece.astype(F32).reshape(1, wide)
    swaps = [
        at.remote(src, dst, w_ss.at[i], w_rs.at[i], at.c, other)
        for i, (src, dst) in enumerate(
            (
                (bias_own, bias_in),
                (wq_hbm, w_in.at[0]),
                (wk_hbm, w_in.at[1]),
                (wv_hbm, w_in.at[2]),
                (order_hbm, order_in),
                (seq_hbm, seq_in),
            )
        )
    ]
    for swap in swaps:
        swap.start()
    for load in loads[:6]:
        load.wait()

    def targets(half):
        for pair in range(2):
            for side in range(2):
                head = half * (H // 2) + 2 * pair + side
                for core in range(2):
                    slot = head * 2 + core
                    yield pair, side, head, core, (
                        kv_send.at[head, pl.ds(core * BLK, BLK)],
                        kv_out.at[2 * at.c + core],
                        kv_ss.at[slot],
                        kv_rs.at[at.c],
                        at.f * H + head,
                        core,
                    ), (
                        q_send.at[head, core],
                        q_out.at[at.c],
                        q_ss.at[slot],
                        q_rs.at[at.c],
                        at.f * H + head,
                        core,
                    )

    def one_half(half, wq, wk, wv, bias):
        low = x_in[...].astype(BF16)
        q = dot_nn(low, wq[...]) + bias[0:1, :]
        k = dot_nn(low, wk[...])
        v = dot_nn(low, wv[...]) + bias[1:2, :]
        for pair, side, head, core, kv_move, q_move in targets(half):
            columns = slice(pair * 128, pair * 128 + 128)
            if core == 0:
                kv_send[head] = side_pair(side, k[:, columns], v[:, columns]).astype(BF16)
            rows = slice(core * HALF, core * HALF + HALF)
            late = slice(BLK + core * HALF, BLK + core * HALF + HALF)
            q_send[head, core] = side_pair(side, q[rows, columns], q[late, columns]).astype(BF16)
            at.send(*kv_move)
            at.send(*q_move)

    one_half(at.f, w_own.at[0], w_own.at[1], w_own.at[2], bias_own)
    for swap in swaps:
        swap.wait()
    one_half(other, w_in.at[0], w_in.at[1], w_in.at[2], bias_in)
    w_other[...] = w_in[...]
    inside = at.inside == 1
    order_out[...] = jnp.where(inside, order_own[...], order_in[...])
    seq_out[...] = jnp.where(inside, seq_own[...], seq_in[...])
    vec_out[...] = whole_rows(bias_own[...], bias_in[...], at.f == 0)
    for row, source in enumerate((bias_own, bias_in)):
        for part in range(expand_out.shape[1] // wide):
            at_row = VECTORS + part
            expand_out[row : row + 1, part * wide : part * wide + wide] = source[
                at_row : at_row + 1, :
            ]

    def relay(source):
        mine = kv_out.at[2 * source + at.f]
        return at.remote(mine, mine, relay_ss.at[source], relay_rs.at[source], at.c, other)

    def relay_in(source):
        theirs = kv_out.at[2 * source + other]
        return at.remote(theirs, theirs, relay_ss.at[source], relay_rs.at[source], at.c, other)

    for source in range(n_ctx):
        arrived = kv_out.at[2 * source + at.f]
        at.remote(arrived, arrived, kv_ss.at[0], kv_rs.at[source], at.c, other).wait_recv()
        relay(source).start()
    for source in range(n_ctx):
        arrived = q_out.at[source]
        at.remote(arrived, arrived, q_ss.at[0], q_rs.at[source], at.c, other).wait_recv()
        relay_in(source).wait_recv()
    for source in range(n_ctx):
        relay(source).wait_send()
    for half in (at.f, other):
        for _, _, _, _, kv_move, q_move in targets(half):
            at.wait_sent(*kv_move)
            at.wait_sent(*q_move)


def project_and_scatter(n_ctx, x, wq, wk, wv, order, seqs, vectors):
    wide = wq.shape[1]
    blocks = order.shape[1]
    units = vectors[VECTORS].shape[0]
    bias_rows = VECTORS + units // wide
    return pl.pallas_call(
        functools.partial(project_kernel, n_ctx),
        out_shape=(
            jax.ShapeDtypeStruct((n_ctx, HALF, 128), BF16),
            jax.ShapeDtypeStruct((2 * n_ctx, BLK, 128), BF16),
            jax.ShapeDtypeStruct((3, D, wide), BF16),
            jax.ShapeDtypeStruct((1, blocks), jnp.int32),
            jax.ShapeDtypeStruct((1, blocks), jnp.int32),
            jax.ShapeDtypeStruct((bias_rows, D), F32),
            jax.ShapeDtypeStruct((2, units), F32),
        ),
        in_specs=[ANY] * (7 + VECTORS),
        out_specs=(ANY, ANY) + (VMEM,) * 5,
        scratch_shapes=[
            pltpu.VMEM((2 * BLK, D), F32),
            pltpu.VMEM((3, D, wide), BF16),
            pltpu.VMEM((3, D, wide), BF16),
            pltpu.VMEM((bias_rows, wide), F32),
            pltpu.VMEM((bias_rows, wide), F32),
            pltpu.VMEM((1, blocks), jnp.int32),
            pltpu.VMEM((1, blocks), jnp.int32),
            pltpu.VMEM((1, blocks), jnp.int32),
            pltpu.VMEM((1, blocks), jnp.int32),
            pltpu.VMEM((H, 2, HALF, 128), BF16),
            pltpu.VMEM((H, 2 * BLK, 128), BF16),
            pltpu.SemaphoreType.DMA((7 + VECTORS,)),
            pltpu.SemaphoreType.DMA((6,)),
            pltpu.SemaphoreType.DMA((6,)),
            pltpu.SemaphoreType.DMA((2 * H,)),
            pltpu.SemaphoreType.DMA((n_ctx,)),
            pltpu.SemaphoreType.DMA((2 * H,)),
            pltpu.SemaphoreType.DMA((n_ctx,)),
            pltpu.SemaphoreType.DMA((n_ctx,)),
            pltpu.SemaphoreType.DMA((n_ctx,)),
        ]
        + [pltpu.VMEM(vector.shape, BF16) for vector in vectors],
        compiler_params=pltpu.CompilerParams(
            collective_id=0, has_side_effects=True, vmem_limit_bytes=ROOM
        ),
        name="project_scatter",
    )(x, wq, wk, wv, order, seqs, *vectors)


def forward_kernel(
    blocks,
    order_ref,
    seq_ref,
    q_ref,
    kv_ref,
    o_ref,
    keep_ref,
    lse_ref,
    pairs_ref,
    place,
    q_low,
    peaks,
    masses,
    total,
    scores,
):
    def place_block(slot, _):
        place[order_ref[0, slot]] = slot
        return 0

    lax.fori_loop(0, blocks, place_block, 0)

    count = jnp.int32(0)
    for gap in range(1, LONG):
        for late in range(gap, blocks):
            pairs_ref[0, count] = place[late]
            pairs_ref[1, count] = place[late - gap]
            count = count + jnp.where(seq_ref[0, late] == seq_ref[0, late - gap], 1, 0)
    for spare in range(TOGETHER):
        pairs_ref[0, count + spare] = blocks
        pairs_ref[1, count + spare] = 0
    turns = (count + TOGETHER - 1) // TOGETHER
    pairs_ref[2, 0] = turns

    def unpack(step, _):
        for part in range(4):
            source = step * 4 + part
            packed = q_ref[source].astype(F32) * (HD**-0.5)
            low = low_lanes(packed)
            q_low[2 * source] = jnp.where(low, packed, 0.0).astype(BF16)
            q_low[2 * source + 1] = jnp.where(low, swap_lanes(packed), 0.0).astype(BF16)
        return 0

    lax.fori_loop(0, blocks // 8, unpack, 0)
    q_low[blocks] = jnp.zeros((HALF, 128), BF16)

    peaks[blocks] = jnp.zeros((HALF, 128), F32)
    masses[blocks] = jnp.zeros((HALF, 128), F32)
    total[blocks] = jnp.zeros((HALF, 128), F32)
    lse_ref[blocks] = jnp.zeros((HALF, 128), F32)

    def own_slots(step):
        return [(step * TOGETHER + part,) * 2 for part in range(TOGETHER)]

    def pair_slots(step):
        return [
            (pairs_ref[0, step * TOGETHER + part], pairs_ref[1, step * TOGETHER + part])
            for part in range(TOGETHER)
        ]

    def score(slots, base):
        results = []
        for part, (q_slot, k_slot) in enumerate(slots):
            result = dot_nt(q_low[q_slot], kv_ref[k_slot])
            scores[base + part] = result
            results.append(jnp.maximum(result[:, :128], result[:, 128:]))
        return results

    def score_own(step, _):
        slots = own_slots(step)
        for (q_slot, _), result in zip(slots, score(slots, step * TOGETHER)):
            peaks[q_slot] = result
        return 0

    def score_pairs(step, _):
        slots = pair_slots(step)
        for (q_slot, _), result in zip(slots, score(slots, blocks + step * TOGETHER)):
            peaks[q_slot] = jnp.maximum(peaks[q_slot], result)
        return 0

    lax.fori_loop(0, blocks // TOGETHER, score_own, 0)
    lax.fori_loop(0, turns, score_pairs, 0)

    def level(step, _):
        for part in range(4):
            slot = step * 4 + part
            peaks[slot] = jnp.broadcast_to(
                jnp.max(peaks[slot], axis=1, keepdims=True), (HALF, 128)
            )
        return 0

    lax.fori_loop(0, blocks // 4, level, 0)

    def weigh(slots, base):
        results = []
        for part, (q_slot, k_slot) in enumerate(slots):
            peak = peaks[q_slot]
            left = jnp.exp(scores[base + part, :, :128] - peak)
            right = jnp.exp(scores[base + part, :, 128:] - peak)
            weights = jnp.concatenate([left, right], axis=1).astype(BF16)
            results.append((left + right, dot_nn(weights, kv_ref[k_slot])))
        return results

    def weigh_own(step, _):
        slots = own_slots(step)
        for (q_slot, _), (mass, result) in zip(slots, weigh(slots, step * TOGETHER)):
            masses[q_slot] = mass
            total[q_slot] = result
        return 0

    def weigh_pairs(step, _):
        slots = pair_slots(step)
        for (q_slot, _), (mass, result) in zip(slots, weigh(slots, blocks + step * TOGETHER)):
            masses[q_slot] = masses[q_slot] + mass
            total[q_slot] = total[q_slot] + result
        return 0

    lax.fori_loop(0, blocks // TOGETHER, weigh_own, 0)
    lax.fori_loop(0, turns, weigh_pairs, 0)

    def finish(step, _):
        for part in range(4):
            source = step * 4 + part
            for side in range(2):
                slot = 2 * source + side
                mass = jnp.broadcast_to(
                    jnp.sum(masses[slot], axis=1, keepdims=True), (HALF, 128)
                )
                result = total[slot] / mass
                lse_ref[slot] = peaks[slot] + jnp.log(mass)
                packed = high_pair(result[: HALF // 2], result[HALF // 2 :])
                keep_ref[source, side] = packed
                o_ref[source, side] = packed.astype(BF16)
        return 0

    lax.fori_loop(0, blocks // 8, finish, 0)


def pair_room(blocks):
    return blocks * MOST // 2 + 2 * TOGETHER


def attend(order, seqs, q, kv):
    blocks = kv.shape[0]
    room = pair_room(blocks)
    return pl.pallas_call(
        functools.partial(forward_kernel, blocks),
        out_shape=(
            jax.ShapeDtypeStruct((blocks // 2, 2, HALF // 2, 128), BF16),
            jax.ShapeDtypeStruct((blocks // 2, 2, HALF // 2, 128), F32),
            jax.ShapeDtypeStruct((blocks + 1, HALF, 128), F32),
            jax.ShapeDtypeStruct((3, room), jnp.int32),
        ),
        in_specs=[SMEM, SMEM, VMEM, VMEM],
        out_specs=(VMEM, VMEM, VMEM, SMEM),
        scratch_shapes=[
            pltpu.SMEM((blocks,), jnp.int32),
            pltpu.VMEM((blocks + 1, HALF, 128), BF16),
            pltpu.VMEM((blocks + 1, HALF, 128), F32),
            pltpu.VMEM((blocks + 1, HALF, 128), F32),
            pltpu.VMEM((blocks + 1, HALF, 128), F32),
            pltpu.VMEM((room, HALF, BLK), F32),
        ],
        compiler_params=pltpu.CompilerParams(vmem_limit_bytes=ROOM),
        name="attend",
    )(order, seqs, q, kv)


def backward_kernel(
    blocks,
    pairs_ref,
    q_ref,
    tan_ref,
    keep_ref,
    lse_ref,
    kv_ref,
    pass_a,
    pass_b,
    dq_ref,
    dkv_sum,
    out_a,
    out_b,
    both,
    turned,
    deltas,
    dq_sum,
    held,
    pass_sem,
):
    fetches = [
        pltpu.make_async_copy(src, held.at[i], pass_sem.at[i])
        for i, src in enumerate((pass_a, pass_b))
    ]
    passes = [
        pltpu.make_async_copy(held.at[i], dst, pass_sem.at[2 + i])
        for i, dst in enumerate((out_a, out_b))
    ]
    for fetch in fetches:
        fetch.start()

    def unpack(step, _):
        for part in range(4):
            source = step * 4 + part
            packed = q_ref[source].astype(F32) * (HD**-0.5)
            low = low_lanes(packed)
            for side in range(2):
                slot = 2 * source + side
                q = packed if side == 0 else swap_lanes(packed)
                both[slot, 0:HALF] = jnp.where(low, q, 0.0).astype(BF16)
                tangent = tan_ref[source, side].astype(F32)
                first = low_lanes(tangent)
                both[slot, HALF : HALF + HALF // 2] = jnp.where(
                    first, 0.0, swap_lanes(tangent)
                ).astype(BF16)
                both[slot, HALF + HALF // 2 : BLK] = jnp.where(first, 0.0, tangent).astype(BF16)
                turned[slot] = jnp.transpose(both[slot])
                product = tangent * keep_ref[source, side]
                delta = jnp.concatenate(
                    [
                        jnp.sum(jnp.where(first, product, 0.0), axis=1, keepdims=True),
                        jnp.sum(jnp.where(first, 0.0, product), axis=1, keepdims=True),
                    ],
                    axis=0,
                )
                deltas[slot] = jnp.broadcast_to(delta, (HALF, 128))
        return 0

    lax.fori_loop(0, blocks // 8, unpack, 0)
    both[blocks] = jnp.zeros((BLK, 128), BF16)
    turned[blocks] = jnp.zeros((128, BLK), BF16)
    deltas[blocks] = jnp.zeros((HALF, 128), F32)
    dq_sum[blocks] = jnp.zeros((HALF, 128), F32)

    def one_pair(q_slot, k_slot):
        kv = kv_ref[k_slot]
        products = dot_nt(both[q_slot], kv)
        mass, delta = lse_ref[q_slot], deltas[q_slot]
        weights = jnp.exp(products[:HALF] - jnp.concatenate([mass, mass], axis=1))
        score_tan = weights * (products[HALF:] - jnp.concatenate([delta, delta], axis=1))
        score_tan = score_tan.astype(BF16)
        sides = jnp.concatenate([score_tan, weights.astype(BF16)], axis=0)
        return dot_nn(turned[q_slot], sides), dot_nn(score_tan, kv)

    def own_turn(step, _):
        slots = [step * TOGETHER + part for part in range(TOGETHER)]
        results = [one_pair(slot, slot) for slot in slots]
        for slot, (dkv, dq) in zip(slots, results):
            dkv_sum[slot] = dkv
            dq_sum[slot] = dq
        return 0

    def pair_turn(step, _):
        slots = [
            (pairs_ref[0, step * TOGETHER + part], pairs_ref[1, step * TOGETHER + part])
            for part in range(TOGETHER)
        ]
        results = [one_pair(*slot) for slot in slots]
        for (q_slot, k_slot), (dkv, dq) in zip(slots, results):
            dkv_sum[k_slot] = dkv_sum[k_slot] + dkv
            dq_sum[q_slot] = dq_sum[q_slot] + dq
        return 0

    lax.fori_loop(0, blocks // TOGETHER, own_turn, 0)
    for fetch, move in zip(fetches, passes):
        fetch.wait()
        move.start()
    lax.fori_loop(0, pairs_ref[2, 0], pair_turn, 0)

    def finish_rows(step, _):
        for part in range(4):
            source = step * 4 + part
            packed = low_pair(dq_sum[2 * source], dq_sum[2 * source + 1]) * (HD**-0.5)
            dq_ref[source] = packed.astype(BF16)
        return 0

    lax.fori_loop(0, blocks // 8, finish_rows, 0)
    for move in passes:
        move.wait()


def attend_back(pairs, q, tangent, keep, lse, kv, passed):
    blocks = kv.shape[0]
    return pl.pallas_call(
        functools.partial(backward_kernel, blocks),
        out_shape=(
            jax.ShapeDtypeStruct((blocks // 2, HALF, 128), BF16),
            jax.ShapeDtypeStruct((blocks, 128, BLK), F32),
            jax.ShapeDtypeStruct(passed[0].shape, F32),
            jax.ShapeDtypeStruct(passed[1].shape, F32),
        ),
        in_specs=[SMEM, VMEM, VMEM, VMEM, VMEM, VMEM, ANY, ANY],
        out_specs=(VMEM, VMEM, ANY, ANY),
        scratch_shapes=[
            pltpu.VMEM((blocks + 1, BLK, 128), BF16),
            pltpu.VMEM((blocks + 1, 128, BLK), BF16),
            pltpu.VMEM((blocks + 1, HALF, 128), F32),
            pltpu.VMEM((blocks + 1, HALF, 128), F32),
            pltpu.VMEM((2,) + passed[0].shape, F32),
            pltpu.SemaphoreType.DMA((4,)),
        ],
        compiler_params=pltpu.CompilerParams(vmem_limit_bytes=ROOM),
        name="attend_back",
    )(pairs, q, tangent, keep, lse, kv, *passed)


def pieces_of(start, size, body):
    piece = max(n for n in range(16, 97, 16) if size % n == 0)
    lax.fori_loop(
        0,
        size // piece,
        lambda i, _: (body(i * piece, span(start + i * piece, piece), piece), 0)[1],
        0,
    )


def span(start, size):
    return pl.ds(pl.multiple_of(start, 16), size)


def step_of(c, stride):
    bit = (c // stride) % 2
    return bit, c + stride * (1 - 2 * bit)


REGIONS = 4


def columns_of(region):
    wide = D // (REGIONS // 2)
    return slice(region // 2 * wide, region // 2 * wide + wide)


class Ladder:
    def __init__(self, at, plans, starts, size, acc, stage, landing, out, sems, bases=(0, 0)):
        self.bases = bases
        self.at, self.acc, self.stage, self.landing, self.out = at, acc, stage, landing, out
        self.down_ss, self.down_rs, self.up_ss, self.up_rs = sems
        self.ranges = []
        for region in range(REGIONS):
            plan, start = plans[region % 2], starts[region % 2]
            listed, rows = [], size
            for bit, peer in plan[:-1]:
                rows = rows // 2
                listed.append((start + bit * rows, start + (1 - bit) * rows, rows, peer))
                start = start + bit * rows
            listed.append((start, start, rows, plan[-1][1]))
            self.ranges.append(listed)
        self.last = len(plans[0]) - 1

    def slot(self, region, step):
        return region * (self.last + 1) + step

    def down(self, region, step, sent):
        kept, given, size, peer = self.ranges[region][step]
        where, slot = span(given if sent else kept, size), self.slot(region, step)
        columns = columns_of(region)
        return self.at.remote(
            self.stage[region % 2].at[where, columns],
            self.landing[region % 2][step].at[where, columns],
            self.down_ss.at[slot],
            self.down_rs.at[slot],
            peer,
            self.at.f,
        )

    def up(self, region, step, sent):
        kept, given, size, peer = self.ranges[region][step]
        start = self.bases[region % 2] + (kept if sent else given)
        columns = columns_of(region)
        where, slot = span(start, size), self.slot(region, step)
        return self.at.remote(
            self.out.at[where, columns],
            self.out.at[where, columns],
            self.up_ss.at[slot],
            self.up_rs.at[slot],
            peer,
            self.at.f,
        )

    def join(self, region, start, size, arrived, target):
        columns, acc = columns_of(region), self.acc[region % 2]

        def body(offset, where, _):
            total = acc[where, columns] + arrived[where, columns].astype(F32)
            target[where, columns] = total.astype(target.dtype)

        pieces_of(start, size, body)

    def give(self, region, step, arrived):
        kept, given, size, _ = self.ranges[region][step]
        self.join(region, given, size, arrived, self.stage[region % 2])
        self.down(region, step, True).start()
        if step < self.last:
            self.join(region, kept, size, arrived, self.acc[region % 2])

    def settle(self, region):
        kept, _, size, _ = self.ranges[region][self.last]
        arrived = self.landing[region % 2][self.last]
        columns, stage = columns_of(region), self.stage[region % 2]

        def body(offset, where, rows):
            total = stage[where, columns].astype(F32) + arrived[where, columns].astype(F32)
            row = span(self.bases[region % 2] + kept + offset, rows)
            self.out[row, columns] = total.astype(BF16)

        self.down(region, self.last, False).wait_recv()
        pieces_of(kept, size, body)
        self.up(region, self.last - 1, True).start()

    def wait_sent(self):
        for region in range(REGIONS):
            for step in range(self.last + 1):
                self.down(region, step, True).wait_send()
            for step in range(self.last):
                self.up(region, step, True).wait_send()


COLS = 512


def whole_rows(own, other, first):
    return jnp.where(
        first,
        jnp.concatenate([own, other], axis=1),
        jnp.concatenate([other, own], axis=1),
    )


def row_mean(values):
    return jnp.mean(values, axis=1, keepdims=True)


def normalize(values):
    centre = values - row_mean(values)
    scale = lax.rsqrt(row_mean(centre * centre) + norm_eps)
    return centre * scale, scale


def norm_back(tangent, normed, scale, gain):
    pushed = tangent * gain
    return scale * (pushed - row_mean(pushed) - normed * row_mean(pushed * normed))


def column_sum(values):
    return jnp.sum(values, axis=0, keepdims=True)


def feed_slopes(kind, target, mixed, low_turned, hidden, before_tan, feed_tan, branch_tan):
    unit_count = hidden.shape[2] // COLS

    def chunk_slopes(chunk, _):
        columns = pl.ds(pl.multiple_of(chunk * COLS, COLS), COLS)
        target[columns, :] = dot_tn(hidden[kind, :, columns], feed_tan[...]).astype(target.dtype)
        below = pl.ds(pl.multiple_of((unit_count + chunk) * COLS, COLS), COLS)
        target[below, :] = dot_nn(low_turned[...], before_tan[kind, :, columns]).astype(
            target.dtype
        )
        return 0

    lax.fori_loop(0, unit_count, chunk_slopes, 0)
    start = 2 * unit_count * COLS
    target[start : start + D // 2, :] = dot_tn(mixed[kind], branch_tan[...]).astype(target.dtype)


def middle_kernel(
    n_ctx,
    o_hbm, x_hbm, sum_hbm, cot_hbm, wo_a, wo_b, we_a, we_b, ws_a, ws_b, be_ref, vec_in,
    out_hbm, sum_tan_hbm, entry_hbm, tan_out, vec_ref, stage_a, stage_b, keep_ref,
    o_in, x_ref, sum_ref, cot_ref, wo, we, ws, out_ref, sum_tan_ref, entry_ref,
    mixed, low, hidden, before_tan, feed_tan, branch_tan, slope, mixed_tan, tan_send,
    own_grads, send_grads, first_in, low_turned,
    load_sem, store_sem, o_ss, o_rs, tan_ss, tan_rs, core_ss, core_rs,
):
    at = Place()
    f = at.f
    other = 1 - f
    halves = (f, other)
    piece = HALF // 2
    loads = [
        pltpu.make_async_copy(src, dst, load_sem.at[i])
        for i, (src, dst) in enumerate(
            (
                (x_hbm, x_ref),
                (wo_a, wo.at[0]),
                (wo_b, wo.at[1]),
                (we_a, we.at[0]),
                (we_b, we.at[1]),
                (ws_a, ws.at[0]),
                (ws_b, ws.at[1]),
                (sum_hbm, sum_ref),
                (cot_hbm, cot_ref),
            )
        )
    ]
    for load in loads:
        load.start()
    barrier = pltpu.get_barrier_semaphore()
    for target in range(n_ctx):
        at.signal(barrier, target, at.group)
    at.greet_owners(n_ctx, True, 2 * H - at.inside)

    def o_move(target, side):
        return (
            o_hbm.at[target, side],
            o_in.at[side, at.head, f],
            o_ss.at[2 * target + side],
            o_rs.at[side * 2 * H + at.head * 2 + f],
            target,
            at.group,
        )

    def tan_move(side, head, core):
        return (
            tan_send.at[side, head, core],
            tan_out.at[at.c, side],
            tan_ss.at[side * 2 * H + head * 2 + core],
            tan_rs.at[at.c * 2 + side],
            f * H + head,
            core,
        )

    for side in range(2):
        for target in range(n_ctx):
            at.send(*o_move(target, side))
    vec_ref[...] = jnp.zeros_like(vec_ref)
    vectors = vec_in[...]
    (out_bias, gain_one, shift_one, shrink_bias, gain_two, shift_two, gain_last, shift_last) = (
        vectors[i : i + 1] for i in range(2, 10)
    )
    be = (be_ref.at[0:1], be_ref.at[1:2])
    for load in loads:
        load.wait()

    def stores(step):
        rows = pl.ds(pl.multiple_of(step * BLK, BLK), BLK)
        return [
            pltpu.make_async_copy(src.at[rows], dst.at[rows], store_sem.at[3 * step + i])
            for i, (src, dst) in enumerate(
                ((out_ref, out_hbm), (sum_tan_ref, sum_tan_hbm), (entry_ref, entry_hbm))
            )
        ]

    def tile(step, _):
        first_row = pl.multiple_of(step * BLK, BLK)
        rows = pl.ds(first_row, BLK)
        for head in range(H):
            for core in range(2):
                arrived = o_in.at[step, head, core]
                at.remote(
                    arrived, arrived, o_ss.at[0], o_rs.at[step * 2 * H + head * 2 + core],
                    at.c, other,
                ).wait_recv()
        for kind in range(2):
            for pair in range(2):
                head = halves[kind] * (H // 2) + 2 * pair
                columns = slice(pair * 128, pair * 128 + 128)
                for core in range(2):
                    early = o_in[step, head, core].astype(F32)
                    late = o_in[step, head + 1, core].astype(F32)
                    for part in range(2):
                        start = pl.multiple_of(first_row + core * HALF + part * piece, piece)
                        mixed[kind, pl.ds(start, piece), columns] = side_pair(
                            part, early, late
                        ).astype(BF16)
        branch = dot_nn(mixed[0, rows, :], wo[0]) + dot_nn(mixed[1, rows, :], wo[1]) + out_bias
        n_one, scale_one = normalize(x_ref[rows, :] + branch)
        normed_one = n_one * gain_one + shift_one
        stream_one = sum_ref[rows, :] + branch
        normed_low = normed_one.astype(BF16)
        low[rows, :] = normed_low
        feed = jnp.zeros((BLK, D), F32)
        for kind in range(2):

            def expand(chunk, carried):
                columns = pl.ds(pl.multiple_of(chunk * COLS, COLS), COLS)
                v = dot_nn(normed_low, we[kind, :, columns]) + be[kind][:, columns]
                square = v * v
                t = jnp.tanh(gelu_coeff * (v + gelu_cubic * square * v))
                half_up = 0.5 + 0.5 * t
                hidden_part = (v * half_up).astype(BF16)
                hidden[kind, rows, columns] = hidden_part
                slope[kind, :, columns] = half_up + v * half_up * (1.0 - t) * (
                    gelu_coeff + (3.0 * gelu_coeff * gelu_cubic) * square
                )
                return carried + dot_nn(hidden_part, ws[kind, columns, :])

            feed = lax.fori_loop(0, ws.shape[1] // COLS, expand, feed)
        feed_out = feed + shrink_bias
        n_two, scale_two = normalize(normed_one + feed_out)
        n_last, scale_last = normalize(stream_one + feed_out)
        out_ref[rows, :] = (n_two * gain_two + shift_two) + (n_last * gain_last + shift_last)
        u = cot_ref[rows, :]
        nudge = column_sum(u)
        sum_tan = norm_back(u, n_last, scale_last, gain_last)
        inflow = norm_back(u, n_two, scale_two, gain_two)
        sum_tan_ref[rows, :] = sum_tan
        feed_low = (sum_tan + inflow).astype(BF16)
        feed_tan[rows, :] = feed_low
        vec_ref[0:1, :] += column_sum(feed_low.astype(F32))
        vec_ref[1:2, :] += column_sum(u * n_two)
        vec_ref[2:3, :] += nudge
        vec_ref[3:4, :] += column_sum(u * n_last)
        vec_ref[4:5, :] += nudge
        normed_tan = inflow
        for kind in range(2):

            def expand_back(chunk, carried):
                columns = pl.ds(pl.multiple_of(chunk * COLS, COLS), COLS)
                pushed = dot_nt(feed_low, ws[kind, columns, :])
                tan_part = (pushed * slope[kind, :, columns]).astype(BF16)
                before_tan[kind, rows, columns] = tan_part
                vec_row = pl.ds(8 + 2 * halves[kind] + chunk, 1)
                vec_ref[vec_row, :] += column_sum(tan_part.astype(F32))
                return carried + dot_nt(tan_part, we[kind, :, columns])

            normed_tan = lax.fori_loop(0, ws.shape[1] // COLS, expand_back, normed_tan)
        vec_ref[5:6, :] += column_sum(normed_tan * n_one)
        vec_ref[6:7, :] += column_sum(normed_tan)
        entry = norm_back(normed_tan, n_one, scale_one, gain_one)
        entry_ref[rows, :] = entry
        branch_low = (sum_tan + entry).astype(BF16)
        branch_tan[rows, :] = branch_low
        vec_ref[7:8, :] += column_sum(branch_low.astype(F32))
        for kind in range(2):
            mixed_tan[kind] = dot_nt(branch_low, wo[kind])
        for kind in range(2):
            for pair in range(2):
                columns = slice(pair * 128, pair * 128 + 128)
                for side in range(2):
                    head = halves[kind] * (H // 2) + 2 * pair + side
                    for core in range(2):
                        start = core * HALF
                        early = mixed_tan[kind, start : start + piece, columns]
                        late = mixed_tan[kind, start + piece : start + HALF, columns]
                        tan_send[step, head, core] = side_pair(side, early, late).astype(BF16)
                        at.send(*tan_move(step, head, core))
        for store in stores(step):
            store.start()
        return 0

    lax.fori_loop(0, 2, tile, 0)

    quarter = first_in.shape[0] // 4
    bits = (step_of(at.c, 1)[0], step_of(at.c, 2)[0])
    stages = (stage_a, stage_b)

    def core_move(region, give):
        bit = bits[region]
        start = region * 2 * quarter + (1 - bit if give else bit) * quarter
        where = span(start, quarter)
        slot = region + 2 * (0 if give else 1)
        return start, at.remote(
            send_grads.at[where], first_in.at[where], core_ss.at[slot], core_rs.at[slot],
            at.c, other,
        )

    order = [(0, True), (1, True), (0, False), (1, False)]
    low_turned[...] = jnp.transpose(low[...])
    operands = (mixed, low_turned, hidden, before_tan, feed_tan, branch_tan)
    feed_slopes(1, send_grads, *operands)
    for step in order:
        core_move(*step)[1].start()
    feed_slopes(0, own_grads, *operands)
    for region, give in order:
        start, move = core_move(region, give)
        move.wait_recv()

        def join(offset, where, size):
            total = own_grads[where, :] + first_in[where, :].astype(F32)
            if give:
                stages[region][span(offset, size), :] = total.astype(BF16)
            else:
                keep_ref[region, span(offset, size), :] = total

        pieces_of(start, quarter, join)
    for source in range(n_ctx):
        for side in range(2):
            arrived = tan_out.at[source, side]
            at.remote(
                arrived, arrived, tan_ss.at[0], tan_rs.at[source * 2 + side], at.c, other
            ).wait_recv()
    for step in range(2):
        for store in stores(step):
            store.wait()
    for side in range(2):
        for target in range(n_ctx):
            at.wait_sent(*o_move(target, side))
        for head in range(H):
            for core in range(2):
                at.wait_sent(*tan_move(side, head, core))
    for step in order:
        core_move(*step)[1].wait_send()


def middle(n_ctx, o, x, summed, cotangent, wo, we, ws, be, vec):
    tokens, wide, units = x.shape[0], D // 2, ws[0].shape[0]
    grad_rows = 2 * units + wide
    rows = jax.ShapeDtypeStruct((tokens, D), F32)

    def sems(*counts):
        return [pltpu.SemaphoreType.DMA((count,)) for count in counts]

    return pl.pallas_call(
        functools.partial(middle_kernel, n_ctx),
        out_shape=(
            rows,
            rows,
            rows,
            jax.ShapeDtypeStruct((n_ctx, 2, HALF // 2, 128), BF16),
            jax.ShapeDtypeStruct((16, D), F32),
            jax.ShapeDtypeStruct((grad_rows // 4, D), BF16),
            jax.ShapeDtypeStruct((grad_rows // 4, D), BF16),
            jax.ShapeDtypeStruct((2, grad_rows // 4, D), F32),
        ),
        in_specs=[ANY] * 10 + [VMEM] * 2,
        out_specs=(ANY,) * 4 + (VMEM,) * 4,
        scratch_shapes=[
            pltpu.VMEM((2, H, 2, HALF // 2, 128), BF16),
            pltpu.VMEM((tokens, D), F32),
            pltpu.VMEM((tokens, D), F32),
            pltpu.VMEM((tokens, D), F32),
            pltpu.VMEM((2, wide, D), BF16),
            pltpu.VMEM((2, D, units), BF16),
            pltpu.VMEM((2, units, D), BF16),
            pltpu.VMEM((tokens, D), F32),
            pltpu.VMEM((tokens, D), F32),
            pltpu.VMEM((tokens, D), F32),
            pltpu.VMEM((2, tokens, wide), BF16),
            pltpu.VMEM((tokens, D), BF16),
            pltpu.VMEM((2, tokens, units), BF16),
            pltpu.VMEM((2, tokens, units), BF16),
            pltpu.VMEM((tokens, D), BF16),
            pltpu.VMEM((tokens, D), BF16),
            pltpu.VMEM((2, BLK, units), F32),
            pltpu.VMEM((2, BLK, wide), F32),
            pltpu.VMEM((2, H, 2, HALF // 2, 128), BF16),
            pltpu.VMEM((grad_rows, D), F32),
            pltpu.VMEM((grad_rows, D), BF16),
            pltpu.VMEM((grad_rows, D), BF16),
            pltpu.VMEM((D, tokens), BF16),
        ]
        + sems(9, 6, 2 * n_ctx, 4 * H, 4 * H, 2 * n_ctx, 4, 4),
        compiler_params=pltpu.CompilerParams(
            collective_id=1, has_side_effects=True, vmem_limit_bytes=ROOM
        ),
        name="middle",
    )(o, x, summed, cotangent, *wo, *we, *ws, be, vec)


def finish_kernel(
    n_ctx,
    dq_ref, dkv_ref, keep_hbm, land_a, land_b, x_hbm, entry_hbm, wq_hbm, wk_hbm, wv_hbm,
    w_other_hbm, vec_feed,
    post_ref, feed_ref, grads_ref, vec_out,
    own, part, ready, dq_in, dkv_in, keep, acc, stage, landing,
    x_in, entry_in, w_in, w_far, low_turned, tangents,
    own_grads, send_grads, first_in, acc_last, stage_last, landing_last, vec_sum, vec_in,
    load_sem, q_ss, q_rs, kv_ss, kv_rs, part_ss, part_rs, own_sem,
    down_ss, down_rs, up_ss, up_rs, top_ss, top_rs,
    core_ss, core_rs, down_ss2, down_rs2, up_ss2, up_rs2, vec_ss, vec_rs,
):
    at = Place()
    c, f = at.c, at.f
    other = 1 - f
    halves = (f, other)
    wide = D // 2
    loads = [
        pltpu.make_async_copy(src, dst, load_sem.at[i])
        for i, (src, dst) in enumerate(
            (
                (keep_hbm, keep),
                (x_hbm, x_in),
                (entry_hbm, entry_in),
                (wq_hbm, w_in.at[0]),
                (wk_hbm, w_in.at[1]),
                (wv_hbm, w_in.at[2]),
                (w_other_hbm, w_far),
            )
        )
    ]
    for load in loads:
        load.start()
    x_step, y_step, near, far = (step_of(c, stride) for stride in (1, 2, 4, 8))
    barrier = pltpu.get_barrier_semaphore()
    for _, peer in (x_step, y_step, near, far):
        pl.semaphore_signal(barrier, 1, device_id=(peer, f), device_id_type=MESH)
    at.greet_owners(n_ctx, True, 4)

    def partial_move(source):
        return at.remote(
            dkv_ref.at[2 * source + other],
            part.at[source],
            part_ss.at[source],
            part_rs.at[source],
            c,
            other,
        )

    def own_move(source):
        return pltpu.make_async_copy(
            dkv_ref.at[2 * source + f], own.at[source], own_sem.at[source]
        )

    def q_move(target):
        return (
            dq_ref.at[target],
            dq_in.at[at.head, f],
            q_ss.at[target],
            q_rs.at[at.head * 2 + f],
            target,
            at.group,
        )

    def kv_move(target):
        return (
            ready.at[target],
            dkv_in.at[at.head, pl.ds(pl.multiple_of(f * BLK, BLK), BLK)],
            kv_ss.at[target],
            kv_rs.at[at.head * 2 + f],
            target,
            at.group,
        )

    for source in range(n_ctx):
        partial_move(source).start()
        own_move(source).start()
    for target in range(n_ctx):
        at.send(*q_move(target))

    size = keep.shape[1]
    firsts = (x_step, y_step)
    bases = [2 * size * region + firsts[region][0] * size for region in range(2)]
    feed = Ladder(
        at,
        ((y_step, near, far), (x_step, near, far)),
        (0, 0),
        size,
        [keep.at[region] for region in range(2)],
        [stage.at[region] for region in range(2)],
        [[landing.at[region, step] for step in range(3)] for region in range(2)],
        feed_ref,
        (down_ss, down_rs, up_ss, up_rs),
        bases,
    )

    def top_move(region, sent):
        side, columns = region % 2, columns_of(region)
        given = 2 * size * side + (1 - firsts[side][0]) * size
        where = span(bases[side] if sent else given, size)
        return at.remote(
            feed_ref.at[where, columns],
            feed_ref.at[where, columns],
            top_ss.at[region],
            top_rs.at[region],
            firsts[side][1],
            f,
        )

    loads[0].wait()
    kept_acc = [keep.at[region] for region in range(2)]
    sums = [acc.at[region] for region in range(2)]
    for region in range(REGIONS):
        first = (land_a, land_b)[region % 2]
        kept, given, half, _ = feed.ranges[region][0]
        feed.acc = kept_acc
        feed.join(region, given, half, first, stage.at[region % 2])
        feed.down(region, 0, True).start()
        feed.join(region, kept, half, first, sums[region % 2])
    feed.acc = sums
    for source in range(n_ctx):
        own_move(source).wait()
        partial_move(source).wait_recv()
        ready[source] = jnp.transpose(own[source] + part[source]).astype(BF16)
        at.send(*kv_move(source))
    for load in loads[1:]:
        load.wait()
    low_turned[...] = jnp.transpose(x_in[...]).astype(BF16)
    for step in (1, 2):
        for region in range(REGIONS):
            feed.down(region, step - 1, False).wait_recv()
            feed.give(region, step, feed.landing[region % 2][step - 1])

    for head in range(H):
        for core in range(2):
            slot = head * 2 + core
            arrived = dq_in.at[head, core]
            at.remote(arrived, arrived, q_ss.at[0], q_rs.at[slot], c, other).wait_recv()
            arrived = dkv_in.at[head, pl.ds(core * BLK, BLK)]
            at.remote(arrived, arrived, kv_ss.at[0], kv_rs.at[slot], c, other).wait_recv()
    feed_rows = vec_feed.shape[0]
    vec_sum[0, 0:feed_rows] = vec_feed[...]
    vec_sum[0, feed_rows:] = jnp.zeros_like(vec_sum[0, feed_rows:])

    plans = ((x_step, y_step, near, far), (y_step, x_step, near, far))
    quarter = first_in.shape[0] // 4
    last = Ladder(
        at,
        plans,
        (0, 2 * quarter),
        2 * quarter,
        [acc_last, acc_last],
        [stage_last, stage_last],
        [[landing_last.at[step] for step in range(4)]] * 2,
        grads_ref,
        (down_ss2, down_rs2, up_ss2, up_rs2),
    )

    def core_move(region, give):
        kept, given, rows, _ = last.ranges[region][0]
        where = span(given if give else kept, rows)
        slot, columns = region + REGIONS * (0 if give else 1), columns_of(region)
        return at.remote(
            send_grads.at[where, columns],
            first_in.at[where, columns],
            core_ss.at[slot],
            core_rs.at[slot],
            c,
            other,
        )

    order = [(region, give) for give in (True, False) for region in range(REGIONS)]
    vec_peers = [(c, other)] + [(peer, f) for _, peer in (x_step, y_step, near, far)]

    def vec_move(step):
        return at.remote(
            vec_sum.at[step], vec_in.at[step], vec_ss.at[step], vec_rs.at[step], *vec_peers[step]
        )

    def vec_next(step):
        vec_move(step).wait_recv()
        target = vec_sum.at[step + 1] if step < 4 else vec_out
        target[...] = vec_sum[step] + vec_in[step]
        if step < 4:
            vec_move(step + 1).start()

    for kind, grad_ref in ((1, send_grads), (0, own_grads)):
        for pair in range(2):
            head = halves[kind] * (H // 2) + 2 * pair
            columns = slice(pair * 128, pair * 128 + 128)
            for core in range(2):
                early = dq_in[head, core].astype(F32)
                late = dq_in[head + 1, core].astype(F32)
                for side in range(2):
                    start = side * BLK + core * HALF
                    tangents[kind, 0, start : start + HALF, columns] = side_pair(
                        side, early, late
                    ).astype(BF16)
            early = dkv_in[head].astype(F32)
            late = dkv_in[head + 1].astype(F32)
            tangents[kind, 1, :, columns] = low_pair(early, late).astype(BF16)
            tangents[kind, 2, :, columns] = high_pair(early, late).astype(BF16)
        turned = low_turned[...]
        grad_ref[0:D, 0:wide] = dot_nn(turned, tangents[kind, 0]).astype(grad_ref.dtype)
        grad_ref[0:D, wide:D] = dot_nn(turned, tangents[kind, 1]).astype(grad_ref.dtype)
        value_grad = dot_nn(turned, tangents[kind, 2]).astype(grad_ref.dtype)
        grad_ref[D : D + wide, 0:wide] = value_grad[0:wide]
        grad_ref[D : D + wide, wide:D] = value_grad[wide:D]
        columns = pl.ds(pl.multiple_of(halves[kind] * wide, wide), wide)
        vec_sum[0, feed_rows : feed_rows + 1, columns] = column_sum(tangents[kind, 0].astype(F32))
        vec_sum[0, feed_rows + 1 : feed_rows + 2, columns] = column_sum(
            tangents[kind, 2].astype(F32)
        )
        if kind == 1:
            for step in order:
                core_move(*step).start()
    vec_move(0).start()
    for region in range(REGIONS):
        feed.settle(region)
    for region, give in order:
        core_move(region, give).wait_recv()
        kept, given, rows, _ = last.ranges[region][0]
        columns = columns_of(region)

        def join(offset, where, _):
            total = own_grads[where, columns] + first_in[where, columns].astype(F32)
            if give:
                stage_last[where, columns] = total.astype(BF16)
            else:
                acc_last[where, columns] = total

        pieces_of(given if give else kept, rows, join)
        if give:
            last.down(region, 0, True).start()
    vec_next(0)
    total = entry_in[...]
    for which in range(3):
        total = total + dot_nt(tangents[0, which], w_in[which])
        total = total + dot_nt(tangents[1, which], w_far[which])
    post_ref[...] = total
    for region in range(REGIONS):
        feed.up(region, 1, False).wait_recv()
        feed.up(region, 0, True).start()
    for step in (1, 2):
        for region in range(REGIONS):
            last.down(region, step - 1, False).wait_recv()
            last.give(region, step, last.landing[region % 2][step - 1])
        vec_next(step)
    for region in range(REGIONS):
        feed.up(region, 0, False).wait_recv()
        top_move(region, True).start()
    for region in range(REGIONS):
        last.down(region, 2, False).wait_recv()
        last.give(region, 3, last.landing[region % 2][2])
    vec_next(3)
    for region in range(REGIONS):
        last.settle(region)
    vec_next(4)
    for step in (2, 1, 0):
        for region in range(REGIONS):
            last.up(region, step, False).wait_recv()
            if step > 0:
                last.up(region, step - 1, True).start()
    for region in range(REGIONS):
        top_move(region, False).wait_recv()

    for target in range(n_ctx):
        partial_move(target).wait_send()
        at.wait_sent(*q_move(target))
        at.wait_sent(*kv_move(target))
    for step in order:
        core_move(*step).wait_send()
    for step in range(5):
        vec_move(step).wait_send()
    for region in range(REGIONS):
        top_move(region, True).wait_send()
    feed.wait_sent()
    last.wait_sent()


def finish(n_ctx, dq, dkv, keep, land_a, land_b, x, entry, wq, wk, wv, w_other, vec_feed):
    size, tokens, wide = keep.shape[1], x.shape[0], D // 2
    last_shape = (D + wide, D)
    vec_shape = (vec_feed.shape[0] + 8, D)

    def sems(*counts):
        return [pltpu.SemaphoreType.DMA((count,)) for count in counts]

    return pl.pallas_call(
        functools.partial(finish_kernel, n_ctx),
        out_shape=(
            jax.ShapeDtypeStruct((tokens, D), F32),
            jax.ShapeDtypeStruct((4 * size, D), BF16),
            jax.ShapeDtypeStruct(last_shape, BF16),
            jax.ShapeDtypeStruct(vec_shape, F32),
        ),
        in_specs=[ANY, ANY, ANY, VMEM, VMEM] + [ANY] * 6 + [VMEM],
        out_specs=(VMEM,) * 4,
        scratch_shapes=[
            pltpu.VMEM((n_ctx, 128, BLK), F32),
            pltpu.VMEM((n_ctx, 128, BLK), F32),
            pltpu.VMEM((n_ctx, BLK, 128), BF16),
            pltpu.VMEM((H, 2, HALF, 128), BF16),
            pltpu.VMEM((H, 2 * BLK, 128), BF16),
            pltpu.VMEM((2, size, D), F32),
            pltpu.VMEM((2, size, D), F32),
            pltpu.VMEM((2, size, D), BF16),
            pltpu.VMEM((2, 3, size, D), BF16),
            pltpu.VMEM((tokens, D), F32),
            pltpu.VMEM((tokens, D), F32),
            pltpu.VMEM((3, D, wide), BF16),
            pltpu.VMEM((3, D, wide), BF16),
            pltpu.VMEM((D, tokens), BF16),
            pltpu.VMEM((2, 3, tokens, wide), BF16),
            pltpu.VMEM(last_shape, F32),
            pltpu.VMEM(last_shape, BF16),
            pltpu.VMEM(last_shape, BF16),
            pltpu.VMEM(last_shape, F32),
            pltpu.VMEM(last_shape, BF16),
            pltpu.VMEM((4,) + last_shape, BF16),
            pltpu.VMEM((5,) + vec_shape, F32),
            pltpu.VMEM((5,) + vec_shape, F32),
        ]
        + sems(7, n_ctx, 2 * H, n_ctx, 2 * H, n_ctx, n_ctx, n_ctx)
        + sems(12, 12, 12, 12, 4, 4, 8, 8, 16, 16, 16, 16, 5, 5),
        compiler_params=pltpu.CompilerParams(
            collective_id=3, has_side_effects=True, vmem_limit_bytes=ROOM
        ),
        name="finish",
    )(dq, dkv, keep, land_a, land_b, x, entry, wq, wk, wv, w_other, vec_feed)


def unpack_kernel(
    full_hbm, grads_hbm, post_hbm, vec_ref,
    query_hbm, key_hbm, value_hbm, output_hbm, expand_hbm, shrink_hbm, post_out, *rest,
):
    vector_outs, (low_full, low_last, full, last, held, load_sem, store_sem, post_sem) = (
        rest[:11],
        rest[11:],
    )
    f = lax.axis_index("fsdp")
    units, wide = shrink_hbm.shape[0], D // 2
    post_in = pltpu.make_async_copy(post_hbm, held, post_sem.at[0])
    post = pltpu.make_async_copy(held, post_out, post_sem.at[1])
    post_in.start()
    parts = [
        (low_last, last, 0, D, [(query_hbm, slice(0, wide)), (key_hbm, slice(wide, D))]),
        (
            low_last,
            last,
            D,
            wide,
            [
                (value_hbm.at[0:wide], slice(0, wide)),
                (value_hbm.at[wide:D], slice(wide, D)),
            ],
        ),
    ]
    for part in range(units // D):
        parts.append(
            (
                low_full,
                full,
                part * D,
                D,
                [(shrink_hbm.at[part * D : part * D + D], slice(0, D))],
            )
        )
    for part in range(units // D):
        parts.append(
            (
                low_full,
                full,
                units + part * D,
                D,
                [(expand_hbm.at[:, part * D : part * D + D], slice(0, D))],
            )
        )
    parts.append((low_full, full, 2 * units, wide, [(output_hbm, slice(0, D))]))
    loads = []
    for i, (low, _, start, rows, _) in enumerate(parts):
        src = grads_hbm if low is low_last else full_hbm
        where = pl.ds(start, rows)
        loads.append(pltpu.make_async_copy(src.at[where], low.at[where], load_sem.at[i]))
        loads[-1].start()
    post_in.wait()
    post.start()
    stores = []
    for load, (low, wide_rows, start, rows, targets) in zip(loads, parts):
        load.wait()
        where = pl.ds(start, rows)
        wide_rows[where, :] = low[where, :].astype(F32)
        for target, columns in targets:
            stores.append(
                pltpu.make_async_copy(
                    wide_rows.at[where, columns], target, store_sem.at[len(stores)]
                )
            )
            stores[-1].start()
    vectors = vec_ref[...]
    mine = jnp.where(f == 0, vectors[:, 0:wide], vectors[:, wide:D])
    for row, ref in zip((16, 17, 7, 5, 6, 0, 1, 2, 3, 4), vector_outs):
        ref[...] = mine[row : row + 1]
    drift = jnp.where(f == 0, vectors[8:10], vectors[10:12])
    for part in range(units // D):
        vector_outs[10][:, part * D : part * D + D] = drift[part : part + 1]
    for store in stores:
        store.wait()
    post.wait()


def unpack_grads(units, full, grads, post, vecs):
    wide = D // 2
    shapes = [(D, wide)] * 3 + [(wide, D), (D, units), (units, D), post.shape]
    vectors = [(1, wide)] * 10 + [(1, units)]
    part_count = 3 + 2 * (units // D)
    return pl.pallas_call(
        unpack_kernel,
        out_shape=tuple(jax.ShapeDtypeStruct(shape, F32) for shape in shapes + vectors),
        in_specs=[ANY] * 3 + [VMEM],
        out_specs=(ANY,) * len(shapes) + (VMEM,) * len(vectors),
        scratch_shapes=[
            pltpu.VMEM(full.shape, BF16),
            pltpu.VMEM(grads.shape, BF16),
            pltpu.VMEM(full.shape, F32),
            pltpu.VMEM(grads.shape, F32),
            pltpu.VMEM(post.shape, F32),
            pltpu.SemaphoreType.DMA((part_count,)),
            pltpu.SemaphoreType.DMA((part_count + 2,)),
            pltpu.SemaphoreType.DMA((2,)),
        ],
        compiler_params=pltpu.CompilerParams(vmem_limit_bytes=ROOM),
        name="unpack_grads",
    )(full, grads, post, vecs)


def head_shards(
    n_ctx,
    post_stream,
    sum_stream,
    cotangent,
    block_order,
    block_sequence,
    query_weight,
    key_weight,
    value_weight,
    output_weight,
    query_bias,
    value_bias,
    output_bias,
    attend_gain,
    attend_shift,
    expand_weight,
    expand_bias,
    shrink_weight,
    shrink_bias,
    middle_gain,
    middle_shift,
    final_gain,
    final_shift,
):
    x, summed, tangent = post_stream[0], sum_stream[0], cotangent[0]
    swap = [(0, 1), (1, 0)]

    def from_other(values):
        return lax.ppermute(values, "fsdp", swap)

    def across(values, stride):
        return lax.ppermute(values, "ctx", [(c, c ^ stride) for c in range(n_ctx)])

    vectors = [
        query_bias,
        value_bias,
        output_bias,
        attend_gain,
        attend_shift,
        shrink_bias,
        middle_gain,
        middle_shift,
        final_gain,
        final_shift,
        expand_bias,
    ]
    q, kv, w_other, order, seqs, vec, expand_add = project_and_scatter(
        n_ctx, x, query_weight, key_weight, value_weight, block_order, block_sequence, vectors
    )
    o, keep, lse, pairs = attend(order, seqs, q, kv)
    layer_output, sum_tan, entry, tan, vec_feed, stage_a, stage_b, kept = middle(
        n_ctx,
        o,
        x,
        summed,
        tangent,
        (output_weight, from_other(output_weight)),
        (expand_weight, from_other(expand_weight)),
        (shrink_weight, from_other(shrink_weight)),
        expand_add,
        vec,
    )
    land_a, land_b = across(stage_a, 1), across(stage_b, 2)
    dq, dkv, layer_output, sum_tan = attend_back(
        pairs, q, tan, keep, lse, kv, (layer_output, sum_tan)
    )
    post_tangent, feed_sums, last_sums, vecs = finish(
        n_ctx,
        dq,
        dkv,
        kept,
        land_a,
        land_b,
        x,
        entry,
        query_weight,
        key_weight,
        value_weight,
        w_other,
        vec_feed,
    )
    (
        query_slope,
        key_slope,
        value_slope,
        output_slope,
        expand_slope,
        shrink_slope,
        post_tangent,
        query_drift,
        value_drift,
        output_drift,
        attend_stretch,
        attend_nudge,
        shrink_drift,
        middle_stretch,
        middle_nudge,
        final_stretch,
        final_nudge,
        expand_drift,
    ) = unpack_grads(shrink_weight.shape[0], feed_sums, last_sums, post_tangent, vecs)
    return (
        layer_output[None],
        post_tangent[None],
        sum_tan[None],
        query_slope,
        key_slope,
        value_slope,
        output_slope,
        query_drift[0],
        value_drift[0],
        output_drift[0],
        attend_stretch[0],
        attend_nudge[0],
        expand_slope,
        expand_drift[0],
        shrink_slope,
        shrink_drift[0],
        middle_stretch[0],
        middle_nudge[0],
        final_stretch[0],
        final_nudge[0],
    )


def solution(mesh):
    n_ctx, n_fsdp = mesh.shape["ctx"], mesh.shape["fsdp"]
    if n_fsdp == 2 and n_ctx == n_fsdp * H:
        body = functools.partial(head_shards, n_ctx)
    else:
        body = general_shards
    return jax.shard_map(
        body,
        mesh=mesh,
        in_specs=(
            P("fsdp", "ctx", None),
            P("fsdp", "ctx", None),
            P("fsdp", "ctx", None),
            P("fsdp", None),
            P("fsdp", None),
            P(None, "fsdp"),
            P(None, "fsdp"),
            P(None, "fsdp"),
            P("fsdp", None),
            P("fsdp"),
            P("fsdp"),
            P("fsdp"),
            P("fsdp"),
            P("fsdp"),
            P(None, "fsdp"),
            P("fsdp"),
            P("fsdp", None),
            P("fsdp"),
            P("fsdp"),
            P("fsdp"),
            P("fsdp"),
            P("fsdp"),
        ),
        out_specs=(
            P("fsdp", "ctx", None),
            P("fsdp", "ctx", None),
            P("fsdp", "ctx", None),
            P(None, "fsdp"),
            P(None, "fsdp"),
            P(None, "fsdp"),
            P("fsdp", None),
            P("fsdp"),
            P("fsdp"),
            P("fsdp"),
            P("fsdp"),
            P("fsdp"),
            P(None, "fsdp"),
            P("fsdp"),
            P("fsdp", None),
            P("fsdp"),
            P("fsdp"),
            P("fsdp"),
            P("fsdp"),
            P("fsdp"),
        ),
        check_vma=False,
    )
```

```python
import functools

import jax
import jax.numpy as jnp
from jax import lax
from jax.experimental import pallas as pl
from jax.experimental.pallas import tpu as pltpu
from jax.sharding import PartitionSpec as P

D = 512
H = 8
HD = 64
BLK = 256
HALF = BLK // 2
LONG = 8
TOGETHER = 16
MOST = LONG + 1
F32 = jnp.float32
BF16 = jnp.bfloat16
MESH = pl.DeviceIdType.MESH
ROOM = 60 << 20
VMEM = pl.BlockSpec(memory_space=pltpu.VMEM)
SMEM = pl.BlockSpec(memory_space=pltpu.SMEM)
ANY = pl.BlockSpec(memory_space=pltpu.HBM)


norm_eps = 1e-05
masked_value = -1e30
gelu_coeff = 0.7978845608
gelu_cubic = 0.044715


def smooth_gate(values):
    return (
        0.5
        * values
        * (1.0 + jnp.tanh(gelu_coeff * (values + gelu_cubic * values * values * values)))
    )


def layer_norm(inputs, gain_row, shift_row):
    centre = inputs - jnp.mean(inputs, axis=-1, keepdims=True)
    spread = jnp.mean(centre * centre, axis=-1, keepdims=True)
    return centre * lax.rsqrt(spread + norm_eps) * gain_row + shift_row


def product(left_side, right_side):
    return jnp.dot(left_side, right_side, preferred_element_type=jnp.float32)


def cross_rows(left_side, right_side):
    return lax.dot_general(
        left_side, right_side, (((0,), (0,)), ((), ())), preferred_element_type=jnp.float32
    )


def cross_cols(left_side, right_side):
    return lax.dot_general(
        left_side, right_side, (((1,), (1,)), ((), ())), preferred_element_type=jnp.float32
    )


def column_total(values):
    return jnp.sum(values, axis=0, dtype=jnp.float32)


def lookup(table_row, indices):
    places = jnp.arange(table_row.shape[0], dtype=jnp.int32)
    return jnp.sum(jnp.where(indices[:, None] == places[None, :], table_row[None, :], 0), axis=1)


def block_mask(query_blocks, query_seqs, key_blocks, key_seqs):
    same_seq = query_seqs[:, None] == key_seqs[None, :]
    return same_seq & (key_blocks[None, :] <= query_blocks[:, None])


def token_mask(visible):
    return jnp.repeat(jnp.repeat(visible, BLK, axis=0), BLK, axis=1)


def fold_units(carried, members, unit_step):
    unit_count = members[0].shape[0] // BLK
    inner_count = max((divisor for divisor in range(1, 17) if unit_count % divisor == 0))
    outer_count = unit_count // inner_count

    def outer_turn(outer_index, current):

        def inner_turn(inner_index, inner_state):
            offset = (outer_index * inner_count + inner_index) * BLK
            pieces = tuple((lax.dynamic_slice_in_dim(member, offset, BLK, 0) for member in members))
            return unit_step(inner_state, pieces, offset)

        return lax.fori_loop(0, inner_count, inner_turn, current)

    return lax.fori_loop(0, outer_count, outer_turn, carried)


def general_shards(
    post_stream,
    sum_stream,
    cotangent,
    block_order,
    block_sequence,
    query_weight,
    key_weight,
    value_weight,
    output_weight,
    query_bias,
    value_bias,
    output_bias,
    attend_gain,
    attend_shift,
    expand_weight,
    expand_bias,
    shrink_weight,
    shrink_bias,
    middle_gain,
    middle_shift,
    final_gain,
    final_shift,
):
    (
        query_whole,
        key_whole,
        value_whole,
        output_whole,
        query_add,
        value_add,
        output_add,
        gain_one,
        shift_one,
        expand_whole,
        expand_add,
        shrink_whole,
        shrink_add,
        gain_two,
        shift_two,
        gain_last,
        shift_last,
    ) = (
        lax.all_gather(query_weight, "fsdp", axis=1, tiled=True),
        lax.all_gather(key_weight, "fsdp", axis=1, tiled=True),
        lax.all_gather(value_weight, "fsdp", axis=1, tiled=True),
        lax.all_gather(output_weight, "fsdp", axis=0, tiled=True),
        lax.all_gather(query_bias, "fsdp", axis=0, tiled=True),
        lax.all_gather(value_bias, "fsdp", axis=0, tiled=True),
        lax.all_gather(output_bias, "fsdp", axis=0, tiled=True),
        lax.all_gather(attend_gain, "fsdp", axis=0, tiled=True),
        lax.all_gather(attend_shift, "fsdp", axis=0, tiled=True),
        lax.all_gather(expand_weight, "fsdp", axis=1, tiled=True),
        lax.all_gather(expand_bias, "fsdp", axis=0, tiled=True),
        lax.all_gather(shrink_weight, "fsdp", axis=0, tiled=True),
        lax.all_gather(shrink_bias, "fsdp", axis=0, tiled=True),
        lax.all_gather(middle_gain, "fsdp", axis=0, tiled=True),
        lax.all_gather(middle_shift, "fsdp", axis=0, tiled=True),
        lax.all_gather(final_gain, "fsdp", axis=0, tiled=True),
        lax.all_gather(final_shift, "fsdp", axis=0, tiled=True),
    )
    post_rows = post_stream[0]
    summed = sum_stream[0]
    tangent = cotangent[0]
    order_row = block_order[0]
    seq_row = block_sequence[0]
    token_count = post_rows.shape[0]
    score_scale = HD ** (-0.5)
    own_blocks = lax.dynamic_slice_in_dim(
        order_row, lax.axis_index("ctx") * (token_count // BLK), token_count // BLK
    )
    own_seqs = lookup(seq_row, own_blocks)
    post_low = post_rows.astype(jnp.bfloat16)
    queries = (product(post_low, query_whole) + query_add).astype(jnp.bfloat16)
    key_rows = product(post_low, key_whole).astype(jnp.bfloat16)
    value_rows = (product(post_low, value_whole) + value_add).astype(jnp.bfloat16)
    query_heads = queries.reshape(token_count, H, HD)

    def keys_visible(first_row):
        key_block = lax.dynamic_slice_in_dim(order_row, first_row // BLK, 1)
        return block_mask(own_blocks, own_seqs, key_block, lookup(seq_row, key_block))

    def masked_fold(block_step):

        def unit_step(current, pieces, first_row):
            visible = keys_visible(first_row)
            return lax.cond(
                jnp.any(visible),
                lambda inner_state: block_step(inner_state, pieces, visible),
                lambda inner_state: inner_state,
                current,
            )

        def folded(current, pieces, first_row):
            return fold_units(current, pieces, unit_step)

        return folded

    def stats_block(current, pieces, visible):
        row_peaks, masses = current
        key_heads = pieces[0].reshape(BLK, H, HD)
        row_mask = token_mask(visible)[None]
        scores = (
            jnp.einsum("qhd,khd->hqk", query_heads, key_heads, preferred_element_type=jnp.float32)
            * score_scale
        )
        new_peaks = jnp.maximum(
            row_peaks, jnp.max(jnp.where(row_mask, scores, masked_value), axis=2)
        )
        weights = jnp.where(row_mask, jnp.exp(scores - new_peaks[:, :, None]), 0.0)
        return (new_peaks, masses * jnp.exp(row_peaks - new_peaks) + jnp.sum(weights, axis=2))

    stats_fold = masked_fold(stats_block)
    stats_start = (
        jnp.full((H, token_count), masked_value, jnp.float32),
        jnp.zeros((H, token_count), jnp.float32),
    )
    row_peaks, masses = stats_fold(
        stats_start, (lax.all_gather(key_rows, "ctx", axis=0, tiled=True),), jnp.int32(0)
    )
    log_mass = row_peaks + jnp.log(masses)

    def forward_block(current, pieces, visible):
        key_heads = pieces[0].reshape(BLK, H, HD)
        value_heads = pieces[1].reshape(BLK, H, HD)
        row_mask = token_mask(visible)[None]
        scores = (
            jnp.einsum("qhd,khd->hqk", query_heads, key_heads, preferred_element_type=jnp.float32)
            * score_scale
        )
        weights = jnp.where(row_mask, jnp.exp(scores - log_mass[:, :, None]), 0.0).astype(
            jnp.bfloat16
        )
        addition = jnp.einsum(
            "hqk,khd->qhd", weights, value_heads, preferred_element_type=jnp.float32
        )
        return current + addition.reshape(token_count, D)

    forward_fold = masked_fold(forward_block)
    zero_rows = jnp.zeros((token_count, D), jnp.float32)
    attended = forward_fold(
        zero_rows,
        (
            lax.all_gather(key_rows, "ctx", axis=0, tiled=True),
            lax.all_gather(value_rows, "ctx", axis=0, tiled=True),
        ),
        jnp.int32(0),
    )
    mixed_low = attended.astype(jnp.bfloat16)
    branch = product(mixed_low, output_whole) + output_add
    normed_one, first_pull = jax.vjp(
        layer_norm, post_rows + branch, gain_one.astype(jnp.float32), shift_one.astype(jnp.float32)
    )
    stream_one = summed + branch
    normed_low = normed_one.astype(jnp.bfloat16)
    before = product(normed_low, expand_whole) + expand_add
    gated, gate_pull = jax.vjp(smooth_gate, before)
    hidden = gated.astype(jnp.bfloat16)
    feed_out = product(hidden, shrink_whole) + shrink_add
    normed_two, middle_pull = jax.vjp(
        layer_norm,
        normed_one + feed_out,
        gain_two.astype(jnp.float32),
        shift_two.astype(jnp.float32),
    )
    stream_two = stream_one + feed_out
    last_norm, last_pull = jax.vjp(
        layer_norm, stream_two, gain_last.astype(jnp.float32), shift_last.astype(jnp.float32)
    )
    layer_output = normed_two + last_norm
    stream_tan, stretch_last, nudge_last = last_pull(tangent)
    inflow_tan, stretch_two, nudge_two = middle_pull(tangent)
    feed_tan = (stream_tan + inflow_tan).astype(jnp.bfloat16)
    slope_shrink = cross_rows(hidden, feed_tan)
    drift_shrink = column_total(feed_tan)
    before_tan = gate_pull(cross_cols(feed_tan, shrink_whole))[0].astype(jnp.bfloat16)
    slope_expand = cross_rows(normed_low, before_tan)
    drift_expand = column_total(before_tan)
    normed_tan = inflow_tan + cross_cols(before_tan, expand_whole)
    feed_parts = lax.psum(
        (
            slope_expand,
            drift_expand,
            slope_shrink,
            drift_shrink,
            stretch_two,
            nudge_two,
            stretch_last,
            nudge_last,
        ),
        "ctx",
    )
    feed_sums = (
        lax.psum_scatter(feed_parts[0], "fsdp", scatter_dimension=1, tiled=True),
        lax.psum_scatter(feed_parts[1], "fsdp", scatter_dimension=0, tiled=True),
        lax.psum_scatter(feed_parts[2], "fsdp", scatter_dimension=0, tiled=True),
        lax.psum_scatter(feed_parts[3], "fsdp", scatter_dimension=0, tiled=True),
        lax.psum_scatter(feed_parts[4], "fsdp", scatter_dimension=0, tiled=True),
        lax.psum_scatter(feed_parts[5], "fsdp", scatter_dimension=0, tiled=True),
        lax.psum_scatter(feed_parts[6], "fsdp", scatter_dimension=0, tiled=True),
        lax.psum_scatter(feed_parts[7], "fsdp", scatter_dimension=0, tiled=True),
    )
    entry_tan, stretch_one, nudge_one = first_pull(normed_tan)
    branch_tan = (stream_tan + entry_tan).astype(jnp.bfloat16)
    slope_output = cross_rows(mixed_low, branch_tan)
    drift_output = column_total(branch_tan)
    mixed_tan = cross_cols(branch_tan, output_whole).astype(jnp.bfloat16)
    tangent_heads = mixed_tan.reshape(token_count, H, HD)
    deltas = jnp.sum((mixed_tan * attended).reshape(token_count, H, HD), axis=2).T

    def query_block(current, pieces, visible):
        key_heads = pieces[0].reshape(BLK, H, HD)
        value_heads = pieces[1].reshape(BLK, H, HD)
        row_mask = token_mask(visible)[None]
        scores = (
            jnp.einsum("qhd,khd->hqk", query_heads, key_heads, preferred_element_type=jnp.float32)
            * score_scale
        )
        probability = jnp.where(row_mask, jnp.exp(scores - log_mass[:, :, None]), 0.0)
        prob_tan = jnp.einsum(
            "qhd,khd->hqk", tangent_heads, value_heads, preferred_element_type=jnp.float32
        )
        score_tan = (probability * (prob_tan - deltas[:, :, None])).astype(jnp.bfloat16)
        addition = jnp.einsum(
            "hqk,khd->qhd", score_tan, key_heads, preferred_element_type=jnp.float32
        )
        return current + addition.reshape(token_count, D) * score_scale

    query_fold = masked_fold(query_block)
    query_sum = query_fold(
        zero_rows,
        (
            lax.all_gather(key_rows, "ctx", axis=0, tiled=True),
            lax.all_gather(value_rows, "ctx", axis=0, tiled=True),
        ),
        jnp.int32(0),
    )
    gathered_mass, gathered_delta = (
        lax.all_gather(log_mass.T, "ctx", axis=0, tiled=True),
        lax.all_gather(deltas.T, "ctx", axis=0, tiled=True),
    )
    own_keys = key_rows.reshape(token_count, H, HD)
    own_values = value_rows.reshape(token_count, H, HD)

    def owner_block(current, pieces, first_row, visible):
        key_acc, value_acc = current
        part_queries = pieces[0].reshape(BLK, H, HD)
        part_tangent = pieces[1].reshape(BLK, H, HD)
        part_mass = lax.dynamic_slice_in_dim(gathered_mass, first_row, BLK, 0).T
        part_delta = lax.dynamic_slice_in_dim(gathered_delta, first_row, BLK, 0).T
        row_mask = token_mask(visible)[None]
        scores = (
            jnp.einsum("qhd,khd->hqk", part_queries, own_keys, preferred_element_type=jnp.float32)
            * score_scale
        )
        probability = jnp.where(row_mask, jnp.exp(scores - part_mass[:, :, None]), 0.0)
        value_add_rows = jnp.einsum(
            "hqk,qhd->khd",
            probability.astype(jnp.bfloat16),
            part_tangent,
            preferred_element_type=jnp.float32,
        )
        prob_tan = jnp.einsum(
            "qhd,khd->hqk", part_tangent, own_values, preferred_element_type=jnp.float32
        )
        score_tan = (probability * (prob_tan - part_delta[:, :, None])).astype(jnp.bfloat16)
        key_add_rows = jnp.einsum(
            "hqk,qhd->khd", score_tan, part_queries, preferred_element_type=jnp.float32
        )
        return (
            key_acc + key_add_rows.reshape(token_count, D) * score_scale,
            value_acc + value_add_rows.reshape(token_count, D),
        )

    def owner_unit(current, pieces, first_row):
        query_blocks = lax.dynamic_slice_in_dim(order_row, first_row // BLK, 1)
        visible = block_mask(query_blocks, lookup(seq_row, query_blocks), own_blocks, own_seqs)
        return lax.cond(
            jnp.any(visible),
            lambda inner_state: owner_block(inner_state, pieces, first_row, visible),
            lambda inner_state: inner_state,
            current,
        )

    key_sum, value_sum = fold_units(
        (zero_rows, zero_rows),
        (
            lax.all_gather(queries, "ctx", axis=0, tiled=True),
            lax.all_gather(mixed_tan, "ctx", axis=0, tiled=True),
        ),
        owner_unit,
    )
    query_tan = query_sum.astype(jnp.bfloat16)
    key_tan = key_sum.astype(jnp.bfloat16)
    value_tan = value_sum.astype(jnp.bfloat16)
    slope_query = cross_rows(post_low, query_tan)
    slope_key = cross_rows(post_low, key_tan)
    slope_value = cross_rows(post_low, value_tan)
    drift_query = column_total(query_tan)
    drift_value = column_total(value_tan)
    post_tangent = (
        entry_tan
        + cross_cols(query_tan, query_whole)
        + cross_cols(key_tan, key_whole)
        + cross_cols(value_tan, value_whole)
    )
    heads_parts = lax.psum(
        (
            slope_query,
            slope_key,
            slope_value,
            slope_output,
            drift_query,
            drift_value,
            drift_output,
            stretch_one,
            nudge_one,
        ),
        "ctx",
    )
    heads_sums = (
        lax.psum_scatter(heads_parts[0], "fsdp", scatter_dimension=1, tiled=True),
        lax.psum_scatter(heads_parts[1], "fsdp", scatter_dimension=1, tiled=True),
        lax.psum_scatter(heads_parts[2], "fsdp", scatter_dimension=1, tiled=True),
        lax.psum_scatter(heads_parts[3], "fsdp", scatter_dimension=0, tiled=True),
        lax.psum_scatter(heads_parts[4], "fsdp", scatter_dimension=0, tiled=True),
        lax.psum_scatter(heads_parts[5], "fsdp", scatter_dimension=0, tiled=True),
        lax.psum_scatter(heads_parts[6], "fsdp", scatter_dimension=0, tiled=True),
        lax.psum_scatter(heads_parts[7], "fsdp", scatter_dimension=0, tiled=True),
        lax.psum_scatter(heads_parts[8], "fsdp", scatter_dimension=0, tiled=True),
    )
    return (
        layer_output[None],
        post_tangent[None],
        stream_tan[None],
        heads_sums[0],
        heads_sums[1],
        heads_sums[2],
        heads_sums[3],
        heads_sums[4],
        heads_sums[5],
        heads_sums[6],
        heads_sums[7],
        heads_sums[8],
        feed_sums[0],
        feed_sums[1],
        feed_sums[2],
        feed_sums[3],
        feed_sums[4],
        feed_sums[5],
        feed_sums[6],
        feed_sums[7],
    )


def low_lanes(values):
    return lax.broadcasted_iota(jnp.int32, values.shape, 1) < HD


def swap_lanes(values):
    return pltpu.roll(values, HD, 1)


def low_pair(first, second):
    return jnp.where(low_lanes(first), first, swap_lanes(second))


def high_pair(first, second):
    return jnp.where(low_lanes(first), swap_lanes(first), second)


def side_pair(side, first, second):
    return low_pair(first, second) if side == 0 else high_pair(first, second)


def dot_nn(left, right):
    return jnp.dot(left, right, preferred_element_type=F32)


def dot_nt(left, right):
    return lax.dot_general(left, right, (((1,), (1,)), ((), ())), preferred_element_type=F32)


def dot_tn(left, right):
    return lax.dot_general(left, right, (((0,), (0,)), ((), ())), preferred_element_type=F32)


class Place:
    def __init__(self):
        self.c = lax.axis_index("ctx")
        self.f = lax.axis_index("fsdp")
        self.group = self.c // H
        self.head = self.c % H
        self.inside = jnp.where(self.group == self.f, 1, 0)

    def is_me(self, tc, tf):
        return jnp.logical_and(self.c == tc, self.f == tf)

    def signal(self, barrier, tc, tf):
        @pl.when(jnp.logical_not(self.is_me(tc, tf)))
        def _():
            pl.semaphore_signal(barrier, 1, device_id=(tc, tf), device_id_type=MESH)

    def turn(self, i, n):
        return (self.c + 5 * i) % n

    def greet_sources(self, n_ctx, partner):
        barrier = pltpu.get_barrier_semaphore()
        for tc in range(n_ctx):
            self.signal(barrier, tc, self.group)
        if partner:
            pl.semaphore_signal(
                barrier, 1, device_id=(self.c, 1 - self.f), device_id_type=MESH
            )
        pl.semaphore_wait(barrier, 2 * H + (1 if partner else 0) - self.inside)

    def greet_owners(self, n_ctx, partner, more=0):
        barrier = pltpu.get_barrier_semaphore()
        for head in range(H):
            for core in range(2):
                self.signal(barrier, self.f * H + head, core)
        if partner:
            pl.semaphore_signal(
                barrier, 1, device_id=(self.c, 1 - self.f), device_id_type=MESH
            )
        pl.semaphore_wait(barrier, n_ctx + (1 if partner else 0) + more - self.inside)

    def send(self, src, dst, send_sem, recv_sem, tc, tf):
        me = self.is_me(tc, tf)

        @pl.when(me)
        def _():
            pltpu.make_async_copy(src, dst, recv_sem).start()

        @pl.when(jnp.logical_not(me))
        def _():
            self.remote(src, dst, send_sem, recv_sem, tc, tf).start()

    def remote(self, src, dst, send_sem, recv_sem, tc, tf):
        return pltpu.make_async_remote_copy(
            src_ref=src,
            dst_ref=dst,
            send_sem=send_sem,
            recv_sem=recv_sem,
            device_id=(tc, tf),
            device_id_type=MESH,
        )

    def wait_sent(self, src, dst, send_sem, recv_sem, tc, tf):
        @pl.when(jnp.logical_not(self.is_me(tc, tf)))
        def _():
            self.remote(src, dst, send_sem, recv_sem, tc, tf).wait_send()


VECTORS = 10


def project_kernel(
    n_ctx,
    x_hbm,
    wq_hbm,
    wk_hbm,
    wv_hbm,
    order_hbm,
    seq_hbm,
    *rest,
):
    vector_hbm, rest = rest[: VECTORS + 1], rest[VECTORS + 1 :]
    vector_in, rest = rest[-VECTORS - 1 :], rest[: -VECTORS - 1]
    (
        q_out,
        kv_out,
        w_other,
        order_out,
        seq_out,
        vec_out,
        expand_out,
        x_in,
        w_own,
        w_in,
        bias_own,
        bias_in,
        order_own,
        seq_own,
        order_in,
        seq_in,
        q_send,
        kv_send,
        load_sem,
        w_ss,
        w_rs,
        q_ss,
        q_rs,
        kv_ss,
        kv_rs,
        relay_ss,
        relay_rs,
    ) = rest
    at = Place()
    other = 1 - at.f
    loads = [
        pltpu.make_async_copy(src, dst, load_sem.at[i])
        for i, (src, dst) in enumerate(
            (
                (x_hbm, x_in),
                (wq_hbm, w_own.at[0]),
                (wk_hbm, w_own.at[1]),
                (wv_hbm, w_own.at[2]),
                (order_hbm, order_own),
                (seq_hbm, seq_own),
                *zip(vector_hbm, vector_in),
            )
        )
    ]
    for load in loads:
        load.start()
    at.greet_sources(n_ctx, True)
    wide = bias_own.shape[1]
    swaps = [
        at.remote(src, dst, w_ss.at[i], w_rs.at[i], at.c, other)
        for i, (src, dst) in enumerate(
            (
                (wq_hbm, w_in.at[0]),
                (wk_hbm, w_in.at[1]),
                (wv_hbm, w_in.at[2]),
                (order_hbm, order_in),
                (seq_hbm, seq_in),
                (bias_own, bias_in),
            )
        )
    ]
    for swap in swaps[:-1]:
        swap.start()
    for load in loads:
        load.wait()
    for row, ref in enumerate(vector_in[:VECTORS]):
        bias_own[row : row + 1, :] = ref[...].astype(F32).reshape(1, wide)
    for part in range(vector_in[VECTORS].shape[0] // wide):
        piece = vector_in[VECTORS][part * wide : part * wide + wide]
        bias_own[VECTORS + part : VECTORS + part + 1, :] = piece.astype(F32).reshape(1, wide)
    swaps[-1].start()

    def moves(half):
        for i in range(H // 2):
            head = half * (H // 2) + at.turn(i, H // 2)
            for core in range(2):
                slot = head * 2 + core
                yield (
                    kv_send.at[head, pl.ds(core * BLK, BLK)],
                    kv_out.at[2 * at.c + core],
                    kv_ss.at[slot],
                    kv_rs.at[at.c],
                    at.f * H + head,
                    core,
                )
                yield (
                    q_send.at[head, core],
                    q_out.at[at.c],
                    q_ss.at[slot],
                    q_rs.at[at.c],
                    at.f * H + head,
                    core,
                )

    def one_half(half, wq, wk, wv, bias):
        low = x_in[...].astype(BF16)
        q = dot_nn(low, wq[...]) + bias[0:1, :]
        k = dot_nn(low, wk[...])
        v = dot_nn(low, wv[...]) + bias[1:2, :]
        for pair in range(2):
            columns = slice(pair * 128, pair * 128 + 128)
            for side in range(2):
                head = half * (H // 2) + 2 * pair + side
                kv_send[head] = side_pair(side, k[:, columns], v[:, columns]).astype(BF16)
                for core in range(2):
                    rows = slice(core * HALF, core * HALF + HALF)
                    late = slice(BLK + core * HALF, BLK + core * HALF + HALF)
                    q_send[head, core] = side_pair(side, q[rows, columns], q[late, columns]).astype(
                        BF16
                    )
        for move in moves(half):
            at.send(*move)

    one_half(at.f, w_own.at[0], w_own.at[1], w_own.at[2], bias_own)
    for swap in swaps:
        swap.wait()
    one_half(other, w_in.at[0], w_in.at[1], w_in.at[2], bias_in)
    w_other[...] = w_in[...]
    inside = at.inside == 1
    order_out[...] = jnp.where(inside, order_own[...], order_in[...])
    seq_out[...] = jnp.where(inside, seq_own[...], seq_in[...])
    vec_out[...] = whole_rows(bias_own[...], bias_in[...], at.f == 0)
    for row, source in enumerate((bias_own, bias_in)):
        for part in range(expand_out.shape[1] // wide):
            at_row = VECTORS + part
            expand_out[row : row + 1, part * wide : part * wide + wide] = source[
                at_row : at_row + 1, :
            ]

    def relay(source):
        mine = kv_out.at[2 * source + at.f]
        return at.remote(mine, mine, relay_ss.at[source], relay_rs.at[source], at.c, other)

    def relay_in(source):
        theirs = kv_out.at[2 * source + other]
        return at.remote(theirs, theirs, relay_ss.at[source], relay_rs.at[source], at.c, other)

    for source in range(n_ctx):
        arrived = kv_out.at[2 * source + at.f]
        at.remote(arrived, arrived, kv_ss.at[0], kv_rs.at[source], at.c, other).wait_recv()
        relay(source).start()
    for source in range(n_ctx):
        arrived = q_out.at[source]
        at.remote(arrived, arrived, q_ss.at[0], q_rs.at[source], at.c, other).wait_recv()
        relay_in(source).wait_recv()
    for source in range(n_ctx):
        relay(source).wait_send()
    for half in (at.f, other):
        for move in moves(half):
            at.wait_sent(*move)


def project_and_scatter(n_ctx, x, wq, wk, wv, order, seqs, vectors):
    wide = wq.shape[1]
    blocks = order.shape[1]
    units = vectors[VECTORS].shape[0]
    bias_rows = VECTORS + units // wide
    return pl.pallas_call(
        functools.partial(project_kernel, n_ctx),
        out_shape=(
            jax.ShapeDtypeStruct((n_ctx, HALF, 128), BF16),
            jax.ShapeDtypeStruct((2 * n_ctx, BLK, 128), BF16),
            jax.ShapeDtypeStruct((3, D, wide), BF16),
            jax.ShapeDtypeStruct((1, blocks), jnp.int32),
            jax.ShapeDtypeStruct((1, blocks), jnp.int32),
            jax.ShapeDtypeStruct((bias_rows, D), F32),
            jax.ShapeDtypeStruct((2, units), F32),
        ),
        in_specs=[ANY] * (7 + VECTORS),
        out_specs=(ANY, ANY) + (VMEM,) * 5,
        scratch_shapes=[
            pltpu.VMEM((2 * BLK, D), F32),
            pltpu.VMEM((3, D, wide), BF16),
            pltpu.VMEM((3, D, wide), BF16),
            pltpu.VMEM((bias_rows, wide), F32),
            pltpu.VMEM((bias_rows, wide), F32),
            pltpu.VMEM((1, blocks), jnp.int32),
            pltpu.VMEM((1, blocks), jnp.int32),
            pltpu.VMEM((1, blocks), jnp.int32),
            pltpu.VMEM((1, blocks), jnp.int32),
            pltpu.VMEM((H, 2, HALF, 128), BF16),
            pltpu.VMEM((H, 2 * BLK, 128), BF16),
            pltpu.SemaphoreType.DMA((7 + VECTORS,)),
            pltpu.SemaphoreType.DMA((6,)),
            pltpu.SemaphoreType.DMA((6,)),
            pltpu.SemaphoreType.DMA((2 * H,)),
            pltpu.SemaphoreType.DMA((n_ctx,)),
            pltpu.SemaphoreType.DMA((2 * H,)),
            pltpu.SemaphoreType.DMA((n_ctx,)),
            pltpu.SemaphoreType.DMA((n_ctx,)),
            pltpu.SemaphoreType.DMA((n_ctx,)),
        ]
        + [pltpu.VMEM(vector.shape, BF16) for vector in vectors],
        compiler_params=pltpu.CompilerParams(
            collective_id=0, has_side_effects=True, vmem_limit_bytes=ROOM
        ),
        name="project_scatter",
    )(x, wq, wk, wv, order, seqs, *vectors)


def forward_kernel(
    blocks,
    order_ref,
    seq_ref,
    q_ref,
    kv_ref,
    o_ref,
    keep_ref,
    lse_ref,
    pairs_ref,
    place,
    q_low,
    peaks,
    masses,
    total,
    scores,
):
    def place_block(slot, _):
        place[order_ref[0, slot]] = slot
        return 0

    lax.fori_loop(0, blocks, place_block, 0)

    count = jnp.int32(0)
    for gap in range(1, LONG):
        for late in range(gap, blocks):
            pairs_ref[0, count] = place[late]
            pairs_ref[1, count] = place[late - gap]
            count = count + jnp.where(seq_ref[0, late] == seq_ref[0, late - gap], 1, 0)
    for spare in range(TOGETHER):
        pairs_ref[0, count + spare] = blocks
        pairs_ref[1, count + spare] = 0
    turns = (count + TOGETHER - 1) // TOGETHER
    pairs_ref[2, 0] = turns

    def unpack(step, _):
        for part in range(4):
            source = step * 4 + part
            packed = q_ref[source].astype(F32) * (HD**-0.5)
            low = low_lanes(packed)
            q_low[2 * source] = jnp.where(low, packed, 0.0).astype(BF16)
            q_low[2 * source + 1] = jnp.where(low, swap_lanes(packed), 0.0).astype(BF16)
        return 0

    lax.fori_loop(0, blocks // 8, unpack, 0)
    q_low[blocks] = jnp.zeros((HALF, 128), BF16)

    peaks[blocks] = jnp.zeros((HALF, 128), F32)
    masses[blocks] = jnp.zeros((HALF, 128), F32)
    total[blocks] = jnp.zeros((HALF, 128), F32)
    lse_ref[blocks] = jnp.zeros((HALF, 128), F32)

    def own_slots(step):
        return [(step * TOGETHER + part,) * 2 for part in range(TOGETHER)]

    def pair_slots(step):
        return [
            (pairs_ref[0, step * TOGETHER + part], pairs_ref[1, step * TOGETHER + part])
            for part in range(TOGETHER)
        ]

    def score(slots, base):
        results = []
        for part, (q_slot, k_slot) in enumerate(slots):
            result = dot_nt(q_low[q_slot], kv_ref[k_slot])
            scores[base + part] = result
            results.append(jnp.maximum(result[:, :128], result[:, 128:]))
        return results

    def score_own(step, _):
        slots = own_slots(step)
        for (q_slot, _), result in zip(slots, score(slots, step * TOGETHER)):
            peaks[q_slot] = result
        return 0

    def score_pairs(step, _):
        slots = pair_slots(step)
        for (q_slot, _), result in zip(slots, score(slots, blocks + step * TOGETHER)):
            peaks[q_slot] = jnp.maximum(peaks[q_slot], result)
        return 0

    lax.fori_loop(0, blocks // TOGETHER, score_own, 0)
    lax.fori_loop(0, turns, score_pairs, 0)

    def level(step, _):
        for part in range(4):
            slot = step * 4 + part
            peaks[slot] = jnp.broadcast_to(
                jnp.max(peaks[slot], axis=1, keepdims=True), (HALF, 128)
            )
        return 0

    lax.fori_loop(0, blocks // 4, level, 0)

    def weigh(slots, base):
        results = []
        for part, (q_slot, k_slot) in enumerate(slots):
            peak = peaks[q_slot]
            left = jnp.exp(scores[base + part, :, :128] - peak)
            right = jnp.exp(scores[base + part, :, 128:] - peak)
            weights = jnp.concatenate([left, right], axis=1).astype(BF16)
            results.append((left + right, dot_nn(weights, kv_ref[k_slot])))
        return results

    def weigh_own(step, _):
        slots = own_slots(step)
        for (q_slot, _), (mass, result) in zip(slots, weigh(slots, step * TOGETHER)):
            masses[q_slot] = mass
            total[q_slot] = result
        return 0

    def weigh_pairs(step, _):
        slots = pair_slots(step)
        for (q_slot, _), (mass, result) in zip(slots, weigh(slots, blocks + step * TOGETHER)):
            masses[q_slot] = masses[q_slot] + mass
            total[q_slot] = total[q_slot] + result
        return 0

    lax.fori_loop(0, blocks // TOGETHER, weigh_own, 0)
    lax.fori_loop(0, turns, weigh_pairs, 0)

    def finish(step, _):
        for part in range(4):
            source = step * 4 + part
            for side in range(2):
                slot = 2 * source + side
                mass = jnp.broadcast_to(
                    jnp.sum(masses[slot], axis=1, keepdims=True), (HALF, 128)
                )
                result = total[slot] / mass
                lse_ref[slot] = peaks[slot] + jnp.log(mass)
                packed = high_pair(result[: HALF // 2], result[HALF // 2 :])
                keep_ref[source, side] = packed
                o_ref[source, side] = packed.astype(BF16)
        return 0

    lax.fori_loop(0, blocks // 8, finish, 0)


def pair_room(blocks):
    return blocks * MOST // 2 + 2 * TOGETHER


def attend(order, seqs, q, kv):
    blocks = kv.shape[0]
    room = pair_room(blocks)
    return pl.pallas_call(
        functools.partial(forward_kernel, blocks),
        out_shape=(
            jax.ShapeDtypeStruct((blocks // 2, 2, HALF // 2, 128), BF16),
            jax.ShapeDtypeStruct((blocks // 2, 2, HALF // 2, 128), F32),
            jax.ShapeDtypeStruct((blocks + 1, HALF, 128), F32),
            jax.ShapeDtypeStruct((3, room), jnp.int32),
        ),
        in_specs=[SMEM, SMEM, VMEM, VMEM],
        out_specs=(VMEM, VMEM, VMEM, SMEM),
        scratch_shapes=[
            pltpu.SMEM((blocks,), jnp.int32),
            pltpu.VMEM((blocks + 1, HALF, 128), BF16),
            pltpu.VMEM((blocks + 1, HALF, 128), F32),
            pltpu.VMEM((blocks + 1, HALF, 128), F32),
            pltpu.VMEM((blocks + 1, HALF, 128), F32),
            pltpu.VMEM((room, HALF, BLK), F32),
        ],
        compiler_params=pltpu.CompilerParams(vmem_limit_bytes=ROOM),
        name="attend",
    )(order, seqs, q, kv)


def backward_kernel(
    blocks,
    pairs_ref,
    q_ref,
    tan_ref,
    keep_ref,
    lse_ref,
    kv_ref,
    pass_a,
    pass_b,
    dq_ref,
    dkv_sum,
    out_a,
    out_b,
    both,
    turned,
    deltas,
    dq_sum,
    held,
    pass_sem,
):
    fetches = [
        pltpu.make_async_copy(src, held.at[i], pass_sem.at[i])
        for i, src in enumerate((pass_a, pass_b))
    ]
    passes = [
        pltpu.make_async_copy(held.at[i], dst, pass_sem.at[2 + i])
        for i, dst in enumerate((out_a, out_b))
    ]
    for fetch in fetches:
        fetch.start()

    def unpack(step, _):
        for part in range(4):
            source = step * 4 + part
            packed = q_ref[source].astype(F32) * (HD**-0.5)
            low = low_lanes(packed)
            for side in range(2):
                slot = 2 * source + side
                q = packed if side == 0 else swap_lanes(packed)
                both[slot, 0:HALF] = jnp.where(low, q, 0.0).astype(BF16)
                tangent = tan_ref[source, side].astype(F32)
                first = low_lanes(tangent)
                both[slot, HALF : HALF + HALF // 2] = jnp.where(
                    first, 0.0, swap_lanes(tangent)
                ).astype(BF16)
                both[slot, HALF + HALF // 2 : BLK] = jnp.where(first, 0.0, tangent).astype(BF16)
                turned[slot] = jnp.transpose(both[slot])
                product = tangent * keep_ref[source, side]
                delta = jnp.concatenate(
                    [
                        jnp.sum(jnp.where(first, product, 0.0), axis=1, keepdims=True),
                        jnp.sum(jnp.where(first, 0.0, product), axis=1, keepdims=True),
                    ],
                    axis=0,
                )
                deltas[slot] = jnp.broadcast_to(delta, (HALF, 128))
        return 0

    lax.fori_loop(0, blocks // 8, unpack, 0)
    both[blocks] = jnp.zeros((BLK, 128), BF16)
    turned[blocks] = jnp.zeros((128, BLK), BF16)
    deltas[blocks] = jnp.zeros((HALF, 128), F32)
    dq_sum[blocks] = jnp.zeros((HALF, 128), F32)

    def one_pair(q_slot, k_slot):
        kv = kv_ref[k_slot]
        products = dot_nt(both[q_slot], kv)
        mass, delta = lse_ref[q_slot], deltas[q_slot]
        weights = jnp.exp(products[:HALF] - jnp.concatenate([mass, mass], axis=1))
        score_tan = weights * (products[HALF:] - jnp.concatenate([delta, delta], axis=1))
        score_tan = score_tan.astype(BF16)
        sides = jnp.concatenate([score_tan, weights.astype(BF16)], axis=0)
        return dot_nn(turned[q_slot], sides), dot_nn(score_tan, kv)

    def own_turn(step, _):
        slots = [step * TOGETHER + part for part in range(TOGETHER)]
        results = [one_pair(slot, slot) for slot in slots]
        for slot, (dkv, dq) in zip(slots, results):
            dkv_sum[slot] = dkv
            dq_sum[slot] = dq
        return 0

    def pair_turn(step, _):
        slots = [
            (pairs_ref[0, step * TOGETHER + part], pairs_ref[1, step * TOGETHER + part])
            for part in range(TOGETHER)
        ]
        results = [one_pair(*slot) for slot in slots]
        for (q_slot, k_slot), (dkv, dq) in zip(slots, results):
            dkv_sum[k_slot] = dkv_sum[k_slot] + dkv
            dq_sum[q_slot] = dq_sum[q_slot] + dq
        return 0

    lax.fori_loop(0, blocks // TOGETHER, own_turn, 0)
    for fetch, move in zip(fetches, passes):
        fetch.wait()
        move.start()
    lax.fori_loop(0, pairs_ref[2, 0], pair_turn, 0)

    def finish_rows(step, _):
        for part in range(4):
            source = step * 4 + part
            packed = low_pair(dq_sum[2 * source], dq_sum[2 * source + 1]) * (HD**-0.5)
            dq_ref[source] = packed.astype(BF16)
        return 0

    lax.fori_loop(0, blocks // 8, finish_rows, 0)
    for move in passes:
        move.wait()


def attend_back(pairs, q, tangent, keep, lse, kv, passed):
    blocks = kv.shape[0]
    return pl.pallas_call(
        functools.partial(backward_kernel, blocks),
        out_shape=(
            jax.ShapeDtypeStruct((blocks // 2, HALF, 128), BF16),
            jax.ShapeDtypeStruct((blocks, 128, BLK), F32),
            jax.ShapeDtypeStruct(passed[0].shape, F32),
            jax.ShapeDtypeStruct(passed[1].shape, F32),
        ),
        in_specs=[SMEM, VMEM, VMEM, VMEM, VMEM, VMEM, ANY, ANY],
        out_specs=(VMEM, VMEM, ANY, ANY),
        scratch_shapes=[
            pltpu.VMEM((blocks + 1, BLK, 128), BF16),
            pltpu.VMEM((blocks + 1, 128, BLK), BF16),
            pltpu.VMEM((blocks + 1, HALF, 128), F32),
            pltpu.VMEM((blocks + 1, HALF, 128), F32),
            pltpu.VMEM((2,) + passed[0].shape, F32),
            pltpu.SemaphoreType.DMA((4,)),
        ],
        compiler_params=pltpu.CompilerParams(vmem_limit_bytes=ROOM),
        name="attend_back",
    )(pairs, q, tangent, keep, lse, kv, *passed)


def pieces_of(start, size, body):
    piece = max(n for n in range(16, 97, 16) if size % n == 0)
    lax.fori_loop(
        0,
        size // piece,
        lambda i, _: (body(i * piece, span(start + i * piece, piece), piece), 0)[1],
        0,
    )


def span(start, size):
    return pl.ds(pl.multiple_of(start, 16), size)


def step_of(c, stride):
    bit = (c // stride) % 2
    return bit, c + stride * (1 - 2 * bit)


REGIONS = 4


def columns_of(region):
    wide = D // (REGIONS // 2)
    return slice(region // 2 * wide, region // 2 * wide + wide)


class Ladder:
    def __init__(self, at, plans, starts, size, acc, stage, landing, out, sems, bases=(0, 0)):
        self.bases = bases
        self.at, self.acc, self.stage, self.landing, self.out = at, acc, stage, landing, out
        self.down_ss, self.down_rs, self.up_ss, self.up_rs = sems
        self.ranges = []
        for region in range(REGIONS):
            plan, start = plans[region % 2], starts[region % 2]
            listed, rows = [], size
            for bit, peer in plan[:-1]:
                rows = rows // 2
                listed.append((start + bit * rows, start + (1 - bit) * rows, rows, peer))
                start = start + bit * rows
            listed.append((start, start, rows, plan[-1][1]))
            self.ranges.append(listed)
        self.last = len(plans[0]) - 1

    def slot(self, region, step):
        return region * (self.last + 1) + step

    def down(self, region, step, sent):
        kept, given, size, peer = self.ranges[region][step]
        where, slot = span(given if sent else kept, size), self.slot(region, step)
        columns = columns_of(region)
        return self.at.remote(
            self.stage[region % 2].at[where, columns],
            self.landing[region % 2][step].at[where, columns],
            self.down_ss.at[slot],
            self.down_rs.at[slot],
            peer,
            self.at.f,
        )

    def up(self, region, step, sent):
        kept, given, size, peer = self.ranges[region][step]
        start = self.bases[region % 2] + (kept if sent else given)
        columns = columns_of(region)
        where, slot = span(start, size), self.slot(region, step)
        return self.at.remote(
            self.out.at[where, columns],
            self.out.at[where, columns],
            self.up_ss.at[slot],
            self.up_rs.at[slot],
            peer,
            self.at.f,
        )

    def join(self, region, start, size, arrived, target):
        columns, acc = columns_of(region), self.acc[region % 2]

        def body(offset, where, _):
            total = acc[where, columns] + arrived[where, columns].astype(F32)
            target[where, columns] = total.astype(target.dtype)

        pieces_of(start, size, body)

    def give(self, region, step, arrived):
        kept, given, size, _ = self.ranges[region][step]
        self.join(region, given, size, arrived, self.stage[region % 2])
        self.down(region, step, True).start()
        if step < self.last:
            self.join(region, kept, size, arrived, self.acc[region % 2])

    def settle(self, region):
        kept, _, size, _ = self.ranges[region][self.last]
        arrived = self.landing[region % 2][self.last]
        columns, stage = columns_of(region), self.stage[region % 2]

        def body(offset, where, rows):
            total = stage[where, columns].astype(F32) + arrived[where, columns].astype(F32)
            row = span(self.bases[region % 2] + kept + offset, rows)
            self.out[row, columns] = total.astype(BF16)

        self.down(region, self.last, False).wait_recv()
        pieces_of(kept, size, body)
        self.up(region, self.last - 1, True).start()

    def wait_sent(self):
        for region in range(REGIONS):
            for step in range(self.last + 1):
                self.down(region, step, True).wait_send()
            for step in range(self.last):
                self.up(region, step, True).wait_send()


COLS = 512


def whole_rows(own, other, first):
    return jnp.where(
        first,
        jnp.concatenate([own, other], axis=1),
        jnp.concatenate([other, own], axis=1),
    )


def row_mean(values):
    return jnp.mean(values, axis=1, keepdims=True)


def normalize(values):
    centre = values - row_mean(values)
    scale = lax.rsqrt(row_mean(centre * centre) + norm_eps)
    return centre * scale, scale


def norm_back(tangent, normed, scale, gain):
    pushed = tangent * gain
    return scale * (pushed - row_mean(pushed) - normed * row_mean(pushed * normed))


def column_sum(values):
    return jnp.sum(values, axis=0, keepdims=True)


def feed_slopes(kind, target, mixed, low_turned, hidden, before_tan, feed_tan, branch_tan):
    unit_count = hidden.shape[2] // COLS

    def chunk_slopes(chunk, _):
        columns = pl.ds(pl.multiple_of(chunk * COLS, COLS), COLS)
        target[columns, :] = dot_tn(hidden[kind, :, columns], feed_tan[...]).astype(target.dtype)
        below = pl.ds(pl.multiple_of((unit_count + chunk) * COLS, COLS), COLS)
        target[below, :] = dot_nn(low_turned[...], before_tan[kind, :, columns]).astype(
            target.dtype
        )
        return 0

    lax.fori_loop(0, unit_count, chunk_slopes, 0)
    start = 2 * unit_count * COLS
    target[start : start + D // 2, :] = dot_tn(mixed[kind], branch_tan[...]).astype(target.dtype)


def middle_kernel(
    n_ctx,
    o_hbm, x_hbm, sum_hbm, cot_hbm, wo_a, wo_b, we_a, we_b, ws_a, ws_b, be_ref, vec_in,
    out_hbm, sum_tan_hbm, entry_hbm, tan_out, vec_ref, stage_a, stage_b, keep_ref,
    o_in, x_ref, sum_ref, cot_ref, wo, we, ws, out_ref, sum_tan_ref, entry_ref,
    mixed, low, hidden, before_tan, feed_tan, branch_tan, slope, mixed_tan, tan_send,
    own_grads, send_grads, first_in, low_turned,
    load_sem, store_sem, o_ss, o_rs, tan_ss, tan_rs, core_ss, core_rs,
):
    at = Place()
    f = at.f
    other = 1 - f
    halves = (f, other)
    piece = HALF // 2
    loads = [
        pltpu.make_async_copy(src, dst, load_sem.at[i])
        for i, (src, dst) in enumerate(
            (
                (x_hbm, x_ref),
                (wo_a, wo.at[0]),
                (wo_b, wo.at[1]),
                (we_a, we.at[0]),
                (we_b, we.at[1]),
                (ws_a, ws.at[0]),
                (ws_b, ws.at[1]),
                (sum_hbm, sum_ref),
                (cot_hbm, cot_ref),
            )
        )
    ]
    for load in loads:
        load.start()
    barrier = pltpu.get_barrier_semaphore()
    for target in range(n_ctx):
        at.signal(barrier, target, at.group)
    at.greet_owners(n_ctx, True, 2 * H - at.inside)

    def o_move(target, side):
        return (
            o_hbm.at[target, side],
            o_in.at[side, at.head, f],
            o_ss.at[2 * target + side],
            o_rs.at[side * 2 * H + at.head * 2 + f],
            target,
            at.group,
        )

    def tan_move(side, head, core):
        return (
            tan_send.at[side, head, core],
            tan_out.at[at.c, side],
            tan_ss.at[side * 2 * H + head * 2 + core],
            tan_rs.at[at.c * 2 + side],
            f * H + head,
            core,
        )

    for side in range(2):
        for i in range(n_ctx):
            at.send(*o_move(at.turn(i, n_ctx), side))
    vec_ref[...] = jnp.zeros_like(vec_ref)
    vectors = vec_in[...]
    (out_bias, gain_one, shift_one, shrink_bias, gain_two, shift_two, gain_last, shift_last) = (
        vectors[i : i + 1] for i in range(2, 10)
    )
    be = (be_ref.at[0:1], be_ref.at[1:2])
    for load in loads:
        load.wait()

    def stores(step):
        rows = pl.ds(pl.multiple_of(step * BLK, BLK), BLK)
        return [
            pltpu.make_async_copy(src.at[rows], dst.at[rows], store_sem.at[3 * step + i])
            for i, (src, dst) in enumerate(
                ((out_ref, out_hbm), (sum_tan_ref, sum_tan_hbm), (entry_ref, entry_hbm))
            )
        ]

    def tile(step, _):
        first_row = pl.multiple_of(step * BLK, BLK)
        rows = pl.ds(first_row, BLK)
        for head in range(H):
            for core in range(2):
                arrived = o_in.at[step, head, core]
                at.remote(
                    arrived, arrived, o_ss.at[0], o_rs.at[step * 2 * H + head * 2 + core],
                    at.c, other,
                ).wait_recv()
        for kind in range(2):
            for pair in range(2):
                head = halves[kind] * (H // 2) + 2 * pair
                columns = slice(pair * 128, pair * 128 + 128)
                for core in range(2):
                    early = o_in[step, head, core].astype(F32)
                    late = o_in[step, head + 1, core].astype(F32)
                    for part in range(2):
                        start = pl.multiple_of(first_row + core * HALF + part * piece, piece)
                        mixed[kind, pl.ds(start, piece), columns] = side_pair(
                            part, early, late
                        ).astype(BF16)
        branch = dot_nn(mixed[0, rows, :], wo[0]) + dot_nn(mixed[1, rows, :], wo[1]) + out_bias
        n_one, scale_one = normalize(x_ref[rows, :] + branch)
        normed_one = n_one * gain_one + shift_one
        stream_one = sum_ref[rows, :] + branch
        normed_low = normed_one.astype(BF16)
        low[rows, :] = normed_low
        feed = jnp.zeros((BLK, D), F32)
        for kind in range(2):

            def expand(chunk, carried):
                columns = slice(chunk * COLS, chunk * COLS + COLS)
                v = dot_nn(normed_low, we[kind, :, columns]) + be[kind][:, columns]
                square = v * v
                t = jnp.tanh(gelu_coeff * (v + gelu_cubic * square * v))
                half_up = 0.5 + 0.5 * t
                hidden_part = (v * half_up).astype(BF16)
                hidden[kind, rows, columns] = hidden_part
                slope[kind, :, columns] = half_up + v * half_up * (1.0 - t) * (
                    gelu_coeff + (3.0 * gelu_coeff * gelu_cubic) * square
                )
                return carried + dot_nn(hidden_part, ws[kind, columns, :])

            for chunk in range(ws.shape[1] // COLS):
                feed = expand(chunk, feed)
        feed_out = feed + shrink_bias
        n_two, scale_two = normalize(normed_one + feed_out)
        n_last, scale_last = normalize(stream_one + feed_out)
        out_ref[rows, :] = (n_two * gain_two + shift_two) + (n_last * gain_last + shift_last)
        u = cot_ref[rows, :]
        nudge = column_sum(u)
        sum_tan = norm_back(u, n_last, scale_last, gain_last)
        inflow = norm_back(u, n_two, scale_two, gain_two)
        sum_tan_ref[rows, :] = sum_tan
        feed_low = (sum_tan + inflow).astype(BF16)
        feed_tan[rows, :] = feed_low
        vec_ref[0:1, :] += column_sum(feed_low.astype(F32))
        vec_ref[1:2, :] += column_sum(u * n_two)
        vec_ref[2:3, :] += nudge
        vec_ref[3:4, :] += column_sum(u * n_last)
        vec_ref[4:5, :] += nudge
        normed_tan = inflow
        for kind in range(2):

            def expand_back(chunk, carried):
                columns = slice(chunk * COLS, chunk * COLS + COLS)
                pushed = dot_nt(feed_low, ws[kind, columns, :])
                tan_part = (pushed * slope[kind, :, columns]).astype(BF16)
                before_tan[kind, rows, columns] = tan_part
                vec_row = pl.ds(8 + 2 * halves[kind] + chunk, 1)
                vec_ref[vec_row, :] += column_sum(tan_part.astype(F32))
                return carried + dot_nt(tan_part, we[kind, :, columns])

            for chunk in range(ws.shape[1] // COLS):
                normed_tan = expand_back(chunk, normed_tan)
        vec_ref[5:6, :] += column_sum(normed_tan * n_one)
        vec_ref[6:7, :] += column_sum(normed_tan)
        entry = norm_back(normed_tan, n_one, scale_one, gain_one)
        entry_ref[rows, :] = entry
        branch_low = (sum_tan + entry).astype(BF16)
        branch_tan[rows, :] = branch_low
        vec_ref[7:8, :] += column_sum(branch_low.astype(F32))
        for kind in range(2):
            mixed_tan[kind] = dot_nt(branch_low, wo[kind])
        for kind in range(2):
            for pair in range(2):
                columns = slice(pair * 128, pair * 128 + 128)
                for side in range(2):
                    head = halves[kind] * (H // 2) + 2 * pair + side
                    for core in range(2):
                        start = core * HALF
                        early = mixed_tan[kind, start : start + piece, columns]
                        late = mixed_tan[kind, start + piece : start + HALF, columns]
                        tan_send[step, head, core] = side_pair(side, early, late).astype(BF16)
        for i in range(H):
            for core in range(2):
                at.send(*tan_move(step, at.turn(i, H), core))
        for store in stores(step):
            store.start()
        return 0

    lax.fori_loop(0, 2, tile, 0)

    quarter = first_in.shape[0] // 4
    bits = (step_of(at.c, 1)[0], step_of(at.c, 2)[0])
    stages = (stage_a, stage_b)

    def core_move(region, give):
        bit = bits[region]
        start = region * 2 * quarter + (1 - bit if give else bit) * quarter
        where = span(start, quarter)
        slot = region + 2 * (0 if give else 1)
        return start, at.remote(
            send_grads.at[where], first_in.at[where], core_ss.at[slot], core_rs.at[slot],
            at.c, other,
        )

    order = [(0, True), (1, True), (0, False), (1, False)]
    low_turned[...] = jnp.transpose(low[...])
    operands = (mixed, low_turned, hidden, before_tan, feed_tan, branch_tan)
    feed_slopes(1, send_grads, *operands)
    for step in order:
        core_move(*step)[1].start()
    feed_slopes(0, own_grads, *operands)
    for region, give in order:
        start, move = core_move(region, give)
        move.wait_recv()

        def join(offset, where, size):
            total = own_grads[where, :] + first_in[where, :].astype(F32)
            if give:
                stages[region][span(offset, size), :] = total.astype(BF16)
            else:
                keep_ref[region, span(offset, size), :] = total

        pieces_of(start, quarter, join)
    for source in range(n_ctx):
        for side in range(2):
            arrived = tan_out.at[source, side]
            at.remote(
                arrived, arrived, tan_ss.at[0], tan_rs.at[source * 2 + side], at.c, other
            ).wait_recv()
    for step in range(2):
        for store in stores(step):
            store.wait()
    for side in range(2):
        for target in range(n_ctx):
            at.wait_sent(*o_move(target, side))
        for head in range(H):
            for core in range(2):
                at.wait_sent(*tan_move(side, head, core))
    for step in order:
        core_move(*step)[1].wait_send()


def middle(n_ctx, o, x, summed, cotangent, wo, we, ws, be, vec):
    tokens, wide, units = x.shape[0], D // 2, ws[0].shape[0]
    grad_rows = 2 * units + wide
    rows = jax.ShapeDtypeStruct((tokens, D), F32)

    def sems(*counts):
        return [pltpu.SemaphoreType.DMA((count,)) for count in counts]

    return pl.pallas_call(
        functools.partial(middle_kernel, n_ctx),
        out_shape=(
            rows,
            rows,
            rows,
            jax.ShapeDtypeStruct((n_ctx, 2, HALF // 2, 128), BF16),
            jax.ShapeDtypeStruct((16, D), F32),
            jax.ShapeDtypeStruct((grad_rows // 4, D), BF16),
            jax.ShapeDtypeStruct((grad_rows // 4, D), BF16),
            jax.ShapeDtypeStruct((2, grad_rows // 4, D), F32),
        ),
        in_specs=[ANY] * 10 + [VMEM] * 2,
        out_specs=(ANY,) * 4 + (VMEM,) * 4,
        scratch_shapes=[
            pltpu.VMEM((2, H, 2, HALF // 2, 128), BF16),
            pltpu.VMEM((tokens, D), F32),
            pltpu.VMEM((tokens, D), F32),
            pltpu.VMEM((tokens, D), F32),
            pltpu.VMEM((2, wide, D), BF16),
            pltpu.VMEM((2, D, units), BF16),
            pltpu.VMEM((2, units, D), BF16),
            pltpu.VMEM((tokens, D), F32),
            pltpu.VMEM((tokens, D), F32),
            pltpu.VMEM((tokens, D), F32),
            pltpu.VMEM((2, tokens, wide), BF16),
            pltpu.VMEM((tokens, D), BF16),
            pltpu.VMEM((2, tokens, units), BF16),
            pltpu.VMEM((2, tokens, units), BF16),
            pltpu.VMEM((tokens, D), BF16),
            pltpu.VMEM((tokens, D), BF16),
            pltpu.VMEM((2, BLK, units), F32),
            pltpu.VMEM((2, BLK, wide), F32),
            pltpu.VMEM((2, H, 2, HALF // 2, 128), BF16),
            pltpu.VMEM((grad_rows, D), F32),
            pltpu.VMEM((grad_rows, D), BF16),
            pltpu.VMEM((grad_rows, D), BF16),
            pltpu.VMEM((D, tokens), BF16),
        ]
        + sems(9, 6, 2 * n_ctx, 4 * H, 4 * H, 2 * n_ctx, 4, 4),
        compiler_params=pltpu.CompilerParams(
            collective_id=1, has_side_effects=True, vmem_limit_bytes=ROOM
        ),
        name="middle",
    )(o, x, summed, cotangent, *wo, *we, *ws, be, vec)


def finish_kernel(
    n_ctx,
    dq_ref, dkv_ref, keep_hbm, land_a, land_b, x_hbm, entry_hbm, wq_hbm, wk_hbm, wv_hbm,
    w_other_hbm, vec_feed,
    post_ref, feed_ref, grads_ref, vec_out,
    own, part, ready, dq_in, dkv_in, keep, acc, stage, landing,
    x_in, entry_in, w_in, w_far, low_turned, tangents,
    own_grads, send_grads, first_in, acc_last, stage_last, landing_last, vec_sum, vec_in,
    load_sem, q_ss, q_rs, kv_ss, kv_rs, part_ss, part_rs, own_sem,
    down_ss, down_rs, up_ss, up_rs, top_ss, top_rs,
    core_ss, core_rs, down_ss2, down_rs2, up_ss2, up_rs2, vec_ss, vec_rs,
):
    at = Place()
    c, f = at.c, at.f
    other = 1 - f
    halves = (f, other)
    wide = D // 2
    loads = [
        pltpu.make_async_copy(src, dst, load_sem.at[i])
        for i, (src, dst) in enumerate(
            (
                (keep_hbm, keep),
                (x_hbm, x_in),
                (entry_hbm, entry_in),
                (wq_hbm, w_in.at[0]),
                (wk_hbm, w_in.at[1]),
                (wv_hbm, w_in.at[2]),
                (w_other_hbm, w_far),
            )
        )
    ]
    for load in loads:
        load.start()
    x_step, y_step, near, far = (step_of(c, stride) for stride in (1, 2, 4, 8))
    barrier = pltpu.get_barrier_semaphore()
    for _, peer in (x_step, y_step, near, far):
        pl.semaphore_signal(barrier, 1, device_id=(peer, f), device_id_type=MESH)
    at.greet_owners(n_ctx, True, 4)

    def partial_move(source):
        return at.remote(
            dkv_ref.at[2 * source + other],
            part.at[source],
            part_ss.at[source],
            part_rs.at[source],
            c,
            other,
        )

    def own_move(source):
        return pltpu.make_async_copy(
            dkv_ref.at[2 * source + f], own.at[source], own_sem.at[source]
        )

    def q_move(target):
        return (
            dq_ref.at[target],
            dq_in.at[at.head, f],
            q_ss.at[target],
            q_rs.at[at.head * 2 + f],
            target,
            at.group,
        )

    def kv_move(target):
        return (
            ready.at[target],
            dkv_in.at[at.head, pl.ds(pl.multiple_of(f * BLK, BLK), BLK)],
            kv_ss.at[target],
            kv_rs.at[at.head * 2 + f],
            target,
            at.group,
        )

    for i in range(n_ctx):
        source = at.turn(i, n_ctx)
        partial_move(source).start()
        own_move(source).start()
    for i in range(n_ctx):
        at.send(*q_move(at.turn(i, n_ctx)))

    size = keep.shape[1]
    firsts = (x_step, y_step)
    bases = [2 * size * region + firsts[region][0] * size for region in range(2)]
    feed = Ladder(
        at,
        ((y_step, near, far), (x_step, near, far)),
        (0, 0),
        size,
        [keep.at[region] for region in range(2)],
        [stage.at[region] for region in range(2)],
        [[landing.at[region, step] for step in range(3)] for region in range(2)],
        feed_ref,
        (down_ss, down_rs, up_ss, up_rs),
        bases,
    )

    def top_move(region, sent):
        side, columns = region % 2, columns_of(region)
        given = 2 * size * side + (1 - firsts[side][0]) * size
        where = span(bases[side] if sent else given, size)
        return at.remote(
            feed_ref.at[where, columns],
            feed_ref.at[where, columns],
            top_ss.at[region],
            top_rs.at[region],
            firsts[side][1],
            f,
        )

    loads[0].wait()
    kept_acc = [keep.at[region] for region in range(2)]
    sums = [acc.at[region] for region in range(2)]
    for region in range(REGIONS):
        first = (land_a, land_b)[region % 2]
        kept, given, half, _ = feed.ranges[region][0]
        feed.acc = kept_acc
        feed.join(region, given, half, first, stage.at[region % 2])
        feed.down(region, 0, True).start()
        feed.join(region, kept, half, first, sums[region % 2])
    feed.acc = sums
    for i in range(n_ctx):
        source = at.turn(i, n_ctx)
        own_move(source).wait()
        partial_move(source).wait_recv()
        ready[source] = jnp.transpose(own[source] + part[source]).astype(BF16)
        at.send(*kv_move(source))
    for load in loads[1:]:
        load.wait()
    low_turned[...] = jnp.transpose(x_in[...]).astype(BF16)
    for step in (1, 2):
        for region in range(REGIONS):
            feed.down(region, step - 1, False).wait_recv()
            feed.give(region, step, feed.landing[region % 2][step - 1])

    for head in range(H):
        for core in range(2):
            slot = head * 2 + core
            arrived = dq_in.at[head, core]
            at.remote(arrived, arrived, q_ss.at[0], q_rs.at[slot], c, other).wait_recv()
            arrived = dkv_in.at[head, pl.ds(core * BLK, BLK)]
            at.remote(arrived, arrived, kv_ss.at[0], kv_rs.at[slot], c, other).wait_recv()
    feed_rows = vec_feed.shape[0]
    vec_sum[0, 0:feed_rows] = vec_feed[...]
    vec_sum[0, feed_rows:] = jnp.zeros_like(vec_sum[0, feed_rows:])

    plans = ((x_step, y_step, near, far), (y_step, x_step, near, far))
    quarter = first_in.shape[0] // 4
    last = Ladder(
        at,
        plans,
        (0, 2 * quarter),
        2 * quarter,
        [acc_last, acc_last],
        [stage_last, stage_last],
        [[landing_last.at[step] for step in range(4)]] * 2,
        grads_ref,
        (down_ss2, down_rs2, up_ss2, up_rs2),
    )

    def core_move(region, give):
        kept, given, rows, _ = last.ranges[region][0]
        where = span(given if give else kept, rows)
        slot, columns = region + REGIONS * (0 if give else 1), columns_of(region)
        return at.remote(
            send_grads.at[where, columns],
            first_in.at[where, columns],
            core_ss.at[slot],
            core_rs.at[slot],
            c,
            other,
        )

    order = [(region, give) for give in (True, False) for region in range(REGIONS)]
    vec_peers = [(c, other)] + [(peer, f) for _, peer in (x_step, y_step, near, far)]

    def vec_move(step):
        return at.remote(
            vec_sum.at[step], vec_in.at[step], vec_ss.at[step], vec_rs.at[step], *vec_peers[step]
        )

    def vec_next(step):
        vec_move(step).wait_recv()
        target = vec_sum.at[step + 1] if step < 4 else vec_out
        target[...] = vec_sum[step] + vec_in[step]
        if step < 4:
            vec_move(step + 1).start()

    for kind, grad_ref in ((1, send_grads), (0, own_grads)):
        for pair in range(2):
            head = halves[kind] * (H // 2) + 2 * pair
            columns = slice(pair * 128, pair * 128 + 128)
            for core in range(2):
                early = dq_in[head, core].astype(F32)
                late = dq_in[head + 1, core].astype(F32)
                for side in range(2):
                    start = side * BLK + core * HALF
                    tangents[kind, 0, start : start + HALF, columns] = side_pair(
                        side, early, late
                    ).astype(BF16)
            early = dkv_in[head].astype(F32)
            late = dkv_in[head + 1].astype(F32)
            tangents[kind, 1, :, columns] = low_pair(early, late).astype(BF16)
            tangents[kind, 2, :, columns] = high_pair(early, late).astype(BF16)
        turned = low_turned[...]
        grad_ref[0:D, 0:wide] = dot_nn(turned, tangents[kind, 0]).astype(grad_ref.dtype)
        grad_ref[0:D, wide:D] = dot_nn(turned, tangents[kind, 1]).astype(grad_ref.dtype)
        value_grad = dot_nn(turned, tangents[kind, 2]).astype(grad_ref.dtype)
        grad_ref[D : D + wide, 0:wide] = value_grad[0:wide]
        grad_ref[D : D + wide, wide:D] = value_grad[wide:D]
        columns = pl.ds(pl.multiple_of(halves[kind] * wide, wide), wide)
        vec_sum[0, feed_rows : feed_rows + 1, columns] = column_sum(tangents[kind, 0].astype(F32))
        vec_sum[0, feed_rows + 1 : feed_rows + 2, columns] = column_sum(
            tangents[kind, 2].astype(F32)
        )
        if kind == 1:
            for step in order:
                core_move(*step).start()
    vec_move(0).start()
    for region in range(REGIONS):
        feed.settle(region)
    for region, give in order:
        core_move(region, give).wait_recv()
        kept, given, rows, _ = last.ranges[region][0]
        columns = columns_of(region)

        def join(offset, where, _):
            total = own_grads[where, columns] + first_in[where, columns].astype(F32)
            if give:
                stage_last[where, columns] = total.astype(BF16)
            else:
                acc_last[where, columns] = total

        pieces_of(given if give else kept, rows, join)
        if give:
            last.down(region, 0, True).start()
    vec_next(0)
    total = entry_in[...]
    for which in range(3):
        total = total + dot_nt(tangents[0, which], w_in[which])
        total = total + dot_nt(tangents[1, which], w_far[which])
    post_ref[...] = total
    for region in range(REGIONS):
        feed.up(region, 1, False).wait_recv()
        feed.up(region, 0, True).start()
    for step in (1, 2):
        for region in range(REGIONS):
            last.down(region, step - 1, False).wait_recv()
            last.give(region, step, last.landing[region % 2][step - 1])
        vec_next(step)
    for region in range(REGIONS):
        feed.up(region, 0, False).wait_recv()
        top_move(region, True).start()
    for region in range(REGIONS):
        last.down(region, 2, False).wait_recv()
        last.give(region, 3, last.landing[region % 2][2])
    vec_next(3)
    for region in range(REGIONS):
        last.settle(region)
    vec_next(4)
    for step in (2, 1, 0):
        for region in range(REGIONS):
            last.up(region, step, False).wait_recv()
            if step > 0:
                last.up(region, step - 1, True).start()
    for region in range(REGIONS):
        top_move(region, False).wait_recv()

    for target in range(n_ctx):
        partial_move(target).wait_send()
        at.wait_sent(*q_move(target))
        at.wait_sent(*kv_move(target))
    for step in order:
        core_move(*step).wait_send()
    for step in range(5):
        vec_move(step).wait_send()
    for region in range(REGIONS):
        top_move(region, True).wait_send()
    feed.wait_sent()
    last.wait_sent()


def finish(n_ctx, dq, dkv, keep, land_a, land_b, x, entry, wq, wk, wv, w_other, vec_feed):
    size, tokens, wide = keep.shape[1], x.shape[0], D // 2
    last_shape = (D + wide, D)
    vec_shape = (vec_feed.shape[0] + 8, D)

    def sems(*counts):
        return [pltpu.SemaphoreType.DMA((count,)) for count in counts]

    return pl.pallas_call(
        functools.partial(finish_kernel, n_ctx),
        out_shape=(
            jax.ShapeDtypeStruct((tokens, D), F32),
            jax.ShapeDtypeStruct((4 * size, D), BF16),
            jax.ShapeDtypeStruct(last_shape, BF16),
            jax.ShapeDtypeStruct(vec_shape, F32),
        ),
        in_specs=[ANY, ANY, ANY, VMEM, VMEM] + [ANY] * 6 + [VMEM],
        out_specs=(VMEM,) * 4,
        scratch_shapes=[
            pltpu.VMEM((n_ctx, 128, BLK), F32),
            pltpu.VMEM((n_ctx, 128, BLK), F32),
            pltpu.VMEM((n_ctx, BLK, 128), BF16),
            pltpu.VMEM((H, 2, HALF, 128), BF16),
            pltpu.VMEM((H, 2 * BLK, 128), BF16),
            pltpu.VMEM((2, size, D), F32),
            pltpu.VMEM((2, size, D), F32),
            pltpu.VMEM((2, size, D), BF16),
            pltpu.VMEM((2, 3, size, D), BF16),
            pltpu.VMEM((tokens, D), F32),
            pltpu.VMEM((tokens, D), F32),
            pltpu.VMEM((3, D, wide), BF16),
            pltpu.VMEM((3, D, wide), BF16),
            pltpu.VMEM((D, tokens), BF16),
            pltpu.VMEM((2, 3, tokens, wide), BF16),
            pltpu.VMEM(last_shape, F32),
            pltpu.VMEM(last_shape, BF16),
            pltpu.VMEM(last_shape, BF16),
            pltpu.VMEM(last_shape, F32),
            pltpu.VMEM(last_shape, BF16),
            pltpu.VMEM((4,) + last_shape, BF16),
            pltpu.VMEM((5,) + vec_shape, F32),
            pltpu.VMEM((5,) + vec_shape, F32),
        ]
        + sems(7, n_ctx, 2 * H, n_ctx, 2 * H, n_ctx, n_ctx, n_ctx)
        + sems(12, 12, 12, 12, 4, 4, 8, 8, 16, 16, 16, 16, 5, 5),
        compiler_params=pltpu.CompilerParams(
            collective_id=3, has_side_effects=True, vmem_limit_bytes=ROOM
        ),
        name="finish",
    )(dq, dkv, keep, land_a, land_b, x, entry, wq, wk, wv, w_other, vec_feed)


def unpack_kernel(
    full_hbm, grads_hbm, post_hbm, vec_ref,
    query_hbm, key_hbm, value_hbm, output_hbm, expand_hbm, shrink_hbm, post_out, *rest,
):
    vector_outs, (low_full, low_last, full, last, held, load_sem, store_sem, post_sem) = (
        rest[:11],
        rest[11:],
    )
    f = lax.axis_index("fsdp")
    units, wide = shrink_hbm.shape[0], D // 2
    post_in = pltpu.make_async_copy(post_hbm, held, post_sem.at[0])
    post = pltpu.make_async_copy(held, post_out, post_sem.at[1])
    post_in.start()
    parts = [
        (low_last, last, 0, D, [(query_hbm, slice(0, wide)), (key_hbm, slice(wide, D))]),
        (
            low_last,
            last,
            D,
            wide,
            [
                (value_hbm.at[0:wide], slice(0, wide)),
                (value_hbm.at[wide:D], slice(wide, D)),
            ],
        ),
    ]
    for part in range(units // D):
        parts.append(
            (
                low_full,
                full,
                part * D,
                D,
                [(shrink_hbm.at[part * D : part * D + D], slice(0, D))],
            )
        )
    for part in range(units // D):
        parts.append(
            (
                low_full,
                full,
                units + part * D,
                D,
                [(expand_hbm.at[:, part * D : part * D + D], slice(0, D))],
            )
        )
    parts.append((low_full, full, 2 * units, wide, [(output_hbm, slice(0, D))]))
    loads = []
    for i, (low, _, start, rows, _) in enumerate(parts):
        src = grads_hbm if low is low_last else full_hbm
        where = pl.ds(start, rows)
        loads.append(pltpu.make_async_copy(src.at[where], low.at[where], load_sem.at[i]))
        loads[-1].start()
    post_in.wait()
    post.start()
    stores = []
    for load, (low, wide_rows, start, rows, targets) in zip(loads, parts):
        load.wait()
        where = pl.ds(start, rows)
        wide_rows[where, :] = low[where, :].astype(F32)
        for target, columns in targets:
            stores.append(
                pltpu.make_async_copy(
                    wide_rows.at[where, columns], target, store_sem.at[len(stores)]
                )
            )
            stores[-1].start()
    vectors = vec_ref[...]
    mine = jnp.where(f == 0, vectors[:, 0:wide], vectors[:, wide:D])
    for row, ref in zip((16, 17, 7, 5, 6, 0, 1, 2, 3, 4), vector_outs):
        ref[...] = mine[row : row + 1]
    drift = jnp.where(f == 0, vectors[8:10], vectors[10:12])
    for part in range(units // D):
        vector_outs[10][:, part * D : part * D + D] = drift[part : part + 1]
    for store in stores:
        store.wait()
    post.wait()


def unpack_grads(units, full, grads, post, vecs):
    wide = D // 2
    shapes = [(D, wide)] * 3 + [(wide, D), (D, units), (units, D), post.shape]
    vectors = [(1, wide)] * 10 + [(1, units)]
    part_count = 3 + 2 * (units // D)
    return pl.pallas_call(
        unpack_kernel,
        out_shape=tuple(jax.ShapeDtypeStruct(shape, F32) for shape in shapes + vectors),
        in_specs=[ANY] * 3 + [VMEM],
        out_specs=(ANY,) * len(shapes) + (VMEM,) * len(vectors),
        scratch_shapes=[
            pltpu.VMEM(full.shape, BF16),
            pltpu.VMEM(grads.shape, BF16),
            pltpu.VMEM(full.shape, F32),
            pltpu.VMEM(grads.shape, F32),
            pltpu.VMEM(post.shape, F32),
            pltpu.SemaphoreType.DMA((part_count,)),
            pltpu.SemaphoreType.DMA((part_count + 2,)),
            pltpu.SemaphoreType.DMA((2,)),
        ],
        compiler_params=pltpu.CompilerParams(vmem_limit_bytes=ROOM),
        name="unpack_grads",
    )(full, grads, post, vecs)


def head_shards(
    n_ctx,
    post_stream,
    sum_stream,
    cotangent,
    block_order,
    block_sequence,
    query_weight,
    key_weight,
    value_weight,
    output_weight,
    query_bias,
    value_bias,
    output_bias,
    attend_gain,
    attend_shift,
    expand_weight,
    expand_bias,
    shrink_weight,
    shrink_bias,
    middle_gain,
    middle_shift,
    final_gain,
    final_shift,
):
    x, summed, tangent = post_stream[0], sum_stream[0], cotangent[0]
    swap = [(0, 1), (1, 0)]

    def from_other(values):
        return lax.ppermute(values, "fsdp", swap)

    def across(values, stride):
        return lax.ppermute(values, "ctx", [(c, c ^ stride) for c in range(n_ctx)])

    vectors = [
        query_bias,
        value_bias,
        output_bias,
        attend_gain,
        attend_shift,
        shrink_bias,
        middle_gain,
        middle_shift,
        final_gain,
        final_shift,
        expand_bias,
    ]
    q, kv, w_other, order, seqs, vec, expand_add = project_and_scatter(
        n_ctx, x, query_weight, key_weight, value_weight, block_order, block_sequence, vectors
    )
    o, keep, lse, pairs = attend(order, seqs, q, kv)
    layer_output, sum_tan, entry, tan, vec_feed, stage_a, stage_b, kept = middle(
        n_ctx,
        o,
        x,
        summed,
        tangent,
        (output_weight, from_other(output_weight)),
        (expand_weight, from_other(expand_weight)),
        (shrink_weight, from_other(shrink_weight)),
        expand_add,
        vec,
    )
    land_a, land_b = across(stage_a, 1), across(stage_b, 2)
    dq, dkv, layer_output, sum_tan = attend_back(
        pairs, q, tan, keep, lse, kv, (layer_output, sum_tan)
    )
    post_tangent, feed_sums, last_sums, vecs = finish(
        n_ctx,
        dq,
        dkv,
        kept,
        land_a,
        land_b,
        x,
        entry,
        query_weight,
        key_weight,
        value_weight,
        w_other,
        vec_feed,
    )
    (
        query_slope,
        key_slope,
        value_slope,
        output_slope,
        expand_slope,
        shrink_slope,
        post_tangent,
        query_drift,
        value_drift,
        output_drift,
        attend_stretch,
        attend_nudge,
        shrink_drift,
        middle_stretch,
        middle_nudge,
        final_stretch,
        final_nudge,
        expand_drift,
    ) = unpack_grads(shrink_weight.shape[0], feed_sums, last_sums, post_tangent, vecs)
    return (
        layer_output[None],
        post_tangent[None],
        sum_tan[None],
        query_slope,
        key_slope,
        value_slope,
        output_slope,
        query_drift[0],
        value_drift[0],
        output_drift[0],
        attend_stretch[0],
        attend_nudge[0],
        expand_slope,
        expand_drift[0],
        shrink_slope,
        shrink_drift[0],
        middle_stretch[0],
        middle_nudge[0],
        final_stretch[0],
        final_nudge[0],
    )


def solution(mesh):
    n_ctx, n_fsdp = mesh.shape["ctx"], mesh.shape["fsdp"]
    if n_fsdp == 2 and n_ctx == n_fsdp * H:
        body = functools.partial(head_shards, n_ctx)
    else:
        body = general_shards
    return jax.shard_map(
        body,
        mesh=mesh,
        in_specs=(
            P("fsdp", "ctx", None),
            P("fsdp", "ctx", None),
            P("fsdp", "ctx", None),
            P("fsdp", None),
            P("fsdp", None),
            P(None, "fsdp"),
            P(None, "fsdp"),
            P(None, "fsdp"),
            P("fsdp", None),
            P("fsdp"),
            P("fsdp"),
            P("fsdp"),
            P("fsdp"),
            P("fsdp"),
            P(None, "fsdp"),
            P("fsdp"),
            P("fsdp", None),
            P("fsdp"),
            P("fsdp"),
            P("fsdp"),
            P("fsdp"),
            P("fsdp"),
        ),
        out_specs=(
            P("fsdp", "ctx", None),
            P("fsdp", "ctx", None),
            P("fsdp", "ctx", None),
            P(None, "fsdp"),
            P(None, "fsdp"),
            P(None, "fsdp"),
            P("fsdp", None),
            P("fsdp"),
            P("fsdp"),
            P("fsdp"),
            P("fsdp"),
            P("fsdp"),
            P(None, "fsdp"),
            P("fsdp"),
            P("fsdp", None),
            P("fsdp"),
            P("fsdp"),
            P("fsdp"),
            P("fsdp"),
            P("fsdp"),
        ),
        check_vma=False,
    )
```

```python
import functools

import jax
import jax.numpy as jnp
from jax import lax
from jax.experimental import pallas as pl
from jax.experimental.pallas import tpu as pltpu
from jax.sharding import PartitionSpec as P

D = 512
H = 8
HD = 64
BLK = 256
HALF = BLK // 2
LONG = 8
TOGETHER = 16
MOST = LONG + 1
F32 = jnp.float32
BF16 = jnp.bfloat16
MESH = pl.DeviceIdType.MESH
ROOM = 60 << 20
UNPACK_ROOM = 60 << 20
VMEM = pl.BlockSpec(memory_space=pltpu.VMEM)
SMEM = pl.BlockSpec(memory_space=pltpu.SMEM)
ANY = pl.BlockSpec(memory_space=pltpu.HBM)


norm_eps = 1e-05
masked_value = -1e30
gelu_coeff = 0.7978845608
gelu_cubic = 0.044715


def smooth_gate(values):
    return (
        0.5
        * values
        * (1.0 + jnp.tanh(gelu_coeff * (values + gelu_cubic * values * values * values)))
    )


def layer_norm(inputs, gain_row, shift_row):
    centre = inputs - jnp.mean(inputs, axis=-1, keepdims=True)
    spread = jnp.mean(centre * centre, axis=-1, keepdims=True)
    return centre * lax.rsqrt(spread + norm_eps) * gain_row + shift_row


def product(left_side, right_side):
    return jnp.dot(left_side, right_side, preferred_element_type=jnp.float32)


def cross_rows(left_side, right_side):
    return lax.dot_general(
        left_side, right_side, (((0,), (0,)), ((), ())), preferred_element_type=jnp.float32
    )


def cross_cols(left_side, right_side):
    return lax.dot_general(
        left_side, right_side, (((1,), (1,)), ((), ())), preferred_element_type=jnp.float32
    )


def column_total(values):
    return jnp.sum(values, axis=0, dtype=jnp.float32)


def lookup(table_row, indices):
    places = jnp.arange(table_row.shape[0], dtype=jnp.int32)
    return jnp.sum(jnp.where(indices[:, None] == places[None, :], table_row[None, :], 0), axis=1)


def block_mask(query_blocks, query_seqs, key_blocks, key_seqs):
    same_seq = query_seqs[:, None] == key_seqs[None, :]
    return same_seq & (key_blocks[None, :] <= query_blocks[:, None])


def token_mask(visible):
    return jnp.repeat(jnp.repeat(visible, BLK, axis=0), BLK, axis=1)


def fold_units(carried, members, unit_step):
    unit_count = members[0].shape[0] // BLK
    inner_count = max((divisor for divisor in range(1, 17) if unit_count % divisor == 0))
    outer_count = unit_count // inner_count

    def outer_turn(outer_index, current):

        def inner_turn(inner_index, inner_state):
            offset = (outer_index * inner_count + inner_index) * BLK
            pieces = tuple((lax.dynamic_slice_in_dim(member, offset, BLK, 0) for member in members))
            return unit_step(inner_state, pieces, offset)

        return lax.fori_loop(0, inner_count, inner_turn, current)

    return lax.fori_loop(0, outer_count, outer_turn, carried)


def general_shards(
    post_stream,
    sum_stream,
    cotangent,
    block_order,
    block_sequence,
    query_weight,
    key_weight,
    value_weight,
    output_weight,
    query_bias,
    value_bias,
    output_bias,
    attend_gain,
    attend_shift,
    expand_weight,
    expand_bias,
    shrink_weight,
    shrink_bias,
    middle_gain,
    middle_shift,
    final_gain,
    final_shift,
):
    (
        query_whole,
        key_whole,
        value_whole,
        output_whole,
        query_add,
        value_add,
        output_add,
        gain_one,
        shift_one,
        expand_whole,
        expand_add,
        shrink_whole,
        shrink_add,
        gain_two,
        shift_two,
        gain_last,
        shift_last,
    ) = (
        lax.all_gather(query_weight, "fsdp", axis=1, tiled=True),
        lax.all_gather(key_weight, "fsdp", axis=1, tiled=True),
        lax.all_gather(value_weight, "fsdp", axis=1, tiled=True),
        lax.all_gather(output_weight, "fsdp", axis=0, tiled=True),
        lax.all_gather(query_bias, "fsdp", axis=0, tiled=True),
        lax.all_gather(value_bias, "fsdp", axis=0, tiled=True),
        lax.all_gather(output_bias, "fsdp", axis=0, tiled=True),
        lax.all_gather(attend_gain, "fsdp", axis=0, tiled=True),
        lax.all_gather(attend_shift, "fsdp", axis=0, tiled=True),
        lax.all_gather(expand_weight, "fsdp", axis=1, tiled=True),
        lax.all_gather(expand_bias, "fsdp", axis=0, tiled=True),
        lax.all_gather(shrink_weight, "fsdp", axis=0, tiled=True),
        lax.all_gather(shrink_bias, "fsdp", axis=0, tiled=True),
        lax.all_gather(middle_gain, "fsdp", axis=0, tiled=True),
        lax.all_gather(middle_shift, "fsdp", axis=0, tiled=True),
        lax.all_gather(final_gain, "fsdp", axis=0, tiled=True),
        lax.all_gather(final_shift, "fsdp", axis=0, tiled=True),
    )
    post_rows = post_stream[0]
    summed = sum_stream[0]
    tangent = cotangent[0]
    order_row = block_order[0]
    seq_row = block_sequence[0]
    token_count = post_rows.shape[0]
    score_scale = HD ** (-0.5)
    own_blocks = lax.dynamic_slice_in_dim(
        order_row, lax.axis_index("ctx") * (token_count // BLK), token_count // BLK
    )
    own_seqs = lookup(seq_row, own_blocks)
    post_low = post_rows.astype(jnp.bfloat16)
    queries = (product(post_low, query_whole) + query_add).astype(jnp.bfloat16)
    key_rows = product(post_low, key_whole).astype(jnp.bfloat16)
    value_rows = (product(post_low, value_whole) + value_add).astype(jnp.bfloat16)
    query_heads = queries.reshape(token_count, H, HD)

    def keys_visible(first_row):
        key_block = lax.dynamic_slice_in_dim(order_row, first_row // BLK, 1)
        return block_mask(own_blocks, own_seqs, key_block, lookup(seq_row, key_block))

    def masked_fold(block_step):

        def unit_step(current, pieces, first_row):
            visible = keys_visible(first_row)
            return lax.cond(
                jnp.any(visible),
                lambda inner_state: block_step(inner_state, pieces, visible),
                lambda inner_state: inner_state,
                current,
            )

        def folded(current, pieces, first_row):
            return fold_units(current, pieces, unit_step)

        return folded

    def stats_block(current, pieces, visible):
        row_peaks, masses = current
        key_heads = pieces[0].reshape(BLK, H, HD)
        row_mask = token_mask(visible)[None]
        scores = (
            jnp.einsum("qhd,khd->hqk", query_heads, key_heads, preferred_element_type=jnp.float32)
            * score_scale
        )
        new_peaks = jnp.maximum(
            row_peaks, jnp.max(jnp.where(row_mask, scores, masked_value), axis=2)
        )
        weights = jnp.where(row_mask, jnp.exp(scores - new_peaks[:, :, None]), 0.0)
        return (new_peaks, masses * jnp.exp(row_peaks - new_peaks) + jnp.sum(weights, axis=2))

    stats_fold = masked_fold(stats_block)
    stats_start = (
        jnp.full((H, token_count), masked_value, jnp.float32),
        jnp.zeros((H, token_count), jnp.float32),
    )
    row_peaks, masses = stats_fold(
        stats_start, (lax.all_gather(key_rows, "ctx", axis=0, tiled=True),), jnp.int32(0)
    )
    log_mass = row_peaks + jnp.log(masses)

    def forward_block(current, pieces, visible):
        key_heads = pieces[0].reshape(BLK, H, HD)
        value_heads = pieces[1].reshape(BLK, H, HD)
        row_mask = token_mask(visible)[None]
        scores = (
            jnp.einsum("qhd,khd->hqk", query_heads, key_heads, preferred_element_type=jnp.float32)
            * score_scale
        )
        weights = jnp.where(row_mask, jnp.exp(scores - log_mass[:, :, None]), 0.0).astype(
            jnp.bfloat16
        )
        addition = jnp.einsum(
            "hqk,khd->qhd", weights, value_heads, preferred_element_type=jnp.float32
        )
        return current + addition.reshape(token_count, D)

    forward_fold = masked_fold(forward_block)
    zero_rows = jnp.zeros((token_count, D), jnp.float32)
    attended = forward_fold(
        zero_rows,
        (
            lax.all_gather(key_rows, "ctx", axis=0, tiled=True),
            lax.all_gather(value_rows, "ctx", axis=0, tiled=True),
        ),
        jnp.int32(0),
    )
    mixed_low = attended.astype(jnp.bfloat16)
    branch = product(mixed_low, output_whole) + output_add
    normed_one, first_pull = jax.vjp(
        layer_norm, post_rows + branch, gain_one.astype(jnp.float32), shift_one.astype(jnp.float32)
    )
    stream_one = summed + branch
    normed_low = normed_one.astype(jnp.bfloat16)
    before = product(normed_low, expand_whole) + expand_add
    gated, gate_pull = jax.vjp(smooth_gate, before)
    hidden = gated.astype(jnp.bfloat16)
    feed_out = product(hidden, shrink_whole) + shrink_add
    normed_two, middle_pull = jax.vjp(
        layer_norm,
        normed_one + feed_out,
        gain_two.astype(jnp.float32),
        shift_two.astype(jnp.float32),
    )
    stream_two = stream_one + feed_out
    last_norm, last_pull = jax.vjp(
        layer_norm, stream_two, gain_last.astype(jnp.float32), shift_last.astype(jnp.float32)
    )
    layer_output = normed_two + last_norm
    stream_tan, stretch_last, nudge_last = last_pull(tangent)
    inflow_tan, stretch_two, nudge_two = middle_pull(tangent)
    feed_tan = (stream_tan + inflow_tan).astype(jnp.bfloat16)
    slope_shrink = cross_rows(hidden, feed_tan)
    drift_shrink = column_total(feed_tan)
    before_tan = gate_pull(cross_cols(feed_tan, shrink_whole))[0].astype(jnp.bfloat16)
    slope_expand = cross_rows(normed_low, before_tan)
    drift_expand = column_total(before_tan)
    normed_tan = inflow_tan + cross_cols(before_tan, expand_whole)
    feed_parts = lax.psum(
        (
            slope_expand,
            drift_expand,
            slope_shrink,
            drift_shrink,
            stretch_two,
            nudge_two,
            stretch_last,
            nudge_last,
        ),
        "ctx",
    )
    feed_sums = (
        lax.psum_scatter(feed_parts[0], "fsdp", scatter_dimension=1, tiled=True),
        lax.psum_scatter(feed_parts[1], "fsdp", scatter_dimension=0, tiled=True),
        lax.psum_scatter(feed_parts[2], "fsdp", scatter_dimension=0, tiled=True),
        lax.psum_scatter(feed_parts[3], "fsdp", scatter_dimension=0, tiled=True),
        lax.psum_scatter(feed_parts[4], "fsdp", scatter_dimension=0, tiled=True),
        lax.psum_scatter(feed_parts[5], "fsdp", scatter_dimension=0, tiled=True),
        lax.psum_scatter(feed_parts[6], "fsdp", scatter_dimension=0, tiled=True),
        lax.psum_scatter(feed_parts[7], "fsdp", scatter_dimension=0, tiled=True),
    )
    entry_tan, stretch_one, nudge_one = first_pull(normed_tan)
    branch_tan = (stream_tan + entry_tan).astype(jnp.bfloat16)
    slope_output = cross_rows(mixed_low, branch_tan)
    drift_output = column_total(branch_tan)
    mixed_tan = cross_cols(branch_tan, output_whole).astype(jnp.bfloat16)
    tangent_heads = mixed_tan.reshape(token_count, H, HD)
    deltas = jnp.sum((mixed_tan * attended).reshape(token_count, H, HD), axis=2).T

    def query_block(current, pieces, visible):
        key_heads = pieces[0].reshape(BLK, H, HD)
        value_heads = pieces[1].reshape(BLK, H, HD)
        row_mask = token_mask(visible)[None]
        scores = (
            jnp.einsum("qhd,khd->hqk", query_heads, key_heads, preferred_element_type=jnp.float32)
            * score_scale
        )
        probability = jnp.where(row_mask, jnp.exp(scores - log_mass[:, :, None]), 0.0)
        prob_tan = jnp.einsum(
            "qhd,khd->hqk", tangent_heads, value_heads, preferred_element_type=jnp.float32
        )
        score_tan = (probability * (prob_tan - deltas[:, :, None])).astype(jnp.bfloat16)
        addition = jnp.einsum(
            "hqk,khd->qhd", score_tan, key_heads, preferred_element_type=jnp.float32
        )
        return current + addition.reshape(token_count, D) * score_scale

    query_fold = masked_fold(query_block)
    query_sum = query_fold(
        zero_rows,
        (
            lax.all_gather(key_rows, "ctx", axis=0, tiled=True),
            lax.all_gather(value_rows, "ctx", axis=0, tiled=True),
        ),
        jnp.int32(0),
    )
    gathered_mass, gathered_delta = (
        lax.all_gather(log_mass.T, "ctx", axis=0, tiled=True),
        lax.all_gather(deltas.T, "ctx", axis=0, tiled=True),
    )
    own_keys = key_rows.reshape(token_count, H, HD)
    own_values = value_rows.reshape(token_count, H, HD)

    def owner_block(current, pieces, first_row, visible):
        key_acc, value_acc = current
        part_queries = pieces[0].reshape(BLK, H, HD)
        part_tangent = pieces[1].reshape(BLK, H, HD)
        part_mass = lax.dynamic_slice_in_dim(gathered_mass, first_row, BLK, 0).T
        part_delta = lax.dynamic_slice_in_dim(gathered_delta, first_row, BLK, 0).T
        row_mask = token_mask(visible)[None]
        scores = (
            jnp.einsum("qhd,khd->hqk", part_queries, own_keys, preferred_element_type=jnp.float32)
            * score_scale
        )
        probability = jnp.where(row_mask, jnp.exp(scores - part_mass[:, :, None]), 0.0)
        value_add_rows = jnp.einsum(
            "hqk,qhd->khd",
            probability.astype(jnp.bfloat16),
            part_tangent,
            preferred_element_type=jnp.float32,
        )
        prob_tan = jnp.einsum(
            "qhd,khd->hqk", part_tangent, own_values, preferred_element_type=jnp.float32
        )
        score_tan = (probability * (prob_tan - part_delta[:, :, None])).astype(jnp.bfloat16)
        key_add_rows = jnp.einsum(
            "hqk,qhd->khd", score_tan, part_queries, preferred_element_type=jnp.float32
        )
        return (
            key_acc + key_add_rows.reshape(token_count, D) * score_scale,
            value_acc + value_add_rows.reshape(token_count, D),
        )

    def owner_unit(current, pieces, first_row):
        query_blocks = lax.dynamic_slice_in_dim(order_row, first_row // BLK, 1)
        visible = block_mask(query_blocks, lookup(seq_row, query_blocks), own_blocks, own_seqs)
        return lax.cond(
            jnp.any(visible),
            lambda inner_state: owner_block(inner_state, pieces, first_row, visible),
            lambda inner_state: inner_state,
            current,
        )

    key_sum, value_sum = fold_units(
        (zero_rows, zero_rows),
        (
            lax.all_gather(queries, "ctx", axis=0, tiled=True),
            lax.all_gather(mixed_tan, "ctx", axis=0, tiled=True),
        ),
        owner_unit,
    )
    query_tan = query_sum.astype(jnp.bfloat16)
    key_tan = key_sum.astype(jnp.bfloat16)
    value_tan = value_sum.astype(jnp.bfloat16)
    slope_query = cross_rows(post_low, query_tan)
    slope_key = cross_rows(post_low, key_tan)
    slope_value = cross_rows(post_low, value_tan)
    drift_query = column_total(query_tan)
    drift_value = column_total(value_tan)
    post_tangent = (
        entry_tan
        + cross_cols(query_tan, query_whole)
        + cross_cols(key_tan, key_whole)
        + cross_cols(value_tan, value_whole)
    )
    heads_parts = lax.psum(
        (
            slope_query,
            slope_key,
            slope_value,
            slope_output,
            drift_query,
            drift_value,
            drift_output,
            stretch_one,
            nudge_one,
        ),
        "ctx",
    )
    heads_sums = (
        lax.psum_scatter(heads_parts[0], "fsdp", scatter_dimension=1, tiled=True),
        lax.psum_scatter(heads_parts[1], "fsdp", scatter_dimension=1, tiled=True),
        lax.psum_scatter(heads_parts[2], "fsdp", scatter_dimension=1, tiled=True),
        lax.psum_scatter(heads_parts[3], "fsdp", scatter_dimension=0, tiled=True),
        lax.psum_scatter(heads_parts[4], "fsdp", scatter_dimension=0, tiled=True),
        lax.psum_scatter(heads_parts[5], "fsdp", scatter_dimension=0, tiled=True),
        lax.psum_scatter(heads_parts[6], "fsdp", scatter_dimension=0, tiled=True),
        lax.psum_scatter(heads_parts[7], "fsdp", scatter_dimension=0, tiled=True),
        lax.psum_scatter(heads_parts[8], "fsdp", scatter_dimension=0, tiled=True),
    )
    return (
        layer_output[None],
        post_tangent[None],
        stream_tan[None],
        heads_sums[0],
        heads_sums[1],
        heads_sums[2],
        heads_sums[3],
        heads_sums[4],
        heads_sums[5],
        heads_sums[6],
        heads_sums[7],
        heads_sums[8],
        feed_sums[0],
        feed_sums[1],
        feed_sums[2],
        feed_sums[3],
        feed_sums[4],
        feed_sums[5],
        feed_sums[6],
        feed_sums[7],
    )


def low_lanes(values):
    return lax.broadcasted_iota(jnp.int32, values.shape, 1) < HD


def swap_lanes(values):
    return pltpu.roll(values, HD, 1)


def low_pair(first, second):
    return jnp.where(low_lanes(first), first, swap_lanes(second))


def high_pair(first, second):
    return jnp.where(low_lanes(first), swap_lanes(first), second)


def side_pair(side, first, second):
    return low_pair(first, second) if side == 0 else high_pair(first, second)


def dot_nn(left, right):
    return jnp.dot(left, right, preferred_element_type=F32)


def dot_nt(left, right):
    return lax.dot_general(left, right, (((1,), (1,)), ((), ())), preferred_element_type=F32)


def dot_tn(left, right):
    return lax.dot_general(left, right, (((0,), (0,)), ((), ())), preferred_element_type=F32)


class Place:
    def __init__(self):
        self.c = lax.axis_index("ctx")
        self.f = lax.axis_index("fsdp")
        self.group = self.c // H
        self.head = self.c % H
        self.inside = jnp.where(self.group == self.f, 1, 0)

    def is_me(self, tc, tf):
        return jnp.logical_and(self.c == tc, self.f == tf)

    def signal(self, barrier, tc, tf):
        @pl.when(jnp.logical_not(self.is_me(tc, tf)))
        def _():
            pl.semaphore_signal(barrier, 1, device_id=(tc, tf), device_id_type=MESH)

    def turn(self, i, n):
        return (self.c + 5 * i) % n

    def greet_sources(self, n_ctx, partner):
        barrier = pltpu.get_barrier_semaphore()
        for tc in range(n_ctx):
            self.signal(barrier, tc, self.group)
        if partner:
            pl.semaphore_signal(
                barrier, 1, device_id=(self.c, 1 - self.f), device_id_type=MESH
            )
        pl.semaphore_wait(barrier, 2 * H + (1 if partner else 0) - self.inside)

    def greet_owners(self, n_ctx, partner, more=0):
        barrier = pltpu.get_barrier_semaphore()
        for head in range(H):
            for core in range(2):
                self.signal(barrier, self.f * H + head, core)
        if partner:
            pl.semaphore_signal(
                barrier, 1, device_id=(self.c, 1 - self.f), device_id_type=MESH
            )
        pl.semaphore_wait(barrier, n_ctx + (1 if partner else 0) + more - self.inside)

    def send(self, src, dst, send_sem, recv_sem, tc, tf):
        me = self.is_me(tc, tf)

        @pl.when(me)
        def _():
            pltpu.make_async_copy(src, dst, recv_sem).start()

        @pl.when(jnp.logical_not(me))
        def _():
            self.remote(src, dst, send_sem, recv_sem, tc, tf).start()

    def remote(self, src, dst, send_sem, recv_sem, tc, tf):
        return pltpu.make_async_remote_copy(
            src_ref=src,
            dst_ref=dst,
            send_sem=send_sem,
            recv_sem=recv_sem,
            device_id=(tc, tf),
            device_id_type=MESH,
        )

    def wait_sent(self, src, dst, send_sem, recv_sem, tc, tf):
        @pl.when(jnp.logical_not(self.is_me(tc, tf)))
        def _():
            self.remote(src, dst, send_sem, recv_sem, tc, tf).wait_send()


VECTORS = 10


def project_kernel(
    n_ctx,
    x_hbm,
    wq_hbm,
    wk_hbm,
    wv_hbm,
    order_hbm,
    seq_hbm,
    *rest,
):
    dense_hbm, rest = rest[:3], rest[3:]
    vector_hbm, rest = rest[: VECTORS + 1], rest[VECTORS + 1 :]
    vector_in, rest = rest[-VECTORS - 1 :], rest[: -VECTORS - 1]
    (
        q_out,
        kv_out,
        w_other,
        order_out,
        seq_out,
        vec_out,
        expand_out,
        wo_other,
        we_other,
        ws_other,
        x_in,
        w_own,
        w_in,
        bias_own,
        bias_in,
        order_own,
        seq_own,
        order_in,
        seq_in,
        q_send,
        kv_send,
        load_sem,
        w_ss,
        w_rs,
        q_ss,
        q_rs,
        kv_ss,
        kv_rs,
        relay_ss,
        relay_rs,
    ) = rest
    at = Place()
    other = 1 - at.f
    loads = [
        pltpu.make_async_copy(src, dst, load_sem.at[i])
        for i, (src, dst) in enumerate(
            (
                (x_hbm, x_in),
                (wq_hbm, w_own.at[0]),
                (wk_hbm, w_own.at[1]),
                (wv_hbm, w_own.at[2]),
                (order_hbm, order_own),
                (seq_hbm, seq_own),
                *zip(vector_hbm, vector_in),
            )
        )
    ]
    for load in loads:
        load.start()
    at.greet_sources(n_ctx, True)
    wide = bias_own.shape[1]
    swaps = [
        at.remote(src, dst, w_ss.at[i], w_rs.at[i], at.c, other)
        for i, (src, dst) in enumerate(
            (
                (wq_hbm, w_in.at[0]),
                (wk_hbm, w_in.at[1]),
                (wv_hbm, w_in.at[2]),
                (order_hbm, order_in),
                (seq_hbm, seq_in),
                (bias_own, bias_in),
            )
        )
    ]
    for swap in swaps[:-1]:
        swap.start()
    for load in loads:
        load.wait()
    for row, ref in enumerate(vector_in[:VECTORS]):
        bias_own[row : row + 1, :] = ref[...].astype(F32).reshape(1, wide)
    for part in range(vector_in[VECTORS].shape[0] // wide):
        piece = vector_in[VECTORS][part * wide : part * wide + wide]
        bias_own[VECTORS + part : VECTORS + part + 1, :] = piece.astype(F32).reshape(1, wide)
    swaps[-1].start()

    def moves(half):
        for i in range(H // 2):
            head = half * (H // 2) + at.turn(i, H // 2)
            for core in range(2):
                slot = head * 2 + core
                yield (
                    kv_send.at[head, pl.ds(core * BLK, BLK)],
                    kv_out.at[2 * at.c + core],
                    kv_ss.at[slot],
                    kv_rs.at[at.c],
                    at.f * H + head,
                    core,
                )
                yield (
                    q_send.at[head, core],
                    q_out.at[at.c],
                    q_ss.at[slot],
                    q_rs.at[at.c],
                    at.f * H + head,
                    core,
                )

    def one_half(half, wq, wk, wv, bias):
        low = x_in[...].astype(BF16)
        q = dot_nn(low, wq[...]) + bias[0:1, :]
        k = dot_nn(low, wk[...])
        v = dot_nn(low, wv[...]) + bias[1:2, :]
        for pair in range(2):
            columns = slice(pair * 128, pair * 128 + 128)
            for side in range(2):
                head = half * (H // 2) + 2 * pair + side
                kv_send[head] = side_pair(side, k[:, columns], v[:, columns]).astype(BF16)
                for core in range(2):
                    rows = slice(core * HALF, core * HALF + HALF)
                    late = slice(BLK + core * HALF, BLK + core * HALF + HALF)
                    q_send[head, core] = side_pair(side, q[rows, columns], q[late, columns]).astype(
                        BF16
                    )
        for move in moves(half):
            at.send(*move)

    one_half(at.f, w_own.at[0], w_own.at[1], w_own.at[2], bias_own)
    for swap in swaps:
        swap.wait()
    one_half(other, w_in.at[0], w_in.at[1], w_in.at[2], bias_in)
    dense_swaps = [
        at.remote(src, dst, w_ss.at[6 + i], w_rs.at[6 + i], at.c, other)
        for i, (src, dst) in enumerate(zip(dense_hbm, (wo_other, we_other, ws_other)))
    ]
    for swap in dense_swaps:
        swap.start()
    w_other[...] = w_in[...]
    inside = at.inside == 1
    order_out[...] = jnp.where(inside, order_own[...], order_in[...])
    seq_out[...] = jnp.where(inside, seq_own[...], seq_in[...])
    vec_out[...] = whole_rows(bias_own[...], bias_in[...], at.f == 0)
    for row, source in enumerate((bias_own, bias_in)):
        for part in range(expand_out.shape[1] // wide):
            at_row = VECTORS + part
            expand_out[row : row + 1, part * wide : part * wide + wide] = source[
                at_row : at_row + 1, :
            ]

    def relay(source):
        mine = kv_out.at[2 * source + at.f]
        return at.remote(mine, mine, relay_ss.at[source], relay_rs.at[source], at.c, other)

    def relay_in(source):
        theirs = kv_out.at[2 * source + other]
        return at.remote(theirs, theirs, relay_ss.at[source], relay_rs.at[source], at.c, other)

    for source in range(n_ctx):
        arrived = kv_out.at[2 * source + at.f]
        at.remote(arrived, arrived, kv_ss.at[0], kv_rs.at[source], at.c, other).wait_recv()
        relay(source).start()
    for half in (at.f, other):
        for move in moves(half):
            at.wait_sent(*move)
    for source in range(n_ctx):
        arrived = q_out.at[source]
        at.remote(arrived, arrived, q_ss.at[0], q_rs.at[source], at.c, other).wait_recv()
        relay_in(source).wait_recv()
    for source in range(n_ctx):
        relay(source).wait_send()
    for swap in dense_swaps:
        swap.wait()


def project_and_scatter(n_ctx, x, wq, wk, wv, order, seqs, dense_weights, vectors):
    wide = wq.shape[1]
    blocks = order.shape[1]
    units = vectors[VECTORS].shape[0]
    bias_rows = VECTORS + units // wide
    return pl.pallas_call(
        functools.partial(project_kernel, n_ctx),
        out_shape=(
            jax.ShapeDtypeStruct((n_ctx, HALF, 128), BF16),
            jax.ShapeDtypeStruct((2 * n_ctx, BLK, 128), BF16),
            jax.ShapeDtypeStruct((3, D, wide), BF16),
            jax.ShapeDtypeStruct((1, blocks), jnp.int32),
            jax.ShapeDtypeStruct((1, blocks), jnp.int32),
            jax.ShapeDtypeStruct((bias_rows, D), F32),
            jax.ShapeDtypeStruct((2, units), F32),
            *[jax.ShapeDtypeStruct(w.shape, BF16) for w in dense_weights],
        ),
        in_specs=[ANY] * (10 + VECTORS),
        out_specs=(ANY, ANY) + (VMEM,) * 5 + (ANY,) * 3,
        scratch_shapes=[
            pltpu.VMEM((2 * BLK, D), F32),
            pltpu.VMEM((3, D, wide), BF16),
            pltpu.VMEM((3, D, wide), BF16),
            pltpu.VMEM((bias_rows, wide), F32),
            pltpu.VMEM((bias_rows, wide), F32),
            pltpu.VMEM((1, blocks), jnp.int32),
            pltpu.VMEM((1, blocks), jnp.int32),
            pltpu.VMEM((1, blocks), jnp.int32),
            pltpu.VMEM((1, blocks), jnp.int32),
            pltpu.VMEM((H, 2, HALF, 128), BF16),
            pltpu.VMEM((H, 2 * BLK, 128), BF16),
            pltpu.SemaphoreType.DMA((7 + VECTORS,)),
            pltpu.SemaphoreType.DMA((9,)),
            pltpu.SemaphoreType.DMA((9,)),
            pltpu.SemaphoreType.DMA((2 * H,)),
            pltpu.SemaphoreType.DMA((n_ctx,)),
            pltpu.SemaphoreType.DMA((2 * H,)),
            pltpu.SemaphoreType.DMA((n_ctx,)),
            pltpu.SemaphoreType.DMA((n_ctx,)),
            pltpu.SemaphoreType.DMA((n_ctx,)),
        ]
        + [pltpu.VMEM(vector.shape, BF16) for vector in vectors],
        compiler_params=pltpu.CompilerParams(
            collective_id=0, has_side_effects=True, vmem_limit_bytes=ROOM
        ),
        name="project_scatter",
    )(x, wq, wk, wv, order, seqs, *dense_weights, *vectors)


def forward_kernel(
    blocks,
    order_ref,
    seq_ref,
    q_ref,
    kv_ref,
    o_ref,
    keep_ref,
    lse_ref,
    pairs_ref,
    place,
    q_low,
    peaks,
    masses,
    total,
    scores,
):
    def place_block(slot, _):
        place[order_ref[0, slot]] = slot
        return 0

    lax.fori_loop(0, blocks, place_block, 0)

    count = jnp.int32(0)
    for gap in range(1, LONG):
        for late in range(gap, blocks):
            pairs_ref[0, count] = place[late]
            pairs_ref[1, count] = place[late - gap]
            count = count + jnp.where(seq_ref[0, late] == seq_ref[0, late - gap], 1, 0)
    for spare in range(TOGETHER):
        pairs_ref[0, count + spare] = blocks
        pairs_ref[1, count + spare] = 0
    turns = (count + TOGETHER - 1) // TOGETHER
    pairs_ref[2, 0] = turns

    def unpack(step, _):
        for part in range(4):
            source = step * 4 + part
            packed = q_ref[source].astype(F32) * (HD**-0.5)
            low = low_lanes(packed)
            q_low[2 * source] = jnp.where(low, packed, 0.0).astype(BF16)
            q_low[2 * source + 1] = jnp.where(low, swap_lanes(packed), 0.0).astype(BF16)
        return 0

    lax.fori_loop(0, blocks // 8, unpack, 0)
    q_low[blocks] = jnp.zeros((HALF, 128), BF16)

    peaks[blocks] = jnp.zeros((HALF, 128), F32)
    masses[blocks] = jnp.zeros((HALF, 128), F32)
    total[blocks] = jnp.zeros((HALF, 128), F32)
    lse_ref[blocks] = jnp.zeros((HALF, 128), F32)

    def own_slots(step):
        return [(step * TOGETHER + part,) * 2 for part in range(TOGETHER)]

    def pair_slots(step):
        return [
            (pairs_ref[0, step * TOGETHER + part], pairs_ref[1, step * TOGETHER + part])
            for part in range(TOGETHER)
        ]

    def score(slots, base):
        results = []
        for part, (q_slot, k_slot) in enumerate(slots):
            result = dot_nt(q_low[q_slot], kv_ref[k_slot])
            scores[base + part] = result
            results.append(jnp.maximum(result[:, :128], result[:, 128:]))
        return results

    def score_own(step, _):
        slots = own_slots(step)
        for (q_slot, _), result in zip(slots, score(slots, step * TOGETHER)):
            peaks[q_slot] = result
        return 0

    def score_pairs(step, _):
        slots = pair_slots(step)
        for (q_slot, _), result in zip(slots, score(slots, blocks + step * TOGETHER)):
            peaks[q_slot] = jnp.maximum(peaks[q_slot], result)
        return 0

    lax.fori_loop(0, blocks // TOGETHER, score_own, 0)
    lax.fori_loop(0, turns, score_pairs, 0)

    def level(step, _):
        for part in range(4):
            slot = step * 4 + part
            peaks[slot] = jnp.broadcast_to(
                jnp.max(peaks[slot], axis=1, keepdims=True), (HALF, 128)
            )
        return 0

    lax.fori_loop(0, blocks // 4, level, 0)

    def weigh(slots, base):
        results = []
        for part, (q_slot, k_slot) in enumerate(slots):
            peak = peaks[q_slot]
            left = jnp.exp(scores[base + part, :, :128] - peak)
            right = jnp.exp(scores[base + part, :, 128:] - peak)
            weights = jnp.concatenate([left, right], axis=1).astype(BF16)
            results.append((left + right, dot_nn(weights, kv_ref[k_slot])))
        return results

    def weigh_own(step, _):
        slots = own_slots(step)
        for (q_slot, _), (mass, result) in zip(slots, weigh(slots, step * TOGETHER)):
            masses[q_slot] = mass
            total[q_slot] = result
        return 0

    def weigh_pairs(step, _):
        slots = pair_slots(step)
        for (q_slot, _), (mass, result) in zip(slots, weigh(slots, blocks + step * TOGETHER)):
            masses[q_slot] = masses[q_slot] + mass
            total[q_slot] = total[q_slot] + result
        return 0

    lax.fori_loop(0, blocks // TOGETHER, weigh_own, 0)
    lax.fori_loop(0, turns, weigh_pairs, 0)

    def finish(step, _):
        for part in range(4):
            source = step * 4 + part
            for side in range(2):
                slot = 2 * source + side
                mass = jnp.broadcast_to(
                    jnp.sum(masses[slot], axis=1, keepdims=True), (HALF, 128)
                )
                result = total[slot] / mass
                lse_ref[slot] = peaks[slot] + jnp.log(mass)
                packed = high_pair(result[: HALF // 2], result[HALF // 2 :])
                keep_ref[source, side] = packed
                o_ref[source, side] = packed.astype(BF16)
        return 0

    lax.fori_loop(0, blocks // 8, finish, 0)


def pair_room(blocks):
    return blocks * MOST // 2 + 2 * TOGETHER


def attend(order, seqs, q, kv):
    blocks = kv.shape[0]
    room = pair_room(blocks)
    return pl.pallas_call(
        functools.partial(forward_kernel, blocks),
        out_shape=(
            jax.ShapeDtypeStruct((blocks // 2, 2, HALF // 2, 128), BF16),
            jax.ShapeDtypeStruct((blocks // 2, 2, HALF // 2, 128), F32),
            jax.ShapeDtypeStruct((blocks + 1, HALF, 128), F32),
            jax.ShapeDtypeStruct((3, room), jnp.int32),
        ),
        in_specs=[SMEM, SMEM, VMEM, VMEM],
        out_specs=(VMEM, VMEM, VMEM, SMEM),
        scratch_shapes=[
            pltpu.SMEM((blocks,), jnp.int32),
            pltpu.VMEM((blocks + 1, HALF, 128), BF16),
            pltpu.VMEM((blocks + 1, HALF, 128), F32),
            pltpu.VMEM((blocks + 1, HALF, 128), F32),
            pltpu.VMEM((blocks + 1, HALF, 128), F32),
            pltpu.VMEM((room, HALF, BLK), F32),
        ],
        compiler_params=pltpu.CompilerParams(vmem_limit_bytes=ROOM),
        name="attend",
    )(order, seqs, q, kv)


def backward_kernel(
    blocks,
    pairs_ref,
    q_ref,
    tan_ref,
    keep_ref,
    lse_ref,
    kv_ref,
    pass_a,
    pass_b,
    dq_ref,
    dkv_sum,
    out_a,
    out_b,
    both,
    turned,
    deltas,
    dq_sum,
    held,
    pass_sem,
):
    fetches = [
        pltpu.make_async_copy(src, held.at[i], pass_sem.at[i])
        for i, src in enumerate((pass_a, pass_b))
    ]
    passes = [
        pltpu.make_async_copy(held.at[i], dst, pass_sem.at[2 + i])
        for i, dst in enumerate((out_a, out_b))
    ]
    for fetch in fetches:
        fetch.start()

    def unpack(step, _):
        for part in range(4):
            source = step * 4 + part
            packed = q_ref[source].astype(F32) * (HD**-0.5)
            low = low_lanes(packed)
            for side in range(2):
                slot = 2 * source + side
                q = packed if side == 0 else swap_lanes(packed)
                both[slot, 0:HALF] = jnp.where(low, q, 0.0).astype(BF16)
                tangent = tan_ref[source, side].astype(F32)
                first = low_lanes(tangent)
                both[slot, HALF : HALF + HALF // 2] = jnp.where(
                    first, 0.0, swap_lanes(tangent)
                ).astype(BF16)
                both[slot, HALF + HALF // 2 : BLK] = jnp.where(first, 0.0, tangent).astype(BF16)
                turned[slot] = jnp.transpose(both[slot])
                product = tangent * keep_ref[source, side]
                delta = jnp.concatenate(
                    [
                        jnp.sum(jnp.where(first, product, 0.0), axis=1, keepdims=True),
                        jnp.sum(jnp.where(first, 0.0, product), axis=1, keepdims=True),
                    ],
                    axis=0,
                )
                deltas[slot] = jnp.broadcast_to(delta, (HALF, 128))
        return 0

    lax.fori_loop(0, blocks // 8, unpack, 0)
    both[blocks] = jnp.zeros((BLK, 128), BF16)
    turned[blocks] = jnp.zeros((128, BLK), BF16)
    deltas[blocks] = jnp.zeros((HALF, 128), F32)
    dq_sum[blocks] = jnp.zeros((HALF, 128), F32)

    def one_pair(q_slot, k_slot):
        kv = kv_ref[k_slot]
        products = dot_nt(both[q_slot], kv)
        mass, delta = lse_ref[q_slot], deltas[q_slot]
        weights = jnp.exp(products[:HALF] - jnp.concatenate([mass, mass], axis=1))
        score_tan = weights * (products[HALF:] - jnp.concatenate([delta, delta], axis=1))
        score_tan = score_tan.astype(BF16)
        sides = jnp.concatenate([score_tan, weights.astype(BF16)], axis=0)
        return dot_nn(turned[q_slot], sides), dot_nn(score_tan, kv)

    def own_turn(step, _):
        slots = [step * TOGETHER + part for part in range(TOGETHER)]
        results = [one_pair(slot, slot) for slot in slots]
        for slot, (dkv, dq) in zip(slots, results):
            dkv_sum[slot] = dkv
            dq_sum[slot] = dq
        return 0

    def pair_turn(step, _):
        slots = [
            (pairs_ref[0, step * TOGETHER + part], pairs_ref[1, step * TOGETHER + part])
            for part in range(TOGETHER)
        ]
        results = [one_pair(*slot) for slot in slots]
        for (q_slot, k_slot), (dkv, dq) in zip(slots, results):
            dkv_sum[k_slot] = dkv_sum[k_slot] + dkv
            dq_sum[q_slot] = dq_sum[q_slot] + dq
        return 0

    lax.fori_loop(0, blocks // TOGETHER, own_turn, 0)
    for fetch, move in zip(fetches, passes):
        fetch.wait()
        move.start()
    lax.fori_loop(0, pairs_ref[2, 0], pair_turn, 0)

    def finish_rows(step, _):
        for part in range(4):
            source = step * 4 + part
            packed = low_pair(dq_sum[2 * source], dq_sum[2 * source + 1]) * (HD**-0.5)
            dq_ref[source] = packed.astype(BF16)
        return 0

    lax.fori_loop(0, blocks // 8, finish_rows, 0)
    for move in passes:
        move.wait()


def attend_back(pairs, q, tangent, keep, lse, kv, passed):
    blocks = kv.shape[0]
    return pl.pallas_call(
        functools.partial(backward_kernel, blocks),
        out_shape=(
            jax.ShapeDtypeStruct((blocks // 2, HALF, 128), BF16),
            jax.ShapeDtypeStruct((blocks, 128, BLK), F32),
            jax.ShapeDtypeStruct(passed[0].shape, F32),
            jax.ShapeDtypeStruct(passed[1].shape, F32),
        ),
        in_specs=[SMEM, VMEM, VMEM, VMEM, VMEM, VMEM, ANY, ANY],
        out_specs=(VMEM, VMEM, ANY, ANY),
        scratch_shapes=[
            pltpu.VMEM((blocks + 1, BLK, 128), BF16),
            pltpu.VMEM((blocks + 1, 128, BLK), BF16),
            pltpu.VMEM((blocks + 1, HALF, 128), F32),
            pltpu.VMEM((blocks + 1, HALF, 128), F32),
            pltpu.VMEM((2,) + passed[0].shape, F32),
            pltpu.SemaphoreType.DMA((4,)),
        ],
        compiler_params=pltpu.CompilerParams(vmem_limit_bytes=ROOM),
        name="attend_back",
    )(pairs, q, tangent, keep, lse, kv, *passed)


def pieces_of(start, size, body):
    piece = max(n for n in range(16, 289, 16) if size % n == 0)
    lax.fori_loop(
        0,
        size // piece,
        lambda i, _: (body(i * piece, span(start + i * piece, piece), piece), 0)[1],
        0,
    )


def span(start, size):
    return pl.ds(pl.multiple_of(start, 16), size)


def step_of(c, stride):
    bit = (c // stride) % 2
    return bit, c + stride * (1 - 2 * bit)


REGIONS = 4


def columns_of(region):
    wide = D // (REGIONS // 2)
    return slice(region // 2 * wide, region // 2 * wide + wide)


class Ladder:
    def __init__(self, at, plans, starts, size, acc, stage, landing, out, sems, bases=(0, 0)):
        self.bases = bases
        self.at, self.acc, self.stage, self.landing, self.out = at, acc, stage, landing, out
        self.down_ss, self.down_rs, self.up_ss, self.up_rs = sems
        self.ranges = []
        for region in range(REGIONS):
            plan, start = plans[region % 2], starts[region % 2]
            listed, rows = [], size
            for bit, peer in plan[:-1]:
                rows = rows // 2
                listed.append((start + bit * rows, start + (1 - bit) * rows, rows, peer))
                start = start + bit * rows
            listed.append((start, start, rows, plan[-1][1]))
            self.ranges.append(listed)
        self.last = len(plans[0]) - 1

    def slot(self, region, step):
        return region * (self.last + 1) + step

    def down(self, region, step, sent):
        kept, given, size, peer = self.ranges[region][step]
        where, slot = span(given if sent else kept, size), self.slot(region, step)
        columns = columns_of(region)
        return self.at.remote(
            self.stage[region % 2].at[where, columns],
            self.landing[region % 2][step].at[where, columns],
            self.down_ss.at[slot],
            self.down_rs.at[slot],
            peer,
            self.at.f,
        )

    def up(self, region, step, sent):
        kept, given, size, peer = self.ranges[region][step]
        start = self.bases[region % 2] + (kept if sent else given)
        columns = columns_of(region)
        where, slot = span(start, size), self.slot(region, step)
        return self.at.remote(
            self.out.at[where, columns],
            self.out.at[where, columns],
            self.up_ss.at[slot],
            self.up_rs.at[slot],
            peer,
            self.at.f,
        )

    def join(self, region, start, size, arrived, target):
        columns, acc = columns_of(region), self.acc[region % 2]

        def body(offset, where, _):
            total = acc[where, columns] + arrived[where, columns].astype(F32)
            target[where, columns] = total.astype(target.dtype)

        pieces_of(start, size, body)

    def give(self, region, step, arrived):
        kept, given, size, _ = self.ranges[region][step]
        self.join(region, given, size, arrived, self.stage[region % 2])
        self.down(region, step, True).start()
        if step < self.last:
            self.join(region, kept, size, arrived, self.acc[region % 2])

    def settle(self, region):
        kept, _, size, _ = self.ranges[region][self.last]
        arrived = self.landing[region % 2][self.last]
        columns, stage = columns_of(region), self.stage[region % 2]

        def body(offset, where, rows):
            total = stage[where, columns].astype(F32) + arrived[where, columns].astype(F32)
            row = span(self.bases[region % 2] + kept + offset, rows)
            self.out[row, columns] = total.astype(BF16)

        self.down(region, self.last, False).wait_recv()
        pieces_of(kept, size, body)
        self.up(region, self.last - 1, True).start()

    def wait_sent(self):
        for region in range(REGIONS):
            for step in range(self.last + 1):
                self.down(region, step, True).wait_send()
            for step in range(self.last):
                self.up(region, step, True).wait_send()


COLS = 512


def whole_rows(own, other, first):
    return jnp.where(
        first,
        jnp.concatenate([own, other], axis=1),
        jnp.concatenate([other, own], axis=1),
    )


def row_mean(values):
    return jnp.mean(values, axis=1, keepdims=True)


def normalize(values):
    centre = values - row_mean(values)
    scale = lax.rsqrt(row_mean(centre * centre) + norm_eps)
    return centre * scale, scale


def norm_back(tangent, normed, scale, gain):
    pushed = tangent * gain
    return scale * (pushed - row_mean(pushed) - normed * row_mean(pushed * normed))


def column_sum(values):
    return jnp.sum(values, axis=0, keepdims=True)


def feed_slopes(kind, target, mixed, low_turned, hidden, before_tan, feed_tan, branch_tan):
    unit_count = hidden.shape[2] // COLS

    def chunk_slopes(chunk, _):
        columns = pl.ds(pl.multiple_of(chunk * COLS, COLS), COLS)
        target[columns, :] = dot_tn(hidden[kind, :, columns], feed_tan[...]).astype(target.dtype)
        below = pl.ds(pl.multiple_of((unit_count + chunk) * COLS, COLS), COLS)
        target[below, :] = dot_nn(low_turned[...], before_tan[kind, :, columns]).astype(
            target.dtype
        )
        return 0

    lax.fori_loop(0, unit_count, chunk_slopes, 0)
    start = 2 * unit_count * COLS
    target[start : start + D // 2, :] = dot_tn(mixed[kind], branch_tan[...]).astype(target.dtype)


def middle_kernel(
    n_ctx,
    o_hbm, x_hbm, sum_hbm, cot_hbm, wo_a, wo_b, we_a, we_b, ws_a, ws_b, be_ref, vec_in,
    out_hbm, sum_tan_hbm, entry_hbm, tan_out, vec_ref, stage_a, stage_b, keep_ref,
    o_in, x_ref, sum_ref, cot_ref, wo, we, ws, out_ref, sum_tan_ref, entry_ref,
    mixed, low, hidden, before_tan, feed_tan, branch_tan, slope, mixed_tan, tan_send,
    own_grads, send_grads, first_in, low_turned,
    load_sem, store_sem, o_ss, o_rs, tan_ss, tan_rs, core_ss, core_rs,
):
    at = Place()
    f = at.f
    other = 1 - f
    halves = (f, other)
    piece = HALF // 2
    loads = [
        pltpu.make_async_copy(src, dst, load_sem.at[i])
        for i, (src, dst) in enumerate(
            (
                (x_hbm, x_ref),
                (wo_a, wo.at[0]),
                (wo_b, wo.at[1]),
                (we_a, we.at[0]),
                (we_b, we.at[1]),
                (ws_a, ws.at[0]),
                (ws_b, ws.at[1]),
                (sum_hbm, sum_ref),
                (cot_hbm, cot_ref),
            )
        )
    ]
    for load in loads:
        load.start()
    barrier = pltpu.get_barrier_semaphore()
    for target in range(n_ctx):
        at.signal(barrier, target, at.group)
    at.greet_owners(n_ctx, True, 2 * H - at.inside)

    def o_move(target, side):
        return (
            o_hbm.at[target, side],
            o_in.at[side, at.head, f],
            o_ss.at[2 * target + side],
            o_rs.at[side * 2 * H + at.head * 2 + f],
            target,
            at.group,
        )

    def tan_move(side, head, core):
        return (
            tan_send.at[side, head, core],
            tan_out.at[at.c, side],
            tan_ss.at[side * 2 * H + head * 2 + core],
            tan_rs.at[at.c * 2 + side],
            f * H + head,
            core,
        )

    for side in range(2):
        for i in range(n_ctx):
            at.send(*o_move(at.turn(i, n_ctx), side))
    vec_ref[...] = jnp.zeros_like(vec_ref)
    vectors = vec_in[...]
    (out_bias, gain_one, shift_one, shrink_bias, gain_two, shift_two, gain_last, shift_last) = (
        vectors[i : i + 1] for i in range(2, 10)
    )
    be = (be_ref.at[0:1], be_ref.at[1:2])
    for load in loads:
        load.wait()

    def stores(step):
        rows = pl.ds(pl.multiple_of(step * BLK, BLK), BLK)
        return [
            pltpu.make_async_copy(src.at[rows], dst.at[rows], store_sem.at[3 * step + i])
            for i, (src, dst) in enumerate(
                ((out_ref, out_hbm), (sum_tan_ref, sum_tan_hbm), (entry_ref, entry_hbm))
            )
        ]

    def tile(step, _):
        first_row = pl.multiple_of(step * BLK, BLK)
        rows = pl.ds(first_row, BLK)
        for head in range(H):
            for core in range(2):
                arrived = o_in.at[step, head, core]
                at.remote(
                    arrived, arrived, o_ss.at[0], o_rs.at[step * 2 * H + head * 2 + core],
                    at.c, other,
                ).wait_recv()
        for kind in range(2):
            for pair in range(2):
                head = halves[kind] * (H // 2) + 2 * pair
                columns = slice(pair * 128, pair * 128 + 128)
                for core in range(2):
                    early = o_in[step, head, core].astype(F32)
                    late = o_in[step, head + 1, core].astype(F32)
                    for part in range(2):
                        start = pl.multiple_of(first_row + core * HALF + part * piece, piece)
                        mixed[kind, pl.ds(start, piece), columns] = side_pair(
                            part, early, late
                        ).astype(BF16)
        branch = dot_nn(mixed[0, rows, :], wo[0]) + dot_nn(mixed[1, rows, :], wo[1]) + out_bias
        n_one, scale_one = normalize(x_ref[rows, :] + branch)
        normed_one = n_one * gain_one + shift_one
        stream_one = sum_ref[rows, :] + branch
        normed_low = normed_one.astype(BF16)
        low[rows, :] = normed_low
        feed = jnp.zeros((BLK, D), F32)
        for kind in range(2):

            def expand(chunk, carried):
                columns = slice(chunk * COLS, chunk * COLS + COLS)
                v = dot_nn(normed_low, we[kind, :, columns]) + be[kind][:, columns]
                square = v * v
                t = jnp.tanh(gelu_coeff * (v + gelu_cubic * square * v))
                half_up = 0.5 + 0.5 * t
                hidden_part = (v * half_up).astype(BF16)
                hidden[kind, rows, columns] = hidden_part
                slope[kind, :, columns] = half_up + v * half_up * (1.0 - t) * (
                    gelu_coeff + (3.0 * gelu_coeff * gelu_cubic) * square
                )
                return carried + dot_nn(hidden_part, ws[kind, columns, :])

            for chunk in range(ws.shape[1] // COLS):
                feed = expand(chunk, feed)
        feed_out = feed + shrink_bias
        n_two, scale_two = normalize(normed_one + feed_out)
        n_last, scale_last = normalize(stream_one + feed_out)
        out_ref[rows, :] = (n_two * gain_two + shift_two) + (n_last * gain_last + shift_last)
        u = cot_ref[rows, :]
        nudge = column_sum(u)
        sum_tan = norm_back(u, n_last, scale_last, gain_last)
        inflow = norm_back(u, n_two, scale_two, gain_two)
        sum_tan_ref[rows, :] = sum_tan
        feed_low = (sum_tan + inflow).astype(BF16)
        feed_tan[rows, :] = feed_low
        vec_ref[0:1, :] += column_sum(feed_low.astype(F32))
        vec_ref[1:2, :] += column_sum(u * n_two)
        vec_ref[2:3, :] += nudge
        vec_ref[3:4, :] += column_sum(u * n_last)
        vec_ref[4:5, :] += nudge
        normed_tan = inflow
        for kind in range(2):

            def expand_back(chunk, carried):
                columns = slice(chunk * COLS, chunk * COLS + COLS)
                pushed = dot_nt(feed_low, ws[kind, columns, :])
                tan_part = (pushed * slope[kind, :, columns]).astype(BF16)
                before_tan[kind, rows, columns] = tan_part
                vec_row = pl.ds(8 + 2 * halves[kind] + chunk, 1)
                vec_ref[vec_row, :] += column_sum(tan_part.astype(F32))
                return carried + dot_nt(tan_part, we[kind, :, columns])

            for chunk in range(ws.shape[1] // COLS):
                normed_tan = expand_back(chunk, normed_tan)
        vec_ref[5:6, :] += column_sum(normed_tan * n_one)
        vec_ref[6:7, :] += column_sum(normed_tan)
        entry = norm_back(normed_tan, n_one, scale_one, gain_one)
        entry_ref[rows, :] = entry
        branch_low = (sum_tan + entry).astype(BF16)
        branch_tan[rows, :] = branch_low
        vec_ref[7:8, :] += column_sum(branch_low.astype(F32))
        for kind in range(2):
            mixed_tan[kind] = dot_nt(branch_low, wo[kind])
        for kind in range(2):
            for pair in range(2):
                columns = slice(pair * 128, pair * 128 + 128)
                for side in range(2):
                    head = halves[kind] * (H // 2) + 2 * pair + side
                    for core in range(2):
                        start = core * HALF
                        early = mixed_tan[kind, start : start + piece, columns]
                        late = mixed_tan[kind, start + piece : start + HALF, columns]
                        tan_send[step, head, core] = side_pair(side, early, late).astype(BF16)
        for i in range(H):
            for core in range(2):
                at.send(*tan_move(step, at.turn(i, H), core))
        for store in stores(step):
            store.start()
        return 0

    lax.fori_loop(0, 2, tile, 0)

    quarter = first_in.shape[0] // 4
    bits = (step_of(at.c, 1)[0], step_of(at.c, 2)[0])
    stages = (stage_a, stage_b)

    def core_move(region, give):
        bit = bits[region]
        start = region * 2 * quarter + (1 - bit if give else bit) * quarter
        where = span(start, quarter)
        slot = region + 2 * (0 if give else 1)
        return start, at.remote(
            send_grads.at[where], first_in.at[where], core_ss.at[slot], core_rs.at[slot],
            at.c, other,
        )

    order = [(0, True), (1, True), (0, False), (1, False)]
    low_turned[...] = jnp.transpose(low[...])
    operands = (mixed, low_turned, hidden, before_tan, feed_tan, branch_tan)
    feed_slopes(1, send_grads, *operands)
    for step in order:
        core_move(*step)[1].start()
    feed_slopes(0, own_grads, *operands)
    for side in range(2):
        for target in range(n_ctx):
            at.wait_sent(*o_move(target, side))
    for region, give in order:
        start, move = core_move(region, give)
        move.wait_recv()

        def join(offset, where, size):
            total = own_grads[where, :] + first_in[where, :].astype(F32)
            if give:
                stages[region][span(offset, size), :] = total.astype(BF16)
            else:
                keep_ref[region, span(offset, size), :] = total

        pieces_of(start, quarter, join)
    for source in range(n_ctx):
        for side in range(2):
            arrived = tan_out.at[source, side]
            at.remote(
                arrived, arrived, tan_ss.at[0], tan_rs.at[source * 2 + side], at.c, other
            ).wait_recv()
    for step in range(2):
        for store in stores(step):
            store.wait()
    for side in range(2):
        for head in range(H):
            for core in range(2):
                at.wait_sent(*tan_move(side, head, core))
    for step in order:
        core_move(*step)[1].wait_send()


def middle(n_ctx, o, x, summed, cotangent, wo, we, ws, be, vec):
    tokens, wide, units = x.shape[0], D // 2, ws[0].shape[0]
    grad_rows = 2 * units + wide
    rows = jax.ShapeDtypeStruct((tokens, D), F32)

    def sems(*counts):
        return [pltpu.SemaphoreType.DMA((count,)) for count in counts]

    return pl.pallas_call(
        functools.partial(middle_kernel, n_ctx),
        out_shape=(
            rows,
            rows,
            rows,
            jax.ShapeDtypeStruct((n_ctx, 2, HALF // 2, 128), BF16),
            jax.ShapeDtypeStruct((16, D), F32),
            jax.ShapeDtypeStruct((grad_rows // 4, D), BF16),
            jax.ShapeDtypeStruct((grad_rows // 4, D), BF16),
            jax.ShapeDtypeStruct((2, grad_rows // 4, D), F32),
        ),
        in_specs=[ANY] * 10 + [VMEM] * 2,
        out_specs=(ANY,) * 4 + (VMEM,) * 4,
        scratch_shapes=[
            pltpu.VMEM((2, H, 2, HALF // 2, 128), BF16),
            pltpu.VMEM((tokens, D), F32),
            pltpu.VMEM((tokens, D), F32),
            pltpu.VMEM((tokens, D), F32),
            pltpu.VMEM((2, wide, D), BF16),
            pltpu.VMEM((2, D, units), BF16),
            pltpu.VMEM((2, units, D), BF16),
            pltpu.VMEM((tokens, D), F32),
            pltpu.VMEM((tokens, D), F32),
            pltpu.VMEM((tokens, D), F32),
            pltpu.VMEM((2, tokens, wide), BF16),
            pltpu.VMEM((tokens, D), BF16),
            pltpu.VMEM((2, tokens, units), BF16),
            pltpu.VMEM((2, tokens, units), BF16),
            pltpu.VMEM((tokens, D), BF16),
            pltpu.VMEM((tokens, D), BF16),
            pltpu.VMEM((2, BLK, units), F32),
            pltpu.VMEM((2, BLK, wide), F32),
            pltpu.VMEM((2, H, 2, HALF // 2, 128), BF16),
            pltpu.VMEM((grad_rows, D), F32),
            pltpu.VMEM((grad_rows, D), BF16),
            pltpu.VMEM((grad_rows, D), BF16),
            pltpu.VMEM((D, tokens), BF16),
        ]
        + sems(9, 6, 2 * n_ctx, 4 * H, 4 * H, 2 * n_ctx, 4, 4),
        compiler_params=pltpu.CompilerParams(
            collective_id=1, has_side_effects=True, vmem_limit_bytes=ROOM
        ),
        name="middle",
    )(o, x, summed, cotangent, *wo, *we, *ws, be, vec)


def finish_kernel(
    n_ctx,
    dq_ref, dkv_ref, keep_hbm, land_a, land_b, x_hbm, entry_hbm, wq_hbm, wk_hbm, wv_hbm,
    w_other_hbm, vec_feed,
    post_ref, feed_ref, grads_ref, vec_out,
    own, part, ready, dq_in, dkv_in, keep, acc, stage, landing,
    x_in, entry_in, w_in, w_far, low_turned, tangents,
    own_grads, send_grads, first_in, acc_last, stage_last, landing_last, vec_sum, vec_in,
    load_sem, q_ss, q_rs, kv_ss, kv_rs, part_ss, part_rs, own_sem,
    down_ss, down_rs, up_ss, up_rs, top_ss, top_rs,
    core_ss, core_rs, down_ss2, down_rs2, up_ss2, up_rs2, vec_ss, vec_rs,
):
    at = Place()
    c, f = at.c, at.f
    other = 1 - f
    halves = (f, other)
    wide = D // 2
    loads = [
        pltpu.make_async_copy(src, dst, load_sem.at[i])
        for i, (src, dst) in enumerate(
            (
                (keep_hbm, keep),
                (x_hbm, x_in),
                (entry_hbm, entry_in),
                (wq_hbm, w_in.at[0]),
                (wk_hbm, w_in.at[1]),
                (wv_hbm, w_in.at[2]),
                (w_other_hbm, w_far),
            )
        )
    ]
    for load in loads:
        load.start()
    x_step, y_step, near, far = (step_of(c, stride) for stride in (1, 2, 4, 8))
    barrier = pltpu.get_barrier_semaphore()
    for _, peer in (x_step, y_step, near, far):
        pl.semaphore_signal(barrier, 1, device_id=(peer, f), device_id_type=MESH)
    at.greet_owners(n_ctx, True, 4)

    def partial_move(source):
        return at.remote(
            dkv_ref.at[2 * source + other],
            part.at[source],
            part_ss.at[source],
            part_rs.at[source],
            c,
            other,
        )

    def own_move(source):
        return pltpu.make_async_copy(
            dkv_ref.at[2 * source + f], own.at[source], own_sem.at[source]
        )

    def q_move(target):
        return (
            dq_ref.at[target],
            dq_in.at[at.head, f],
            q_ss.at[target],
            q_rs.at[at.head * 2 + f],
            target,
            at.group,
        )

    def kv_move(target):
        return (
            ready.at[target],
            dkv_in.at[at.head, pl.ds(pl.multiple_of(f * BLK, BLK), BLK)],
            kv_ss.at[target],
            kv_rs.at[at.head * 2 + f],
            target,
            at.group,
        )

    for i in range(n_ctx):
        source = at.turn(i, n_ctx)
        partial_move(source).start()
        own_move(source).start()
    for i in range(n_ctx):
        at.send(*q_move(at.turn(i, n_ctx)))

    size = keep.shape[1]
    firsts = (x_step, y_step)
    bases = [2 * size * region + firsts[region][0] * size for region in range(2)]
    feed = Ladder(
        at,
        ((y_step, near, far), (x_step, near, far)),
        (0, 0),
        size,
        [keep.at[region] for region in range(2)],
        [stage.at[region] for region in range(2)],
        [[landing.at[region, step] for step in range(3)] for region in range(2)],
        feed_ref,
        (down_ss, down_rs, up_ss, up_rs),
        bases,
    )

    def top_move(region, sent):
        side, columns = region % 2, columns_of(region)
        given = 2 * size * side + (1 - firsts[side][0]) * size
        where = span(bases[side] if sent else given, size)
        return at.remote(
            feed_ref.at[where, columns],
            feed_ref.at[where, columns],
            top_ss.at[region],
            top_rs.at[region],
            firsts[side][1],
            f,
        )

    loads[0].wait()
    kept_acc = [keep.at[region] for region in range(2)]
    sums = [acc.at[region] for region in range(2)]
    for region in range(REGIONS):
        first = (land_a, land_b)[region % 2]
        kept, given, half, _ = feed.ranges[region][0]
        feed.acc = kept_acc
        feed.join(region, given, half, first, stage.at[region % 2])
        feed.down(region, 0, True).start()
        feed.join(region, kept, half, first, sums[region % 2])
    feed.acc = sums
    for i in range(n_ctx):
        source = at.turn(i, n_ctx)
        own_move(source).wait()
        partial_move(source).wait_recv()
        ready[source] = jnp.transpose(own[source] + part[source]).astype(BF16)
        at.send(*kv_move(source))
    for load in loads[1:]:
        load.wait()
    low_turned[...] = jnp.transpose(x_in[...]).astype(BF16)
    for step in (1, 2):
        for region in range(REGIONS):
            feed.down(region, step - 1, False).wait_recv()
            feed.give(region, step, feed.landing[region % 2][step - 1])

    for target in range(n_ctx):
        partial_move(target).wait_send()
        at.wait_sent(*q_move(target))

    for head in range(H):
        for core in range(2):
            slot = head * 2 + core
            arrived = dq_in.at[head, core]
            at.remote(arrived, arrived, q_ss.at[0], q_rs.at[slot], c, other).wait_recv()
            arrived = dkv_in.at[head, pl.ds(core * BLK, BLK)]
            at.remote(arrived, arrived, kv_ss.at[0], kv_rs.at[slot], c, other).wait_recv()
    feed_rows = vec_feed.shape[0]
    vec_sum[0, 0:feed_rows] = vec_feed[...]
    vec_sum[0, feed_rows:] = jnp.zeros_like(vec_sum[0, feed_rows:])

    plans = ((x_step, y_step, near, far), (y_step, x_step, near, far))
    quarter = first_in.shape[0] // 4
    last = Ladder(
        at,
        plans,
        (0, 2 * quarter),
        2 * quarter,
        [acc_last, acc_last],
        [stage_last, stage_last],
        [[landing_last.at[step] for step in range(4)]] * 2,
        grads_ref,
        (down_ss2, down_rs2, up_ss2, up_rs2),
    )

    def core_move(region, give):
        kept, given, rows, _ = last.ranges[region][0]
        where = span(given if give else kept, rows)
        slot, columns = region + REGIONS * (0 if give else 1), columns_of(region)
        return at.remote(
            send_grads.at[where, columns],
            first_in.at[where, columns],
            core_ss.at[slot],
            core_rs.at[slot],
            c,
            other,
        )

    order = [(region, give) for give in (True, False) for region in range(REGIONS)]
    vec_peers = [(c, other)] + [(peer, f) for _, peer in (x_step, y_step, near, far)]

    def vec_move(step):
        return at.remote(
            vec_sum.at[step], vec_in.at[step], vec_ss.at[step], vec_rs.at[step], *vec_peers[step]
        )

    def vec_next(step):
        vec_move(step).wait_recv()
        target = vec_sum.at[step + 1] if step < 4 else vec_out
        target[...] = vec_sum[step] + vec_in[step]
        if step < 4:
            vec_move(step + 1).start()

    for kind, grad_ref in ((1, send_grads), (0, own_grads)):
        for pair in range(2):
            head = halves[kind] * (H // 2) + 2 * pair
            columns = slice(pair * 128, pair * 128 + 128)
            for core in range(2):
                early = dq_in[head, core].astype(F32)
                late = dq_in[head + 1, core].astype(F32)
                for side in range(2):
                    start = side * BLK + core * HALF
                    tangents[kind, 0, start : start + HALF, columns] = side_pair(
                        side, early, late
                    ).astype(BF16)
            early = dkv_in[head].astype(F32)
            late = dkv_in[head + 1].astype(F32)
            tangents[kind, 1, :, columns] = low_pair(early, late).astype(BF16)
            tangents[kind, 2, :, columns] = high_pair(early, late).astype(BF16)
        turned = low_turned[...]
        grad_ref[0:D, 0:wide] = dot_nn(turned, tangents[kind, 0]).astype(grad_ref.dtype)
        grad_ref[0:D, wide:D] = dot_nn(turned, tangents[kind, 1]).astype(grad_ref.dtype)
        value_grad = dot_nn(turned, tangents[kind, 2]).astype(grad_ref.dtype)
        grad_ref[D : D + wide, 0:wide] = value_grad[0:wide]
        grad_ref[D : D + wide, wide:D] = value_grad[wide:D]
        columns = pl.ds(pl.multiple_of(halves[kind] * wide, wide), wide)
        vec_sum[0, feed_rows : feed_rows + 1, columns] = column_sum(tangents[kind, 0].astype(F32))
        vec_sum[0, feed_rows + 1 : feed_rows + 2, columns] = column_sum(
            tangents[kind, 2].astype(F32)
        )
        if kind == 1:
            for step in order:
                core_move(*step).start()
    vec_move(0).start()
    for region in range(REGIONS):
        feed.settle(region)
    for region, give in order:
        core_move(region, give).wait_recv()
        kept, given, rows, _ = last.ranges[region][0]
        columns = columns_of(region)

        def join(offset, where, _):
            total = own_grads[where, columns] + first_in[where, columns].astype(F32)
            if give:
                stage_last[where, columns] = total.astype(BF16)
            else:
                acc_last[where, columns] = total

        pieces_of(given if give else kept, rows, join)
        if give:
            last.down(region, 0, True).start()
    vec_next(0)
    total = entry_in[...]
    for which in range(3):
        total = total + dot_nt(tangents[0, which], w_in[which])
        total = total + dot_nt(tangents[1, which], w_far[which])
    post_ref[...] = total
    for target in range(n_ctx):
        at.wait_sent(*kv_move(target))
    for step in order:
        core_move(*step).wait_send()
    for region in range(REGIONS):
        feed.up(region, 1, False).wait_recv()
        feed.up(region, 0, True).start()
    for step in (1, 2):
        for region in range(REGIONS):
            last.down(region, step - 1, False).wait_recv()
            last.give(region, step, last.landing[region % 2][step - 1])
        vec_next(step)
    for region in range(REGIONS):
        feed.up(region, 0, False).wait_recv()
        top_move(region, True).start()
    for region in range(REGIONS):
        last.down(region, 2, False).wait_recv()
        last.give(region, 3, last.landing[region % 2][2])
    vec_next(3)
    for region in range(REGIONS):
        last.settle(region)
    vec_next(4)
    for step in (2, 1, 0):
        for region in range(REGIONS):
            last.up(region, step, False).wait_recv()
            if step > 0:
                last.up(region, step - 1, True).start()
    for region in range(REGIONS):
        top_move(region, False).wait_recv()

    for step in range(5):
        vec_move(step).wait_send()
    for region in range(REGIONS):
        top_move(region, True).wait_send()
    feed.wait_sent()
    last.wait_sent()


def finish(n_ctx, dq, dkv, keep, land_a, land_b, x, entry, wq, wk, wv, w_other, vec_feed):
    size, tokens, wide = keep.shape[1], x.shape[0], D // 2
    last_shape = (D + wide, D)
    vec_shape = (vec_feed.shape[0] + 8, D)

    def sems(*counts):
        return [pltpu.SemaphoreType.DMA((count,)) for count in counts]

    return pl.pallas_call(
        functools.partial(finish_kernel, n_ctx),
        out_shape=(
            jax.ShapeDtypeStruct((tokens, D), F32),
            jax.ShapeDtypeStruct((4 * size, D), BF16),
            jax.ShapeDtypeStruct(last_shape, BF16),
            jax.ShapeDtypeStruct(vec_shape, F32),
        ),
        in_specs=[ANY, ANY, ANY, VMEM, VMEM] + [ANY] * 6 + [VMEM],
        out_specs=(VMEM,) * 4,
        scratch_shapes=[
            pltpu.VMEM((n_ctx, 128, BLK), F32),
            pltpu.VMEM((n_ctx, 128, BLK), F32),
            pltpu.VMEM((n_ctx, BLK, 128), BF16),
            pltpu.VMEM((H, 2, HALF, 128), BF16),
            pltpu.VMEM((H, 2 * BLK, 128), BF16),
            pltpu.VMEM((2, size, D), F32),
            pltpu.VMEM((2, size, D), F32),
            pltpu.VMEM((2, size, D), BF16),
            pltpu.VMEM((2, 3, size, D), BF16),
            pltpu.VMEM((tokens, D), F32),
            pltpu.VMEM((tokens, D), F32),
            pltpu.VMEM((3, D, wide), BF16),
            pltpu.VMEM((3, D, wide), BF16),
            pltpu.VMEM((D, tokens), BF16),
            pltpu.VMEM((2, 3, tokens, wide), BF16),
            pltpu.VMEM(last_shape, F32),
            pltpu.VMEM(last_shape, BF16),
            pltpu.VMEM(last_shape, BF16),
            pltpu.VMEM(last_shape, F32),
            pltpu.VMEM(last_shape, BF16),
            pltpu.VMEM((4,) + last_shape, BF16),
            pltpu.VMEM((5,) + vec_shape, F32),
            pltpu.VMEM((5,) + vec_shape, F32),
        ]
        + sems(7, n_ctx, 2 * H, n_ctx, 2 * H, n_ctx, n_ctx, n_ctx)
        + sems(12, 12, 12, 12, 4, 4, 8, 8, 16, 16, 16, 16, 5, 5),
        compiler_params=pltpu.CompilerParams(
            collective_id=3, has_side_effects=True, vmem_limit_bytes=ROOM
        ),
        name="finish",
    )(dq, dkv, keep, land_a, land_b, x, entry, wq, wk, wv, w_other, vec_feed)


def unpack_kernel(
    full, grads, post, vec_ref,
    query_ref, key_ref, value_ref, output_ref, expand_ref, shrink_ref, post_out, *vector_outs,
):
    f = lax.axis_index("fsdp")
    units, wide = shrink_ref.shape[0], D // 2
    shrink_ref[...] = full[0:units].astype(F32)
    for part in range(units // D):
        start = units + part * D
        expand_ref[:, part * D : part * D + D] = full[start : start + D].astype(F32)
    output_ref[...] = full[2 * units : 2 * units + wide].astype(F32)
    query_ref[...] = grads[0:D, 0:wide].astype(F32)
    key_ref[...] = grads[0:D, wide:D].astype(F32)
    value_ref[0:wide] = grads[D : D + wide, 0:wide].astype(F32)
    value_ref[wide:D] = grads[D : D + wide, wide:D].astype(F32)
    post_out[...] = post[...]
    vectors = vec_ref[...]
    mine = jnp.where(f == 0, vectors[:, 0:wide], vectors[:, wide:D])
    for row, ref in zip((16, 17, 7, 5, 6, 0, 1, 2, 3, 4), vector_outs):
        ref[...] = mine[row : row + 1]
    drift = jnp.where(f == 0, vectors[8:10], vectors[10:12])
    for part in range(units // D):
        vector_outs[10][:, part * D : part * D + D] = drift[part : part + 1]


def unpack_grads(units, full, grads, post, vecs):
    wide = D // 2
    shapes = [(D, wide)] * 3 + [(wide, D), (D, units), (units, D), post.shape]
    shapes = shapes + [(1, wide)] * 10 + [(1, units)]
    return pl.pallas_call(
        unpack_kernel,
        out_shape=tuple(jax.ShapeDtypeStruct(shape, F32) for shape in shapes),
        in_specs=[VMEM] * 4,
        out_specs=(VMEM,) * len(shapes),
        compiler_params=pltpu.CompilerParams(vmem_limit_bytes=UNPACK_ROOM),
        name="unpack_grads",
    )(full, grads, post, vecs)


def head_shards(
    n_ctx,
    post_stream,
    sum_stream,
    cotangent,
    block_order,
    block_sequence,
    query_weight,
    key_weight,
    value_weight,
    output_weight,
    query_bias,
    value_bias,
    output_bias,
    attend_gain,
    attend_shift,
    expand_weight,
    expand_bias,
    shrink_weight,
    shrink_bias,
    middle_gain,
    middle_shift,
    final_gain,
    final_shift,
):
    x, summed, tangent = post_stream[0], sum_stream[0], cotangent[0]
    def across(values, stride):
        return lax.ppermute(values, "ctx", [(c, c ^ stride) for c in range(n_ctx)])

    vectors = [
        query_bias,
        value_bias,
        output_bias,
        attend_gain,
        attend_shift,
        shrink_bias,
        middle_gain,
        middle_shift,
        final_gain,
        final_shift,
        expand_bias,
    ]
    q, kv, w_other, order, seqs, vec, expand_add, wo_other, we_other, ws_other = (
        project_and_scatter(
            n_ctx,
            x,
            query_weight,
            key_weight,
            value_weight,
            block_order,
            block_sequence,
            (output_weight, expand_weight, shrink_weight),
            vectors,
        )
    )
    o, keep, lse, pairs = attend(order, seqs, q, kv)
    layer_output, sum_tan, entry, tan, vec_feed, stage_a, stage_b, kept = middle(
        n_ctx,
        o,
        x,
        summed,
        tangent,
        (output_weight, wo_other),
        (expand_weight, we_other),
        (shrink_weight, ws_other),
        expand_add,
        vec,
    )
    land_a, land_b = across(stage_a, 1), across(stage_b, 2)
    dq, dkv, layer_output, sum_tan = attend_back(
        pairs, q, tan, keep, lse, kv, (layer_output, sum_tan)
    )
    post_tangent, feed_sums, last_sums, vecs = finish(
        n_ctx,
        dq,
        dkv,
        kept,
        land_a,
        land_b,
        x,
        entry,
        query_weight,
        key_weight,
        value_weight,
        w_other,
        vec_feed,
    )
    (
        query_slope,
        key_slope,
        value_slope,
        output_slope,
        expand_slope,
        shrink_slope,
        post_tangent,
        query_drift,
        value_drift,
        output_drift,
        attend_stretch,
        attend_nudge,
        shrink_drift,
        middle_stretch,
        middle_nudge,
        final_stretch,
        final_nudge,
        expand_drift,
    ) = unpack_grads(shrink_weight.shape[0], feed_sums, last_sums, post_tangent, vecs)
    return (
        layer_output[None],
        post_tangent[None],
        sum_tan[None],
        query_slope,
        key_slope,
        value_slope,
        output_slope,
        query_drift[0],
        value_drift[0],
        output_drift[0],
        attend_stretch[0],
        attend_nudge[0],
        expand_slope,
        expand_drift[0],
        shrink_slope,
        shrink_drift[0],
        middle_stretch[0],
        middle_nudge[0],
        final_stretch[0],
        final_nudge[0],
    )


def solution(mesh):
    n_ctx, n_fsdp = mesh.shape["ctx"], mesh.shape["fsdp"]
    if n_fsdp == 2 and n_ctx == n_fsdp * H:
        body = functools.partial(head_shards, n_ctx)
    else:
        body = general_shards
    return jax.shard_map(
        body,
        mesh=mesh,
        in_specs=(
            P("fsdp", "ctx", None),
            P("fsdp", "ctx", None),
            P("fsdp", "ctx", None),
            P("fsdp", None),
            P("fsdp", None),
            P(None, "fsdp"),
            P(None, "fsdp"),
            P(None, "fsdp"),
            P("fsdp", None),
            P("fsdp"),
            P("fsdp"),
            P("fsdp"),
            P("fsdp"),
            P("fsdp"),
            P(None, "fsdp"),
            P("fsdp"),
            P("fsdp", None),
            P("fsdp"),
            P("fsdp"),
            P("fsdp"),
            P("fsdp"),
            P("fsdp"),
        ),
        out_specs=(
            P("fsdp", "ctx", None),
            P("fsdp", "ctx", None),
            P("fsdp", "ctx", None),
            P(None, "fsdp"),
            P(None, "fsdp"),
            P(None, "fsdp"),
            P("fsdp", None),
            P("fsdp"),
            P("fsdp"),
            P("fsdp"),
            P("fsdp"),
            P("fsdp"),
            P(None, "fsdp"),
            P("fsdp"),
            P("fsdp", None),
            P("fsdp"),
            P("fsdp"),
            P("fsdp"),
            P("fsdp"),
            P("fsdp"),
        ),
        check_vma=False,
    )
```

```python
import functools

import jax
import jax.numpy as jnp
from jax import lax
from jax.experimental import pallas as pl
from jax.experimental.pallas import tpu as pltpu
from jax.sharding import PartitionSpec as P

D = 512
H = 8
HD = 64
BLK = 256
HALF = BLK // 2
LONG = 8
TOGETHER = 16
MOST = LONG + 1
F32 = jnp.float32
BF16 = jnp.bfloat16
MESH = pl.DeviceIdType.MESH
ROOM = 60 << 20
UNPACK_ROOM = 60 << 20
VMEM = pl.BlockSpec(memory_space=pltpu.VMEM)
SMEM = pl.BlockSpec(memory_space=pltpu.SMEM)
ANY = pl.BlockSpec(memory_space=pltpu.HBM)


norm_eps = 1e-05
masked_value = -1e30
gelu_coeff = 0.7978845608
gelu_cubic = 0.044715


def smooth_gate(values):
    return (
        0.5
        * values
        * (1.0 + jnp.tanh(gelu_coeff * (values + gelu_cubic * values * values * values)))
    )


def layer_norm(inputs, gain_row, shift_row):
    centre = inputs - jnp.mean(inputs, axis=-1, keepdims=True)
    spread = jnp.mean(centre * centre, axis=-1, keepdims=True)
    return centre * lax.rsqrt(spread + norm_eps) * gain_row + shift_row


def product(left_side, right_side):
    return jnp.dot(left_side, right_side, preferred_element_type=jnp.float32)


def cross_rows(left_side, right_side):
    return lax.dot_general(
        left_side, right_side, (((0,), (0,)), ((), ())), preferred_element_type=jnp.float32
    )


def cross_cols(left_side, right_side):
    return lax.dot_general(
        left_side, right_side, (((1,), (1,)), ((), ())), preferred_element_type=jnp.float32
    )


def column_total(values):
    return jnp.sum(values, axis=0, dtype=jnp.float32)


def lookup(table_row, indices):
    places = jnp.arange(table_row.shape[0], dtype=jnp.int32)
    return jnp.sum(jnp.where(indices[:, None] == places[None, :], table_row[None, :], 0), axis=1)


def block_mask(query_blocks, query_seqs, key_blocks, key_seqs):
    same_seq = query_seqs[:, None] == key_seqs[None, :]
    return same_seq & (key_blocks[None, :] <= query_blocks[:, None])


def token_mask(visible):
    return jnp.repeat(jnp.repeat(visible, BLK, axis=0), BLK, axis=1)


def fold_units(carried, members, unit_step):
    unit_count = members[0].shape[0] // BLK
    inner_count = max((divisor for divisor in range(1, 17) if unit_count % divisor == 0))
    outer_count = unit_count // inner_count

    def outer_turn(outer_index, current):

        def inner_turn(inner_index, inner_state):
            offset = (outer_index * inner_count + inner_index) * BLK
            pieces = tuple((lax.dynamic_slice_in_dim(member, offset, BLK, 0) for member in members))
            return unit_step(inner_state, pieces, offset)

        return lax.fori_loop(0, inner_count, inner_turn, current)

    return lax.fori_loop(0, outer_count, outer_turn, carried)


def general_shards(
    post_stream,
    sum_stream,
    cotangent,
    block_order,
    block_sequence,
    query_weight,
    key_weight,
    value_weight,
    output_weight,
    query_bias,
    value_bias,
    output_bias,
    attend_gain,
    attend_shift,
    expand_weight,
    expand_bias,
    shrink_weight,
    shrink_bias,
    middle_gain,
    middle_shift,
    final_gain,
    final_shift,
):
    (
        query_whole,
        key_whole,
        value_whole,
        output_whole,
        query_add,
        value_add,
        output_add,
        gain_one,
        shift_one,
        expand_whole,
        expand_add,
        shrink_whole,
        shrink_add,
        gain_two,
        shift_two,
        gain_last,
        shift_last,
    ) = (
        lax.all_gather(query_weight, "fsdp", axis=1, tiled=True),
        lax.all_gather(key_weight, "fsdp", axis=1, tiled=True),
        lax.all_gather(value_weight, "fsdp", axis=1, tiled=True),
        lax.all_gather(output_weight, "fsdp", axis=0, tiled=True),
        lax.all_gather(query_bias, "fsdp", axis=0, tiled=True),
        lax.all_gather(value_bias, "fsdp", axis=0, tiled=True),
        lax.all_gather(output_bias, "fsdp", axis=0, tiled=True),
        lax.all_gather(attend_gain, "fsdp", axis=0, tiled=True),
        lax.all_gather(attend_shift, "fsdp", axis=0, tiled=True),
        lax.all_gather(expand_weight, "fsdp", axis=1, tiled=True),
        lax.all_gather(expand_bias, "fsdp", axis=0, tiled=True),
        lax.all_gather(shrink_weight, "fsdp", axis=0, tiled=True),
        lax.all_gather(shrink_bias, "fsdp", axis=0, tiled=True),
        lax.all_gather(middle_gain, "fsdp", axis=0, tiled=True),
        lax.all_gather(middle_shift, "fsdp", axis=0, tiled=True),
        lax.all_gather(final_gain, "fsdp", axis=0, tiled=True),
        lax.all_gather(final_shift, "fsdp", axis=0, tiled=True),
    )
    post_rows = post_stream[0]
    summed = sum_stream[0]
    tangent = cotangent[0]
    order_row = block_order[0]
    seq_row = block_sequence[0]
    token_count = post_rows.shape[0]
    score_scale = HD ** (-0.5)
    own_blocks = lax.dynamic_slice_in_dim(
        order_row, lax.axis_index("ctx") * (token_count // BLK), token_count // BLK
    )
    own_seqs = lookup(seq_row, own_blocks)
    post_low = post_rows.astype(jnp.bfloat16)
    queries = (product(post_low, query_whole) + query_add).astype(jnp.bfloat16)
    key_rows = product(post_low, key_whole).astype(jnp.bfloat16)
    value_rows = (product(post_low, value_whole) + value_add).astype(jnp.bfloat16)
    query_heads = queries.reshape(token_count, H, HD)

    def keys_visible(first_row):
        key_block = lax.dynamic_slice_in_dim(order_row, first_row // BLK, 1)
        return block_mask(own_blocks, own_seqs, key_block, lookup(seq_row, key_block))

    def masked_fold(block_step):

        def unit_step(current, pieces, first_row):
            visible = keys_visible(first_row)
            return lax.cond(
                jnp.any(visible),
                lambda inner_state: block_step(inner_state, pieces, visible),
                lambda inner_state: inner_state,
                current,
            )

        def folded(current, pieces, first_row):
            return fold_units(current, pieces, unit_step)

        return folded

    def stats_block(current, pieces, visible):
        row_peaks, masses = current
        key_heads = pieces[0].reshape(BLK, H, HD)
        row_mask = token_mask(visible)[None]
        scores = (
            jnp.einsum("qhd,khd->hqk", query_heads, key_heads, preferred_element_type=jnp.float32)
            * score_scale
        )
        new_peaks = jnp.maximum(
            row_peaks, jnp.max(jnp.where(row_mask, scores, masked_value), axis=2)
        )
        weights = jnp.where(row_mask, jnp.exp(scores - new_peaks[:, :, None]), 0.0)
        return (new_peaks, masses * jnp.exp(row_peaks - new_peaks) + jnp.sum(weights, axis=2))

    stats_fold = masked_fold(stats_block)
    stats_start = (
        jnp.full((H, token_count), masked_value, jnp.float32),
        jnp.zeros((H, token_count), jnp.float32),
    )
    row_peaks, masses = stats_fold(
        stats_start, (lax.all_gather(key_rows, "ctx", axis=0, tiled=True),), jnp.int32(0)
    )
    log_mass = row_peaks + jnp.log(masses)

    def forward_block(current, pieces, visible):
        key_heads = pieces[0].reshape(BLK, H, HD)
        value_heads = pieces[1].reshape(BLK, H, HD)
        row_mask = token_mask(visible)[None]
        scores = (
            jnp.einsum("qhd,khd->hqk", query_heads, key_heads, preferred_element_type=jnp.float32)
            * score_scale
        )
        weights = jnp.where(row_mask, jnp.exp(scores - log_mass[:, :, None]), 0.0).astype(
            jnp.bfloat16
        )
        addition = jnp.einsum(
            "hqk,khd->qhd", weights, value_heads, preferred_element_type=jnp.float32
        )
        return current + addition.reshape(token_count, D)

    forward_fold = masked_fold(forward_block)
    zero_rows = jnp.zeros((token_count, D), jnp.float32)
    attended = forward_fold(
        zero_rows,
        (
            lax.all_gather(key_rows, "ctx", axis=0, tiled=True),
            lax.all_gather(value_rows, "ctx", axis=0, tiled=True),
        ),
        jnp.int32(0),
    )
    mixed_low = attended.astype(jnp.bfloat16)
    branch = product(mixed_low, output_whole) + output_add
    normed_one, first_pull = jax.vjp(
        layer_norm, post_rows + branch, gain_one.astype(jnp.float32), shift_one.astype(jnp.float32)
    )
    stream_one = summed + branch
    normed_low = normed_one.astype(jnp.bfloat16)
    before = product(normed_low, expand_whole) + expand_add
    gated, gate_pull = jax.vjp(smooth_gate, before)
    hidden = gated.astype(jnp.bfloat16)
    feed_out = product(hidden, shrink_whole) + shrink_add
    normed_two, middle_pull = jax.vjp(
        layer_norm,
        normed_one + feed_out,
        gain_two.astype(jnp.float32),
        shift_two.astype(jnp.float32),
    )
    stream_two = stream_one + feed_out
    last_norm, last_pull = jax.vjp(
        layer_norm, stream_two, gain_last.astype(jnp.float32), shift_last.astype(jnp.float32)
    )
    layer_output = normed_two + last_norm
    stream_tan, stretch_last, nudge_last = last_pull(tangent)
    inflow_tan, stretch_two, nudge_two = middle_pull(tangent)
    feed_tan = (stream_tan + inflow_tan).astype(jnp.bfloat16)
    slope_shrink = cross_rows(hidden, feed_tan)
    drift_shrink = column_total(feed_tan)
    before_tan = gate_pull(cross_cols(feed_tan, shrink_whole))[0].astype(jnp.bfloat16)
    slope_expand = cross_rows(normed_low, before_tan)
    drift_expand = column_total(before_tan)
    normed_tan = inflow_tan + cross_cols(before_tan, expand_whole)
    feed_parts = lax.psum(
        (
            slope_expand,
            drift_expand,
            slope_shrink,
            drift_shrink,
            stretch_two,
            nudge_two,
            stretch_last,
            nudge_last,
        ),
        "ctx",
    )
    feed_sums = (
        lax.psum_scatter(feed_parts[0], "fsdp", scatter_dimension=1, tiled=True),
        lax.psum_scatter(feed_parts[1], "fsdp", scatter_dimension=0, tiled=True),
        lax.psum_scatter(feed_parts[2], "fsdp", scatter_dimension=0, tiled=True),
        lax.psum_scatter(feed_parts[3], "fsdp", scatter_dimension=0, tiled=True),
        lax.psum_scatter(feed_parts[4], "fsdp", scatter_dimension=0, tiled=True),
        lax.psum_scatter(feed_parts[5], "fsdp", scatter_dimension=0, tiled=True),
        lax.psum_scatter(feed_parts[6], "fsdp", scatter_dimension=0, tiled=True),
        lax.psum_scatter(feed_parts[7], "fsdp", scatter_dimension=0, tiled=True),
    )
    entry_tan, stretch_one, nudge_one = first_pull(normed_tan)
    branch_tan = (stream_tan + entry_tan).astype(jnp.bfloat16)
    slope_output = cross_rows(mixed_low, branch_tan)
    drift_output = column_total(branch_tan)
    mixed_tan = cross_cols(branch_tan, output_whole).astype(jnp.bfloat16)
    tangent_heads = mixed_tan.reshape(token_count, H, HD)
    deltas = jnp.sum((mixed_tan * attended).reshape(token_count, H, HD), axis=2).T

    def query_block(current, pieces, visible):
        key_heads = pieces[0].reshape(BLK, H, HD)
        value_heads = pieces[1].reshape(BLK, H, HD)
        row_mask = token_mask(visible)[None]
        scores = (
            jnp.einsum("qhd,khd->hqk", query_heads, key_heads, preferred_element_type=jnp.float32)
            * score_scale
        )
        probability = jnp.where(row_mask, jnp.exp(scores - log_mass[:, :, None]), 0.0)
        prob_tan = jnp.einsum(
            "qhd,khd->hqk", tangent_heads, value_heads, preferred_element_type=jnp.float32
        )
        score_tan = (probability * (prob_tan - deltas[:, :, None])).astype(jnp.bfloat16)
        addition = jnp.einsum(
            "hqk,khd->qhd", score_tan, key_heads, preferred_element_type=jnp.float32
        )
        return current + addition.reshape(token_count, D) * score_scale

    query_fold = masked_fold(query_block)
    query_sum = query_fold(
        zero_rows,
        (
            lax.all_gather(key_rows, "ctx", axis=0, tiled=True),
            lax.all_gather(value_rows, "ctx", axis=0, tiled=True),
        ),
        jnp.int32(0),
    )
    gathered_mass, gathered_delta = (
        lax.all_gather(log_mass.T, "ctx", axis=0, tiled=True),
        lax.all_gather(deltas.T, "ctx", axis=0, tiled=True),
    )
    own_keys = key_rows.reshape(token_count, H, HD)
    own_values = value_rows.reshape(token_count, H, HD)

    def owner_block(current, pieces, first_row, visible):
        key_acc, value_acc = current
        part_queries = pieces[0].reshape(BLK, H, HD)
        part_tangent = pieces[1].reshape(BLK, H, HD)
        part_mass = lax.dynamic_slice_in_dim(gathered_mass, first_row, BLK, 0).T
        part_delta = lax.dynamic_slice_in_dim(gathered_delta, first_row, BLK, 0).T
        row_mask = token_mask(visible)[None]
        scores = (
            jnp.einsum("qhd,khd->hqk", part_queries, own_keys, preferred_element_type=jnp.float32)
            * score_scale
        )
        probability = jnp.where(row_mask, jnp.exp(scores - part_mass[:, :, None]), 0.0)
        value_add_rows = jnp.einsum(
            "hqk,qhd->khd",
            probability.astype(jnp.bfloat16),
            part_tangent,
            preferred_element_type=jnp.float32,
        )
        prob_tan = jnp.einsum(
            "qhd,khd->hqk", part_tangent, own_values, preferred_element_type=jnp.float32
        )
        score_tan = (probability * (prob_tan - part_delta[:, :, None])).astype(jnp.bfloat16)
        key_add_rows = jnp.einsum(
            "hqk,qhd->khd", score_tan, part_queries, preferred_element_type=jnp.float32
        )
        return (
            key_acc + key_add_rows.reshape(token_count, D) * score_scale,
            value_acc + value_add_rows.reshape(token_count, D),
        )

    def owner_unit(current, pieces, first_row):
        query_blocks = lax.dynamic_slice_in_dim(order_row, first_row // BLK, 1)
        visible = block_mask(query_blocks, lookup(seq_row, query_blocks), own_blocks, own_seqs)
        return lax.cond(
            jnp.any(visible),
            lambda inner_state: owner_block(inner_state, pieces, first_row, visible),
            lambda inner_state: inner_state,
            current,
        )

    key_sum, value_sum = fold_units(
        (zero_rows, zero_rows),
        (
            lax.all_gather(queries, "ctx", axis=0, tiled=True),
            lax.all_gather(mixed_tan, "ctx", axis=0, tiled=True),
        ),
        owner_unit,
    )
    query_tan = query_sum.astype(jnp.bfloat16)
    key_tan = key_sum.astype(jnp.bfloat16)
    value_tan = value_sum.astype(jnp.bfloat16)
    slope_query = cross_rows(post_low, query_tan)
    slope_key = cross_rows(post_low, key_tan)
    slope_value = cross_rows(post_low, value_tan)
    drift_query = column_total(query_tan)
    drift_value = column_total(value_tan)
    post_tangent = (
        entry_tan
        + cross_cols(query_tan, query_whole)
        + cross_cols(key_tan, key_whole)
        + cross_cols(value_tan, value_whole)
    )
    heads_parts = lax.psum(
        (
            slope_query,
            slope_key,
            slope_value,
            slope_output,
            drift_query,
            drift_value,
            drift_output,
            stretch_one,
            nudge_one,
        ),
        "ctx",
    )
    heads_sums = (
        lax.psum_scatter(heads_parts[0], "fsdp", scatter_dimension=1, tiled=True),
        lax.psum_scatter(heads_parts[1], "fsdp", scatter_dimension=1, tiled=True),
        lax.psum_scatter(heads_parts[2], "fsdp", scatter_dimension=1, tiled=True),
        lax.psum_scatter(heads_parts[3], "fsdp", scatter_dimension=0, tiled=True),
        lax.psum_scatter(heads_parts[4], "fsdp", scatter_dimension=0, tiled=True),
        lax.psum_scatter(heads_parts[5], "fsdp", scatter_dimension=0, tiled=True),
        lax.psum_scatter(heads_parts[6], "fsdp", scatter_dimension=0, tiled=True),
        lax.psum_scatter(heads_parts[7], "fsdp", scatter_dimension=0, tiled=True),
        lax.psum_scatter(heads_parts[8], "fsdp", scatter_dimension=0, tiled=True),
    )
    return (
        layer_output[None],
        post_tangent[None],
        stream_tan[None],
        heads_sums[0],
        heads_sums[1],
        heads_sums[2],
        heads_sums[3],
        heads_sums[4],
        heads_sums[5],
        heads_sums[6],
        heads_sums[7],
        heads_sums[8],
        feed_sums[0],
        feed_sums[1],
        feed_sums[2],
        feed_sums[3],
        feed_sums[4],
        feed_sums[5],
        feed_sums[6],
        feed_sums[7],
    )


def low_lanes(values):
    return lax.broadcasted_iota(jnp.int32, values.shape, 1) < HD


def swap_lanes(values):
    return pltpu.roll(values, HD, 1)


def low_pair(first, second):
    return jnp.where(low_lanes(first), first, swap_lanes(second))


def high_pair(first, second):
    return jnp.where(low_lanes(first), swap_lanes(first), second)


def side_pair(side, first, second):
    return low_pair(first, second) if side == 0 else high_pair(first, second)


def dot_nn(left, right):
    return jnp.dot(left, right, preferred_element_type=F32)


def dot_nt(left, right):
    return lax.dot_general(left, right, (((1,), (1,)), ((), ())), preferred_element_type=F32)


def dot_tn(left, right):
    return lax.dot_general(left, right, (((0,), (0,)), ((), ())), preferred_element_type=F32)


class Place:
    def __init__(self):
        self.c = lax.axis_index("ctx")
        self.f = lax.axis_index("fsdp")
        self.group = self.c // H
        self.head = self.c % H
        self.inside = jnp.where(self.group == self.f, 1, 0)

    def is_me(self, tc, tf):
        return jnp.logical_and(self.c == tc, self.f == tf)

    def signal(self, barrier, tc, tf):
        @pl.when(jnp.logical_not(self.is_me(tc, tf)))
        def _():
            pl.semaphore_signal(barrier, 1, device_id=(tc, tf), device_id_type=MESH)

    def turn(self, i, n):
        return (self.c + 5 * i) % n

    def greet_sources(self, n_ctx, partner):
        barrier = pltpu.get_barrier_semaphore()
        for tc in range(n_ctx):
            self.signal(barrier, tc, self.group)
        if partner:
            pl.semaphore_signal(
                barrier, 1, device_id=(self.c, 1 - self.f), device_id_type=MESH
            )
        pl.semaphore_wait(barrier, 2 * H + (1 if partner else 0) - self.inside)

    def greet_owners(self, n_ctx, partner, more=0):
        barrier = pltpu.get_barrier_semaphore()
        for head in range(H):
            for core in range(2):
                self.signal(barrier, self.f * H + head, core)
        if partner:
            pl.semaphore_signal(
                barrier, 1, device_id=(self.c, 1 - self.f), device_id_type=MESH
            )
        pl.semaphore_wait(barrier, n_ctx + (1 if partner else 0) + more - self.inside)

    def send(self, src, dst, send_sem, recv_sem, tc, tf):
        me = self.is_me(tc, tf)

        @pl.when(me)
        def _():
            pltpu.make_async_copy(src, dst, recv_sem).start()

        @pl.when(jnp.logical_not(me))
        def _():
            self.remote(src, dst, send_sem, recv_sem, tc, tf).start()

    def remote(self, src, dst, send_sem, recv_sem, tc, tf):
        return pltpu.make_async_remote_copy(
            src_ref=src,
            dst_ref=dst,
            send_sem=send_sem,
            recv_sem=recv_sem,
            device_id=(tc, tf),
            device_id_type=MESH,
        )

    def wait_sent(self, src, dst, send_sem, recv_sem, tc, tf):
        @pl.when(jnp.logical_not(self.is_me(tc, tf)))
        def _():
            self.remote(src, dst, send_sem, recv_sem, tc, tf).wait_send()


VECTORS = 10


def project_kernel(
    n_ctx,
    x_hbm,
    wq_hbm,
    wk_hbm,
    wv_hbm,
    order_hbm,
    seq_hbm,
    *rest,
):
    dense_hbm, rest = rest[:3], rest[3:]
    vector_hbm, rest = rest[: VECTORS + 1], rest[VECTORS + 1 :]
    vector_in, rest = rest[-VECTORS - 1 :], rest[: -VECTORS - 1]
    (
        q_out,
        kv_out,
        w_other,
        order_out,
        seq_out,
        vec_out,
        expand_out,
        wo_other,
        we_other,
        ws_other,
        x_in,
        w_own,
        w_in,
        bias_own,
        bias_in,
        order_own,
        seq_own,
        order_in,
        seq_in,
        q_send,
        kv_send,
        load_sem,
        w_ss,
        w_rs,
        q_ss,
        q_rs,
        kv_ss,
        kv_rs,
        relay_ss,
        relay_rs,
    ) = rest
    at = Place()
    other = 1 - at.f
    loads = [
        pltpu.make_async_copy(src, dst, load_sem.at[i])
        for i, (src, dst) in enumerate(
            (
                (x_hbm, x_in),
                (wq_hbm, w_own.at[0]),
                (wk_hbm, w_own.at[1]),
                (wv_hbm, w_own.at[2]),
                (order_hbm, order_own),
                (seq_hbm, seq_own),
                *zip(vector_hbm, vector_in),
            )
        )
    ]
    for load in loads:
        load.start()
    at.greet_sources(n_ctx, True)
    wide = bias_own.shape[1]
    swaps = [
        at.remote(src, dst, w_ss.at[i], w_rs.at[i], at.c, other)
        for i, (src, dst) in enumerate(
            (
                (wq_hbm, w_in.at[0]),
                (wk_hbm, w_in.at[1]),
                (wv_hbm, w_in.at[2]),
                (order_hbm, order_in),
                (seq_hbm, seq_in),
                (bias_own, bias_in),
            )
        )
    ]
    for swap in swaps[:-1]:
        swap.start()
    for load in loads:
        load.wait()
    for row, ref in enumerate(vector_in[:VECTORS]):
        bias_own[row : row + 1, :] = ref[...].astype(F32).reshape(1, wide)
    for part in range(vector_in[VECTORS].shape[0] // wide):
        piece = vector_in[VECTORS][part * wide : part * wide + wide]
        bias_own[VECTORS + part : VECTORS + part + 1, :] = piece.astype(F32).reshape(1, wide)
    swaps[-1].start()

    def moves(half):
        for i in range(H // 2):
            head = half * (H // 2) + at.turn(i, H // 2)
            for core in range(2):
                slot = head * 2 + core
                yield (
                    kv_send.at[head, pl.ds(core * BLK, BLK)],
                    kv_out.at[2 * at.c + core],
                    kv_ss.at[slot],
                    kv_rs.at[at.c],
                    at.f * H + head,
                    core,
                )
                yield (
                    q_send.at[head, core],
                    q_out.at[at.c],
                    q_ss.at[slot],
                    q_rs.at[at.c],
                    at.f * H + head,
                    core,
                )

    def one_half(half, wq, wk, wv, bias):
        low = x_in[...].astype(BF16)
        q = dot_nn(low, wq[...]) + bias[0:1, :]
        k = dot_nn(low, wk[...])
        v = dot_nn(low, wv[...]) + bias[1:2, :]
        for pair in range(2):
            columns = slice(pair * 128, pair * 128 + 128)
            for side in range(2):
                head = half * (H // 2) + 2 * pair + side
                kv_send[head] = side_pair(side, k[:, columns], v[:, columns]).astype(BF16)
                for core in range(2):
                    rows = slice(core * HALF, core * HALF + HALF)
                    late = slice(BLK + core * HALF, BLK + core * HALF + HALF)
                    q_send[head, core] = side_pair(side, q[rows, columns], q[late, columns]).astype(
                        BF16
                    )
        for move in moves(half):
            at.send(*move)

    one_half(at.f, w_own.at[0], w_own.at[1], w_own.at[2], bias_own)
    for swap in swaps:
        swap.wait()
    one_half(other, w_in.at[0], w_in.at[1], w_in.at[2], bias_in)
    dense_swaps = [
        at.remote(src, dst, w_ss.at[6 + i], w_rs.at[6 + i], at.c, other)
        for i, (src, dst) in enumerate(zip(dense_hbm, (wo_other, we_other, ws_other)))
    ]
    for swap in dense_swaps:
        swap.start()
    w_other[...] = w_in[...]
    inside = at.inside == 1
    order_out[...] = jnp.where(inside, order_own[...], order_in[...])
    seq_out[...] = jnp.where(inside, seq_own[...], seq_in[...])
    vec_out[...] = whole_rows(bias_own[...], bias_in[...], at.f == 0)
    for row, source in enumerate((bias_own, bias_in)):
        for part in range(expand_out.shape[1] // wide):
            at_row = VECTORS + part
            expand_out[row : row + 1, part * wide : part * wide + wide] = source[
                at_row : at_row + 1, :
            ]

    def relay(source):
        mine = kv_out.at[2 * source + at.f]
        return at.remote(mine, mine, relay_ss.at[source], relay_rs.at[source], at.c, other)

    def relay_in(source):
        theirs = kv_out.at[2 * source + other]
        return at.remote(theirs, theirs, relay_ss.at[source], relay_rs.at[source], at.c, other)

    for source in range(n_ctx):
        arrived = kv_out.at[2 * source + at.f]
        at.remote(arrived, arrived, kv_ss.at[0], kv_rs.at[source], at.c, other).wait_recv()
        relay(source).start()
    for half in (at.f, other):
        for move in moves(half):
            at.wait_sent(*move)
    for source in range(n_ctx):
        arrived = q_out.at[source]
        at.remote(arrived, arrived, q_ss.at[0], q_rs.at[source], at.c, other).wait_recv()
        relay_in(source).wait_recv()
    for source in range(n_ctx):
        relay(source).wait_send()
    for swap in dense_swaps:
        swap.wait()


def project_and_scatter(n_ctx, x, wq, wk, wv, order, seqs, dense_weights, vectors):
    wide = wq.shape[1]
    blocks = order.shape[1]
    units = vectors[VECTORS].shape[0]
    bias_rows = VECTORS + units // wide
    return pl.pallas_call(
        functools.partial(project_kernel, n_ctx),
        out_shape=(
            jax.ShapeDtypeStruct((n_ctx, HALF, 128), BF16),
            jax.ShapeDtypeStruct((2 * n_ctx, BLK, 128), BF16),
            jax.ShapeDtypeStruct((3, D, wide), BF16),
            jax.ShapeDtypeStruct((1, blocks), jnp.int32),
            jax.ShapeDtypeStruct((1, blocks), jnp.int32),
            jax.ShapeDtypeStruct((bias_rows, D), F32),
            jax.ShapeDtypeStruct((2, units), F32),
            *[jax.ShapeDtypeStruct(w.shape, BF16) for w in dense_weights],
        ),
        in_specs=[ANY] * (10 + VECTORS),
        out_specs=(ANY, ANY) + (VMEM,) * 5 + (ANY,) * 3,
        scratch_shapes=[
            pltpu.VMEM((2 * BLK, D), F32),
            pltpu.VMEM((3, D, wide), BF16),
            pltpu.VMEM((3, D, wide), BF16),
            pltpu.VMEM((bias_rows, wide), F32),
            pltpu.VMEM((bias_rows, wide), F32),
            pltpu.VMEM((1, blocks), jnp.int32),
            pltpu.VMEM((1, blocks), jnp.int32),
            pltpu.VMEM((1, blocks), jnp.int32),
            pltpu.VMEM((1, blocks), jnp.int32),
            pltpu.VMEM((H, 2, HALF, 128), BF16),
            pltpu.VMEM((H, 2 * BLK, 128), BF16),
            pltpu.SemaphoreType.DMA((7 + VECTORS,)),
            pltpu.SemaphoreType.DMA((9,)),
            pltpu.SemaphoreType.DMA((9,)),
            pltpu.SemaphoreType.DMA((2 * H,)),
            pltpu.SemaphoreType.DMA((n_ctx,)),
            pltpu.SemaphoreType.DMA((2 * H,)),
            pltpu.SemaphoreType.DMA((n_ctx,)),
            pltpu.SemaphoreType.DMA((n_ctx,)),
            pltpu.SemaphoreType.DMA((n_ctx,)),
        ]
        + [pltpu.VMEM(vector.shape, BF16) for vector in vectors],
        compiler_params=pltpu.CompilerParams(
            collective_id=0, has_side_effects=True, vmem_limit_bytes=ROOM
        ),
        name="project_scatter",
    )(x, wq, wk, wv, order, seqs, *dense_weights, *vectors)


def forward_kernel(
    blocks,
    order_ref,
    seq_ref,
    q_ref,
    kv_ref,
    o_ref,
    keep_ref,
    lse_ref,
    pairs_ref,
    place,
    q_low,
    peaks,
    masses,
    total,
    scores,
):
    def place_block(slot, _):
        place[order_ref[0, slot]] = slot
        return 0

    lax.fori_loop(0, blocks, place_block, 0)

    count = jnp.int32(0)
    for gap in range(1, LONG):
        for late in range(gap, blocks):
            pairs_ref[0, count] = place[late]
            pairs_ref[1, count] = place[late - gap]
            count = count + jnp.where(seq_ref[0, late] == seq_ref[0, late - gap], 1, 0)
    for spare in range(TOGETHER):
        pairs_ref[0, count + spare] = blocks
        pairs_ref[1, count + spare] = 0
    turns = (count + TOGETHER - 1) // TOGETHER
    pairs_ref[2, 0] = turns

    def unpack(step, _):
        for part in range(4):
            source = step * 4 + part
            packed = q_ref[source].astype(F32) * (HD**-0.5)
            low = low_lanes(packed)
            q_low[2 * source] = jnp.where(low, packed, 0.0).astype(BF16)
            q_low[2 * source + 1] = jnp.where(low, swap_lanes(packed), 0.0).astype(BF16)
        return 0

    lax.fori_loop(0, blocks // 8, unpack, 0)
    q_low[blocks] = jnp.zeros((HALF, 128), BF16)

    peaks[blocks] = jnp.zeros((HALF, 128), F32)
    masses[blocks] = jnp.zeros((HALF, 128), F32)
    total[blocks] = jnp.zeros((HALF, 128), F32)
    lse_ref[blocks] = jnp.zeros((HALF, 128), F32)

    def own_slots(step):
        return [(step * TOGETHER + part,) * 2 for part in range(TOGETHER)]

    def pair_slots(step):
        return [
            (pairs_ref[0, step * TOGETHER + part], pairs_ref[1, step * TOGETHER + part])
            for part in range(TOGETHER)
        ]

    def score(slots, base):
        results = []
        for part, (q_slot, k_slot) in enumerate(slots):
            result = dot_nt(q_low[q_slot], kv_ref[k_slot])
            scores[base + part] = result
            results.append(jnp.maximum(result[:, :128], result[:, 128:]))
        return results

    def score_own(step, _):
        slots = own_slots(step)
        for (q_slot, _), result in zip(slots, score(slots, step * TOGETHER)):
            peaks[q_slot] = result
        return 0

    def score_pairs(step, _):
        slots = pair_slots(step)
        for (q_slot, _), result in zip(slots, score(slots, blocks + step * TOGETHER)):
            peaks[q_slot] = jnp.maximum(peaks[q_slot], result)
        return 0

    lax.fori_loop(0, blocks // TOGETHER, score_own, 0)
    lax.fori_loop(0, turns, score_pairs, 0)

    def level(step, _):
        for part in range(4):
            slot = step * 4 + part
            peaks[slot] = jnp.broadcast_to(
                jnp.max(peaks[slot], axis=1, keepdims=True), (HALF, 128)
            )
        return 0

    lax.fori_loop(0, blocks // 4, level, 0)

    def weigh(slots, base):
        results = []
        for part, (q_slot, k_slot) in enumerate(slots):
            peak = peaks[q_slot]
            left = jnp.exp(scores[base + part, :, :128] - peak)
            right = jnp.exp(scores[base + part, :, 128:] - peak)
            weights = jnp.concatenate([left, right], axis=1).astype(BF16)
            results.append((left + right, dot_nn(weights, kv_ref[k_slot])))
        return results

    def weigh_own(step, _):
        slots = own_slots(step)
        for (q_slot, _), (mass, result) in zip(slots, weigh(slots, step * TOGETHER)):
            masses[q_slot] = mass
            total[q_slot] = result
        return 0

    def weigh_pairs(step, _):
        slots = pair_slots(step)
        for (q_slot, _), (mass, result) in zip(slots, weigh(slots, blocks + step * TOGETHER)):
            masses[q_slot] = masses[q_slot] + mass
            total[q_slot] = total[q_slot] + result
        return 0

    lax.fori_loop(0, blocks // TOGETHER, weigh_own, 0)
    lax.fori_loop(0, turns, weigh_pairs, 0)

    def finish(step, _):
        for part in range(4):
            source = step * 4 + part
            for side in range(2):
                slot = 2 * source + side
                mass = jnp.broadcast_to(
                    jnp.sum(masses[slot], axis=1, keepdims=True), (HALF, 128)
                )
                result = total[slot] / mass
                lse_ref[slot] = peaks[slot] + jnp.log(mass)
                packed = high_pair(result[: HALF // 2], result[HALF // 2 :])
                keep_ref[source, side] = packed
                o_ref[source, side] = packed.astype(BF16)
        return 0

    lax.fori_loop(0, blocks // 8, finish, 0)


def pair_room(blocks):
    return blocks * MOST // 2 + 2 * TOGETHER


def attend(order, seqs, q, kv):
    blocks = kv.shape[0]
    room = pair_room(blocks)
    return pl.pallas_call(
        functools.partial(forward_kernel, blocks),
        out_shape=(
            jax.ShapeDtypeStruct((blocks // 2, 2, HALF // 2, 128), BF16),
            jax.ShapeDtypeStruct((blocks // 2, 2, HALF // 2, 128), F32),
            jax.ShapeDtypeStruct((blocks + 1, HALF, 128), F32),
            jax.ShapeDtypeStruct((3, room), jnp.int32),
        ),
        in_specs=[SMEM, SMEM, VMEM, VMEM],
        out_specs=(VMEM, VMEM, VMEM, SMEM),
        scratch_shapes=[
            pltpu.SMEM((blocks,), jnp.int32),
            pltpu.VMEM((blocks + 1, HALF, 128), BF16),
            pltpu.VMEM((blocks + 1, HALF, 128), F32),
            pltpu.VMEM((blocks + 1, HALF, 128), F32),
            pltpu.VMEM((blocks + 1, HALF, 128), F32),
            pltpu.VMEM((room, HALF, BLK), F32),
        ],
        compiler_params=pltpu.CompilerParams(vmem_limit_bytes=ROOM),
        name="attend",
    )(order, seqs, q, kv)


def backward_kernel(
    blocks,
    pairs_ref,
    q_ref,
    tan_ref,
    keep_ref,
    lse_ref,
    kv_ref,
    pass_a,
    pass_b,
    dq_ref,
    dkv_sum,
    out_a,
    out_b,
    both,
    turned,
    deltas,
    dq_sum,
    held,
    pass_sem,
):
    fetches = [
        pltpu.make_async_copy(src, held.at[i], pass_sem.at[i])
        for i, src in enumerate((pass_a, pass_b))
    ]
    passes = [
        pltpu.make_async_copy(held.at[i], dst, pass_sem.at[2 + i])
        for i, dst in enumerate((out_a, out_b))
    ]
    for fetch in fetches:
        fetch.start()

    def unpack(step, _):
        for part in range(4):
            source = step * 4 + part
            packed = q_ref[source].astype(F32) * (HD**-0.5)
            low = low_lanes(packed)
            for side in range(2):
                slot = 2 * source + side
                q = packed if side == 0 else swap_lanes(packed)
                both[slot, 0:HALF] = jnp.where(low, q, 0.0).astype(BF16)
                tangent = tan_ref[source, side].astype(F32)
                first = low_lanes(tangent)
                both[slot, HALF : HALF + HALF // 2] = jnp.where(
                    first, 0.0, swap_lanes(tangent)
                ).astype(BF16)
                both[slot, HALF + HALF // 2 : BLK] = jnp.where(first, 0.0, tangent).astype(BF16)
                turned[slot] = jnp.transpose(both[slot])
                product = tangent * keep_ref[source, side]
                delta = jnp.concatenate(
                    [
                        jnp.sum(jnp.where(first, product, 0.0), axis=1, keepdims=True),
                        jnp.sum(jnp.where(first, 0.0, product), axis=1, keepdims=True),
                    ],
                    axis=0,
                )
                deltas[slot] = jnp.broadcast_to(delta, (HALF, 128))
        return 0

    lax.fori_loop(0, blocks // 8, unpack, 0)
    both[blocks] = jnp.zeros((BLK, 128), BF16)
    turned[blocks] = jnp.zeros((128, BLK), BF16)
    deltas[blocks] = jnp.zeros((HALF, 128), F32)
    dq_sum[blocks] = jnp.zeros((HALF, 128), F32)

    def one_pair(q_slot, k_slot):
        kv = kv_ref[k_slot]
        products = dot_nt(both[q_slot], kv)
        mass, delta = lse_ref[q_slot], deltas[q_slot]
        weights = jnp.exp(products[:HALF] - jnp.concatenate([mass, mass], axis=1))
        score_tan = weights * (products[HALF:] - jnp.concatenate([delta, delta], axis=1))
        score_tan = score_tan.astype(BF16)
        sides = jnp.concatenate([score_tan, weights.astype(BF16)], axis=0)
        return dot_nn(turned[q_slot], sides), dot_nn(score_tan, kv)

    def own_turn(step, _):
        slots = [step * TOGETHER + part for part in range(TOGETHER)]
        results = [one_pair(slot, slot) for slot in slots]
        for slot, (dkv, dq) in zip(slots, results):
            dkv_sum[slot] = dkv
            dq_sum[slot] = dq
        return 0

    def pair_turn(step, _):
        slots = [
            (pairs_ref[0, step * TOGETHER + part], pairs_ref[1, step * TOGETHER + part])
            for part in range(TOGETHER)
        ]
        results = [one_pair(*slot) for slot in slots]
        for (q_slot, k_slot), (dkv, dq) in zip(slots, results):
            dkv_sum[k_slot] = dkv_sum[k_slot] + dkv
            dq_sum[q_slot] = dq_sum[q_slot] + dq
        return 0

    lax.fori_loop(0, blocks // TOGETHER, own_turn, 0)
    for fetch, move in zip(fetches, passes):
        fetch.wait()
        move.start()
    lax.fori_loop(0, pairs_ref[2, 0], pair_turn, 0)

    def finish_rows(step, _):
        for part in range(4):
            source = step * 4 + part
            packed = low_pair(dq_sum[2 * source], dq_sum[2 * source + 1]) * (HD**-0.5)
            dq_ref[source] = packed.astype(BF16)
        return 0

    lax.fori_loop(0, blocks // 8, finish_rows, 0)
    for move in passes:
        move.wait()


def attend_back(pairs, q, tangent, keep, lse, kv, passed):
    blocks = kv.shape[0]
    return pl.pallas_call(
        functools.partial(backward_kernel, blocks),
        out_shape=(
            jax.ShapeDtypeStruct((blocks // 2, HALF, 128), BF16),
            jax.ShapeDtypeStruct((blocks, 128, BLK), F32),
            jax.ShapeDtypeStruct(passed[0].shape, F32),
            jax.ShapeDtypeStruct(passed[1].shape, F32),
        ),
        in_specs=[SMEM, VMEM, VMEM, VMEM, VMEM, VMEM, ANY, ANY],
        out_specs=(VMEM, VMEM, ANY, ANY),
        scratch_shapes=[
            pltpu.VMEM((blocks + 1, BLK, 128), BF16),
            pltpu.VMEM((blocks + 1, 128, BLK), BF16),
            pltpu.VMEM((blocks + 1, HALF, 128), F32),
            pltpu.VMEM((blocks + 1, HALF, 128), F32),
            pltpu.VMEM((2,) + passed[0].shape, F32),
            pltpu.SemaphoreType.DMA((4,)),
        ],
        compiler_params=pltpu.CompilerParams(vmem_limit_bytes=ROOM),
        name="attend_back",
    )(pairs, q, tangent, keep, lse, kv, *passed)


def pieces_of(start, size, body):
    piece = max(n for n in range(16, 289, 16) if size % n == 0)
    lax.fori_loop(
        0,
        size // piece,
        lambda i, _: (body(i * piece, span(start + i * piece, piece), piece), 0)[1],
        0,
    )


def span(start, size):
    return pl.ds(pl.multiple_of(start, 16), size)


def step_of(c, stride):
    bit = (c // stride) % 2
    return bit, c + stride * (1 - 2 * bit)


REGIONS = 4


def columns_of(region):
    wide = D // (REGIONS // 2)
    return slice(region // 2 * wide, region // 2 * wide + wide)


class Ladder:
    def __init__(self, at, plans, starts, size, acc, stage, landing, out, sems, bases=(0, 0)):
        self.bases = bases
        self.at, self.acc, self.stage, self.landing, self.out = at, acc, stage, landing, out
        self.down_ss, self.down_rs, self.up_ss, self.up_rs = sems
        self.ranges = []
        for region in range(REGIONS):
            plan, start = plans[region % 2], starts[region % 2]
            listed, rows = [], size
            for bit, peer in plan[:-1]:
                rows = rows // 2
                listed.append((start + bit * rows, start + (1 - bit) * rows, rows, peer))
                start = start + bit * rows
            listed.append((start, start, rows, plan[-1][1]))
            self.ranges.append(listed)
        self.last = len(plans[0]) - 1

    def slot(self, region, step):
        return region * (self.last + 1) + step

    def down(self, region, step, sent):
        kept, given, size, peer = self.ranges[region][step]
        where, slot = span(given if sent else kept, size), self.slot(region, step)
        columns = columns_of(region)
        return self.at.remote(
            self.stage[region % 2].at[where, columns],
            self.landing[region % 2][step].at[where, columns],
            self.down_ss.at[slot],
            self.down_rs.at[slot],
            peer,
            self.at.f,
        )

    def up(self, region, step, sent):
        kept, given, size, peer = self.ranges[region][step]
        start = self.bases[region % 2] + (kept if sent else given)
        columns = columns_of(region)
        where, slot = span(start, size), self.slot(region, step)
        return self.at.remote(
            self.out.at[where, columns],
            self.out.at[where, columns],
            self.up_ss.at[slot],
            self.up_rs.at[slot],
            peer,
            self.at.f,
        )

    def join(self, region, start, size, arrived, target):
        columns, acc = columns_of(region), self.acc[region % 2]

        def body(offset, where, _):
            total = acc[where, columns] + arrived[where, columns].astype(F32)
            target[where, columns] = total.astype(target.dtype)

        pieces_of(start, size, body)

    def give(self, region, step, arrived):
        kept, given, size, _ = self.ranges[region][step]
        self.join(region, given, size, arrived, self.stage[region % 2])
        self.down(region, step, True).start()
        if step < self.last:
            self.join(region, kept, size, arrived, self.acc[region % 2])

    def settle(self, region):
        kept, _, size, _ = self.ranges[region][self.last]
        arrived = self.landing[region % 2][self.last]
        columns, stage = columns_of(region), self.stage[region % 2]

        def body(offset, where, rows):
            total = stage[where, columns].astype(F32) + arrived[where, columns].astype(F32)
            row = span(self.bases[region % 2] + kept + offset, rows)
            self.out[row, columns] = total.astype(BF16)

        self.down(region, self.last, False).wait_recv()
        pieces_of(kept, size, body)
        self.up(region, self.last - 1, True).start()

    def wait_down(self):
        for region in range(REGIONS):
            for step in range(self.last + 1):
                self.down(region, step, True).wait_send()

    def wait_up(self, steps):
        for region in range(REGIONS):
            for step in steps:
                self.up(region, step, True).wait_send()


COLS = 512


def whole_rows(own, other, first):
    return jnp.where(
        first,
        jnp.concatenate([own, other], axis=1),
        jnp.concatenate([other, own], axis=1),
    )


def row_mean(values):
    return jnp.mean(values, axis=1, keepdims=True)


def normalize(values):
    centre = values - row_mean(values)
    scale = lax.rsqrt(row_mean(centre * centre) + norm_eps)
    return centre * scale, scale


def norm_back(tangent, normed, scale, gain):
    pushed = tangent * gain
    return scale * (pushed - row_mean(pushed) - normed * row_mean(pushed * normed))


def column_sum(values):
    return jnp.sum(values, axis=0, keepdims=True)


def feed_slopes(kind, target, mixed, low_turned, hidden, before_tan, feed_tan, branch_tan):
    unit_count = hidden.shape[2] // COLS

    def chunk_slopes(chunk, _):
        columns = pl.ds(pl.multiple_of(chunk * COLS, COLS), COLS)
        target[columns, :] = dot_tn(hidden[kind, :, columns], feed_tan[...]).astype(target.dtype)
        below = pl.ds(pl.multiple_of((unit_count + chunk) * COLS, COLS), COLS)
        target[below, :] = dot_nn(low_turned[...], before_tan[kind, :, columns]).astype(
            target.dtype
        )
        return 0

    lax.fori_loop(0, unit_count, chunk_slopes, 0)
    start = 2 * unit_count * COLS
    target[start : start + D // 2, :] = dot_tn(mixed[kind], branch_tan[...]).astype(target.dtype)


def middle_kernel(
    n_ctx,
    o_hbm, x_hbm, sum_hbm, cot_hbm, wo_a, wo_b, we_a, we_b, ws_a, ws_b, be_ref, vec_in,
    out_hbm, sum_tan_hbm, entry_hbm, tan_out, vec_ref, stage_a, stage_b, keep_ref,
    o_in, x_ref, sum_ref, cot_ref, wo, we, ws, out_ref, sum_tan_ref, entry_ref,
    mixed, low, hidden, before_tan, feed_tan, branch_tan, slope, mixed_tan, tan_send,
    own_grads, send_grads, first_in, low_turned,
    load_sem, store_sem, o_ss, o_rs, tan_ss, tan_rs, core_ss, core_rs,
):
    at = Place()
    f = at.f
    other = 1 - f
    halves = (f, other)
    piece = HALF // 2
    loads = [
        pltpu.make_async_copy(src, dst, load_sem.at[i])
        for i, (src, dst) in enumerate(
            (
                (x_hbm, x_ref),
                (wo_a, wo.at[0]),
                (wo_b, wo.at[1]),
                (we_a, we.at[0]),
                (we_b, we.at[1]),
                (ws_a, ws.at[0]),
                (ws_b, ws.at[1]),
                (sum_hbm, sum_ref),
                (cot_hbm, cot_ref),
            )
        )
    ]
    for load in loads:
        load.start()
    barrier = pltpu.get_barrier_semaphore()
    for target in range(n_ctx):
        at.signal(barrier, target, at.group)
    at.greet_owners(n_ctx, True, 2 * H - at.inside)

    def o_move(target, side):
        return (
            o_hbm.at[target, side],
            o_in.at[side, at.head, f],
            o_ss.at[2 * target + side],
            o_rs.at[side * 2 * H + at.head * 2 + f],
            target,
            at.group,
        )

    def tan_move(side, head, core):
        return (
            tan_send.at[side, head, core],
            tan_out.at[at.c, side],
            tan_ss.at[side * 2 * H + head * 2 + core],
            tan_rs.at[at.c * 2 + side],
            f * H + head,
            core,
        )

    for side in range(2):
        for i in range(n_ctx):
            at.send(*o_move(at.turn(i, n_ctx), side))
    vec_ref[...] = jnp.zeros_like(vec_ref)
    vectors = vec_in[...]
    (out_bias, gain_one, shift_one, shrink_bias, gain_two, shift_two, gain_last, shift_last) = (
        vectors[i : i + 1] for i in range(2, 10)
    )
    be = (be_ref.at[0:1], be_ref.at[1:2])
    for load in loads:
        load.wait()

    def stores(step):
        rows = pl.ds(pl.multiple_of(step * BLK, BLK), BLK)
        return [
            pltpu.make_async_copy(src.at[rows], dst.at[rows], store_sem.at[3 * step + i])
            for i, (src, dst) in enumerate(
                ((out_ref, out_hbm), (sum_tan_ref, sum_tan_hbm), (entry_ref, entry_hbm))
            )
        ]

    def tile(step, _):
        first_row = pl.multiple_of(step * BLK, BLK)
        rows = pl.ds(first_row, BLK)
        for head in range(H):
            for core in range(2):
                arrived = o_in.at[step, head, core]
                at.remote(
                    arrived, arrived, o_ss.at[0], o_rs.at[step * 2 * H + head * 2 + core],
                    at.c, other,
                ).wait_recv()
        for kind in range(2):
            for pair in range(2):
                head = halves[kind] * (H // 2) + 2 * pair
                columns = slice(pair * 128, pair * 128 + 128)
                for core in range(2):
                    early = o_in[step, head, core].astype(F32)
                    late = o_in[step, head + 1, core].astype(F32)
                    for part in range(2):
                        start = pl.multiple_of(first_row + core * HALF + part * piece, piece)
                        mixed[kind, pl.ds(start, piece), columns] = side_pair(
                            part, early, late
                        ).astype(BF16)
        branch = dot_nn(mixed[0, rows, :], wo[0]) + dot_nn(mixed[1, rows, :], wo[1]) + out_bias
        n_one, scale_one = normalize(x_ref[rows, :] + branch)
        normed_one = n_one * gain_one + shift_one
        stream_one = sum_ref[rows, :] + branch
        normed_low = normed_one.astype(BF16)
        low[rows, :] = normed_low
        feed = jnp.zeros((BLK, D), F32)
        for kind in range(2):

            def expand(chunk, carried):
                columns = slice(chunk * COLS, chunk * COLS + COLS)
                v = dot_nn(normed_low, we[kind, :, columns]) + be[kind][:, columns]
                square = v * v
                t = jnp.tanh(gelu_coeff * (v + gelu_cubic * square * v))
                half_up = 0.5 + 0.5 * t
                hidden_part = (v * half_up).astype(BF16)
                hidden[kind, rows, columns] = hidden_part
                slope[kind, :, columns] = half_up + v * half_up * (1.0 - t) * (
                    gelu_coeff + (3.0 * gelu_coeff * gelu_cubic) * square
                )
                return carried + dot_nn(hidden_part, ws[kind, columns, :])

            for chunk in range(ws.shape[1] // COLS):
                feed = expand(chunk, feed)
        feed_out = feed + shrink_bias
        n_two, scale_two = normalize(normed_one + feed_out)
        n_last, scale_last = normalize(stream_one + feed_out)
        out_ref[rows, :] = (n_two * gain_two + shift_two) + (n_last * gain_last + shift_last)
        u = cot_ref[rows, :]
        nudge = column_sum(u)
        sum_tan = norm_back(u, n_last, scale_last, gain_last)
        inflow = norm_back(u, n_two, scale_two, gain_two)
        sum_tan_ref[rows, :] = sum_tan
        feed_low = (sum_tan + inflow).astype(BF16)
        feed_tan[rows, :] = feed_low
        vec_ref[0:1, :] += column_sum(feed_low.astype(F32))
        vec_ref[1:2, :] += column_sum(u * n_two)
        vec_ref[2:3, :] += nudge
        vec_ref[3:4, :] += column_sum(u * n_last)
        vec_ref[4:5, :] += nudge
        normed_tan = inflow
        for kind in range(2):

            def expand_back(chunk, carried):
                columns = slice(chunk * COLS, chunk * COLS + COLS)
                pushed = dot_nt(feed_low, ws[kind, columns, :])
                tan_part = (pushed * slope[kind, :, columns]).astype(BF16)
                before_tan[kind, rows, columns] = tan_part
                vec_row = pl.ds(8 + 2 * halves[kind] + chunk, 1)
                vec_ref[vec_row, :] += column_sum(tan_part.astype(F32))
                return carried + dot_nt(tan_part, we[kind, :, columns])

            for chunk in range(ws.shape[1] // COLS):
                normed_tan = expand_back(chunk, normed_tan)
        vec_ref[5:6, :] += column_sum(normed_tan * n_one)
        vec_ref[6:7, :] += column_sum(normed_tan)
        entry = norm_back(normed_tan, n_one, scale_one, gain_one)
        entry_ref[rows, :] = entry
        branch_low = (sum_tan + entry).astype(BF16)
        branch_tan[rows, :] = branch_low
        vec_ref[7:8, :] += column_sum(branch_low.astype(F32))
        for kind in range(2):
            mixed_tan[kind] = dot_nt(branch_low, wo[kind])
        for kind in range(2):
            for pair in range(2):
                columns = slice(pair * 128, pair * 128 + 128)
                for side in range(2):
                    head = halves[kind] * (H // 2) + 2 * pair + side
                    for core in range(2):
                        start = core * HALF
                        early = mixed_tan[kind, start : start + piece, columns]
                        late = mixed_tan[kind, start + piece : start + HALF, columns]
                        tan_send[step, head, core] = side_pair(side, early, late).astype(BF16)
        for i in range(H):
            for core in range(2):
                at.send(*tan_move(step, at.turn(i, H), core))
        for store in stores(step):
            store.start()
        return 0

    lax.fori_loop(0, 2, tile, 0)

    quarter = first_in.shape[0] // 4
    bits = (step_of(at.c, 1)[0], step_of(at.c, 2)[0])
    stages = (stage_a, stage_b)

    def core_move(region, give):
        bit = bits[region]
        start = region * 2 * quarter + (1 - bit if give else bit) * quarter
        where = span(start, quarter)
        slot = region + 2 * (0 if give else 1)
        return start, at.remote(
            send_grads.at[where], first_in.at[where], core_ss.at[slot], core_rs.at[slot],
            at.c, other,
        )

    order = [(0, True), (1, True), (0, False), (1, False)]
    low_turned[...] = jnp.transpose(low[...])
    operands = (mixed, low_turned, hidden, before_tan, feed_tan, branch_tan)
    feed_slopes(1, send_grads, *operands)
    for step in order:
        core_move(*step)[1].start()
    feed_slopes(0, own_grads, *operands)
    for side in range(2):
        for target in range(n_ctx):
            at.wait_sent(*o_move(target, side))
    for region, give in order:
        start, move = core_move(region, give)
        move.wait_recv()

        def join(offset, where, size):
            total = own_grads[where, :] + first_in[where, :].astype(F32)
            if give:
                stages[region][span(offset, size), :] = total.astype(BF16)
            else:
                keep_ref[region, span(offset, size), :] = total

        pieces_of(start, quarter, join)
    for source in range(n_ctx):
        for side in range(2):
            arrived = tan_out.at[source, side]
            at.remote(
                arrived, arrived, tan_ss.at[0], tan_rs.at[source * 2 + side], at.c, other
            ).wait_recv()
    for step in range(2):
        for store in stores(step):
            store.wait()
    for side in range(2):
        for head in range(H):
            for core in range(2):
                at.wait_sent(*tan_move(side, head, core))
    for step in order:
        core_move(*step)[1].wait_send()


def middle(n_ctx, o, x, summed, cotangent, wo, we, ws, be, vec):
    tokens, wide, units = x.shape[0], D // 2, ws[0].shape[0]
    grad_rows = 2 * units + wide
    rows = jax.ShapeDtypeStruct((tokens, D), F32)

    def sems(*counts):
        return [pltpu.SemaphoreType.DMA((count,)) for count in counts]

    return pl.pallas_call(
        functools.partial(middle_kernel, n_ctx),
        out_shape=(
            rows,
            rows,
            rows,
            jax.ShapeDtypeStruct((n_ctx, 2, HALF // 2, 128), BF16),
            jax.ShapeDtypeStruct((16, D), F32),
            jax.ShapeDtypeStruct((grad_rows // 4, D), BF16),
            jax.ShapeDtypeStruct((grad_rows // 4, D), BF16),
            jax.ShapeDtypeStruct((2, grad_rows // 4, D), F32),
        ),
        in_specs=[ANY] * 10 + [VMEM] * 2,
        out_specs=(ANY,) * 4 + (VMEM,) * 4,
        scratch_shapes=[
            pltpu.VMEM((2, H, 2, HALF // 2, 128), BF16),
            pltpu.VMEM((tokens, D), F32),
            pltpu.VMEM((tokens, D), F32),
            pltpu.VMEM((tokens, D), F32),
            pltpu.VMEM((2, wide, D), BF16),
            pltpu.VMEM((2, D, units), BF16),
            pltpu.VMEM((2, units, D), BF16),
            pltpu.VMEM((tokens, D), F32),
            pltpu.VMEM((tokens, D), F32),
            pltpu.VMEM((tokens, D), F32),
            pltpu.VMEM((2, tokens, wide), BF16),
            pltpu.VMEM((tokens, D), BF16),
            pltpu.VMEM((2, tokens, units), BF16),
            pltpu.VMEM((2, tokens, units), BF16),
            pltpu.VMEM((tokens, D), BF16),
            pltpu.VMEM((tokens, D), BF16),
            pltpu.VMEM((2, BLK, units), F32),
            pltpu.VMEM((2, BLK, wide), F32),
            pltpu.VMEM((2, H, 2, HALF // 2, 128), BF16),
            pltpu.VMEM((grad_rows, D), F32),
            pltpu.VMEM((grad_rows, D), BF16),
            pltpu.VMEM((grad_rows, D), BF16),
            pltpu.VMEM((D, tokens), BF16),
        ]
        + sems(9, 6, 2 * n_ctx, 4 * H, 4 * H, 2 * n_ctx, 4, 4),
        compiler_params=pltpu.CompilerParams(
            collective_id=1, has_side_effects=True, vmem_limit_bytes=ROOM
        ),
        name="middle",
    )(o, x, summed, cotangent, *wo, *we, *ws, be, vec)


def finish_kernel(
    n_ctx,
    dq_ref, dkv_ref, keep_hbm, land_a, land_b, x_hbm, entry_hbm, wq_hbm, wk_hbm, wv_hbm,
    w_other_hbm, vec_feed,
    post_ref, feed_ref, grads_ref, vec_out,
    own, part, ready, dq_in, dkv_in, keep, acc, stage, landing,
    x_in, entry_in, w_in, w_far, low_turned, tangents,
    own_grads, send_grads, first_in, acc_last, stage_last, landing_last, vec_sum, vec_in,
    load_sem, q_ss, q_rs, kv_ss, kv_rs, part_ss, part_rs, own_sem,
    down_ss, down_rs, up_ss, up_rs, top_ss, top_rs,
    core_ss, core_rs, down_ss2, down_rs2, up_ss2, up_rs2, vec_ss, vec_rs,
):
    at = Place()
    c, f = at.c, at.f
    other = 1 - f
    halves = (f, other)
    wide = D // 2
    loads = [
        pltpu.make_async_copy(src, dst, load_sem.at[i])
        for i, (src, dst) in enumerate(
            (
                (keep_hbm, keep),
                (x_hbm, x_in),
                (entry_hbm, entry_in),
                (wq_hbm, w_in.at[0]),
                (wk_hbm, w_in.at[1]),
                (wv_hbm, w_in.at[2]),
                (w_other_hbm, w_far),
            )
        )
    ]
    for load in loads:
        load.start()
    x_step, y_step, near, far = (step_of(c, stride) for stride in (1, 2, 4, 8))
    barrier = pltpu.get_barrier_semaphore()
    for _, peer in (x_step, y_step, near, far):
        pl.semaphore_signal(barrier, 1, device_id=(peer, f), device_id_type=MESH)
    at.greet_owners(n_ctx, True, 4)

    def partial_move(source):
        return at.remote(
            dkv_ref.at[2 * source + other],
            part.at[source],
            part_ss.at[source],
            part_rs.at[source],
            c,
            other,
        )

    def own_move(source):
        return pltpu.make_async_copy(
            dkv_ref.at[2 * source + f], own.at[source], own_sem.at[source]
        )

    def q_move(target):
        return (
            dq_ref.at[target],
            dq_in.at[at.head, f],
            q_ss.at[target],
            q_rs.at[at.head * 2 + f],
            target,
            at.group,
        )

    def kv_move(target):
        return (
            ready.at[target],
            dkv_in.at[at.head, pl.ds(pl.multiple_of(f * BLK, BLK), BLK)],
            kv_ss.at[target],
            kv_rs.at[at.head * 2 + f],
            target,
            at.group,
        )

    for i in range(n_ctx):
        source = at.turn(i, n_ctx)
        partial_move(source).start()
        own_move(source).start()
    for i in range(n_ctx):
        at.send(*q_move(at.turn(i, n_ctx)))

    size = keep.shape[1]
    firsts = (x_step, y_step)
    bases = [2 * size * region + firsts[region][0] * size for region in range(2)]
    feed = Ladder(
        at,
        ((y_step, near, far), (x_step, near, far)),
        (0, 0),
        size,
        [keep.at[region] for region in range(2)],
        [stage.at[region] for region in range(2)],
        [[landing.at[region, step] for step in range(3)] for region in range(2)],
        feed_ref,
        (down_ss, down_rs, up_ss, up_rs),
        bases,
    )

    def top_move(region, sent):
        side, columns = region % 2, columns_of(region)
        given = 2 * size * side + (1 - firsts[side][0]) * size
        where = span(bases[side] if sent else given, size)
        return at.remote(
            feed_ref.at[where, columns],
            feed_ref.at[where, columns],
            top_ss.at[region],
            top_rs.at[region],
            firsts[side][1],
            f,
        )

    loads[0].wait()
    kept_acc = [keep.at[region] for region in range(2)]
    sums = [acc.at[region] for region in range(2)]
    for region in range(REGIONS):
        first = (land_a, land_b)[region % 2]
        kept, given, half, _ = feed.ranges[region][0]
        feed.acc = kept_acc
        feed.join(region, given, half, first, stage.at[region % 2])
        feed.down(region, 0, True).start()
        feed.join(region, kept, half, first, sums[region % 2])
    feed.acc = sums
    for i in range(n_ctx):
        source = at.turn(i, n_ctx)
        own_move(source).wait()
        partial_move(source).wait_recv()
        ready[source] = jnp.transpose(own[source] + part[source]).astype(BF16)
        if i < n_ctx - 8:
            at.send(*kv_move(source))
    for load in loads[1:]:
        load.wait()
    low_turned[...] = jnp.transpose(x_in[...]).astype(BF16)
    for step in (1, 2):
        for region in range(REGIONS):
            feed.down(region, step - 1, False).wait_recv()
            feed.give(region, step, feed.landing[region % 2][step - 1])
        if step == 1:
            for i in range(n_ctx - 8, n_ctx):
                at.send(*kv_move(at.turn(i, n_ctx)))

    for target in range(n_ctx):
        partial_move(target).wait_send()
        at.wait_sent(*q_move(target))

    for head in range(H):
        for core in range(2):
            slot = head * 2 + core
            arrived = dq_in.at[head, core]
            at.remote(arrived, arrived, q_ss.at[0], q_rs.at[slot], c, other).wait_recv()
            arrived = dkv_in.at[head, pl.ds(core * BLK, BLK)]
            at.remote(arrived, arrived, kv_ss.at[0], kv_rs.at[slot], c, other).wait_recv()
    feed_rows = vec_feed.shape[0]
    vec_sum[0, 0:feed_rows] = vec_feed[...]
    vec_sum[0, feed_rows:] = jnp.zeros_like(vec_sum[0, feed_rows:])

    plans = ((x_step, y_step, near, far), (y_step, x_step, near, far))
    quarter = first_in.shape[0] // 4
    last = Ladder(
        at,
        plans,
        (0, 2 * quarter),
        2 * quarter,
        [acc_last, acc_last],
        [stage_last, stage_last],
        [[landing_last.at[step] for step in range(4)]] * 2,
        grads_ref,
        (down_ss2, down_rs2, up_ss2, up_rs2),
    )

    def core_move(region, give):
        kept, given, rows, _ = last.ranges[region][0]
        where = span(given if give else kept, rows)
        slot, columns = region + REGIONS * (0 if give else 1), columns_of(region)
        return at.remote(
            send_grads.at[where, columns],
            first_in.at[where, columns],
            core_ss.at[slot],
            core_rs.at[slot],
            c,
            other,
        )

    order = [(region, give) for give in (True, False) for region in range(REGIONS)]
    vec_peers = [(c, other)] + [(peer, f) for _, peer in (x_step, y_step, near, far)]

    def vec_move(step):
        return at.remote(
            vec_sum.at[step], vec_in.at[step], vec_ss.at[step], vec_rs.at[step], *vec_peers[step]
        )

    def vec_next(step):
        vec_move(step).wait_recv()
        target = vec_sum.at[step + 1] if step < 4 else vec_out
        target[...] = vec_sum[step] + vec_in[step]
        if step < 4:
            vec_move(step + 1).start()

    for kind, grad_ref in ((1, send_grads), (0, own_grads)):
        for pair in range(2):
            head = halves[kind] * (H // 2) + 2 * pair
            columns = slice(pair * 128, pair * 128 + 128)
            for core in range(2):
                early = dq_in[head, core].astype(F32)
                late = dq_in[head + 1, core].astype(F32)
                for side in range(2):
                    start = side * BLK + core * HALF
                    tangents[kind, 0, start : start + HALF, columns] = side_pair(
                        side, early, late
                    ).astype(BF16)
            early = dkv_in[head].astype(F32)
            late = dkv_in[head + 1].astype(F32)
            tangents[kind, 1, :, columns] = low_pair(early, late).astype(BF16)
            tangents[kind, 2, :, columns] = high_pair(early, late).astype(BF16)
        turned = low_turned[...]
        grad_ref[0:D, 0:wide] = dot_nn(turned, tangents[kind, 0]).astype(grad_ref.dtype)
        grad_ref[0:D, wide:D] = dot_nn(turned, tangents[kind, 1]).astype(grad_ref.dtype)
        value_grad = dot_nn(turned, tangents[kind, 2]).astype(grad_ref.dtype)
        grad_ref[D : D + wide, 0:wide] = value_grad[0:wide]
        grad_ref[D : D + wide, wide:D] = value_grad[wide:D]
        columns = pl.ds(pl.multiple_of(halves[kind] * wide, wide), wide)
        vec_sum[0, feed_rows : feed_rows + 1, columns] = column_sum(tangents[kind, 0].astype(F32))
        vec_sum[0, feed_rows + 1 : feed_rows + 2, columns] = column_sum(
            tangents[kind, 2].astype(F32)
        )
        if kind == 1:
            for step in order:
                core_move(*step).start()
    vec_move(0).start()
    for region, give in order:
        core_move(region, give).wait_recv()
        kept, given, rows, _ = last.ranges[region][0]
        columns = columns_of(region)

        def join(offset, where, _):
            total = own_grads[where, columns] + first_in[where, columns].astype(F32)
            if give:
                stage_last[where, columns] = total.astype(BF16)
            else:
                acc_last[where, columns] = total

        pieces_of(given if give else kept, rows, join)
        if give:
            last.down(region, 0, True).start()
    vec_next(0)
    total = entry_in[...]
    for which in range(3):
        total = total + dot_nt(tangents[0, which], w_in[which])
        total = total + dot_nt(tangents[1, which], w_far[which])
    post_ref[...] = total
    for target in range(n_ctx):
        at.wait_sent(*kv_move(target))
    for step in order:
        core_move(*step).wait_send()
    for region in range(REGIONS):
        feed.settle(region)
    for region in range(REGIONS):
        feed.up(region, 1, False).wait_recv()
        feed.up(region, 0, True).start()
    for region in range(REGIONS):
        last.down(region, 0, False).wait_recv()
        last.give(region, 1, last.landing[region % 2][0])
    vec_next(1)
    for region in range(REGIONS):
        feed.up(region, 0, False).wait_recv()
        top_move(region, True).start()
    for region in range(REGIONS):
        last.down(region, 1, False).wait_recv()
        last.give(region, 2, last.landing[region % 2][1])
    vec_next(2)
    for region in range(REGIONS):
        last.down(region, 2, False).wait_recv()
        last.give(region, 3, last.landing[region % 2][2])
    vec_next(3)
    for region in range(REGIONS):
        last.settle(region)
    vec_next(4)
    feed.wait_down()
    for step in (2, 1, 0):
        for region in range(REGIONS):
            last.up(region, step, False).wait_recv()
            if step > 0:
                last.up(region, step - 1, True).start()
        if step == 2:
            last.wait_down()
        if step == 1:
            feed.wait_up((0, 1))
            last.wait_up((1, 2))
            for index in range(5):
                vec_move(index).wait_send()
    for region in range(REGIONS):
        top_move(region, False).wait_recv()

    for region in range(REGIONS):
        top_move(region, True).wait_send()
    last.wait_up((0,))


def finish(n_ctx, dq, dkv, keep, land_a, land_b, x, entry, wq, wk, wv, w_other, vec_feed):
    size, tokens, wide = keep.shape[1], x.shape[0], D // 2
    last_shape = (D + wide, D)
    vec_shape = (vec_feed.shape[0] + 8, D)

    def sems(*counts):
        return [pltpu.SemaphoreType.DMA((count,)) for count in counts]

    return pl.pallas_call(
        functools.partial(finish_kernel, n_ctx),
        out_shape=(
            jax.ShapeDtypeStruct((tokens, D), F32),
            jax.ShapeDtypeStruct((4 * size, D), BF16),
            jax.ShapeDtypeStruct(last_shape, BF16),
            jax.ShapeDtypeStruct(vec_shape, F32),
        ),
        in_specs=[ANY, ANY, ANY, VMEM, VMEM] + [ANY] * 6 + [VMEM],
        out_specs=(VMEM,) * 4,
        scratch_shapes=[
            pltpu.VMEM((n_ctx, 128, BLK), F32),
            pltpu.VMEM((n_ctx, 128, BLK), F32),
            pltpu.VMEM((n_ctx, BLK, 128), BF16),
            pltpu.VMEM((H, 2, HALF, 128), BF16),
            pltpu.VMEM((H, 2 * BLK, 128), BF16),
            pltpu.VMEM((2, size, D), F32),
            pltpu.VMEM((2, size, D), F32),
            pltpu.VMEM((2, size, D), BF16),
            pltpu.VMEM((2, 3, size, D), BF16),
            pltpu.VMEM((tokens, D), F32),
            pltpu.VMEM((tokens, D), F32),
            pltpu.VMEM((3, D, wide), BF16),
            pltpu.VMEM((3, D, wide), BF16),
            pltpu.VMEM((D, tokens), BF16),
            pltpu.VMEM((2, 3, tokens, wide), BF16),
            pltpu.VMEM(last_shape, F32),
            pltpu.VMEM(last_shape, BF16),
            pltpu.VMEM(last_shape, BF16),
            pltpu.VMEM(last_shape, F32),
            pltpu.VMEM(last_shape, BF16),
            pltpu.VMEM((4,) + last_shape, BF16),
            pltpu.VMEM((5,) + vec_shape, F32),
            pltpu.VMEM((5,) + vec_shape, F32),
        ]
        + sems(7, n_ctx, 2 * H, n_ctx, 2 * H, n_ctx, n_ctx, n_ctx)
        + sems(12, 12, 12, 12, 4, 4, 8, 8, 16, 16, 16, 16, 5, 5),
        compiler_params=pltpu.CompilerParams(
            collective_id=3, has_side_effects=True, vmem_limit_bytes=ROOM
        ),
        name="finish",
    )(dq, dkv, keep, land_a, land_b, x, entry, wq, wk, wv, w_other, vec_feed)


def unpack_kernel(
    full, grads, post, vec_ref,
    query_ref, key_ref, value_ref, output_ref, expand_ref, shrink_ref, post_out, *vector_outs,
):
    f = lax.axis_index("fsdp")
    units, wide = shrink_ref.shape[0], D // 2
    shrink_ref[...] = full[0:units].astype(F32)
    for part in range(units // D):
        start = units + part * D
        expand_ref[:, part * D : part * D + D] = full[start : start + D].astype(F32)
    output_ref[...] = full[2 * units : 2 * units + wide].astype(F32)
    query_ref[...] = grads[0:D, 0:wide].astype(F32)
    key_ref[...] = grads[0:D, wide:D].astype(F32)
    value_ref[0:wide] = grads[D : D + wide, 0:wide].astype(F32)
    value_ref[wide:D] = grads[D : D + wide, wide:D].astype(F32)
    post_out[...] = post[...]
    vectors = vec_ref[...]
    mine = jnp.where(f == 0, vectors[:, 0:wide], vectors[:, wide:D])
    for row, ref in zip((16, 17, 7, 5, 6, 0, 1, 2, 3, 4), vector_outs):
        ref[...] = mine[row : row + 1]
    drift = jnp.where(f == 0, vectors[8:10], vectors[10:12])
    for part in range(units // D):
        vector_outs[10][:, part * D : part * D + D] = drift[part : part + 1]


def unpack_grads(units, full, grads, post, vecs):
    wide = D // 2
    shapes = [(D, wide)] * 3 + [(wide, D), (D, units), (units, D), post.shape]
    shapes = shapes + [(1, wide)] * 10 + [(1, units)]
    return pl.pallas_call(
        unpack_kernel,
        out_shape=tuple(jax.ShapeDtypeStruct(shape, F32) for shape in shapes),
        in_specs=[VMEM] * 4,
        out_specs=(VMEM,) * len(shapes),
        compiler_params=pltpu.CompilerParams(vmem_limit_bytes=UNPACK_ROOM),
        name="unpack_grads",
    )(full, grads, post, vecs)


def head_shards(
    n_ctx,
    post_stream,
    sum_stream,
    cotangent,
    block_order,
    block_sequence,
    query_weight,
    key_weight,
    value_weight,
    output_weight,
    query_bias,
    value_bias,
    output_bias,
    attend_gain,
    attend_shift,
    expand_weight,
    expand_bias,
    shrink_weight,
    shrink_bias,
    middle_gain,
    middle_shift,
    final_gain,
    final_shift,
):
    x, summed, tangent = post_stream[0], sum_stream[0], cotangent[0]
    def across(values, stride):
        return lax.ppermute(values, "ctx", [(c, c ^ stride) for c in range(n_ctx)])

    vectors = [
        query_bias,
        value_bias,
        output_bias,
        attend_gain,
        attend_shift,
        shrink_bias,
        middle_gain,
        middle_shift,
        final_gain,
        final_shift,
        expand_bias,
    ]
    q, kv, w_other, order, seqs, vec, expand_add, wo_other, we_other, ws_other = (
        project_and_scatter(
            n_ctx,
            x,
            query_weight,
            key_weight,
            value_weight,
            block_order,
            block_sequence,
            (output_weight, expand_weight, shrink_weight),
            vectors,
        )
    )
    o, keep, lse, pairs = attend(order, seqs, q, kv)
    layer_output, sum_tan, entry, tan, vec_feed, stage_a, stage_b, kept = middle(
        n_ctx,
        o,
        x,
        summed,
        tangent,
        (output_weight, wo_other),
        (expand_weight, we_other),
        (shrink_weight, ws_other),
        expand_add,
        vec,
    )
    land_a, land_b = across(stage_a, 1), across(stage_b, 2)
    dq, dkv, layer_output, sum_tan = attend_back(
        pairs, q, tan, keep, lse, kv, (layer_output, sum_tan)
    )
    post_tangent, feed_sums, last_sums, vecs = finish(
        n_ctx,
        dq,
        dkv,
        kept,
        land_a,
        land_b,
        x,
        entry,
        query_weight,
        key_weight,
        value_weight,
        w_other,
        vec_feed,
    )
    (
        query_slope,
        key_slope,
        value_slope,
        output_slope,
        expand_slope,
        shrink_slope,
        post_tangent,
        query_drift,
        value_drift,
        output_drift,
        attend_stretch,
        attend_nudge,
        shrink_drift,
        middle_stretch,
        middle_nudge,
        final_stretch,
        final_nudge,
        expand_drift,
    ) = unpack_grads(shrink_weight.shape[0], feed_sums, last_sums, post_tangent, vecs)
    return (
        layer_output[None],
        post_tangent[None],
        sum_tan[None],
        query_slope,
        key_slope,
        value_slope,
        output_slope,
        query_drift[0],
        value_drift[0],
        output_drift[0],
        attend_stretch[0],
        attend_nudge[0],
        expand_slope,
        expand_drift[0],
        shrink_slope,
        shrink_drift[0],
        middle_stretch[0],
        middle_nudge[0],
        final_stretch[0],
        final_nudge[0],
    )


def solution(mesh):
    n_ctx, n_fsdp = mesh.shape["ctx"], mesh.shape["fsdp"]
    if n_fsdp == 2 and n_ctx == n_fsdp * H:
        body = functools.partial(head_shards, n_ctx)
    else:
        body = general_shards
    return jax.shard_map(
        body,
        mesh=mesh,
        in_specs=(
            P("fsdp", "ctx", None),
            P("fsdp", "ctx", None),
            P("fsdp", "ctx", None),
            P("fsdp", None),
            P("fsdp", None),
            P(None, "fsdp"),
            P(None, "fsdp"),
            P(None, "fsdp"),
            P("fsdp", None),
            P("fsdp"),
            P("fsdp"),
            P("fsdp"),
            P("fsdp"),
            P("fsdp"),
            P(None, "fsdp"),
            P("fsdp"),
            P("fsdp", None),
            P("fsdp"),
            P("fsdp"),
            P("fsdp"),
            P("fsdp"),
            P("fsdp"),
        ),
        out_specs=(
            P("fsdp", "ctx", None),
            P("fsdp", "ctx", None),
            P("fsdp", "ctx", None),
            P(None, "fsdp"),
            P(None, "fsdp"),
            P(None, "fsdp"),
            P("fsdp", None),
            P("fsdp"),
            P("fsdp"),
            P("fsdp"),
            P("fsdp"),
            P("fsdp"),
            P(None, "fsdp"),
            P("fsdp"),
            P("fsdp", None),
            P("fsdp"),
            P("fsdp"),
            P("fsdp"),
            P("fsdp"),
            P("fsdp"),
        ),
        check_vma=False,
    )
```

```python
import functools

import jax
import jax.numpy as jnp
from jax import lax
from jax.experimental import pallas as pl
from jax.experimental.pallas import tpu as pltpu
from jax.sharding import PartitionSpec as P

D = 512
H = 8
HD = 64
BLK = 256
HALF = BLK // 2
LONG = 8
TOGETHER = 32
MOST = LONG + 1
F32 = jnp.float32
BF16 = jnp.bfloat16
MESH = pl.DeviceIdType.MESH
ROOM = 60 << 20
UNPACK_ROOM = 60 << 20
VMEM = pl.BlockSpec(memory_space=pltpu.VMEM)
SMEM = pl.BlockSpec(memory_space=pltpu.SMEM)
ANY = pl.BlockSpec(memory_space=pltpu.HBM)


norm_eps = 1e-05
masked_value = -1e30
gelu_coeff = 0.7978845608
gelu_cubic = 0.044715


def smooth_gate(values):
    return (
        0.5
        * values
        * (1.0 + jnp.tanh(gelu_coeff * (values + gelu_cubic * values * values * values)))
    )


def layer_norm(inputs, gain_row, shift_row):
    centre = inputs - jnp.mean(inputs, axis=-1, keepdims=True)
    spread = jnp.mean(centre * centre, axis=-1, keepdims=True)
    return centre * lax.rsqrt(spread + norm_eps) * gain_row + shift_row


def product(left_side, right_side):
    return jnp.dot(left_side, right_side, preferred_element_type=jnp.float32)


def cross_rows(left_side, right_side):
    return lax.dot_general(
        left_side, right_side, (((0,), (0,)), ((), ())), preferred_element_type=jnp.float32
    )


def cross_cols(left_side, right_side):
    return lax.dot_general(
        left_side, right_side, (((1,), (1,)), ((), ())), preferred_element_type=jnp.float32
    )


def column_total(values):
    return jnp.sum(values, axis=0, dtype=jnp.float32)


def lookup(table_row, indices):
    places = jnp.arange(table_row.shape[0], dtype=jnp.int32)
    return jnp.sum(jnp.where(indices[:, None] == places[None, :], table_row[None, :], 0), axis=1)


def block_mask(query_blocks, query_seqs, key_blocks, key_seqs):
    same_seq = query_seqs[:, None] == key_seqs[None, :]
    return same_seq & (key_blocks[None, :] <= query_blocks[:, None])


def token_mask(visible):
    return jnp.repeat(jnp.repeat(visible, BLK, axis=0), BLK, axis=1)


def fold_units(carried, members, unit_step):
    unit_count = members[0].shape[0] // BLK
    inner_count = max((divisor for divisor in range(1, 17) if unit_count % divisor == 0))
    outer_count = unit_count // inner_count

    def outer_turn(outer_index, current):

        def inner_turn(inner_index, inner_state):
            offset = (outer_index * inner_count + inner_index) * BLK
            pieces = tuple((lax.dynamic_slice_in_dim(member, offset, BLK, 0) for member in members))
            return unit_step(inner_state, pieces, offset)

        return lax.fori_loop(0, inner_count, inner_turn, current)

    return lax.fori_loop(0, outer_count, outer_turn, carried)


def general_shards(
    post_stream,
    sum_stream,
    cotangent,
    block_order,
    block_sequence,
    query_weight,
    key_weight,
    value_weight,
    output_weight,
    query_bias,
    value_bias,
    output_bias,
    attend_gain,
    attend_shift,
    expand_weight,
    expand_bias,
    shrink_weight,
    shrink_bias,
    middle_gain,
    middle_shift,
    final_gain,
    final_shift,
):
    (
        query_whole,
        key_whole,
        value_whole,
        output_whole,
        query_add,
        value_add,
        output_add,
        gain_one,
        shift_one,
        expand_whole,
        expand_add,
        shrink_whole,
        shrink_add,
        gain_two,
        shift_two,
        gain_last,
        shift_last,
    ) = (
        lax.all_gather(query_weight, "fsdp", axis=1, tiled=True),
        lax.all_gather(key_weight, "fsdp", axis=1, tiled=True),
        lax.all_gather(value_weight, "fsdp", axis=1, tiled=True),
        lax.all_gather(output_weight, "fsdp", axis=0, tiled=True),
        lax.all_gather(query_bias, "fsdp", axis=0, tiled=True),
        lax.all_gather(value_bias, "fsdp", axis=0, tiled=True),
        lax.all_gather(output_bias, "fsdp", axis=0, tiled=True),
        lax.all_gather(attend_gain, "fsdp", axis=0, tiled=True),
        lax.all_gather(attend_shift, "fsdp", axis=0, tiled=True),
        lax.all_gather(expand_weight, "fsdp", axis=1, tiled=True),
        lax.all_gather(expand_bias, "fsdp", axis=0, tiled=True),
        lax.all_gather(shrink_weight, "fsdp", axis=0, tiled=True),
        lax.all_gather(shrink_bias, "fsdp", axis=0, tiled=True),
        lax.all_gather(middle_gain, "fsdp", axis=0, tiled=True),
        lax.all_gather(middle_shift, "fsdp", axis=0, tiled=True),
        lax.all_gather(final_gain, "fsdp", axis=0, tiled=True),
        lax.all_gather(final_shift, "fsdp", axis=0, tiled=True),
    )
    post_rows = post_stream[0]
    summed = sum_stream[0]
    tangent = cotangent[0]
    order_row = block_order[0]
    seq_row = block_sequence[0]
    token_count = post_rows.shape[0]
    score_scale = HD ** (-0.5)
    own_blocks = lax.dynamic_slice_in_dim(
        order_row, lax.axis_index("ctx") * (token_count // BLK), token_count // BLK
    )
    own_seqs = lookup(seq_row, own_blocks)
    post_low = post_rows.astype(jnp.bfloat16)
    queries = (product(post_low, query_whole) + query_add).astype(jnp.bfloat16)
    key_rows = product(post_low, key_whole).astype(jnp.bfloat16)
    value_rows = (product(post_low, value_whole) + value_add).astype(jnp.bfloat16)
    query_heads = queries.reshape(token_count, H, HD)

    def keys_visible(first_row):
        key_block = lax.dynamic_slice_in_dim(order_row, first_row // BLK, 1)
        return block_mask(own_blocks, own_seqs, key_block, lookup(seq_row, key_block))

    def masked_fold(block_step):

        def unit_step(current, pieces, first_row):
            visible = keys_visible(first_row)
            return lax.cond(
                jnp.any(visible),
                lambda inner_state: block_step(inner_state, pieces, visible),
                lambda inner_state: inner_state,
                current,
            )

        def folded(current, pieces, first_row):
            return fold_units(current, pieces, unit_step)

        return folded

    def stats_block(current, pieces, visible):
        row_peaks, masses = current
        key_heads = pieces[0].reshape(BLK, H, HD)
        row_mask = token_mask(visible)[None]
        scores = (
            jnp.einsum("qhd,khd->hqk", query_heads, key_heads, preferred_element_type=jnp.float32)
            * score_scale
        )
        new_peaks = jnp.maximum(
            row_peaks, jnp.max(jnp.where(row_mask, scores, masked_value), axis=2)
        )
        weights = jnp.where(row_mask, jnp.exp(scores - new_peaks[:, :, None]), 0.0)
        return (new_peaks, masses * jnp.exp(row_peaks - new_peaks) + jnp.sum(weights, axis=2))

    stats_fold = masked_fold(stats_block)
    stats_start = (
        jnp.full((H, token_count), masked_value, jnp.float32),
        jnp.zeros((H, token_count), jnp.float32),
    )
    row_peaks, masses = stats_fold(
        stats_start, (lax.all_gather(key_rows, "ctx", axis=0, tiled=True),), jnp.int32(0)
    )
    log_mass = row_peaks + jnp.log(masses)

    def forward_block(current, pieces, visible):
        key_heads = pieces[0].reshape(BLK, H, HD)
        value_heads = pieces[1].reshape(BLK, H, HD)
        row_mask = token_mask(visible)[None]
        scores = (
            jnp.einsum("qhd,khd->hqk", query_heads, key_heads, preferred_element_type=jnp.float32)
            * score_scale
        )
        weights = jnp.where(row_mask, jnp.exp(scores - log_mass[:, :, None]), 0.0).astype(
            jnp.bfloat16
        )
        addition = jnp.einsum(
            "hqk,khd->qhd", weights, value_heads, preferred_element_type=jnp.float32
        )
        return current + addition.reshape(token_count, D)

    forward_fold = masked_fold(forward_block)
    zero_rows = jnp.zeros((token_count, D), jnp.float32)
    attended = forward_fold(
        zero_rows,
        (
            lax.all_gather(key_rows, "ctx", axis=0, tiled=True),
            lax.all_gather(value_rows, "ctx", axis=0, tiled=True),
        ),
        jnp.int32(0),
    )
    mixed_low = attended.astype(jnp.bfloat16)
    branch = product(mixed_low, output_whole) + output_add
    normed_one, first_pull = jax.vjp(
        layer_norm, post_rows + branch, gain_one.astype(jnp.float32), shift_one.astype(jnp.float32)
    )
    stream_one = summed + branch
    normed_low = normed_one.astype(jnp.bfloat16)
    before = product(normed_low, expand_whole) + expand_add
    gated, gate_pull = jax.vjp(smooth_gate, before)
    hidden = gated.astype(jnp.bfloat16)
    feed_out = product(hidden, shrink_whole) + shrink_add
    normed_two, middle_pull = jax.vjp(
        layer_norm,
        normed_one + feed_out,
        gain_two.astype(jnp.float32),
        shift_two.astype(jnp.float32),
    )
    stream_two = stream_one + feed_out
    last_norm, last_pull = jax.vjp(
        layer_norm, stream_two, gain_last.astype(jnp.float32), shift_last.astype(jnp.float32)
    )
    layer_output = normed_two + last_norm
    stream_tan, stretch_last, nudge_last = last_pull(tangent)
    inflow_tan, stretch_two, nudge_two = middle_pull(tangent)
    feed_tan = (stream_tan + inflow_tan).astype(jnp.bfloat16)
    slope_shrink = cross_rows(hidden, feed_tan)
    drift_shrink = column_total(feed_tan)
    before_tan = gate_pull(cross_cols(feed_tan, shrink_whole))[0].astype(jnp.bfloat16)
    slope_expand = cross_rows(normed_low, before_tan)
    drift_expand = column_total(before_tan)
    normed_tan = inflow_tan + cross_cols(before_tan, expand_whole)
    feed_parts = lax.psum(
        (
            slope_expand,
            drift_expand,
            slope_shrink,
            drift_shrink,
            stretch_two,
            nudge_two,
            stretch_last,
            nudge_last,
        ),
        "ctx",
    )
    feed_sums = (
        lax.psum_scatter(feed_parts[0], "fsdp", scatter_dimension=1, tiled=True),
        lax.psum_scatter(feed_parts[1], "fsdp", scatter_dimension=0, tiled=True),
        lax.psum_scatter(feed_parts[2], "fsdp", scatter_dimension=0, tiled=True),
        lax.psum_scatter(feed_parts[3], "fsdp", scatter_dimension=0, tiled=True),
        lax.psum_scatter(feed_parts[4], "fsdp", scatter_dimension=0, tiled=True),
        lax.psum_scatter(feed_parts[5], "fsdp", scatter_dimension=0, tiled=True),
        lax.psum_scatter(feed_parts[6], "fsdp", scatter_dimension=0, tiled=True),
        lax.psum_scatter(feed_parts[7], "fsdp", scatter_dimension=0, tiled=True),
    )
    entry_tan, stretch_one, nudge_one = first_pull(normed_tan)
    branch_tan = (stream_tan + entry_tan).astype(jnp.bfloat16)
    slope_output = cross_rows(mixed_low, branch_tan)
    drift_output = column_total(branch_tan)
    mixed_tan = cross_cols(branch_tan, output_whole).astype(jnp.bfloat16)
    tangent_heads = mixed_tan.reshape(token_count, H, HD)
    deltas = jnp.sum((mixed_tan * attended).reshape(token_count, H, HD), axis=2).T

    def query_block(current, pieces, visible):
        key_heads = pieces[0].reshape(BLK, H, HD)
        value_heads = pieces[1].reshape(BLK, H, HD)
        row_mask = token_mask(visible)[None]
        scores = (
            jnp.einsum("qhd,khd->hqk", query_heads, key_heads, preferred_element_type=jnp.float32)
            * score_scale
        )
        probability = jnp.where(row_mask, jnp.exp(scores - log_mass[:, :, None]), 0.0)
        prob_tan = jnp.einsum(
            "qhd,khd->hqk", tangent_heads, value_heads, preferred_element_type=jnp.float32
        )
        score_tan = (probability * (prob_tan - deltas[:, :, None])).astype(jnp.bfloat16)
        addition = jnp.einsum(
            "hqk,khd->qhd", score_tan, key_heads, preferred_element_type=jnp.float32
        )
        return current + addition.reshape(token_count, D) * score_scale

    query_fold = masked_fold(query_block)
    query_sum = query_fold(
        zero_rows,
        (
            lax.all_gather(key_rows, "ctx", axis=0, tiled=True),
            lax.all_gather(value_rows, "ctx", axis=0, tiled=True),
        ),
        jnp.int32(0),
    )
    gathered_mass, gathered_delta = (
        lax.all_gather(log_mass.T, "ctx", axis=0, tiled=True),
        lax.all_gather(deltas.T, "ctx", axis=0, tiled=True),
    )
    own_keys = key_rows.reshape(token_count, H, HD)
    own_values = value_rows.reshape(token_count, H, HD)

    def owner_block(current, pieces, first_row, visible):
        key_acc, value_acc = current
        part_queries = pieces[0].reshape(BLK, H, HD)
        part_tangent = pieces[1].reshape(BLK, H, HD)
        part_mass = lax.dynamic_slice_in_dim(gathered_mass, first_row, BLK, 0).T
        part_delta = lax.dynamic_slice_in_dim(gathered_delta, first_row, BLK, 0).T
        row_mask = token_mask(visible)[None]
        scores = (
            jnp.einsum("qhd,khd->hqk", part_queries, own_keys, preferred_element_type=jnp.float32)
            * score_scale
        )
        probability = jnp.where(row_mask, jnp.exp(scores - part_mass[:, :, None]), 0.0)
        value_add_rows = jnp.einsum(
            "hqk,qhd->khd",
            probability.astype(jnp.bfloat16),
            part_tangent,
            preferred_element_type=jnp.float32,
        )
        prob_tan = jnp.einsum(
            "qhd,khd->hqk", part_tangent, own_values, preferred_element_type=jnp.float32
        )
        score_tan = (probability * (prob_tan - part_delta[:, :, None])).astype(jnp.bfloat16)
        key_add_rows = jnp.einsum(
            "hqk,qhd->khd", score_tan, part_queries, preferred_element_type=jnp.float32
        )
        return (
            key_acc + key_add_rows.reshape(token_count, D) * score_scale,
            value_acc + value_add_rows.reshape(token_count, D),
        )

    def owner_unit(current, pieces, first_row):
        query_blocks = lax.dynamic_slice_in_dim(order_row, first_row // BLK, 1)
        visible = block_mask(query_blocks, lookup(seq_row, query_blocks), own_blocks, own_seqs)
        return lax.cond(
            jnp.any(visible),
            lambda inner_state: owner_block(inner_state, pieces, first_row, visible),
            lambda inner_state: inner_state,
            current,
        )

    key_sum, value_sum = fold_units(
        (zero_rows, zero_rows),
        (
            lax.all_gather(queries, "ctx", axis=0, tiled=True),
            lax.all_gather(mixed_tan, "ctx", axis=0, tiled=True),
        ),
        owner_unit,
    )
    query_tan = query_sum.astype(jnp.bfloat16)
    key_tan = key_sum.astype(jnp.bfloat16)
    value_tan = value_sum.astype(jnp.bfloat16)
    slope_query = cross_rows(post_low, query_tan)
    slope_key = cross_rows(post_low, key_tan)
    slope_value = cross_rows(post_low, value_tan)
    drift_query = column_total(query_tan)
    drift_value = column_total(value_tan)
    post_tangent = (
        entry_tan
        + cross_cols(query_tan, query_whole)
        + cross_cols(key_tan, key_whole)
        + cross_cols(value_tan, value_whole)
    )
    heads_parts = lax.psum(
        (
            slope_query,
            slope_key,
            slope_value,
            slope_output,
            drift_query,
            drift_value,
            drift_output,
            stretch_one,
            nudge_one,
        ),
        "ctx",
    )
    heads_sums = (
        lax.psum_scatter(heads_parts[0], "fsdp", scatter_dimension=1, tiled=True),
        lax.psum_scatter(heads_parts[1], "fsdp", scatter_dimension=1, tiled=True),
        lax.psum_scatter(heads_parts[2], "fsdp", scatter_dimension=1, tiled=True),
        lax.psum_scatter(heads_parts[3], "fsdp", scatter_dimension=0, tiled=True),
        lax.psum_scatter(heads_parts[4], "fsdp", scatter_dimension=0, tiled=True),
        lax.psum_scatter(heads_parts[5], "fsdp", scatter_dimension=0, tiled=True),
        lax.psum_scatter(heads_parts[6], "fsdp", scatter_dimension=0, tiled=True),
        lax.psum_scatter(heads_parts[7], "fsdp", scatter_dimension=0, tiled=True),
        lax.psum_scatter(heads_parts[8], "fsdp", scatter_dimension=0, tiled=True),
    )
    return (
        layer_output[None],
        post_tangent[None],
        stream_tan[None],
        heads_sums[0],
        heads_sums[1],
        heads_sums[2],
        heads_sums[3],
        heads_sums[4],
        heads_sums[5],
        heads_sums[6],
        heads_sums[7],
        heads_sums[8],
        feed_sums[0],
        feed_sums[1],
        feed_sums[2],
        feed_sums[3],
        feed_sums[4],
        feed_sums[5],
        feed_sums[6],
        feed_sums[7],
    )


def low_lanes(values):
    return lax.broadcasted_iota(jnp.int32, values.shape, 1) < HD


def swap_lanes(values):
    return pltpu.roll(values, HD, 1)


def low_pair(first, second):
    return jnp.where(low_lanes(first), first, swap_lanes(second))


def high_pair(first, second):
    return jnp.where(low_lanes(first), swap_lanes(first), second)


def side_pair(side, first, second):
    return low_pair(first, second) if side == 0 else high_pair(first, second)


def dot_nn(left, right):
    return jnp.dot(left, right, preferred_element_type=F32)


def dot_nt(left, right):
    return lax.dot_general(left, right, (((1,), (1,)), ((), ())), preferred_element_type=F32)


def dot_tn(left, right):
    return lax.dot_general(left, right, (((0,), (0,)), ((), ())), preferred_element_type=F32)


class Place:
    def __init__(self):
        self.c = lax.axis_index("ctx")
        self.f = lax.axis_index("fsdp")
        self.group = self.c // H
        self.head = self.c % H
        self.inside = jnp.where(self.group == self.f, 1, 0)

    def is_me(self, tc, tf):
        return jnp.logical_and(self.c == tc, self.f == tf)

    def signal(self, barrier, tc, tf):
        @pl.when(jnp.logical_not(self.is_me(tc, tf)))
        def _():
            pl.semaphore_signal(barrier, 1, device_id=(tc, tf), device_id_type=MESH)

    def turn(self, i, n):
        return (self.c + 5 * i) % n

    def greet_sources(self, n_ctx, partner):
        barrier = pltpu.get_barrier_semaphore()
        for tc in range(n_ctx):
            self.signal(barrier, tc, self.group)
        if partner:
            pl.semaphore_signal(
                barrier, 1, device_id=(self.c, 1 - self.f), device_id_type=MESH
            )
        pl.semaphore_wait(barrier, 2 * H + (1 if partner else 0) - self.inside)

    def greet_owners(self, n_ctx, partner, more=0):
        barrier = pltpu.get_barrier_semaphore()
        for head in range(H):
            for core in range(2):
                self.signal(barrier, self.f * H + head, core)
        if partner:
            pl.semaphore_signal(
                barrier, 1, device_id=(self.c, 1 - self.f), device_id_type=MESH
            )
        pl.semaphore_wait(barrier, n_ctx + (1 if partner else 0) + more - self.inside)

    def send(self, src, dst, send_sem, recv_sem, tc, tf):
        me = self.is_me(tc, tf)

        @pl.when(me)
        def _():
            pltpu.make_async_copy(src, dst, recv_sem).start()

        @pl.when(jnp.logical_not(me))
        def _():
            self.remote(src, dst, send_sem, recv_sem, tc, tf).start()

    def remote(self, src, dst, send_sem, recv_sem, tc, tf):
        return pltpu.make_async_remote_copy(
            src_ref=src,
            dst_ref=dst,
            send_sem=send_sem,
            recv_sem=recv_sem,
            device_id=(tc, tf),
            device_id_type=MESH,
        )

    def wait_sent(self, src, dst, send_sem, recv_sem, tc, tf):
        @pl.when(jnp.logical_not(self.is_me(tc, tf)))
        def _():
            self.remote(src, dst, send_sem, recv_sem, tc, tf).wait_send()


VECTORS = 10


def project_kernel(
    n_ctx,
    x_hbm,
    wq_hbm,
    wk_hbm,
    wv_hbm,
    order_hbm,
    seq_hbm,
    *rest,
):
    dense_hbm, rest = rest[:3], rest[3:]
    vector_hbm, rest = rest[: VECTORS + 1], rest[VECTORS + 1 :]
    vector_in, rest = rest[-VECTORS - 1 :], rest[: -VECTORS - 1]
    (
        q_out,
        kv_out,
        w_other,
        order_out,
        seq_out,
        vec_out,
        expand_out,
        wo_other,
        we_other,
        ws_other,
        x_in,
        w_own,
        w_in,
        bias_own,
        bias_in,
        order_own,
        seq_own,
        order_in,
        seq_in,
        q_send,
        kv_send,
        load_sem,
        w_ss,
        w_rs,
        q_ss,
        q_rs,
        kv_ss,
        kv_rs,
        relay_ss,
        relay_rs,
    ) = rest
    at = Place()
    other = 1 - at.f
    loads = [
        pltpu.make_async_copy(src, dst, load_sem.at[i])
        for i, (src, dst) in enumerate(
            (
                (x_hbm, x_in),
                (wq_hbm, w_own.at[0]),
                (wk_hbm, w_own.at[1]),
                (wv_hbm, w_own.at[2]),
                (order_hbm, order_own),
                (seq_hbm, seq_own),
                *zip(vector_hbm, vector_in),
            )
        )
    ]
    for load in loads:
        load.start()
    at.greet_sources(n_ctx, True)
    wide = bias_own.shape[1]
    swaps = [
        at.remote(src, dst, w_ss.at[i], w_rs.at[i], at.c, other)
        for i, (src, dst) in enumerate(
            (
                (wq_hbm, w_in.at[0]),
                (wk_hbm, w_in.at[1]),
                (wv_hbm, w_in.at[2]),
                (order_hbm, order_in),
                (seq_hbm, seq_in),
                (bias_own, bias_in),
            )
        )
    ]
    for swap in swaps[:-1]:
        swap.start()
    for load in loads:
        load.wait()
    for row, ref in enumerate(vector_in[:VECTORS]):
        bias_own[row : row + 1, :] = ref[...].astype(F32).reshape(1, wide)
    for part in range(vector_in[VECTORS].shape[0] // wide):
        piece = vector_in[VECTORS][part * wide : part * wide + wide]
        bias_own[VECTORS + part : VECTORS + part + 1, :] = piece.astype(F32).reshape(1, wide)
    swaps[-1].start()

    def kv_moves(half):
        for i in range(H // 2):
            head = half * (H // 2) + at.turn(i, H // 2)
            for core in range(2):
                yield (
                    kv_send.at[head, pl.ds(core * BLK, BLK)],
                    kv_out.at[2 * at.c + core],
                    kv_ss.at[head * 2 + core],
                    kv_rs.at[at.c],
                    at.f * H + head,
                    core,
                )

    def q_moves(half):
        for i in range(H // 2):
            head = half * (H // 2) + at.turn(i, H // 2)
            for core in range(2):
                yield (
                    q_send.at[head, core],
                    q_out.at[at.c],
                    q_ss.at[head * 2 + core],
                    q_rs.at[at.c],
                    at.f * H + head,
                    core,
                )

    def heads_of(half):
        for pair in range(2):
            for side in range(2):
                yield side, half * (H // 2) + 2 * pair + side, slice(pair * 128, pair * 128 + 128)

    def one_half(half, wq, wk, wv, bias):
        low = x_in[...].astype(BF16)
        k = dot_nn(low, wk[...])
        v = dot_nn(low, wv[...]) + bias[1:2, :]
        for side, head, columns in heads_of(half):
            kv_send[head] = side_pair(side, k[:, columns], v[:, columns]).astype(BF16)
        for move in kv_moves(half):
            at.send(*move)
        q = dot_nn(low, wq[...]) + bias[0:1, :]
        for side, head, columns in heads_of(half):
            for core in range(2):
                rows = slice(core * HALF, core * HALF + HALF)
                late = slice(BLK + core * HALF, BLK + core * HALF + HALF)
                q_send[head, core] = side_pair(side, q[rows, columns], q[late, columns]).astype(
                    BF16
                )
        for move in q_moves(half):
            at.send(*move)

    one_half(at.f, w_own.at[0], w_own.at[1], w_own.at[2], bias_own)
    for swap in swaps:
        swap.wait()
    one_half(other, w_in.at[0], w_in.at[1], w_in.at[2], bias_in)
    dense_swaps = [
        at.remote(src, dst, w_ss.at[6 + i], w_rs.at[6 + i], at.c, other)
        for i, (src, dst) in enumerate(zip(dense_hbm, (wo_other, we_other, ws_other)))
    ]
    for swap in dense_swaps:
        swap.start()
    w_other[...] = w_in[...]
    inside = at.inside == 1
    order_out[...] = jnp.where(inside, order_own[...], order_in[...])
    seq_out[...] = jnp.where(inside, seq_own[...], seq_in[...])
    vec_out[...] = whole_rows(bias_own[...], bias_in[...], at.f == 0)
    for row, source in enumerate((bias_own, bias_in)):
        for part in range(expand_out.shape[1] // wide):
            at_row = VECTORS + part
            expand_out[row : row + 1, part * wide : part * wide + wide] = source[
                at_row : at_row + 1, :
            ]

    def relay(source):
        mine = kv_out.at[2 * source + at.f]
        return at.remote(mine, mine, relay_ss.at[source], relay_rs.at[source], at.c, other)

    def relay_in(source):
        theirs = kv_out.at[2 * source + other]
        return at.remote(theirs, theirs, relay_ss.at[source], relay_rs.at[source], at.c, other)

    for source in range(n_ctx):
        arrived = kv_out.at[2 * source + at.f]
        at.remote(arrived, arrived, kv_ss.at[0], kv_rs.at[source], at.c, other).wait_recv()
        relay(source).start()
    for half in (at.f, other):
        for move in kv_moves(half):
            at.wait_sent(*move)
        for move in q_moves(half):
            at.wait_sent(*move)
    for source in range(n_ctx):
        arrived = q_out.at[source]
        at.remote(arrived, arrived, q_ss.at[0], q_rs.at[source], at.c, other).wait_recv()
        relay_in(source).wait_recv()
    for source in range(n_ctx):
        relay(source).wait_send()
    for swap in dense_swaps:
        swap.wait()


def project_and_scatter(n_ctx, x, wq, wk, wv, order, seqs, dense_weights, vectors):
    wide = wq.shape[1]
    blocks = order.shape[1]
    units = vectors[VECTORS].shape[0]
    bias_rows = VECTORS + units // wide
    return pl.pallas_call(
        functools.partial(project_kernel, n_ctx),
        out_shape=(
            jax.ShapeDtypeStruct((n_ctx, HALF, 128), BF16),
            jax.ShapeDtypeStruct((2 * n_ctx, BLK, 128), BF16),
            jax.ShapeDtypeStruct((3, D, wide), BF16),
            jax.ShapeDtypeStruct((1, blocks), jnp.int32),
            jax.ShapeDtypeStruct((1, blocks), jnp.int32),
            jax.ShapeDtypeStruct((bias_rows, D), F32),
            jax.ShapeDtypeStruct((2, units), F32),
            *[jax.ShapeDtypeStruct(w.shape, BF16) for w in dense_weights],
        ),
        in_specs=[ANY] * (10 + VECTORS),
        out_specs=(ANY, ANY) + (VMEM,) * 5 + (ANY,) * 3,
        scratch_shapes=[
            pltpu.VMEM((2 * BLK, D), F32),
            pltpu.VMEM((3, D, wide), BF16),
            pltpu.VMEM((3, D, wide), BF16),
            pltpu.VMEM((bias_rows, wide), F32),
            pltpu.VMEM((bias_rows, wide), F32),
            pltpu.VMEM((1, blocks), jnp.int32),
            pltpu.VMEM((1, blocks), jnp.int32),
            pltpu.VMEM((1, blocks), jnp.int32),
            pltpu.VMEM((1, blocks), jnp.int32),
            pltpu.VMEM((H, 2, HALF, 128), BF16),
            pltpu.VMEM((H, 2 * BLK, 128), BF16),
            pltpu.SemaphoreType.DMA((7 + VECTORS,)),
            pltpu.SemaphoreType.DMA((9,)),
            pltpu.SemaphoreType.DMA((9,)),
            pltpu.SemaphoreType.DMA((2 * H,)),
            pltpu.SemaphoreType.DMA((n_ctx,)),
            pltpu.SemaphoreType.DMA((2 * H,)),
            pltpu.SemaphoreType.DMA((n_ctx,)),
            pltpu.SemaphoreType.DMA((n_ctx,)),
            pltpu.SemaphoreType.DMA((n_ctx,)),
        ]
        + [pltpu.VMEM(vector.shape, BF16) for vector in vectors],
        compiler_params=pltpu.CompilerParams(
            collective_id=0, has_side_effects=True, vmem_limit_bytes=ROOM
        ),
        name="project_scatter",
    )(x, wq, wk, wv, order, seqs, *dense_weights, *vectors)


def forward_kernel(
    blocks,
    order_ref,
    seq_ref,
    q_ref,
    kv_ref,
    o_ref,
    keep_ref,
    lse_ref,
    pairs_ref,
    place,
    q_low,
    peaks,
    masses,
    total,
    scores,
):
    def place_block(slot, _):
        place[order_ref[0, slot]] = slot
        return 0

    lax.fori_loop(0, blocks, place_block, 0)

    count = jnp.int32(0)
    for gap in range(1, LONG):
        for late in range(gap, blocks):
            pairs_ref[0, count] = place[late]
            pairs_ref[1, count] = place[late - gap]
            count = count + jnp.where(seq_ref[0, late] == seq_ref[0, late - gap], 1, 0)
    for spare in range(TOGETHER):
        pairs_ref[0, count + spare] = blocks
        pairs_ref[1, count + spare] = 0
    turns = (count + TOGETHER - 1) // TOGETHER
    pairs_ref[2, 0] = turns

    def unpack(step, _):
        for part in range(4):
            source = step * 4 + part
            packed = q_ref[source].astype(F32) * (HD**-0.5)
            low = low_lanes(packed)
            q_low[2 * source] = jnp.where(low, packed, 0.0).astype(BF16)
            q_low[2 * source + 1] = jnp.where(low, swap_lanes(packed), 0.0).astype(BF16)
        return 0

    lax.fori_loop(0, blocks // 8, unpack, 0)
    q_low[blocks] = jnp.zeros((HALF, 128), BF16)

    peaks[blocks] = jnp.zeros((HALF, 128), F32)
    masses[blocks] = jnp.zeros((HALF, 128), F32)
    total[blocks] = jnp.zeros((HALF, 128), F32)
    lse_ref[blocks] = jnp.zeros((HALF, 128), F32)

    def own_slots(step):
        return [(step * TOGETHER + part,) * 2 for part in range(TOGETHER)]

    def pair_slots(step):
        return [
            (pairs_ref[0, step * TOGETHER + part], pairs_ref[1, step * TOGETHER + part])
            for part in range(TOGETHER)
        ]

    def score(slots, base):
        results = []
        for part, (q_slot, k_slot) in enumerate(slots):
            result = dot_nt(q_low[q_slot], kv_ref[k_slot])
            scores[base + part] = result
            results.append(jnp.maximum(result[:, :128], result[:, 128:]))
        return results

    def score_own(step, _):
        slots = own_slots(step)
        for (q_slot, _), result in zip(slots, score(slots, step * TOGETHER)):
            peaks[q_slot] = result
        return 0

    def score_pairs(step, _):
        slots = pair_slots(step)
        for (q_slot, _), result in zip(slots, score(slots, blocks + step * TOGETHER)):
            peaks[q_slot] = jnp.maximum(peaks[q_slot], result)
        return 0

    lax.fori_loop(0, blocks // TOGETHER, score_own, 0)
    lax.fori_loop(0, turns, score_pairs, 0)

    def level(step, _):
        for part in range(4):
            slot = step * 4 + part
            peaks[slot] = jnp.broadcast_to(
                jnp.max(peaks[slot], axis=1, keepdims=True), (HALF, 128)
            )
        return 0

    lax.fori_loop(0, blocks // 4, level, 0)

    def weigh(slots, base):
        results = []
        for part, (q_slot, k_slot) in enumerate(slots):
            peak = peaks[q_slot]
            left = jnp.exp(scores[base + part, :, :128] - peak)
            right = jnp.exp(scores[base + part, :, 128:] - peak)
            weights = jnp.concatenate([left, right], axis=1).astype(BF16)
            results.append((left + right, dot_nn(weights, kv_ref[k_slot])))
        return results

    def weigh_own(step, _):
        slots = own_slots(step)
        for (q_slot, _), (mass, result) in zip(slots, weigh(slots, step * TOGETHER)):
            masses[q_slot] = mass
            total[q_slot] = result
        return 0

    def weigh_pairs(step, _):
        slots = pair_slots(step)
        for (q_slot, _), (mass, result) in zip(slots, weigh(slots, blocks + step * TOGETHER)):
            masses[q_slot] = masses[q_slot] + mass
            total[q_slot] = total[q_slot] + result
        return 0

    lax.fori_loop(0, blocks // TOGETHER, weigh_own, 0)
    lax.fori_loop(0, turns, weigh_pairs, 0)

    def finish(step, _):
        for part in range(4):
            source = step * 4 + part
            for side in range(2):
                slot = 2 * source + side
                mass = jnp.broadcast_to(
                    jnp.sum(masses[slot], axis=1, keepdims=True), (HALF, 128)
                )
                result = total[slot] / mass
                lse_ref[slot] = peaks[slot] + jnp.log(mass)
                packed = high_pair(result[: HALF // 2], result[HALF // 2 :])
                keep_ref[source, side] = packed
                o_ref[source, side] = packed.astype(BF16)
        return 0

    lax.fori_loop(0, blocks // 8, finish, 0)


def pair_room(blocks):
    return blocks * MOST // 2 + 2 * TOGETHER


def attend(order, seqs, q, kv):
    blocks = kv.shape[0]
    room = pair_room(blocks)
    return pl.pallas_call(
        functools.partial(forward_kernel, blocks),
        out_shape=(
            jax.ShapeDtypeStruct((blocks // 2, 2, HALF // 2, 128), BF16),
            jax.ShapeDtypeStruct((blocks // 2, 2, HALF // 2, 128), F32),
            jax.ShapeDtypeStruct((blocks + 1, HALF, 128), F32),
            jax.ShapeDtypeStruct((3, room), jnp.int32),
        ),
        in_specs=[SMEM, SMEM, VMEM, VMEM],
        out_specs=(VMEM, VMEM, VMEM, SMEM),
        scratch_shapes=[
            pltpu.SMEM((blocks,), jnp.int32),
            pltpu.VMEM((blocks + 1, HALF, 128), BF16),
            pltpu.VMEM((blocks + 1, HALF, 128), F32),
            pltpu.VMEM((blocks + 1, HALF, 128), F32),
            pltpu.VMEM((blocks + 1, HALF, 128), F32),
            pltpu.VMEM((room, HALF, BLK), F32),
        ],
        compiler_params=pltpu.CompilerParams(vmem_limit_bytes=ROOM),
        name="attend",
    )(order, seqs, q, kv)


def backward_kernel(
    blocks,
    pairs_ref,
    q_ref,
    tan_ref,
    keep_ref,
    lse_ref,
    kv_ref,
    pass_a,
    pass_b,
    dq_ref,
    dkv_sum,
    out_a,
    out_b,
    both,
    turned,
    deltas,
    dq_sum,
    held,
    pass_sem,
):
    fetches = [
        pltpu.make_async_copy(src, held.at[i], pass_sem.at[i])
        for i, src in enumerate((pass_a, pass_b))
    ]
    passes = [
        pltpu.make_async_copy(held.at[i], dst, pass_sem.at[2 + i])
        for i, dst in enumerate((out_a, out_b))
    ]
    for fetch in fetches:
        fetch.start()

    def unpack(step, _):
        for part in range(4):
            source = step * 4 + part
            packed = q_ref[source].astype(F32) * (HD**-0.5)
            low = low_lanes(packed)
            for side in range(2):
                slot = 2 * source + side
                q = packed if side == 0 else swap_lanes(packed)
                both[slot, 0:HALF] = jnp.where(low, q, 0.0).astype(BF16)
                tangent = tan_ref[source, side].astype(F32)
                first = low_lanes(tangent)
                both[slot, HALF : HALF + HALF // 2] = jnp.where(
                    first, 0.0, swap_lanes(tangent)
                ).astype(BF16)
                both[slot, HALF + HALF // 2 : BLK] = jnp.where(first, 0.0, tangent).astype(BF16)
                turned[slot] = jnp.transpose(both[slot])
                product = tangent * keep_ref[source, side]
                delta = jnp.concatenate(
                    [
                        jnp.sum(jnp.where(first, product, 0.0), axis=1, keepdims=True),
                        jnp.sum(jnp.where(first, 0.0, product), axis=1, keepdims=True),
                    ],
                    axis=0,
                )
                deltas[slot] = jnp.broadcast_to(delta, (HALF, 128))
        return 0

    lax.fori_loop(0, blocks // 8, unpack, 0)
    both[blocks] = jnp.zeros((BLK, 128), BF16)
    turned[blocks] = jnp.zeros((128, BLK), BF16)
    deltas[blocks] = jnp.zeros((HALF, 128), F32)
    dq_sum[blocks] = jnp.zeros((HALF, 128), F32)

    def one_pair(q_slot, k_slot):
        kv = kv_ref[k_slot]
        products = dot_nt(both[q_slot], kv)
        mass, delta = lse_ref[q_slot], deltas[q_slot]
        weights = jnp.exp(products[:HALF] - jnp.concatenate([mass, mass], axis=1))
        score_tan = weights * (products[HALF:] - jnp.concatenate([delta, delta], axis=1))
        score_tan = score_tan.astype(BF16)
        sides = jnp.concatenate([score_tan, weights.astype(BF16)], axis=0)
        return dot_nn(turned[q_slot], sides), dot_nn(score_tan, kv)

    def own_turn(step, _):
        slots = [step * TOGETHER + part for part in range(TOGETHER)]
        results = [one_pair(slot, slot) for slot in slots]
        for slot, (dkv, dq) in zip(slots, results):
            dkv_sum[slot] = dkv
            dq_sum[slot] = dq
        return 0

    def pair_turn(step, _):
        slots = [
            (pairs_ref[0, step * TOGETHER + part], pairs_ref[1, step * TOGETHER + part])
            for part in range(TOGETHER)
        ]
        results = [one_pair(*slot) for slot in slots]
        for (q_slot, k_slot), (dkv, dq) in zip(slots, results):
            dkv_sum[k_slot] = dkv_sum[k_slot] + dkv
            dq_sum[q_slot] = dq_sum[q_slot] + dq
        return 0

    lax.fori_loop(0, blocks // TOGETHER, own_turn, 0)
    for fetch, move in zip(fetches, passes):
        fetch.wait()
        move.start()
    lax.fori_loop(0, pairs_ref[2, 0], pair_turn, 0)

    def finish_rows(step, _):
        for part in range(4):
            source = step * 4 + part
            packed = low_pair(dq_sum[2 * source], dq_sum[2 * source + 1]) * (HD**-0.5)
            dq_ref[source] = packed.astype(BF16)
        return 0

    lax.fori_loop(0, blocks // 8, finish_rows, 0)
    for move in passes:
        move.wait()


def attend_back(pairs, q, tangent, keep, lse, kv, passed):
    blocks = kv.shape[0]
    return pl.pallas_call(
        functools.partial(backward_kernel, blocks),
        out_shape=(
            jax.ShapeDtypeStruct((blocks // 2, HALF, 128), BF16),
            jax.ShapeDtypeStruct((blocks, 128, BLK), F32),
            jax.ShapeDtypeStruct(passed[0].shape, F32),
            jax.ShapeDtypeStruct(passed[1].shape, F32),
        ),
        in_specs=[SMEM, VMEM, VMEM, VMEM, VMEM, VMEM, ANY, ANY],
        out_specs=(VMEM, VMEM, ANY, ANY),
        scratch_shapes=[
            pltpu.VMEM((blocks + 1, BLK, 128), BF16),
            pltpu.VMEM((blocks + 1, 128, BLK), BF16),
            pltpu.VMEM((blocks + 1, HALF, 128), F32),
            pltpu.VMEM((blocks + 1, HALF, 128), F32),
            pltpu.VMEM((2,) + passed[0].shape, F32),
            pltpu.SemaphoreType.DMA((4,)),
        ],
        compiler_params=pltpu.CompilerParams(vmem_limit_bytes=ROOM),
        name="attend_back",
    )(pairs, q, tangent, keep, lse, kv, *passed)


def pieces_of(start, size, body):
    piece = max(n for n in range(16, 289, 16) if size % n == 0)
    lax.fori_loop(
        0,
        size // piece,
        lambda i, _: (body(i * piece, span(start + i * piece, piece), piece), 0)[1],
        0,
    )


def span(start, size):
    return pl.ds(pl.multiple_of(start, 16), size)


def step_of(c, stride):
    bit = (c // stride) % 2
    return bit, c + stride * (1 - 2 * bit)


REGIONS = 4


def columns_of(region):
    wide = D // (REGIONS // 2)
    return slice(region // 2 * wide, region // 2 * wide + wide)


class Ladder:
    def __init__(self, at, plans, starts, size, acc, stage, landing, out, sems, bases=(0, 0)):
        self.bases = bases
        self.at, self.acc, self.stage, self.landing, self.out = at, acc, stage, landing, out
        self.down_ss, self.down_rs, self.up_ss, self.up_rs = sems
        self.ranges = []
        for region in range(REGIONS):
            plan, start = plans[region % 2], starts[region % 2]
            listed, rows = [], size
            for bit, peer in plan[:-1]:
                rows = rows // 2
                listed.append((start + bit * rows, start + (1 - bit) * rows, rows, peer))
                start = start + bit * rows
            listed.append((start, start, rows, plan[-1][1]))
            self.ranges.append(listed)
        self.last = len(plans[0]) - 1

    def slot(self, region, step):
        return region * (self.last + 1) + step

    def down(self, region, step, sent):
        kept, given, size, peer = self.ranges[region][step]
        where, slot = span(given if sent else kept, size), self.slot(region, step)
        columns = columns_of(region)
        return self.at.remote(
            self.stage[region % 2].at[where, columns],
            self.landing[region % 2][step].at[where, columns],
            self.down_ss.at[slot],
            self.down_rs.at[slot],
            peer,
            self.at.f,
        )

    def up(self, region, step, sent):
        kept, given, size, peer = self.ranges[region][step]
        start = self.bases[region % 2] + (kept if sent else given)
        columns = columns_of(region)
        where, slot = span(start, size), self.slot(region, step)
        return self.at.remote(
            self.out.at[where, columns],
            self.out.at[where, columns],
            self.up_ss.at[slot],
            self.up_rs.at[slot],
            peer,
            self.at.f,
        )

    def join(self, region, start, size, arrived, target):
        columns, acc = columns_of(region), self.acc[region % 2]

        def body(offset, where, _):
            total = acc[where, columns] + arrived[where, columns].astype(F32)
            target[where, columns] = total.astype(target.dtype)

        pieces_of(start, size, body)

    def give(self, region, step, arrived):
        kept, given, size, _ = self.ranges[region][step]
        self.join(region, given, size, arrived, self.stage[region % 2])
        self.down(region, step, True).start()
        if step < self.last:
            self.join(region, kept, size, arrived, self.acc[region % 2])

    def settle(self, region):
        kept, _, size, _ = self.ranges[region][self.last]
        arrived = self.landing[region % 2][self.last]
        columns, stage = columns_of(region), self.stage[region % 2]

        def body(offset, where, rows):
            total = stage[where, columns].astype(F32) + arrived[where, columns].astype(F32)
            row = span(self.bases[region % 2] + kept + offset, rows)
            self.out[row, columns] = total.astype(BF16)

        self.down(region, self.last, False).wait_recv()
        pieces_of(kept, size, body)
        self.up(region, self.last - 1, True).start()

    def wait_down(self):
        for region in range(REGIONS):
            for step in range(self.last + 1):
                self.down(region, step, True).wait_send()

    def wait_up(self, steps):
        for region in range(REGIONS):
            for step in steps:
                self.up(region, step, True).wait_send()


COLS = 512


def whole_rows(own, other, first):
    return jnp.where(
        first,
        jnp.concatenate([own, other], axis=1),
        jnp.concatenate([other, own], axis=1),
    )


def row_mean(values):
    return jnp.mean(values, axis=1, keepdims=True)


def normalize(values):
    centre = values - row_mean(values)
    scale = lax.rsqrt(row_mean(centre * centre) + norm_eps)
    return centre * scale, scale


def norm_back(tangent, normed, scale, gain):
    pushed = tangent * gain
    return scale * (pushed - row_mean(pushed) - normed * row_mean(pushed * normed))


def column_sum(values):
    return jnp.sum(values, axis=0, keepdims=True)


def feed_slopes(kind, target, mixed, low_turned, hidden, before_tan, feed_tan, branch_tan):
    unit_count = hidden.shape[2] // COLS

    def chunk_slopes(chunk, _):
        columns = pl.ds(pl.multiple_of(chunk * COLS, COLS), COLS)
        target[columns, :] = dot_tn(hidden[kind, :, columns], feed_tan[...]).astype(target.dtype)
        below = pl.ds(pl.multiple_of((unit_count + chunk) * COLS, COLS), COLS)
        target[below, :] = dot_nn(low_turned[...], before_tan[kind, :, columns]).astype(
            target.dtype
        )
        return 0

    lax.fori_loop(0, unit_count, chunk_slopes, 0)
    start = 2 * unit_count * COLS
    target[start : start + D // 2, :] = dot_tn(mixed[kind], branch_tan[...]).astype(target.dtype)


def middle_kernel(
    n_ctx,
    o_hbm, x_hbm, sum_hbm, cot_hbm, wo_a, wo_b, we_a, we_b, ws_a, ws_b, be_ref, vec_in,
    out_hbm, sum_tan_hbm, entry_hbm, tan_out, vec_ref, stage_a, stage_b, keep_ref,
    o_in, x_ref, sum_ref, cot_ref, wo, we, ws, out_ref, sum_tan_ref, entry_ref,
    mixed, low, hidden, before_tan, feed_tan, branch_tan, slope, mixed_tan, tan_send,
    own_grads, send_grads, first_in, low_turned,
    load_sem, store_sem, o_ss, o_rs, tan_ss, tan_rs, core_ss, core_rs,
):
    at = Place()
    f = at.f
    other = 1 - f
    halves = (f, other)
    piece = HALF // 2
    loads = [
        pltpu.make_async_copy(src, dst, load_sem.at[i])
        for i, (src, dst) in enumerate(
            (
                (x_hbm, x_ref),
                (wo_a, wo.at[0]),
                (wo_b, wo.at[1]),
                (we_a, we.at[0]),
                (we_b, we.at[1]),
                (ws_a, ws.at[0]),
                (ws_b, ws.at[1]),
                (sum_hbm, sum_ref),
                (cot_hbm, cot_ref),
            )
        )
    ]
    for load in loads:
        load.start()
    barrier = pltpu.get_barrier_semaphore()
    for target in range(n_ctx):
        at.signal(barrier, target, at.group)
    at.greet_owners(n_ctx, True, 2 * H - at.inside)

    def o_move(target, side):
        return (
            o_hbm.at[target, side],
            o_in.at[side, at.head, f],
            o_ss.at[2 * target + side],
            o_rs.at[side * 2 * H + at.head * 2 + f],
            target,
            at.group,
        )

    def tan_move(side, head, core):
        return (
            tan_send.at[side, head, core],
            tan_out.at[at.c, side],
            tan_ss.at[side * 2 * H + head * 2 + core],
            tan_rs.at[at.c * 2 + side],
            f * H + head,
            core,
        )

    for side in range(2):
        for i in range(n_ctx):
            at.send(*o_move(at.turn(i, n_ctx), side))
    vec_ref[...] = jnp.zeros_like(vec_ref)
    vectors = vec_in[...]
    (out_bias, gain_one, shift_one, shrink_bias, gain_two, shift_two, gain_last, shift_last) = (
        vectors[i : i + 1] for i in range(2, 10)
    )
    be = (be_ref.at[0:1], be_ref.at[1:2])
    for load in loads:
        load.wait()

    def stores(step):
        rows = pl.ds(pl.multiple_of(step * BLK, BLK), BLK)
        return [
            pltpu.make_async_copy(src.at[rows], dst.at[rows], store_sem.at[3 * step + i])
            for i, (src, dst) in enumerate(
                ((out_ref, out_hbm), (sum_tan_ref, sum_tan_hbm), (entry_ref, entry_hbm))
            )
        ]

    def tile(step, _):
        first_row = pl.multiple_of(step * BLK, BLK)
        rows = pl.ds(first_row, BLK)
        for head in range(H):
            for core in range(2):
                arrived = o_in.at[step, head, core]
                at.remote(
                    arrived, arrived, o_ss.at[0], o_rs.at[step * 2 * H + head * 2 + core],
                    at.c, other,
                ).wait_recv()
        for kind in range(2):
            for pair in range(2):
                head = halves[kind] * (H // 2) + 2 * pair
                columns = slice(pair * 128, pair * 128 + 128)
                for core in range(2):
                    early = o_in[step, head, core].astype(F32)
                    late = o_in[step, head + 1, core].astype(F32)
                    for part in range(2):
                        start = pl.multiple_of(first_row + core * HALF + part * piece, piece)
                        mixed[kind, pl.ds(start, piece), columns] = side_pair(
                            part, early, late
                        ).astype(BF16)
        branch = dot_nn(mixed[0, rows, :], wo[0]) + dot_nn(mixed[1, rows, :], wo[1]) + out_bias
        n_one, scale_one = normalize(x_ref[rows, :] + branch)
        normed_one = n_one * gain_one + shift_one
        stream_one = sum_ref[rows, :] + branch
        normed_low = normed_one.astype(BF16)
        low[rows, :] = normed_low
        feed = jnp.zeros((BLK, D), F32)
        for kind in range(2):

            def expand(chunk, carried):
                columns = slice(chunk * COLS, chunk * COLS + COLS)
                v = dot_nn(normed_low, we[kind, :, columns]) + be[kind][:, columns]
                square = v * v
                t = jnp.tanh(gelu_coeff * (v + gelu_cubic * square * v))
                half_up = 0.5 + 0.5 * t
                hidden_part = (v * half_up).astype(BF16)
                hidden[kind, rows, columns] = hidden_part
                slope[kind, :, columns] = half_up + v * half_up * (1.0 - t) * (
                    gelu_coeff + (3.0 * gelu_coeff * gelu_cubic) * square
                )
                return carried + dot_nn(hidden_part, ws[kind, columns, :])

            for chunk in range(ws.shape[1] // COLS):
                feed = expand(chunk, feed)
        feed_out = feed + shrink_bias
        n_two, scale_two = normalize(normed_one + feed_out)
        n_last, scale_last = normalize(stream_one + feed_out)
        out_ref[rows, :] = (n_two * gain_two + shift_two) + (n_last * gain_last + shift_last)
        u = cot_ref[rows, :]
        nudge = column_sum(u)
        sum_tan = norm_back(u, n_last, scale_last, gain_last)
        inflow = norm_back(u, n_two, scale_two, gain_two)
        sum_tan_ref[rows, :] = sum_tan
        feed_low = (sum_tan + inflow).astype(BF16)
        feed_tan[rows, :] = feed_low
        vec_ref[0:1, :] += column_sum(feed_low.astype(F32))
        vec_ref[1:2, :] += column_sum(u * n_two)
        vec_ref[2:3, :] += nudge
        vec_ref[3:4, :] += column_sum(u * n_last)
        vec_ref[4:5, :] += nudge
        normed_tan = inflow
        for kind in range(2):

            def expand_back(chunk, carried):
                columns = slice(chunk * COLS, chunk * COLS + COLS)
                pushed = dot_nt(feed_low, ws[kind, columns, :])
                tan_part = (pushed * slope[kind, :, columns]).astype(BF16)
                before_tan[kind, rows, columns] = tan_part
                vec_row = pl.ds(8 + 2 * halves[kind] + chunk, 1)
                vec_ref[vec_row, :] += column_sum(tan_part.astype(F32))
                return carried + dot_nt(tan_part, we[kind, :, columns])

            for chunk in range(ws.shape[1] // COLS):
                normed_tan = expand_back(chunk, normed_tan)
        vec_ref[5:6, :] += column_sum(normed_tan * n_one)
        vec_ref[6:7, :] += column_sum(normed_tan)
        entry = norm_back(normed_tan, n_one, scale_one, gain_one)
        entry_ref[rows, :] = entry
        branch_low = (sum_tan + entry).astype(BF16)
        branch_tan[rows, :] = branch_low
        vec_ref[7:8, :] += column_sum(branch_low.astype(F32))
        for kind in range(2):
            mixed_tan[kind] = dot_nt(branch_low, wo[kind])
        for kind in range(2):
            for pair in range(2):
                columns = slice(pair * 128, pair * 128 + 128)
                for side in range(2):
                    head = halves[kind] * (H // 2) + 2 * pair + side
                    for core in range(2):
                        start = core * HALF
                        early = mixed_tan[kind, start : start + piece, columns]
                        late = mixed_tan[kind, start + piece : start + HALF, columns]
                        tan_send[step, head, core] = side_pair(side, early, late).astype(BF16)
        for i in range(H):
            for core in range(2):
                at.send(*tan_move(step, at.turn(i, H), core))
        for store in stores(step):
            store.start()
        return 0

    lax.fori_loop(0, 2, tile, 0)

    quarter = first_in.shape[0] // 4
    bits = (step_of(at.c, 1)[0], step_of(at.c, 2)[0])
    stages = (stage_a, stage_b)

    def core_move(region, give):
        bit = bits[region]
        start = region * 2 * quarter + (1 - bit if give else bit) * quarter
        where = span(start, quarter)
        slot = region + 2 * (0 if give else 1)
        return start, at.remote(
            send_grads.at[where], first_in.at[where], core_ss.at[slot], core_rs.at[slot],
            at.c, other,
        )

    order = [(0, True), (1, True), (0, False), (1, False)]
    low_turned[...] = jnp.transpose(low[...])
    operands = (mixed, low_turned, hidden, before_tan, feed_tan, branch_tan)
    feed_slopes(1, send_grads, *operands)
    for step in order:
        core_move(*step)[1].start()
    feed_slopes(0, own_grads, *operands)
    for side in range(2):
        for target in range(n_ctx):
            at.wait_sent(*o_move(target, side))
    for region, give in order:
        start, move = core_move(region, give)
        move.wait_recv()

        def join(offset, where, size):
            total = own_grads[where, :] + first_in[where, :].astype(F32)
            if give:
                stages[region][span(offset, size), :] = total.astype(BF16)
            else:
                keep_ref[region, span(offset, size), :] = total

        pieces_of(start, quarter, join)
    for source in range(n_ctx):
        for side in range(2):
            arrived = tan_out.at[source, side]
            at.remote(
                arrived, arrived, tan_ss.at[0], tan_rs.at[source * 2 + side], at.c, other
            ).wait_recv()
    for step in range(2):
        for store in stores(step):
            store.wait()
    for side in range(2):
        for head in range(H):
            for core in range(2):
                at.wait_sent(*tan_move(side, head, core))
    for step in order:
        core_move(*step)[1].wait_send()


def middle(n_ctx, o, x, summed, cotangent, wo, we, ws, be, vec):
    tokens, wide, units = x.shape[0], D // 2, ws[0].shape[0]
    grad_rows = 2 * units + wide
    rows = jax.ShapeDtypeStruct((tokens, D), F32)

    def sems(*counts):
        return [pltpu.SemaphoreType.DMA((count,)) for count in counts]

    return pl.pallas_call(
        functools.partial(middle_kernel, n_ctx),
        out_shape=(
            rows,
            rows,
            rows,
            jax.ShapeDtypeStruct((n_ctx, 2, HALF // 2, 128), BF16),
            jax.ShapeDtypeStruct((16, D), F32),
            jax.ShapeDtypeStruct((grad_rows // 4, D), BF16),
            jax.ShapeDtypeStruct((grad_rows // 4, D), BF16),
            jax.ShapeDtypeStruct((2, grad_rows // 4, D), F32),
        ),
        in_specs=[ANY] * 10 + [VMEM] * 2,
        out_specs=(ANY,) * 4 + (VMEM,) * 4,
        scratch_shapes=[
            pltpu.VMEM((2, H, 2, HALF // 2, 128), BF16),
            pltpu.VMEM((tokens, D), F32),
            pltpu.VMEM((tokens, D), F32),
            pltpu.VMEM((tokens, D), F32),
            pltpu.VMEM((2, wide, D), BF16),
            pltpu.VMEM((2, D, units), BF16),
            pltpu.VMEM((2, units, D), BF16),
            pltpu.VMEM((tokens, D), F32),
            pltpu.VMEM((tokens, D), F32),
            pltpu.VMEM((tokens, D), F32),
            pltpu.VMEM((2, tokens, wide), BF16),
            pltpu.VMEM((tokens, D), BF16),
            pltpu.VMEM((2, tokens, units), BF16),
            pltpu.VMEM((2, tokens, units), BF16),
            pltpu.VMEM((tokens, D), BF16),
            pltpu.VMEM((tokens, D), BF16),
            pltpu.VMEM((2, BLK, units), F32),
            pltpu.VMEM((2, BLK, wide), F32),
            pltpu.VMEM((2, H, 2, HALF // 2, 128), BF16),
            pltpu.VMEM((grad_rows, D), F32),
            pltpu.VMEM((grad_rows, D), BF16),
            pltpu.VMEM((grad_rows, D), BF16),
            pltpu.VMEM((D, tokens), BF16),
        ]
        + sems(9, 6, 2 * n_ctx, 4 * H, 4 * H, 2 * n_ctx, 4, 4),
        compiler_params=pltpu.CompilerParams(
            collective_id=1, has_side_effects=True, vmem_limit_bytes=ROOM
        ),
        name="middle",
    )(o, x, summed, cotangent, *wo, *we, *ws, be, vec)


def finish_kernel(
    n_ctx,
    dq_ref, dkv_ref, keep_hbm, land_a, land_b, x_hbm, entry_hbm, wq_hbm, wk_hbm, wv_hbm,
    w_other_hbm, vec_feed,
    post_ref, feed_ref, grads_ref, vec_out,
    own, part, ready, dq_in, dkv_in, keep, acc, stage, landing,
    x_in, entry_in, w_in, w_far, low_turned, tangents,
    own_grads, send_grads, first_in, acc_last, stage_last, landing_last, vec_sum, vec_in,
    load_sem, q_ss, q_rs, kv_ss, kv_rs, part_ss, part_rs, own_sem,
    down_ss, down_rs, up_ss, up_rs, top_ss, top_rs,
    core_ss, core_rs, down_ss2, down_rs2, up_ss2, up_rs2, vec_ss, vec_rs,
):
    at = Place()
    c, f = at.c, at.f
    other = 1 - f
    halves = (f, other)
    wide = D // 2
    loads = [
        pltpu.make_async_copy(src, dst, load_sem.at[i])
        for i, (src, dst) in enumerate(
            (
                (keep_hbm, keep),
                (x_hbm, x_in),
                (entry_hbm, entry_in),
                (wq_hbm, w_in.at[0]),
                (wk_hbm, w_in.at[1]),
                (wv_hbm, w_in.at[2]),
                (w_other_hbm, w_far),
            )
        )
    ]
    for load in loads:
        load.start()
    x_step, y_step, near, far = (step_of(c, stride) for stride in (1, 2, 4, 8))
    barrier = pltpu.get_barrier_semaphore()
    for _, peer in (x_step, y_step, near, far):
        pl.semaphore_signal(barrier, 1, device_id=(peer, f), device_id_type=MESH)
    at.greet_owners(n_ctx, True, 4)

    def partial_move(source):
        return at.remote(
            dkv_ref.at[2 * source + other],
            part.at[source],
            part_ss.at[source],
            part_rs.at[source],
            c,
            other,
        )

    def own_move(source):
        return pltpu.make_async_copy(
            dkv_ref.at[2 * source + f], own.at[source], own_sem.at[source]
        )

    def q_move(target):
        return (
            dq_ref.at[target],
            dq_in.at[at.head, f],
            q_ss.at[target],
            q_rs.at[at.head * 2 + f],
            target,
            at.group,
        )

    def kv_move(target):
        return (
            ready.at[target],
            dkv_in.at[at.head, pl.ds(pl.multiple_of(f * BLK, BLK), BLK)],
            kv_ss.at[target],
            kv_rs.at[at.head * 2 + f],
            target,
            at.group,
        )

    for i in range(n_ctx):
        source = at.turn(i, n_ctx)
        partial_move(source).start()
        own_move(source).start()
    for i in range(n_ctx):
        at.send(*q_move(at.turn(i, n_ctx)))

    size = keep.shape[1]
    firsts = (x_step, y_step)
    bases = [2 * size * region + firsts[region][0] * size for region in range(2)]
    feed = Ladder(
        at,
        ((y_step, near, far), (x_step, near, far)),
        (0, 0),
        size,
        [keep.at[region] for region in range(2)],
        [stage.at[region] for region in range(2)],
        [[landing.at[region, step] for step in range(3)] for region in range(2)],
        feed_ref,
        (down_ss, down_rs, up_ss, up_rs),
        bases,
    )

    def top_move(region, sent):
        side, columns = region % 2, columns_of(region)
        given = 2 * size * side + (1 - firsts[side][0]) * size
        where = span(bases[side] if sent else given, size)
        return at.remote(
            feed_ref.at[where, columns],
            feed_ref.at[where, columns],
            top_ss.at[region],
            top_rs.at[region],
            firsts[side][1],
            f,
        )

    loads[0].wait()
    kept_acc = [keep.at[region] for region in range(2)]
    sums = [acc.at[region] for region in range(2)]
    for region in range(REGIONS):
        first = (land_a, land_b)[region % 2]
        kept, given, half, _ = feed.ranges[region][0]
        feed.acc = kept_acc
        feed.join(region, given, half, first, stage.at[region % 2])
        feed.down(region, 0, True).start()
        feed.join(region, kept, half, first, sums[region % 2])
    feed.acc = sums
    for i in range(n_ctx):
        source = at.turn(i, n_ctx)
        own_move(source).wait()
        partial_move(source).wait_recv()
        ready[source] = jnp.transpose(own[source] + part[source]).astype(BF16)
        if i < n_ctx - 8:
            at.send(*kv_move(source))
    for load in loads[1:]:
        load.wait()
    low_turned[...] = jnp.transpose(x_in[...]).astype(BF16)
    for step in (1, 2):
        for region in range(REGIONS):
            feed.down(region, step - 1, False).wait_recv()
            feed.give(region, step, feed.landing[region % 2][step - 1])
        if step == 1:
            for i in range(n_ctx - 8, n_ctx):
                at.send(*kv_move(at.turn(i, n_ctx)))

    for target in range(n_ctx):
        partial_move(target).wait_send()
        at.wait_sent(*q_move(target))

    for head in range(H):
        for core in range(2):
            slot = head * 2 + core
            arrived = dq_in.at[head, core]
            at.remote(arrived, arrived, q_ss.at[0], q_rs.at[slot], c, other).wait_recv()
            arrived = dkv_in.at[head, pl.ds(core * BLK, BLK)]
            at.remote(arrived, arrived, kv_ss.at[0], kv_rs.at[slot], c, other).wait_recv()
    feed_rows = vec_feed.shape[0]
    vec_sum[0, 0:feed_rows] = vec_feed[...]
    vec_sum[0, feed_rows:] = jnp.zeros_like(vec_sum[0, feed_rows:])

    plans = ((x_step, y_step, near, far), (y_step, x_step, near, far))
    quarter = first_in.shape[0] // 4
    last = Ladder(
        at,
        plans,
        (0, 2 * quarter),
        2 * quarter,
        [acc_last, acc_last],
        [stage_last, stage_last],
        [[landing_last.at[step] for step in range(4)]] * 2,
        grads_ref,
        (down_ss2, down_rs2, up_ss2, up_rs2),
    )

    def core_move(region, give):
        kept, given, rows, _ = last.ranges[region][0]
        where = span(given if give else kept, rows)
        slot, columns = region + REGIONS * (0 if give else 1), columns_of(region)
        return at.remote(
            send_grads.at[where, columns],
            first_in.at[where, columns],
            core_ss.at[slot],
            core_rs.at[slot],
            c,
            other,
        )

    order = [(region, give) for give in (True, False) for region in range(REGIONS)]
    vec_peers = [(c, other)] + [(peer, f) for _, peer in (x_step, y_step, near, far)]

    def vec_move(step):
        return at.remote(
            vec_sum.at[step], vec_in.at[step], vec_ss.at[step], vec_rs.at[step], *vec_peers[step]
        )

    def vec_next(step):
        vec_move(step).wait_recv()
        target = vec_sum.at[step + 1] if step < 4 else vec_out
        target[...] = vec_sum[step] + vec_in[step]
        if step < 4:
            vec_move(step + 1).start()

    for kind, grad_ref in ((1, send_grads), (0, own_grads)):
        for pair in range(2):
            head = halves[kind] * (H // 2) + 2 * pair
            columns = slice(pair * 128, pair * 128 + 128)
            for core in range(2):
                early = dq_in[head, core].astype(F32)
                late = dq_in[head + 1, core].astype(F32)
                for side in range(2):
                    start = side * BLK + core * HALF
                    tangents[kind, 0, start : start + HALF, columns] = side_pair(
                        side, early, late
                    ).astype(BF16)
            early = dkv_in[head].astype(F32)
            late = dkv_in[head + 1].astype(F32)
            tangents[kind, 1, :, columns] = low_pair(early, late).astype(BF16)
            tangents[kind, 2, :, columns] = high_pair(early, late).astype(BF16)
        turned = low_turned[...]
        grad_ref[0:D, 0:wide] = dot_nn(turned, tangents[kind, 0]).astype(grad_ref.dtype)
        grad_ref[0:D, wide:D] = dot_nn(turned, tangents[kind, 1]).astype(grad_ref.dtype)
        value_grad = dot_nn(turned, tangents[kind, 2]).astype(grad_ref.dtype)
        grad_ref[D : D + wide, 0:wide] = value_grad[0:wide]
        grad_ref[D : D + wide, wide:D] = value_grad[wide:D]
        columns = pl.ds(pl.multiple_of(halves[kind] * wide, wide), wide)
        vec_sum[0, feed_rows : feed_rows + 1, columns] = column_sum(tangents[kind, 0].astype(F32))
        vec_sum[0, feed_rows + 1 : feed_rows + 2, columns] = column_sum(
            tangents[kind, 2].astype(F32)
        )
        if kind == 1:
            for step in order:
                core_move(*step).start()
    vec_move(0).start()
    for region, give in order:
        core_move(region, give).wait_recv()
        kept, given, rows, _ = last.ranges[region][0]
        columns = columns_of(region)

        def join(offset, where, _):
            total = own_grads[where, columns] + first_in[where, columns].astype(F32)
            if give:
                stage_last[where, columns] = total.astype(BF16)
            else:
                acc_last[where, columns] = total

        pieces_of(given if give else kept, rows, join)
        if give:
            last.down(region, 0, True).start()
    vec_next(0)
    total = entry_in[...]
    for which in range(3):
        total = total + dot_nt(tangents[0, which], w_in[which])
        total = total + dot_nt(tangents[1, which], w_far[which])
    post_ref[...] = total
    for target in range(n_ctx):
        at.wait_sent(*kv_move(target))
    for step in order:
        core_move(*step).wait_send()
    for region in range(REGIONS):
        feed.settle(region)
    for region in range(REGIONS):
        feed.up(region, 1, False).wait_recv()
        feed.up(region, 0, True).start()
    for region in range(REGIONS):
        last.down(region, 0, False).wait_recv()
        last.give(region, 1, last.landing[region % 2][0])
    vec_next(1)
    for region in range(REGIONS):
        feed.up(region, 0, False).wait_recv()
        top_move(region, True).start()
    for region in range(REGIONS):
        last.down(region, 1, False).wait_recv()
        last.give(region, 2, last.landing[region % 2][1])
    vec_next(2)
    for region in range(REGIONS):
        last.down(region, 2, False).wait_recv()
        last.give(region, 3, last.landing[region % 2][2])
    vec_next(3)
    for region in range(REGIONS):
        last.settle(region)
    vec_next(4)
    feed.wait_down()
    for step in (2, 1, 0):
        for region in range(REGIONS):
            last.up(region, step, False).wait_recv()
            if step > 0:
                last.up(region, step - 1, True).start()
        if step == 2:
            last.wait_down()
        if step == 1:
            feed.wait_up((0, 1))
            last.wait_up((1, 2))
            for index in range(5):
                vec_move(index).wait_send()
    for region in range(REGIONS):
        top_move(region, False).wait_recv()

    for region in range(REGIONS):
        top_move(region, True).wait_send()
    last.wait_up((0,))


def finish(n_ctx, dq, dkv, keep, land_a, land_b, x, entry, wq, wk, wv, w_other, vec_feed):
    size, tokens, wide = keep.shape[1], x.shape[0], D // 2
    last_shape = (D + wide, D)
    vec_shape = (vec_feed.shape[0] + 8, D)

    def sems(*counts):
        return [pltpu.SemaphoreType.DMA((count,)) for count in counts]

    return pl.pallas_call(
        functools.partial(finish_kernel, n_ctx),
        out_shape=(
            jax.ShapeDtypeStruct((tokens, D), F32),
            jax.ShapeDtypeStruct((4 * size, D), BF16),
            jax.ShapeDtypeStruct(last_shape, BF16),
            jax.ShapeDtypeStruct(vec_shape, F32),
        ),
        in_specs=[ANY, ANY, ANY, VMEM, VMEM] + [ANY] * 6 + [VMEM],
        out_specs=(VMEM,) * 4,
        scratch_shapes=[
            pltpu.VMEM((n_ctx, 128, BLK), F32),
            pltpu.VMEM((n_ctx, 128, BLK), F32),
            pltpu.VMEM((n_ctx, BLK, 128), BF16),
            pltpu.VMEM((H, 2, HALF, 128), BF16),
            pltpu.VMEM((H, 2 * BLK, 128), BF16),
            pltpu.VMEM((2, size, D), F32),
            pltpu.VMEM((2, size, D), F32),
            pltpu.VMEM((2, size, D), BF16),
            pltpu.VMEM((2, 3, size, D), BF16),
            pltpu.VMEM((tokens, D), F32),
            pltpu.VMEM((tokens, D), F32),
            pltpu.VMEM((3, D, wide), BF16),
            pltpu.VMEM((3, D, wide), BF16),
            pltpu.VMEM((D, tokens), BF16),
            pltpu.VMEM((2, 3, tokens, wide), BF16),
            pltpu.VMEM(last_shape, F32),
            pltpu.VMEM(last_shape, BF16),
            pltpu.VMEM(last_shape, BF16),
            pltpu.VMEM(last_shape, F32),
            pltpu.VMEM(last_shape, BF16),
            pltpu.VMEM((4,) + last_shape, BF16),
            pltpu.VMEM((5,) + vec_shape, F32),
            pltpu.VMEM((5,) + vec_shape, F32),
        ]
        + sems(7, n_ctx, 2 * H, n_ctx, 2 * H, n_ctx, n_ctx, n_ctx)
        + sems(12, 12, 12, 12, 4, 4, 8, 8, 16, 16, 16, 16, 5, 5),
        compiler_params=pltpu.CompilerParams(
            collective_id=3, has_side_effects=True, vmem_limit_bytes=ROOM
        ),
        name="finish",
    )(dq, dkv, keep, land_a, land_b, x, entry, wq, wk, wv, w_other, vec_feed)


def unpack_kernel(
    full, grads, post, vec_ref,
    query_ref, key_ref, value_ref, output_ref, expand_ref, shrink_ref, post_out, *vector_outs,
):
    f = lax.axis_index("fsdp")
    units, wide = shrink_ref.shape[0], D // 2
    shrink_ref[...] = full[0:units].astype(F32)
    for part in range(units // D):
        start = units + part * D
        expand_ref[:, part * D : part * D + D] = full[start : start + D].astype(F32)
    output_ref[...] = full[2 * units : 2 * units + wide].astype(F32)
    query_ref[...] = grads[0:D, 0:wide].astype(F32)
    key_ref[...] = grads[0:D, wide:D].astype(F32)
    value_ref[0:wide] = grads[D : D + wide, 0:wide].astype(F32)
    value_ref[wide:D] = grads[D : D + wide, wide:D].astype(F32)
    post_out[...] = post[...]
    vectors = vec_ref[...]
    mine = jnp.where(f == 0, vectors[:, 0:wide], vectors[:, wide:D])
    for row, ref in zip((16, 17, 7, 5, 6, 0, 1, 2, 3, 4), vector_outs):
        ref[...] = mine[row : row + 1]
    drift = jnp.where(f == 0, vectors[8:10], vectors[10:12])
    for part in range(units // D):
        vector_outs[10][:, part * D : part * D + D] = drift[part : part + 1]


def unpack_grads(units, full, grads, post, vecs):
    wide = D // 2
    shapes = [(D, wide)] * 3 + [(wide, D), (D, units), (units, D), post.shape]
    shapes = shapes + [(1, wide)] * 10 + [(1, units)]
    return pl.pallas_call(
        unpack_kernel,
        out_shape=tuple(jax.ShapeDtypeStruct(shape, F32) for shape in shapes),
        in_specs=[VMEM] * 4,
        out_specs=(VMEM,) * len(shapes),
        compiler_params=pltpu.CompilerParams(vmem_limit_bytes=UNPACK_ROOM),
        name="unpack_grads",
    )(full, grads, post, vecs)


def head_shards(
    n_ctx,
    post_stream,
    sum_stream,
    cotangent,
    block_order,
    block_sequence,
    query_weight,
    key_weight,
    value_weight,
    output_weight,
    query_bias,
    value_bias,
    output_bias,
    attend_gain,
    attend_shift,
    expand_weight,
    expand_bias,
    shrink_weight,
    shrink_bias,
    middle_gain,
    middle_shift,
    final_gain,
    final_shift,
):
    x, summed, tangent = post_stream[0], sum_stream[0], cotangent[0]
    def across(values, stride):
        return lax.ppermute(values, "ctx", [(c, c ^ stride) for c in range(n_ctx)])

    vectors = [
        query_bias,
        value_bias,
        output_bias,
        attend_gain,
        attend_shift,
        shrink_bias,
        middle_gain,
        middle_shift,
        final_gain,
        final_shift,
        expand_bias,
    ]
    q, kv, w_other, order, seqs, vec, expand_add, wo_other, we_other, ws_other = (
        project_and_scatter(
            n_ctx,
            x,
            query_weight,
            key_weight,
            value_weight,
            block_order,
            block_sequence,
            (output_weight, expand_weight, shrink_weight),
            vectors,
        )
    )
    o, keep, lse, pairs = attend(order, seqs, q, kv)
    layer_output, sum_tan, entry, tan, vec_feed, stage_a, stage_b, kept = middle(
        n_ctx,
        o,
        x,
        summed,
        tangent,
        (output_weight, wo_other),
        (expand_weight, we_other),
        (shrink_weight, ws_other),
        expand_add,
        vec,
    )
    land_a, land_b = across(stage_a, 1), across(stage_b, 2)
    dq, dkv, layer_output, sum_tan = attend_back(
        pairs, q, tan, keep, lse, kv, (layer_output, sum_tan)
    )
    post_tangent, feed_sums, last_sums, vecs = finish(
        n_ctx,
        dq,
        dkv,
        kept,
        land_a,
        land_b,
        x,
        entry,
        query_weight,
        key_weight,
        value_weight,
        w_other,
        vec_feed,
    )
    (
        query_slope,
        key_slope,
        value_slope,
        output_slope,
        expand_slope,
        shrink_slope,
        post_tangent,
        query_drift,
        value_drift,
        output_drift,
        attend_stretch,
        attend_nudge,
        shrink_drift,
        middle_stretch,
        middle_nudge,
        final_stretch,
        final_nudge,
        expand_drift,
    ) = unpack_grads(shrink_weight.shape[0], feed_sums, last_sums, post_tangent, vecs)
    return (
        layer_output[None],
        post_tangent[None],
        sum_tan[None],
        query_slope,
        key_slope,
        value_slope,
        output_slope,
        query_drift[0],
        value_drift[0],
        output_drift[0],
        attend_stretch[0],
        attend_nudge[0],
        expand_slope,
        expand_drift[0],
        shrink_slope,
        shrink_drift[0],
        middle_stretch[0],
        middle_nudge[0],
        final_stretch[0],
        final_nudge[0],
    )


def solution(mesh):
    n_ctx, n_fsdp = mesh.shape["ctx"], mesh.shape["fsdp"]
    if n_fsdp == 2 and n_ctx == n_fsdp * H:
        body = functools.partial(head_shards, n_ctx)
    else:
        body = general_shards
    return jax.shard_map(
        body,
        mesh=mesh,
        in_specs=(
            P("fsdp", "ctx", None),
            P("fsdp", "ctx", None),
            P("fsdp", "ctx", None),
            P("fsdp", None),
            P("fsdp", None),
            P(None, "fsdp"),
            P(None, "fsdp"),
            P(None, "fsdp"),
            P("fsdp", None),
            P("fsdp"),
            P("fsdp"),
            P("fsdp"),
            P("fsdp"),
            P("fsdp"),
            P(None, "fsdp"),
            P("fsdp"),
            P("fsdp", None),
            P("fsdp"),
            P("fsdp"),
            P("fsdp"),
            P("fsdp"),
            P("fsdp"),
        ),
        out_specs=(
            P("fsdp", "ctx", None),
            P("fsdp", "ctx", None),
            P("fsdp", "ctx", None),
            P(None, "fsdp"),
            P(None, "fsdp"),
            P(None, "fsdp"),
            P("fsdp", None),
            P("fsdp"),
            P("fsdp"),
            P("fsdp"),
            P("fsdp"),
            P("fsdp"),
            P(None, "fsdp"),
            P("fsdp"),
            P("fsdp", None),
            P("fsdp"),
            P("fsdp"),
            P("fsdp"),
            P("fsdp"),
            P("fsdp"),
        ),
        check_vma=False,
    )
```

```python
import functools

import jax
import jax.numpy as jnp
from jax import lax
from jax.experimental import pallas as pl
from jax.experimental.pallas import tpu as pltpu
from jax.sharding import PartitionSpec as P

D = 512
H = 8
HD = 64
BLK = 256
HALF = BLK // 2
LONG = 8
TOGETHER = 32
MOST = LONG + 1
F32 = jnp.float32
BF16 = jnp.bfloat16
MESH = pl.DeviceIdType.MESH
ROOM = 60 << 20
UNPACK_ROOM = 60 << 20
VMEM = pl.BlockSpec(memory_space=pltpu.VMEM)
SMEM = pl.BlockSpec(memory_space=pltpu.SMEM)
ANY = pl.BlockSpec(memory_space=pltpu.HBM)


norm_eps = 1e-05
masked_value = -1e30
gelu_coeff = 0.7978845608
gelu_cubic = 0.044715


def smooth_gate(values):
    return (
        0.5
        * values
        * (1.0 + jnp.tanh(gelu_coeff * (values + gelu_cubic * values * values * values)))
    )


def layer_norm(inputs, gain_row, shift_row):
    centre = inputs - jnp.mean(inputs, axis=-1, keepdims=True)
    spread = jnp.mean(centre * centre, axis=-1, keepdims=True)
    return centre * lax.rsqrt(spread + norm_eps) * gain_row + shift_row


def product(left_side, right_side):
    return jnp.dot(left_side, right_side, preferred_element_type=jnp.float32)


def cross_rows(left_side, right_side):
    return lax.dot_general(
        left_side, right_side, (((0,), (0,)), ((), ())), preferred_element_type=jnp.float32
    )


def cross_cols(left_side, right_side):
    return lax.dot_general(
        left_side, right_side, (((1,), (1,)), ((), ())), preferred_element_type=jnp.float32
    )


def column_total(values):
    return jnp.sum(values, axis=0, dtype=jnp.float32)


def lookup(table_row, indices):
    places = jnp.arange(table_row.shape[0], dtype=jnp.int32)
    return jnp.sum(jnp.where(indices[:, None] == places[None, :], table_row[None, :], 0), axis=1)


def block_mask(query_blocks, query_seqs, key_blocks, key_seqs):
    same_seq = query_seqs[:, None] == key_seqs[None, :]
    return same_seq & (key_blocks[None, :] <= query_blocks[:, None])


def token_mask(visible):
    return jnp.repeat(jnp.repeat(visible, BLK, axis=0), BLK, axis=1)


def fold_units(carried, members, unit_step):
    unit_count = members[0].shape[0] // BLK
    inner_count = max((divisor for divisor in range(1, 17) if unit_count % divisor == 0))
    outer_count = unit_count // inner_count

    def outer_turn(outer_index, current):

        def inner_turn(inner_index, inner_state):
            offset = (outer_index * inner_count + inner_index) * BLK
            pieces = tuple((lax.dynamic_slice_in_dim(member, offset, BLK, 0) for member in members))
            return unit_step(inner_state, pieces, offset)

        return lax.fori_loop(0, inner_count, inner_turn, current)

    return lax.fori_loop(0, outer_count, outer_turn, carried)


def general_shards(
    post_stream,
    sum_stream,
    cotangent,
    block_order,
    block_sequence,
    query_weight,
    key_weight,
    value_weight,
    output_weight,
    query_bias,
    value_bias,
    output_bias,
    attend_gain,
    attend_shift,
    expand_weight,
    expand_bias,
    shrink_weight,
    shrink_bias,
    middle_gain,
    middle_shift,
    final_gain,
    final_shift,
):
    (
        query_whole,
        key_whole,
        value_whole,
        output_whole,
        query_add,
        value_add,
        output_add,
        gain_one,
        shift_one,
        expand_whole,
        expand_add,
        shrink_whole,
        shrink_add,
        gain_two,
        shift_two,
        gain_last,
        shift_last,
    ) = (
        lax.all_gather(query_weight, "fsdp", axis=1, tiled=True),
        lax.all_gather(key_weight, "fsdp", axis=1, tiled=True),
        lax.all_gather(value_weight, "fsdp", axis=1, tiled=True),
        lax.all_gather(output_weight, "fsdp", axis=0, tiled=True),
        lax.all_gather(query_bias, "fsdp", axis=0, tiled=True),
        lax.all_gather(value_bias, "fsdp", axis=0, tiled=True),
        lax.all_gather(output_bias, "fsdp", axis=0, tiled=True),
        lax.all_gather(attend_gain, "fsdp", axis=0, tiled=True),
        lax.all_gather(attend_shift, "fsdp", axis=0, tiled=True),
        lax.all_gather(expand_weight, "fsdp", axis=1, tiled=True),
        lax.all_gather(expand_bias, "fsdp", axis=0, tiled=True),
        lax.all_gather(shrink_weight, "fsdp", axis=0, tiled=True),
        lax.all_gather(shrink_bias, "fsdp", axis=0, tiled=True),
        lax.all_gather(middle_gain, "fsdp", axis=0, tiled=True),
        lax.all_gather(middle_shift, "fsdp", axis=0, tiled=True),
        lax.all_gather(final_gain, "fsdp", axis=0, tiled=True),
        lax.all_gather(final_shift, "fsdp", axis=0, tiled=True),
    )
    post_rows = post_stream[0]
    summed = sum_stream[0]
    tangent = cotangent[0]
    order_row = block_order[0]
    seq_row = block_sequence[0]
    token_count = post_rows.shape[0]
    score_scale = HD ** (-0.5)
    own_blocks = lax.dynamic_slice_in_dim(
        order_row, lax.axis_index("ctx") * (token_count // BLK), token_count // BLK
    )
    own_seqs = lookup(seq_row, own_blocks)
    post_low = post_rows.astype(jnp.bfloat16)
    queries = (product(post_low, query_whole) + query_add).astype(jnp.bfloat16)
    key_rows = product(post_low, key_whole).astype(jnp.bfloat16)
    value_rows = (product(post_low, value_whole) + value_add).astype(jnp.bfloat16)
    query_heads = queries.reshape(token_count, H, HD)

    def keys_visible(first_row):
        key_block = lax.dynamic_slice_in_dim(order_row, first_row // BLK, 1)
        return block_mask(own_blocks, own_seqs, key_block, lookup(seq_row, key_block))

    def masked_fold(block_step):

        def unit_step(current, pieces, first_row):
            visible = keys_visible(first_row)
            return lax.cond(
                jnp.any(visible),
                lambda inner_state: block_step(inner_state, pieces, visible),
                lambda inner_state: inner_state,
                current,
            )

        def folded(current, pieces, first_row):
            return fold_units(current, pieces, unit_step)

        return folded

    def stats_block(current, pieces, visible):
        row_peaks, masses = current
        key_heads = pieces[0].reshape(BLK, H, HD)
        row_mask = token_mask(visible)[None]
        scores = (
            jnp.einsum("qhd,khd->hqk", query_heads, key_heads, preferred_element_type=jnp.float32)
            * score_scale
        )
        new_peaks = jnp.maximum(
            row_peaks, jnp.max(jnp.where(row_mask, scores, masked_value), axis=2)
        )
        weights = jnp.where(row_mask, jnp.exp(scores - new_peaks[:, :, None]), 0.0)
        return (new_peaks, masses * jnp.exp(row_peaks - new_peaks) + jnp.sum(weights, axis=2))

    stats_fold = masked_fold(stats_block)
    stats_start = (
        jnp.full((H, token_count), masked_value, jnp.float32),
        jnp.zeros((H, token_count), jnp.float32),
    )
    row_peaks, masses = stats_fold(
        stats_start, (lax.all_gather(key_rows, "ctx", axis=0, tiled=True),), jnp.int32(0)
    )
    log_mass = row_peaks + jnp.log(masses)

    def forward_block(current, pieces, visible):
        key_heads = pieces[0].reshape(BLK, H, HD)
        value_heads = pieces[1].reshape(BLK, H, HD)
        row_mask = token_mask(visible)[None]
        scores = (
            jnp.einsum("qhd,khd->hqk", query_heads, key_heads, preferred_element_type=jnp.float32)
            * score_scale
        )
        weights = jnp.where(row_mask, jnp.exp(scores - log_mass[:, :, None]), 0.0).astype(
            jnp.bfloat16
        )
        addition = jnp.einsum(
            "hqk,khd->qhd", weights, value_heads, preferred_element_type=jnp.float32
        )
        return current + addition.reshape(token_count, D)

    forward_fold = masked_fold(forward_block)
    zero_rows = jnp.zeros((token_count, D), jnp.float32)
    attended = forward_fold(
        zero_rows,
        (
            lax.all_gather(key_rows, "ctx", axis=0, tiled=True),
            lax.all_gather(value_rows, "ctx", axis=0, tiled=True),
        ),
        jnp.int32(0),
    )
    mixed_low = attended.astype(jnp.bfloat16)
    branch = product(mixed_low, output_whole) + output_add
    normed_one, first_pull = jax.vjp(
        layer_norm, post_rows + branch, gain_one.astype(jnp.float32), shift_one.astype(jnp.float32)
    )
    stream_one = summed + branch
    normed_low = normed_one.astype(jnp.bfloat16)
    before = product(normed_low, expand_whole) + expand_add
    gated, gate_pull = jax.vjp(smooth_gate, before)
    hidden = gated.astype(jnp.bfloat16)
    feed_out = product(hidden, shrink_whole) + shrink_add
    normed_two, middle_pull = jax.vjp(
        layer_norm,
        normed_one + feed_out,
        gain_two.astype(jnp.float32),
        shift_two.astype(jnp.float32),
    )
    stream_two = stream_one + feed_out
    last_norm, last_pull = jax.vjp(
        layer_norm, stream_two, gain_last.astype(jnp.float32), shift_last.astype(jnp.float32)
    )
    layer_output = normed_two + last_norm
    stream_tan, stretch_last, nudge_last = last_pull(tangent)
    inflow_tan, stretch_two, nudge_two = middle_pull(tangent)
    feed_tan = (stream_tan + inflow_tan).astype(jnp.bfloat16)
    slope_shrink = cross_rows(hidden, feed_tan)
    drift_shrink = column_total(feed_tan)
    before_tan = gate_pull(cross_cols(feed_tan, shrink_whole))[0].astype(jnp.bfloat16)
    slope_expand = cross_rows(normed_low, before_tan)
    drift_expand = column_total(before_tan)
    normed_tan = inflow_tan + cross_cols(before_tan, expand_whole)
    feed_parts = lax.psum(
        (
            slope_expand,
            drift_expand,
            slope_shrink,
            drift_shrink,
            stretch_two,
            nudge_two,
            stretch_last,
            nudge_last,
        ),
        "ctx",
    )
    feed_sums = (
        lax.psum_scatter(feed_parts[0], "fsdp", scatter_dimension=1, tiled=True),
        lax.psum_scatter(feed_parts[1], "fsdp", scatter_dimension=0, tiled=True),
        lax.psum_scatter(feed_parts[2], "fsdp", scatter_dimension=0, tiled=True),
        lax.psum_scatter(feed_parts[3], "fsdp", scatter_dimension=0, tiled=True),
        lax.psum_scatter(feed_parts[4], "fsdp", scatter_dimension=0, tiled=True),
        lax.psum_scatter(feed_parts[5], "fsdp", scatter_dimension=0, tiled=True),
        lax.psum_scatter(feed_parts[6], "fsdp", scatter_dimension=0, tiled=True),
        lax.psum_scatter(feed_parts[7], "fsdp", scatter_dimension=0, tiled=True),
    )
    entry_tan, stretch_one, nudge_one = first_pull(normed_tan)
    branch_tan = (stream_tan + entry_tan).astype(jnp.bfloat16)
    slope_output = cross_rows(mixed_low, branch_tan)
    drift_output = column_total(branch_tan)
    mixed_tan = cross_cols(branch_tan, output_whole).astype(jnp.bfloat16)
    tangent_heads = mixed_tan.reshape(token_count, H, HD)
    deltas = jnp.sum((mixed_tan * attended).reshape(token_count, H, HD), axis=2).T

    def query_block(current, pieces, visible):
        key_heads = pieces[0].reshape(BLK, H, HD)
        value_heads = pieces[1].reshape(BLK, H, HD)
        row_mask = token_mask(visible)[None]
        scores = (
            jnp.einsum("qhd,khd->hqk", query_heads, key_heads, preferred_element_type=jnp.float32)
            * score_scale
        )
        probability = jnp.where(row_mask, jnp.exp(scores - log_mass[:, :, None]), 0.0)
        prob_tan = jnp.einsum(
            "qhd,khd->hqk", tangent_heads, value_heads, preferred_element_type=jnp.float32
        )
        score_tan = (probability * (prob_tan - deltas[:, :, None])).astype(jnp.bfloat16)
        addition = jnp.einsum(
            "hqk,khd->qhd", score_tan, key_heads, preferred_element_type=jnp.float32
        )
        return current + addition.reshape(token_count, D) * score_scale

    query_fold = masked_fold(query_block)
    query_sum = query_fold(
        zero_rows,
        (
            lax.all_gather(key_rows, "ctx", axis=0, tiled=True),
            lax.all_gather(value_rows, "ctx", axis=0, tiled=True),
        ),
        jnp.int32(0),
    )
    gathered_mass, gathered_delta = (
        lax.all_gather(log_mass.T, "ctx", axis=0, tiled=True),
        lax.all_gather(deltas.T, "ctx", axis=0, tiled=True),
    )
    own_keys = key_rows.reshape(token_count, H, HD)
    own_values = value_rows.reshape(token_count, H, HD)

    def owner_block(current, pieces, first_row, visible):
        key_acc, value_acc = current
        part_queries = pieces[0].reshape(BLK, H, HD)
        part_tangent = pieces[1].reshape(BLK, H, HD)
        part_mass = lax.dynamic_slice_in_dim(gathered_mass, first_row, BLK, 0).T
        part_delta = lax.dynamic_slice_in_dim(gathered_delta, first_row, BLK, 0).T
        row_mask = token_mask(visible)[None]
        scores = (
            jnp.einsum("qhd,khd->hqk", part_queries, own_keys, preferred_element_type=jnp.float32)
            * score_scale
        )
        probability = jnp.where(row_mask, jnp.exp(scores - part_mass[:, :, None]), 0.0)
        value_add_rows = jnp.einsum(
            "hqk,qhd->khd",
            probability.astype(jnp.bfloat16),
            part_tangent,
            preferred_element_type=jnp.float32,
        )
        prob_tan = jnp.einsum(
            "qhd,khd->hqk", part_tangent, own_values, preferred_element_type=jnp.float32
        )
        score_tan = (probability * (prob_tan - part_delta[:, :, None])).astype(jnp.bfloat16)
        key_add_rows = jnp.einsum(
            "hqk,qhd->khd", score_tan, part_queries, preferred_element_type=jnp.float32
        )
        return (
            key_acc + key_add_rows.reshape(token_count, D) * score_scale,
            value_acc + value_add_rows.reshape(token_count, D),
        )

    def owner_unit(current, pieces, first_row):
        query_blocks = lax.dynamic_slice_in_dim(order_row, first_row // BLK, 1)
        visible = block_mask(query_blocks, lookup(seq_row, query_blocks), own_blocks, own_seqs)
        return lax.cond(
            jnp.any(visible),
            lambda inner_state: owner_block(inner_state, pieces, first_row, visible),
            lambda inner_state: inner_state,
            current,
        )

    key_sum, value_sum = fold_units(
        (zero_rows, zero_rows),
        (
            lax.all_gather(queries, "ctx", axis=0, tiled=True),
            lax.all_gather(mixed_tan, "ctx", axis=0, tiled=True),
        ),
        owner_unit,
    )
    query_tan = query_sum.astype(jnp.bfloat16)
    key_tan = key_sum.astype(jnp.bfloat16)
    value_tan = value_sum.astype(jnp.bfloat16)
    slope_query = cross_rows(post_low, query_tan)
    slope_key = cross_rows(post_low, key_tan)
    slope_value = cross_rows(post_low, value_tan)
    drift_query = column_total(query_tan)
    drift_value = column_total(value_tan)
    post_tangent = (
        entry_tan
        + cross_cols(query_tan, query_whole)
        + cross_cols(key_tan, key_whole)
        + cross_cols(value_tan, value_whole)
    )
    heads_parts = lax.psum(
        (
            slope_query,
            slope_key,
            slope_value,
            slope_output,
            drift_query,
            drift_value,
            drift_output,
            stretch_one,
            nudge_one,
        ),
        "ctx",
    )
    heads_sums = (
        lax.psum_scatter(heads_parts[0], "fsdp", scatter_dimension=1, tiled=True),
        lax.psum_scatter(heads_parts[1], "fsdp", scatter_dimension=1, tiled=True),
        lax.psum_scatter(heads_parts[2], "fsdp", scatter_dimension=1, tiled=True),
        lax.psum_scatter(heads_parts[3], "fsdp", scatter_dimension=0, tiled=True),
        lax.psum_scatter(heads_parts[4], "fsdp", scatter_dimension=0, tiled=True),
        lax.psum_scatter(heads_parts[5], "fsdp", scatter_dimension=0, tiled=True),
        lax.psum_scatter(heads_parts[6], "fsdp", scatter_dimension=0, tiled=True),
        lax.psum_scatter(heads_parts[7], "fsdp", scatter_dimension=0, tiled=True),
        lax.psum_scatter(heads_parts[8], "fsdp", scatter_dimension=0, tiled=True),
    )
    return (
        layer_output[None],
        post_tangent[None],
        stream_tan[None],
        heads_sums[0],
        heads_sums[1],
        heads_sums[2],
        heads_sums[3],
        heads_sums[4],
        heads_sums[5],
        heads_sums[6],
        heads_sums[7],
        heads_sums[8],
        feed_sums[0],
        feed_sums[1],
        feed_sums[2],
        feed_sums[3],
        feed_sums[4],
        feed_sums[5],
        feed_sums[6],
        feed_sums[7],
    )


def low_lanes(values):
    return lax.broadcasted_iota(jnp.int32, values.shape, 1) < HD


def swap_lanes(values):
    return pltpu.roll(values, HD, 1)


def low_pair(first, second):
    return jnp.where(low_lanes(first), first, swap_lanes(second))


def high_pair(first, second):
    return jnp.where(low_lanes(first), swap_lanes(first), second)


def side_pair(side, first, second):
    return low_pair(first, second) if side == 0 else high_pair(first, second)


def dot_nn(left, right):
    return jnp.dot(left, right, preferred_element_type=F32)


def dot_nt(left, right):
    return lax.dot_general(left, right, (((1,), (1,)), ((), ())), preferred_element_type=F32)


def dot_tn(left, right):
    return lax.dot_general(left, right, (((0,), (0,)), ((), ())), preferred_element_type=F32)


class Place:
    def __init__(self):
        self.c = lax.axis_index("ctx")
        self.f = lax.axis_index("fsdp")
        self.group = self.c // H
        self.head = self.c % H
        self.inside = jnp.where(self.group == self.f, 1, 0)

    def is_me(self, tc, tf):
        return jnp.logical_and(self.c == tc, self.f == tf)

    def signal(self, barrier, tc, tf):
        @pl.when(jnp.logical_not(self.is_me(tc, tf)))
        def _():
            pl.semaphore_signal(barrier, 1, device_id=(tc, tf), device_id_type=MESH)

    def turn(self, i, n):
        return (self.c + 5 * i) % n

    def greet_sources(self, n_ctx, partner):
        barrier = pltpu.get_barrier_semaphore()
        for tc in range(n_ctx):
            self.signal(barrier, tc, self.group)
        if partner:
            pl.semaphore_signal(
                barrier, 1, device_id=(self.c, 1 - self.f), device_id_type=MESH
            )
        pl.semaphore_wait(barrier, 2 * H + (1 if partner else 0) - self.inside)

    def greet_owners(self, n_ctx, partner, more=0):
        barrier = pltpu.get_barrier_semaphore()
        for head in range(H):
            for core in range(2):
                self.signal(barrier, self.f * H + head, core)
        if partner:
            pl.semaphore_signal(
                barrier, 1, device_id=(self.c, 1 - self.f), device_id_type=MESH
            )
        pl.semaphore_wait(barrier, n_ctx + (1 if partner else 0) + more - self.inside)

    def send(self, src, dst, send_sem, recv_sem, tc, tf):
        me = self.is_me(tc, tf)

        @pl.when(me)
        def _():
            pltpu.make_async_copy(src, dst, recv_sem).start()

        @pl.when(jnp.logical_not(me))
        def _():
            self.remote(src, dst, send_sem, recv_sem, tc, tf).start()

    def remote(self, src, dst, send_sem, recv_sem, tc, tf):
        return pltpu.make_async_remote_copy(
            src_ref=src,
            dst_ref=dst,
            send_sem=send_sem,
            recv_sem=recv_sem,
            device_id=(tc, tf),
            device_id_type=MESH,
        )

    def wait_sent(self, src, dst, send_sem, recv_sem, tc, tf):
        @pl.when(jnp.logical_not(self.is_me(tc, tf)))
        def _():
            self.remote(src, dst, send_sem, recv_sem, tc, tf).wait_send()


VECTORS = 10


def project_kernel(
    n_ctx,
    x_hbm,
    wq_hbm,
    wk_hbm,
    wv_hbm,
    order_hbm,
    seq_hbm,
    *rest,
):
    dense_hbm, rest = rest[:3], rest[3:]
    vector_hbm, rest = rest[: VECTORS + 1], rest[VECTORS + 1 :]
    vector_in, rest = rest[-VECTORS - 1 :], rest[: -VECTORS - 1]
    (
        q_out,
        kv_out,
        w_other,
        order_out,
        seq_out,
        vec_out,
        expand_out,
        wo_other,
        we_other,
        ws_other,
        x_in,
        w_own,
        w_in,
        bias_own,
        bias_in,
        order_own,
        seq_own,
        order_in,
        seq_in,
        q_send,
        kv_send,
        load_sem,
        w_ss,
        w_rs,
        q_ss,
        q_rs,
        kv_ss,
        kv_rs,
        relay_ss,
        relay_rs,
    ) = rest
    at = Place()
    other = 1 - at.f
    loads = [
        pltpu.make_async_copy(src, dst, load_sem.at[i])
        for i, (src, dst) in enumerate(
            (
                (x_hbm, x_in),
                (wq_hbm, w_own.at[0]),
                (wk_hbm, w_own.at[1]),
                (wv_hbm, w_own.at[2]),
                (order_hbm, order_own),
                (seq_hbm, seq_own),
                *zip(vector_hbm, vector_in),
            )
        )
    ]
    for load in loads:
        load.start()
    at.greet_sources(n_ctx, True)
    wide = bias_own.shape[1]
    swaps = [
        at.remote(src, dst, w_ss.at[i], w_rs.at[i], at.c, other)
        for i, (src, dst) in enumerate(
            (
                (wq_hbm, w_in.at[0]),
                (wk_hbm, w_in.at[1]),
                (wv_hbm, w_in.at[2]),
                (order_hbm, order_in),
                (seq_hbm, seq_in),
                (bias_own, bias_in),
            )
        )
    ]
    for swap in swaps[:-1]:
        swap.start()
    for load in loads:
        load.wait()
    for row, ref in enumerate(vector_in[:VECTORS]):
        bias_own[row : row + 1, :] = ref[...].astype(F32).reshape(1, wide)
    for part in range(vector_in[VECTORS].shape[0] // wide):
        piece = vector_in[VECTORS][part * wide : part * wide + wide]
        bias_own[VECTORS + part : VECTORS + part + 1, :] = piece.astype(F32).reshape(1, wide)
    swaps[-1].start()

    def kv_moves(half):
        for i in range(H // 2):
            head = half * (H // 2) + at.turn(i, H // 2)
            for core in range(2):
                yield (
                    kv_send.at[head, pl.ds(core * BLK, BLK)],
                    kv_out.at[2 * at.c + core],
                    kv_ss.at[head * 2 + core],
                    kv_rs.at[at.c],
                    at.f * H + head,
                    core,
                )

    def q_moves(half):
        for i in range(H // 2):
            head = half * (H // 2) + at.turn(i, H // 2)
            for core in range(2):
                yield (
                    q_send.at[head, core],
                    q_out.at[at.c],
                    q_ss.at[head * 2 + core],
                    q_rs.at[at.c],
                    at.f * H + head,
                    core,
                )

    def heads_of(half):
        for pair in range(2):
            for side in range(2):
                yield side, half * (H // 2) + 2 * pair + side, slice(pair * 128, pair * 128 + 128)

    def one_half(half, wq, wk, wv, bias):
        low = x_in[...].astype(BF16)
        k = dot_nn(low, wk[...])
        v = dot_nn(low, wv[...]) + bias[1:2, :]
        for side, head, columns in heads_of(half):
            kv_send[head] = side_pair(side, k[:, columns], v[:, columns]).astype(BF16)
        for move in kv_moves(half):
            at.send(*move)
        q = dot_nn(low, wq[...]) + bias[0:1, :]
        for side, head, columns in heads_of(half):
            for core in range(2):
                rows = slice(core * HALF, core * HALF + HALF)
                late = slice(BLK + core * HALF, BLK + core * HALF + HALF)
                q_send[head, core] = side_pair(side, q[rows, columns], q[late, columns]).astype(
                    BF16
                )
        for move in q_moves(half):
            at.send(*move)

    one_half(at.f, w_own.at[0], w_own.at[1], w_own.at[2], bias_own)
    for swap in swaps:
        swap.wait()
    one_half(other, w_in.at[0], w_in.at[1], w_in.at[2], bias_in)
    dense_swaps = [
        at.remote(src, dst, w_ss.at[6 + i], w_rs.at[6 + i], at.c, other)
        for i, (src, dst) in enumerate(zip(dense_hbm, (wo_other, we_other, ws_other)))
    ]
    for swap in dense_swaps:
        swap.start()
    w_other[...] = w_in[...]
    inside = at.inside == 1
    order_out[...] = jnp.where(inside, order_own[...], order_in[...])
    seq_out[...] = jnp.where(inside, seq_own[...], seq_in[...])
    vec_out[...] = whole_rows(bias_own[...], bias_in[...], at.f == 0)
    for row, source in enumerate((bias_own, bias_in)):
        for part in range(expand_out.shape[1] // wide):
            at_row = VECTORS + part
            expand_out[row : row + 1, part * wide : part * wide + wide] = source[
                at_row : at_row + 1, :
            ]

    def relay(source):
        mine = kv_out.at[2 * source + at.f]
        return at.remote(mine, mine, relay_ss.at[source], relay_rs.at[source], at.c, other)

    def relay_in(source):
        theirs = kv_out.at[2 * source + other]
        return at.remote(theirs, theirs, relay_ss.at[source], relay_rs.at[source], at.c, other)

    for source in range(n_ctx):
        arrived = kv_out.at[2 * source + at.f]
        at.remote(arrived, arrived, kv_ss.at[0], kv_rs.at[source], at.c, other).wait_recv()
        relay(source).start()
    for half in (at.f, other):
        for move in kv_moves(half):
            at.wait_sent(*move)
        for move in q_moves(half):
            at.wait_sent(*move)
    for source in range(n_ctx):
        arrived = q_out.at[source]
        at.remote(arrived, arrived, q_ss.at[0], q_rs.at[source], at.c, other).wait_recv()
        relay_in(source).wait_recv()
    for source in range(n_ctx):
        relay(source).wait_send()
    for swap in dense_swaps:
        swap.wait()


def project_and_scatter(n_ctx, x, wq, wk, wv, order, seqs, dense_weights, vectors):
    wide = wq.shape[1]
    blocks = order.shape[1]
    units = vectors[VECTORS].shape[0]
    bias_rows = VECTORS + units // wide
    return pl.pallas_call(
        functools.partial(project_kernel, n_ctx),
        out_shape=(
            jax.ShapeDtypeStruct((n_ctx, HALF, 128), BF16),
            jax.ShapeDtypeStruct((2 * n_ctx, BLK, 128), BF16),
            jax.ShapeDtypeStruct((3, D, wide), BF16),
            jax.ShapeDtypeStruct((1, blocks), jnp.int32),
            jax.ShapeDtypeStruct((1, blocks), jnp.int32),
            jax.ShapeDtypeStruct((bias_rows, D), F32),
            jax.ShapeDtypeStruct((2, units), F32),
            *[jax.ShapeDtypeStruct(w.shape, BF16) for w in dense_weights],
        ),
        in_specs=[ANY] * (10 + VECTORS),
        out_specs=(ANY, ANY) + (VMEM,) * 5 + (ANY,) * 3,
        scratch_shapes=[
            pltpu.VMEM((2 * BLK, D), F32),
            pltpu.VMEM((3, D, wide), BF16),
            pltpu.VMEM((3, D, wide), BF16),
            pltpu.VMEM((bias_rows, wide), F32),
            pltpu.VMEM((bias_rows, wide), F32),
            pltpu.VMEM((1, blocks), jnp.int32),
            pltpu.VMEM((1, blocks), jnp.int32),
            pltpu.VMEM((1, blocks), jnp.int32),
            pltpu.VMEM((1, blocks), jnp.int32),
            pltpu.VMEM((H, 2, HALF, 128), BF16),
            pltpu.VMEM((H, 2 * BLK, 128), BF16),
            pltpu.SemaphoreType.DMA((7 + VECTORS,)),
            pltpu.SemaphoreType.DMA((9,)),
            pltpu.SemaphoreType.DMA((9,)),
            pltpu.SemaphoreType.DMA((2 * H,)),
            pltpu.SemaphoreType.DMA((n_ctx,)),
            pltpu.SemaphoreType.DMA((2 * H,)),
            pltpu.SemaphoreType.DMA((n_ctx,)),
            pltpu.SemaphoreType.DMA((n_ctx,)),
            pltpu.SemaphoreType.DMA((n_ctx,)),
        ]
        + [pltpu.VMEM(vector.shape, BF16) for vector in vectors],
        compiler_params=pltpu.CompilerParams(
            collective_id=0, has_side_effects=True, vmem_limit_bytes=ROOM
        ),
        name="project_scatter",
    )(x, wq, wk, wv, order, seqs, *dense_weights, *vectors)


def forward_kernel(
    blocks,
    order_ref,
    seq_ref,
    q_ref,
    kv_ref,
    o_ref,
    keep_ref,
    lse_ref,
    pairs_ref,
    place,
    q_low,
    peaks,
    masses,
    total,
    scores,
):
    def place_block(slot, _):
        place[order_ref[0, slot]] = slot
        return 0

    lax.fori_loop(0, blocks, place_block, 0)

    count = jnp.int32(0)
    for gap in range(1, LONG):
        for late in range(gap, blocks):
            pairs_ref[0, count] = place[late]
            pairs_ref[1, count] = place[late - gap]
            count = count + jnp.where(seq_ref[0, late] == seq_ref[0, late - gap], 1, 0)
    for spare in range(TOGETHER):
        pairs_ref[0, count + spare] = blocks
        pairs_ref[1, count + spare] = 0
    turns = (count + TOGETHER - 1) // TOGETHER
    pairs_ref[2, 0] = turns

    def unpack(step, _):
        for part in range(4):
            source = step * 4 + part
            packed = q_ref[source].astype(F32) * (HD**-0.5)
            low = low_lanes(packed)
            q_low[2 * source] = jnp.where(low, packed, 0.0).astype(BF16)
            q_low[2 * source + 1] = jnp.where(low, swap_lanes(packed), 0.0).astype(BF16)
        return 0

    lax.fori_loop(0, blocks // 8, unpack, 0)
    q_low[blocks] = jnp.zeros((HALF, 128), BF16)

    peaks[blocks] = jnp.zeros((HALF, 128), F32)
    masses[blocks] = jnp.zeros((HALF, 128), F32)
    total[blocks] = jnp.zeros((HALF, 128), F32)
    lse_ref[blocks] = jnp.zeros((HALF, 128), F32)

    def own_slots(step):
        return [(step * TOGETHER + part,) * 2 for part in range(TOGETHER)]

    def pair_slots(step):
        return [
            (pairs_ref[0, step * TOGETHER + part], pairs_ref[1, step * TOGETHER + part])
            for part in range(TOGETHER)
        ]

    def score(slots, base):
        results = []
        for part, (q_slot, k_slot) in enumerate(slots):
            result = dot_nt(q_low[q_slot], kv_ref[k_slot])
            scores[base + part] = result
            results.append(jnp.maximum(result[:, :128], result[:, 128:]))
        return results

    def score_own(step, _):
        slots = own_slots(step)
        for (q_slot, _), result in zip(slots, score(slots, step * TOGETHER)):
            peaks[q_slot] = result
        return 0

    def score_pairs(step, _):
        slots = pair_slots(step)
        for (q_slot, _), result in zip(slots, score(slots, blocks + step * TOGETHER)):
            peaks[q_slot] = jnp.maximum(peaks[q_slot], result)
        return 0

    lax.fori_loop(0, blocks // TOGETHER, score_own, 0)
    lax.fori_loop(0, turns, score_pairs, 0)

    def level(step, _):
        for part in range(4):
            slot = step * 4 + part
            peaks[slot] = jnp.broadcast_to(
                jnp.max(peaks[slot], axis=1, keepdims=True), (HALF, 128)
            )
        return 0

    lax.fori_loop(0, blocks // 4, level, 0)

    def weigh(slots, base):
        results = []
        for part, (q_slot, k_slot) in enumerate(slots):
            peak = peaks[q_slot]
            left = jnp.exp(scores[base + part, :, :128] - peak)
            right = jnp.exp(scores[base + part, :, 128:] - peak)
            weights = jnp.concatenate([left, right], axis=1).astype(BF16)
            results.append((left + right, dot_nn(weights, kv_ref[k_slot])))
        return results

    def weigh_own(step, _):
        slots = own_slots(step)
        for (q_slot, _), (mass, result) in zip(slots, weigh(slots, step * TOGETHER)):
            masses[q_slot] = mass
            total[q_slot] = result
        return 0

    def weigh_pairs(step, _):
        slots = pair_slots(step)
        for (q_slot, _), (mass, result) in zip(slots, weigh(slots, blocks + step * TOGETHER)):
            masses[q_slot] = masses[q_slot] + mass
            total[q_slot] = total[q_slot] + result
        return 0

    lax.fori_loop(0, blocks // TOGETHER, weigh_own, 0)
    lax.fori_loop(0, turns, weigh_pairs, 0)

    def finish(step, _):
        for part in range(4):
            source = step * 4 + part
            for side in range(2):
                slot = 2 * source + side
                mass = jnp.broadcast_to(
                    jnp.sum(masses[slot], axis=1, keepdims=True), (HALF, 128)
                )
                result = total[slot] / mass
                lse_ref[slot] = peaks[slot] + jnp.log(mass)
                packed = high_pair(result[: HALF // 2], result[HALF // 2 :])
                keep_ref[source, side] = packed
                o_ref[source, side] = packed.astype(BF16)
        return 0

    lax.fori_loop(0, blocks // 8, finish, 0)


def pair_room(blocks):
    return blocks * MOST // 2 + 2 * TOGETHER


def attend(order, seqs, q, kv):
    blocks = kv.shape[0]
    room = pair_room(blocks)
    return pl.pallas_call(
        functools.partial(forward_kernel, blocks),
        out_shape=(
            jax.ShapeDtypeStruct((blocks // 2, 2, HALF // 2, 128), BF16),
            jax.ShapeDtypeStruct((blocks // 2, 2, HALF // 2, 128), F32),
            jax.ShapeDtypeStruct((blocks + 1, HALF, 128), F32),
            jax.ShapeDtypeStruct((3, room), jnp.int32),
        ),
        in_specs=[SMEM, SMEM, VMEM, VMEM],
        out_specs=(VMEM, VMEM, VMEM, SMEM),
        scratch_shapes=[
            pltpu.SMEM((blocks,), jnp.int32),
            pltpu.VMEM((blocks + 1, HALF, 128), BF16),
            pltpu.VMEM((blocks + 1, HALF, 128), F32),
            pltpu.VMEM((blocks + 1, HALF, 128), F32),
            pltpu.VMEM((blocks + 1, HALF, 128), F32),
            pltpu.VMEM((room, HALF, BLK), F32),
        ],
        compiler_params=pltpu.CompilerParams(vmem_limit_bytes=ROOM),
        name="attend",
    )(order, seqs, q, kv)


def backward_kernel(
    blocks,
    pairs_ref,
    q_ref,
    tan_ref,
    keep_ref,
    lse_ref,
    kv_ref,
    pass_a,
    pass_b,
    dq_ref,
    dkv_sum,
    out_a,
    out_b,
    both,
    turned,
    deltas,
    dq_sum,
    held,
    pass_sem,
):
    fetches = [
        pltpu.make_async_copy(src, held.at[i], pass_sem.at[i])
        for i, src in enumerate((pass_a, pass_b))
    ]
    passes = [
        pltpu.make_async_copy(held.at[i], dst, pass_sem.at[2 + i])
        for i, dst in enumerate((out_a, out_b))
    ]
    for fetch in fetches:
        fetch.start()

    def unpack(step, _):
        for part in range(4):
            source = step * 4 + part
            packed = q_ref[source].astype(F32) * (HD**-0.5)
            low = low_lanes(packed)
            for side in range(2):
                slot = 2 * source + side
                q = packed if side == 0 else swap_lanes(packed)
                both[slot, 0:HALF] = jnp.where(low, q, 0.0).astype(BF16)
                tangent = tan_ref[source, side].astype(F32)
                first = low_lanes(tangent)
                both[slot, HALF : HALF + HALF // 2] = jnp.where(
                    first, 0.0, swap_lanes(tangent)
                ).astype(BF16)
                both[slot, HALF + HALF // 2 : BLK] = jnp.where(first, 0.0, tangent).astype(BF16)
                turned[slot] = jnp.transpose(both[slot])
                product = tangent * keep_ref[source, side]
                delta = jnp.concatenate(
                    [
                        jnp.sum(jnp.where(first, product, 0.0), axis=1, keepdims=True),
                        jnp.sum(jnp.where(first, 0.0, product), axis=1, keepdims=True),
                    ],
                    axis=0,
                )
                deltas[slot] = jnp.broadcast_to(delta, (HALF, 128))
        return 0

    lax.fori_loop(0, blocks // 8, unpack, 0)
    both[blocks] = jnp.zeros((BLK, 128), BF16)
    turned[blocks] = jnp.zeros((128, BLK), BF16)
    deltas[blocks] = jnp.zeros((HALF, 128), F32)
    dq_sum[blocks] = jnp.zeros((HALF, 128), F32)

    def one_pair(q_slot, k_slot):
        kv = kv_ref[k_slot]
        products = dot_nt(both[q_slot], kv)
        mass, delta = lse_ref[q_slot], deltas[q_slot]
        weights = jnp.exp(products[:HALF] - jnp.concatenate([mass, mass], axis=1))
        score_tan = weights * (products[HALF:] - jnp.concatenate([delta, delta], axis=1))
        score_tan = score_tan.astype(BF16)
        sides = jnp.concatenate([score_tan, weights.astype(BF16)], axis=0)
        return dot_nn(turned[q_slot], sides), dot_nn(score_tan, kv)

    def own_turn(step, _):
        slots = [step * TOGETHER + part for part in range(TOGETHER)]
        results = [one_pair(slot, slot) for slot in slots]
        for slot, (dkv, dq) in zip(slots, results):
            dkv_sum[slot] = dkv
            dq_sum[slot] = dq
        return 0

    def pair_turn(step, _):
        slots = [
            (pairs_ref[0, step * TOGETHER + part], pairs_ref[1, step * TOGETHER + part])
            for part in range(TOGETHER)
        ]
        results = [one_pair(*slot) for slot in slots]
        for (q_slot, k_slot), (dkv, dq) in zip(slots, results):
            dkv_sum[k_slot] = dkv_sum[k_slot] + dkv
            dq_sum[q_slot] = dq_sum[q_slot] + dq
        return 0

    lax.fori_loop(0, blocks // TOGETHER, own_turn, 0)
    for fetch, move in zip(fetches, passes):
        fetch.wait()
        move.start()
    lax.fori_loop(0, pairs_ref[2, 0], pair_turn, 0)

    def finish_rows(step, _):
        for part in range(4):
            source = step * 4 + part
            packed = low_pair(dq_sum[2 * source], dq_sum[2 * source + 1]) * (HD**-0.5)
            dq_ref[source] = packed.astype(BF16)
        return 0

    lax.fori_loop(0, blocks // 8, finish_rows, 0)
    for move in passes:
        move.wait()


def attend_back(pairs, q, tangent, keep, lse, kv, passed):
    blocks = kv.shape[0]
    return pl.pallas_call(
        functools.partial(backward_kernel, blocks),
        out_shape=(
            jax.ShapeDtypeStruct((blocks // 2, HALF, 128), BF16),
            jax.ShapeDtypeStruct((blocks, 128, BLK), F32),
            jax.ShapeDtypeStruct(passed[0].shape, F32),
            jax.ShapeDtypeStruct(passed[1].shape, F32),
        ),
        in_specs=[SMEM, VMEM, VMEM, VMEM, VMEM, VMEM, ANY, ANY],
        out_specs=(VMEM, VMEM, ANY, ANY),
        scratch_shapes=[
            pltpu.VMEM((blocks + 1, BLK, 128), BF16),
            pltpu.VMEM((blocks + 1, 128, BLK), BF16),
            pltpu.VMEM((blocks + 1, HALF, 128), F32),
            pltpu.VMEM((blocks + 1, HALF, 128), F32),
            pltpu.VMEM((2,) + passed[0].shape, F32),
            pltpu.SemaphoreType.DMA((4,)),
        ],
        compiler_params=pltpu.CompilerParams(vmem_limit_bytes=ROOM),
        name="attend_back",
    )(pairs, q, tangent, keep, lse, kv, *passed)


def pieces_of(start, size, body):
    piece = max(n for n in range(16, 289, 16) if size % n == 0)
    lax.fori_loop(
        0,
        size // piece,
        lambda i, _: (body(i * piece, span(start + i * piece, piece), piece), 0)[1],
        0,
    )


def span(start, size):
    return pl.ds(pl.multiple_of(start, 16), size)


def step_of(c, stride):
    bit = (c // stride) % 2
    return bit, c + stride * (1 - 2 * bit)


REGIONS = 4


def columns_of(region):
    wide = D // (REGIONS // 2)
    return slice(region // 2 * wide, region // 2 * wide + wide)


class Ladder:
    def __init__(self, at, plans, starts, size, acc, stage, landing, out, sems, bases=(0, 0)):
        self.bases = bases
        self.at, self.acc, self.stage, self.landing, self.out = at, acc, stage, landing, out
        self.down_ss, self.down_rs, self.up_ss, self.up_rs = sems
        self.ranges = []
        for region in range(REGIONS):
            plan, start = plans[region % 2], starts[region % 2]
            listed, rows = [], size
            for bit, peer in plan[:-1]:
                rows = rows // 2
                listed.append((start + bit * rows, start + (1 - bit) * rows, rows, peer))
                start = start + bit * rows
            listed.append((start, start, rows, plan[-1][1]))
            self.ranges.append(listed)
        self.last = len(plans[0]) - 1

    def slot(self, region, step):
        return region * (self.last + 1) + step

    def down(self, region, step, sent):
        kept, given, size, peer = self.ranges[region][step]
        where, slot = span(given if sent else kept, size), self.slot(region, step)
        columns = columns_of(region)
        return self.at.remote(
            self.stage[region % 2].at[where, columns],
            self.landing[region % 2][step].at[where, columns],
            self.down_ss.at[slot],
            self.down_rs.at[slot],
            peer,
            self.at.f,
        )

    def up(self, region, step, sent):
        kept, given, size, peer = self.ranges[region][step]
        start = self.bases[region % 2] + (kept if sent else given)
        columns = columns_of(region)
        where, slot = span(start, size), self.slot(region, step)
        return self.at.remote(
            self.out.at[where, columns],
            self.out.at[where, columns],
            self.up_ss.at[slot],
            self.up_rs.at[slot],
            peer,
            self.at.f,
        )

    def join(self, region, start, size, arrived, target):
        columns, acc = columns_of(region), self.acc[region % 2]

        def body(offset, where, _):
            total = acc[where, columns] + arrived[where, columns].astype(F32)
            target[where, columns] = total.astype(target.dtype)

        pieces_of(start, size, body)

    def give(self, region, step, arrived):
        kept, given, size, _ = self.ranges[region][step]
        self.join(region, given, size, arrived, self.stage[region % 2])
        self.down(region, step, True).start()
        if step < self.last:
            self.join(region, kept, size, arrived, self.acc[region % 2])

    def settle(self, region):
        kept, _, size, _ = self.ranges[region][self.last]
        arrived = self.landing[region % 2][self.last]
        columns, stage = columns_of(region), self.stage[region % 2]

        def body(offset, where, rows):
            total = stage[where, columns].astype(F32) + arrived[where, columns].astype(F32)
            row = span(self.bases[region % 2] + kept + offset, rows)
            self.out[row, columns] = total.astype(BF16)

        self.down(region, self.last, False).wait_recv()
        pieces_of(kept, size, body)
        self.up(region, self.last - 1, True).start()

    def wait_down(self):
        for region in range(REGIONS):
            for step in range(self.last + 1):
                self.down(region, step, True).wait_send()

    def wait_up(self, steps):
        for region in range(REGIONS):
            for step in steps:
                self.up(region, step, True).wait_send()


COLS = 512


def whole_rows(own, other, first):
    return jnp.where(
        first,
        jnp.concatenate([own, other], axis=1),
        jnp.concatenate([other, own], axis=1),
    )


def row_mean(values):
    return jnp.mean(values, axis=1, keepdims=True)


def normalize(values):
    centre = values - row_mean(values)
    scale = lax.rsqrt(row_mean(centre * centre) + norm_eps)
    return centre * scale, scale


def norm_back(tangent, normed, scale, gain):
    pushed = tangent * gain
    return scale * (pushed - row_mean(pushed) - normed * row_mean(pushed * normed))


def column_sum(values):
    return jnp.sum(values, axis=0, keepdims=True)


def feed_slopes(kind, target, mixed, low_turned, hidden, before_tan, feed_tan, branch_tan):
    unit_count = hidden.shape[2] // COLS

    def chunk_slopes(chunk, _):
        columns = pl.ds(pl.multiple_of(chunk * COLS, COLS), COLS)
        target[columns, :] = dot_tn(hidden[kind, :, columns], feed_tan[...]).astype(target.dtype)
        below = pl.ds(pl.multiple_of((unit_count + chunk) * COLS, COLS), COLS)
        target[below, :] = dot_nn(low_turned[...], before_tan[kind, :, columns]).astype(
            target.dtype
        )
        return 0

    lax.fori_loop(0, unit_count, chunk_slopes, 0)
    start = 2 * unit_count * COLS
    target[start : start + D // 2, :] = dot_tn(mixed[kind], branch_tan[...]).astype(target.dtype)


def middle_kernel(
    n_ctx,
    o_hbm, x_hbm, sum_hbm, cot_hbm, wo_a, wo_b, we_a, we_b, ws_a, ws_b, be_ref, vec_in,
    out_hbm, sum_tan_hbm, entry_hbm, tan_out, vec_ref, stage_a, stage_b, keep_ref,
    o_in, x_ref, sum_ref, cot_ref, wo, we, ws, out_ref, sum_tan_ref, entry_ref,
    mixed, low, hidden, before_tan, feed_tan, branch_tan, slope, mixed_tan, tan_send,
    own_grads, send_grads, first_in, low_turned,
    load_sem, store_sem, o_ss, o_rs, tan_ss, tan_rs, core_ss, core_rs,
):
    at = Place()
    f = at.f
    other = 1 - f
    halves = (f, other)
    piece = HALF // 2
    loads = [
        pltpu.make_async_copy(src, dst, load_sem.at[i])
        for i, (src, dst) in enumerate(
            (
                (x_hbm, x_ref),
                (wo_a, wo.at[0]),
                (wo_b, wo.at[1]),
                (we_a, we.at[0]),
                (we_b, we.at[1]),
                (ws_a, ws.at[0]),
                (ws_b, ws.at[1]),
                (sum_hbm, sum_ref),
                (cot_hbm, cot_ref),
            )
        )
    ]
    for load in loads:
        load.start()
    barrier = pltpu.get_barrier_semaphore()
    for target in range(n_ctx):
        at.signal(barrier, target, at.group)
    at.greet_owners(n_ctx, True, 2 * H - at.inside)

    def o_move(target, side):
        return (
            o_hbm.at[target, side],
            o_in.at[side, at.head, f],
            o_ss.at[2 * target + side],
            o_rs.at[side * 2 * H + at.head * 2 + f],
            target,
            at.group,
        )

    def tan_move(side, head, core):
        return (
            tan_send.at[side, head, core],
            tan_out.at[at.c, side],
            tan_ss.at[side * 2 * H + head * 2 + core],
            tan_rs.at[at.c * 2 + side],
            f * H + head,
            core,
        )

    for side in range(2):
        for i in range(n_ctx):
            at.send(*o_move(at.turn(i, n_ctx), side))
    vec_ref[...] = jnp.zeros_like(vec_ref)
    vectors = vec_in[...]
    (out_bias, gain_one, shift_one, shrink_bias, gain_two, shift_two, gain_last, shift_last) = (
        vectors[i : i + 1] for i in range(2, 10)
    )
    be = (be_ref.at[0:1], be_ref.at[1:2])
    for load in loads:
        load.wait()

    def stores(step):
        rows = pl.ds(pl.multiple_of(step * BLK, BLK), BLK)
        return [
            pltpu.make_async_copy(src.at[rows], dst.at[rows], store_sem.at[3 * step + i])
            for i, (src, dst) in enumerate(
                ((out_ref, out_hbm), (sum_tan_ref, sum_tan_hbm), (entry_ref, entry_hbm))
            )
        ]

    def tile(step, _):
        first_row = pl.multiple_of(step * BLK, BLK)
        rows = pl.ds(first_row, BLK)
        for head in range(H):
            for core in range(2):
                arrived = o_in.at[step, head, core]
                at.remote(
                    arrived, arrived, o_ss.at[0], o_rs.at[step * 2 * H + head * 2 + core],
                    at.c, other,
                ).wait_recv()
        for kind in range(2):
            for pair in range(2):
                head = halves[kind] * (H // 2) + 2 * pair
                columns = slice(pair * 128, pair * 128 + 128)
                for core in range(2):
                    early = o_in[step, head, core].astype(F32)
                    late = o_in[step, head + 1, core].astype(F32)
                    for part in range(2):
                        start = pl.multiple_of(first_row + core * HALF + part * piece, piece)
                        mixed[kind, pl.ds(start, piece), columns] = side_pair(
                            part, early, late
                        ).astype(BF16)
        branch = dot_nn(mixed[0, rows, :], wo[0]) + dot_nn(mixed[1, rows, :], wo[1]) + out_bias
        n_one, scale_one = normalize(x_ref[rows, :] + branch)
        normed_one = n_one * gain_one + shift_one
        stream_one = sum_ref[rows, :] + branch
        normed_low = normed_one.astype(BF16)
        low[rows, :] = normed_low
        feed = jnp.zeros((BLK, D), F32)
        for kind in range(2):

            def expand(chunk, carried):
                columns = slice(chunk * COLS, chunk * COLS + COLS)
                v = dot_nn(normed_low, we[kind, :, columns]) + be[kind][:, columns]
                square = v * v
                t = jnp.tanh(gelu_coeff * (v + gelu_cubic * square * v))
                half_up = 0.5 + 0.5 * t
                hidden_part = (v * half_up).astype(BF16)
                hidden[kind, rows, columns] = hidden_part
                slope[kind, :, columns] = half_up + v * half_up * (1.0 - t) * (
                    gelu_coeff + (3.0 * gelu_coeff * gelu_cubic) * square
                )
                return carried + dot_nn(hidden_part, ws[kind, columns, :])

            for chunk in range(ws.shape[1] // COLS):
                feed = expand(chunk, feed)
        feed_out = feed + shrink_bias
        n_two, scale_two = normalize(normed_one + feed_out)
        n_last, scale_last = normalize(stream_one + feed_out)
        out_ref[rows, :] = (n_two * gain_two + shift_two) + (n_last * gain_last + shift_last)
        u = cot_ref[rows, :]
        nudge = column_sum(u)
        sum_tan = norm_back(u, n_last, scale_last, gain_last)
        inflow = norm_back(u, n_two, scale_two, gain_two)
        sum_tan_ref[rows, :] = sum_tan
        feed_low = (sum_tan + inflow).astype(BF16)
        feed_tan[rows, :] = feed_low
        vec_ref[0:1, :] += column_sum(feed_low.astype(F32))
        vec_ref[1:2, :] += column_sum(u * n_two)
        vec_ref[2:3, :] += nudge
        vec_ref[3:4, :] += column_sum(u * n_last)
        vec_ref[4:5, :] += nudge
        normed_tan = inflow
        for kind in range(2):

            def expand_back(chunk, carried):
                columns = slice(chunk * COLS, chunk * COLS + COLS)
                pushed = dot_nt(feed_low, ws[kind, columns, :])
                tan_part = (pushed * slope[kind, :, columns]).astype(BF16)
                before_tan[kind, rows, columns] = tan_part
                vec_row = pl.ds(8 + 2 * halves[kind] + chunk, 1)
                vec_ref[vec_row, :] += column_sum(tan_part.astype(F32))
                return carried + dot_nt(tan_part, we[kind, :, columns])

            for chunk in range(ws.shape[1] // COLS):
                normed_tan = expand_back(chunk, normed_tan)
        vec_ref[5:6, :] += column_sum(normed_tan * n_one)
        vec_ref[6:7, :] += column_sum(normed_tan)
        entry = norm_back(normed_tan, n_one, scale_one, gain_one)
        entry_ref[rows, :] = entry
        branch_low = (sum_tan + entry).astype(BF16)
        branch_tan[rows, :] = branch_low
        vec_ref[7:8, :] += column_sum(branch_low.astype(F32))
        for kind in range(2):
            mixed_tan[kind] = dot_nt(branch_low, wo[kind])
        for kind in range(2):
            for pair in range(2):
                columns = slice(pair * 128, pair * 128 + 128)
                for side in range(2):
                    head = halves[kind] * (H // 2) + 2 * pair + side
                    for core in range(2):
                        start = core * HALF
                        early = mixed_tan[kind, start : start + piece, columns]
                        late = mixed_tan[kind, start + piece : start + HALF, columns]
                        tan_send[step, head, core] = side_pair(side, early, late).astype(BF16)
        for i in range(H):
            for core in range(2):
                at.send(*tan_move(step, at.turn(i, H), core))
        for store in stores(step):
            store.start()
        return 0

    lax.fori_loop(0, 2, tile, 0)

    quarter = first_in.shape[0] // 4
    bits = (step_of(at.c, 1)[0], step_of(at.c, 2)[0])
    stages = (stage_a, stage_b)

    def core_move(region, give):
        bit = bits[region]
        start = region * 2 * quarter + (1 - bit if give else bit) * quarter
        where = span(start, quarter)
        slot = region + 2 * (0 if give else 1)
        return start, at.remote(
            send_grads.at[where], first_in.at[where], core_ss.at[slot], core_rs.at[slot],
            at.c, other,
        )

    order = [(0, True), (1, True), (0, False), (1, False)]
    low_turned[...] = jnp.transpose(low[...])
    operands = (mixed, low_turned, hidden, before_tan, feed_tan, branch_tan)
    feed_slopes(1, send_grads, *operands)
    for step in order:
        core_move(*step)[1].start()
    feed_slopes(0, own_grads, *operands)
    for region, give in order:
        start, move = core_move(region, give)
        move.wait_recv()

        def join(offset, where, size):
            total = own_grads[where, :] + first_in[where, :].astype(F32)
            if give:
                stages[region][span(offset, size), :] = total.astype(BF16)
            else:
                keep_ref[region, span(offset, size), :] = total

        pieces_of(start, quarter, join)
    for source in range(n_ctx):
        for side in range(2):
            arrived = tan_out.at[source, side]
            at.remote(
                arrived, arrived, tan_ss.at[0], tan_rs.at[source * 2 + side], at.c, other
            ).wait_recv()
    for step in range(2):
        for store in stores(step):
            store.wait()
    for side in range(2):
        for target in range(n_ctx):
            at.wait_sent(*o_move(target, side))
    for side in range(2):
        for head in range(H):
            for core in range(2):
                at.wait_sent(*tan_move(side, head, core))
    for step in order:
        core_move(*step)[1].wait_send()


def middle(n_ctx, o, x, summed, cotangent, wo, we, ws, be, vec):
    tokens, wide, units = x.shape[0], D // 2, ws[0].shape[0]
    grad_rows = 2 * units + wide
    rows = jax.ShapeDtypeStruct((tokens, D), F32)

    def sems(*counts):
        return [pltpu.SemaphoreType.DMA((count,)) for count in counts]

    return pl.pallas_call(
        functools.partial(middle_kernel, n_ctx),
        out_shape=(
            rows,
            rows,
            rows,
            jax.ShapeDtypeStruct((n_ctx, 2, HALF // 2, 128), BF16),
            jax.ShapeDtypeStruct((16, D), F32),
            jax.ShapeDtypeStruct((grad_rows // 4, D), BF16),
            jax.ShapeDtypeStruct((grad_rows // 4, D), BF16),
            jax.ShapeDtypeStruct((2, grad_rows // 4, D), F32),
        ),
        in_specs=[ANY] * 10 + [VMEM] * 2,
        out_specs=(ANY,) * 4 + (VMEM,) * 4,
        scratch_shapes=[
            pltpu.VMEM((2, H, 2, HALF // 2, 128), BF16),
            pltpu.VMEM((tokens, D), F32),
            pltpu.VMEM((tokens, D), F32),
            pltpu.VMEM((tokens, D), F32),
            pltpu.VMEM((2, wide, D), BF16),
            pltpu.VMEM((2, D, units), BF16),
            pltpu.VMEM((2, units, D), BF16),
            pltpu.VMEM((tokens, D), F32),
            pltpu.VMEM((tokens, D), F32),
            pltpu.VMEM((tokens, D), F32),
            pltpu.VMEM((2, tokens, wide), BF16),
            pltpu.VMEM((tokens, D), BF16),
            pltpu.VMEM((2, tokens, units), BF16),
            pltpu.VMEM((2, tokens, units), BF16),
            pltpu.VMEM((tokens, D), BF16),
            pltpu.VMEM((tokens, D), BF16),
            pltpu.VMEM((2, BLK, units), F32),
            pltpu.VMEM((2, BLK, wide), F32),
            pltpu.VMEM((2, H, 2, HALF // 2, 128), BF16),
            pltpu.VMEM((grad_rows, D), F32),
            pltpu.VMEM((grad_rows, D), BF16),
            pltpu.VMEM((grad_rows, D), BF16),
            pltpu.VMEM((D, tokens), BF16),
        ]
        + sems(9, 6, 2 * n_ctx, 4 * H, 4 * H, 2 * n_ctx, 4, 4),
        compiler_params=pltpu.CompilerParams(
            collective_id=1, has_side_effects=True, vmem_limit_bytes=ROOM
        ),
        name="middle",
    )(o, x, summed, cotangent, *wo, *we, *ws, be, vec)


def finish_kernel(
    n_ctx,
    dq_ref, dkv_ref, keep_hbm, land_a, land_b, x_hbm, entry_hbm, wq_hbm, wk_hbm, wv_hbm,
    w_other_hbm, vec_feed,
    post_ref, feed_ref, grads_ref, vec_out,
    own, part, ready, dq_in, dkv_in, keep, acc, stage, landing,
    x_in, entry_in, w_in, w_far, low_turned, tangents,
    own_grads, send_grads, first_in, acc_last, stage_last, landing_last, vec_sum, vec_in,
    load_sem, q_ss, q_rs, kv_ss, kv_rs, part_ss, part_rs, own_sem,
    down_ss, down_rs, up_ss, up_rs, top_ss, top_rs,
    core_ss, core_rs, down_ss2, down_rs2, up_ss2, up_rs2, vec_ss, vec_rs,
):
    at = Place()
    c, f = at.c, at.f
    other = 1 - f
    halves = (f, other)
    wide = D // 2
    loads = [
        pltpu.make_async_copy(src, dst, load_sem.at[i])
        for i, (src, dst) in enumerate(
            (
                (keep_hbm, keep),
                (x_hbm, x_in),
                (entry_hbm, entry_in),
                (wq_hbm, w_in.at[0]),
                (wk_hbm, w_in.at[1]),
                (wv_hbm, w_in.at[2]),
                (w_other_hbm, w_far),
            )
        )
    ]
    for load in loads:
        load.start()
    x_step, y_step, near, far = (step_of(c, stride) for stride in (1, 2, 4, 8))
    barrier = pltpu.get_barrier_semaphore()
    for _, peer in (x_step, y_step, near, far):
        pl.semaphore_signal(barrier, 1, device_id=(peer, f), device_id_type=MESH)
    at.greet_owners(n_ctx, True, 4)

    def partial_move(source):
        return at.remote(
            dkv_ref.at[2 * source + other],
            part.at[source],
            part_ss.at[source],
            part_rs.at[source],
            c,
            other,
        )

    def own_move(source):
        return pltpu.make_async_copy(
            dkv_ref.at[2 * source + f], own.at[source], own_sem.at[source]
        )

    def q_move(target):
        return (
            dq_ref.at[target],
            dq_in.at[at.head, f],
            q_ss.at[target],
            q_rs.at[at.head * 2 + f],
            target,
            at.group,
        )

    def kv_move(target):
        return (
            ready.at[target],
            dkv_in.at[at.head, pl.ds(pl.multiple_of(f * BLK, BLK), BLK)],
            kv_ss.at[target],
            kv_rs.at[at.head * 2 + f],
            target,
            at.group,
        )

    for i in range(n_ctx):
        source = at.turn(i, n_ctx)
        partial_move(source).start()
        own_move(source).start()
    for i in range(n_ctx):
        at.send(*q_move(at.turn(i, n_ctx)))

    size = keep.shape[1]
    firsts = (x_step, y_step)
    bases = [2 * size * region + firsts[region][0] * size for region in range(2)]
    feed = Ladder(
        at,
        ((y_step, near, far), (x_step, near, far)),
        (0, 0),
        size,
        [keep.at[region] for region in range(2)],
        [stage.at[region] for region in range(2)],
        [[landing.at[region, step] for step in range(3)] for region in range(2)],
        feed_ref,
        (down_ss, down_rs, up_ss, up_rs),
        bases,
    )

    def top_move(region, sent):
        side, columns = region % 2, columns_of(region)
        given = 2 * size * side + (1 - firsts[side][0]) * size
        where = span(bases[side] if sent else given, size)
        return at.remote(
            feed_ref.at[where, columns],
            feed_ref.at[where, columns],
            top_ss.at[region],
            top_rs.at[region],
            firsts[side][1],
            f,
        )

    loads[0].wait()
    kept_acc = [keep.at[region] for region in range(2)]
    sums = [acc.at[region] for region in range(2)]
    for region in range(REGIONS):
        first = (land_a, land_b)[region % 2]
        kept, given, half, _ = feed.ranges[region][0]
        feed.acc = kept_acc
        feed.join(region, given, half, first, stage.at[region % 2])
        feed.down(region, 0, True).start()
        feed.join(region, kept, half, first, sums[region % 2])
    feed.acc = sums
    for i in range(n_ctx):
        source = at.turn(i, n_ctx)
        own_move(source).wait()
        partial_move(source).wait_recv()
        ready[source] = jnp.transpose(own[source] + part[source]).astype(BF16)
        if i < n_ctx - 6:
            at.send(*kv_move(source))
    for load in loads[1:]:
        load.wait()
    low_turned[...] = jnp.transpose(x_in[...]).astype(BF16)
    for step in (1, 2):
        for region in range(REGIONS):
            feed.down(region, step - 1, False).wait_recv()
            feed.give(region, step, feed.landing[region % 2][step - 1])
        if step == 1:
            for i in range(n_ctx - 6, n_ctx):
                at.send(*kv_move(at.turn(i, n_ctx)))

    for target in range(n_ctx):
        partial_move(target).wait_send()
        at.wait_sent(*q_move(target))

    for head in range(H):
        for core in range(2):
            slot = head * 2 + core
            arrived = dq_in.at[head, core]
            at.remote(arrived, arrived, q_ss.at[0], q_rs.at[slot], c, other).wait_recv()
            arrived = dkv_in.at[head, pl.ds(core * BLK, BLK)]
            at.remote(arrived, arrived, kv_ss.at[0], kv_rs.at[slot], c, other).wait_recv()
    feed_rows = vec_feed.shape[0]
    vec_sum[0, 0:feed_rows] = vec_feed[...]
    vec_sum[0, feed_rows:] = jnp.zeros_like(vec_sum[0, feed_rows:])

    plans = ((x_step, y_step, near, far), (y_step, x_step, near, far))
    quarter = first_in.shape[0] // 4
    last = Ladder(
        at,
        plans,
        (0, 2 * quarter),
        2 * quarter,
        [acc_last, acc_last],
        [stage_last, stage_last],
        [[landing_last.at[step] for step in range(4)]] * 2,
        grads_ref,
        (down_ss2, down_rs2, up_ss2, up_rs2),
    )

    def core_move(region, give):
        kept, given, rows, _ = last.ranges[region][0]
        where = span(given if give else kept, rows)
        slot, columns = region + REGIONS * (0 if give else 1), columns_of(region)
        return at.remote(
            send_grads.at[where, columns],
            first_in.at[where, columns],
            core_ss.at[slot],
            core_rs.at[slot],
            c,
            other,
        )

    order = [(region, give) for give in (True, False) for region in range(REGIONS)]
    vec_peers = [(c, other)] + [(peer, f) for _, peer in (x_step, y_step, near, far)]

    def vec_move(step):
        return at.remote(
            vec_sum.at[step], vec_in.at[step], vec_ss.at[step], vec_rs.at[step], *vec_peers[step]
        )

    def vec_next(step):
        vec_move(step).wait_recv()
        target = vec_sum.at[step + 1] if step < 4 else vec_out
        target[...] = vec_sum[step] + vec_in[step]
        if step < 4:
            vec_move(step + 1).start()

    for kind, grad_ref in ((1, send_grads), (0, own_grads)):
        for pair in range(2):
            head = halves[kind] * (H // 2) + 2 * pair
            columns = slice(pair * 128, pair * 128 + 128)
            for core in range(2):
                early = dq_in[head, core].astype(F32)
                late = dq_in[head + 1, core].astype(F32)
                for side in range(2):
                    start = side * BLK + core * HALF
                    tangents[kind, 0, start : start + HALF, columns] = side_pair(
                        side, early, late
                    ).astype(BF16)
            early = dkv_in[head].astype(F32)
            late = dkv_in[head + 1].astype(F32)
            tangents[kind, 1, :, columns] = low_pair(early, late).astype(BF16)
            tangents[kind, 2, :, columns] = high_pair(early, late).astype(BF16)
        turned = low_turned[...]
        grad_ref[0:D, 0:wide] = dot_nn(turned, tangents[kind, 0]).astype(grad_ref.dtype)
        grad_ref[0:D, wide:D] = dot_nn(turned, tangents[kind, 1]).astype(grad_ref.dtype)
        value_grad = dot_nn(turned, tangents[kind, 2]).astype(grad_ref.dtype)
        grad_ref[D : D + wide, 0:wide] = value_grad[0:wide]
        grad_ref[D : D + wide, wide:D] = value_grad[wide:D]
        columns = pl.ds(pl.multiple_of(halves[kind] * wide, wide), wide)
        vec_sum[0, feed_rows : feed_rows + 1, columns] = column_sum(tangents[kind, 0].astype(F32))
        vec_sum[0, feed_rows + 1 : feed_rows + 2, columns] = column_sum(
            tangents[kind, 2].astype(F32)
        )
        if kind == 1:
            for step in order:
                core_move(*step).start()
    vec_move(0).start()
    for region, give in order:
        core_move(region, give).wait_recv()
        kept, given, rows, _ = last.ranges[region][0]
        columns = columns_of(region)

        def join(offset, where, _):
            total = own_grads[where, columns] + first_in[where, columns].astype(F32)
            if give:
                stage_last[where, columns] = total.astype(BF16)
            else:
                acc_last[where, columns] = total

        pieces_of(given if give else kept, rows, join)
        if give:
            last.down(region, 0, True).start()
    vec_next(0)
    total = entry_in[...]
    for which in range(3):
        total = total + dot_nt(tangents[0, which], w_in[which])
        total = total + dot_nt(tangents[1, which], w_far[which])
    post_ref[...] = total
    for target in range(n_ctx):
        at.wait_sent(*kv_move(target))
    for step in order:
        core_move(*step).wait_send()
    for region in range(REGIONS):
        feed.settle(region)
    for region in range(REGIONS):
        feed.up(region, 1, False).wait_recv()
        feed.up(region, 0, True).start()
    for region in range(REGIONS):
        last.down(region, 0, False).wait_recv()
        last.give(region, 1, last.landing[region % 2][0])
    vec_next(1)
    for region in range(REGIONS):
        feed.up(region, 0, False).wait_recv()
        top_move(region, True).start()
    for region in range(REGIONS):
        last.down(region, 1, False).wait_recv()
        last.give(region, 2, last.landing[region % 2][1])
    vec_next(2)
    for region in range(REGIONS):
        last.down(region, 2, False).wait_recv()
        last.give(region, 3, last.landing[region % 2][2])
    vec_next(3)
    for region in range(REGIONS):
        last.settle(region)
    vec_next(4)
    feed.wait_down()
    for step in (2, 1, 0):
        for region in range(REGIONS):
            last.up(region, step, False).wait_recv()
            if step > 0:
                last.up(region, step - 1, True).start()
        if step == 2:
            last.wait_down()
        if step == 1:
            feed.wait_up((0, 1))
            last.wait_up((1, 2))
            for index in range(5):
                vec_move(index).wait_send()
    for region in range(REGIONS):
        top_move(region, False).wait_recv()

    for region in range(REGIONS):
        top_move(region, True).wait_send()
    last.wait_up((0,))


def finish(n_ctx, dq, dkv, keep, land_a, land_b, x, entry, wq, wk, wv, w_other, vec_feed):
    size, tokens, wide = keep.shape[1], x.shape[0], D // 2
    last_shape = (D + wide, D)
    vec_shape = (vec_feed.shape[0] + 8, D)

    def sems(*counts):
        return [pltpu.SemaphoreType.DMA((count,)) for count in counts]

    return pl.pallas_call(
        functools.partial(finish_kernel, n_ctx),
        out_shape=(
            jax.ShapeDtypeStruct((tokens, D), F32),
            jax.ShapeDtypeStruct((4 * size, D), BF16),
            jax.ShapeDtypeStruct(last_shape, BF16),
            jax.ShapeDtypeStruct(vec_shape, F32),
        ),
        in_specs=[ANY, ANY, ANY, VMEM, VMEM] + [ANY] * 6 + [VMEM],
        out_specs=(VMEM,) * 4,
        scratch_shapes=[
            pltpu.VMEM((n_ctx, 128, BLK), F32),
            pltpu.VMEM((n_ctx, 128, BLK), F32),
            pltpu.VMEM((n_ctx, BLK, 128), BF16),
            pltpu.VMEM((H, 2, HALF, 128), BF16),
            pltpu.VMEM((H, 2 * BLK, 128), BF16),
            pltpu.VMEM((2, size, D), F32),
            pltpu.VMEM((2, size, D), F32),
            pltpu.VMEM((2, size, D), BF16),
            pltpu.VMEM((2, 3, size, D), BF16),
            pltpu.VMEM((tokens, D), F32),
            pltpu.VMEM((tokens, D), F32),
            pltpu.VMEM((3, D, wide), BF16),
            pltpu.VMEM((3, D, wide), BF16),
            pltpu.VMEM((D, tokens), BF16),
            pltpu.VMEM((2, 3, tokens, wide), BF16),
            pltpu.VMEM(last_shape, F32),
            pltpu.VMEM(last_shape, BF16),
            pltpu.VMEM(last_shape, BF16),
            pltpu.VMEM(last_shape, F32),
            pltpu.VMEM(last_shape, BF16),
            pltpu.VMEM((4,) + last_shape, BF16),
            pltpu.VMEM((5,) + vec_shape, F32),
            pltpu.VMEM((5,) + vec_shape, F32),
        ]
        + sems(7, n_ctx, 2 * H, n_ctx, 2 * H, n_ctx, n_ctx, n_ctx)
        + sems(12, 12, 12, 12, 4, 4, 8, 8, 16, 16, 16, 16, 5, 5),
        compiler_params=pltpu.CompilerParams(
            collective_id=3, has_side_effects=True, vmem_limit_bytes=ROOM
        ),
        name="finish",
    )(dq, dkv, keep, land_a, land_b, x, entry, wq, wk, wv, w_other, vec_feed)


def unpack_kernel(
    full, grads, post, vec_ref,
    query_ref, key_ref, value_ref, output_ref, expand_ref, shrink_ref, post_out, *vector_outs,
):
    f = lax.axis_index("fsdp")
    units, wide = shrink_ref.shape[0], D // 2
    shrink_ref[...] = full[0:units].astype(F32)
    for part in range(units // D):
        start = units + part * D
        expand_ref[:, part * D : part * D + D] = full[start : start + D].astype(F32)
    output_ref[...] = full[2 * units : 2 * units + wide].astype(F32)
    query_ref[...] = grads[0:D, 0:wide].astype(F32)
    key_ref[...] = grads[0:D, wide:D].astype(F32)
    value_ref[0:wide] = grads[D : D + wide, 0:wide].astype(F32)
    value_ref[wide:D] = grads[D : D + wide, wide:D].astype(F32)
    post_out[...] = post[...]
    vectors = vec_ref[...]
    mine = jnp.where(f == 0, vectors[:, 0:wide], vectors[:, wide:D])
    for row, ref in zip((16, 17, 7, 5, 6, 0, 1, 2, 3, 4), vector_outs):
        ref[...] = mine[row : row + 1]
    drift = jnp.where(f == 0, vectors[8:10], vectors[10:12])
    for part in range(units // D):
        vector_outs[10][:, part * D : part * D + D] = drift[part : part + 1]


def unpack_grads(units, full, grads, post, vecs):
    wide = D // 2
    shapes = [(D, wide)] * 3 + [(wide, D), (D, units), (units, D), post.shape]
    shapes = shapes + [(1, wide)] * 10 + [(1, units)]
    return pl.pallas_call(
        unpack_kernel,
        out_shape=tuple(jax.ShapeDtypeStruct(shape, F32) for shape in shapes),
        in_specs=[VMEM] * 4,
        out_specs=(VMEM,) * len(shapes),
        compiler_params=pltpu.CompilerParams(vmem_limit_bytes=UNPACK_ROOM),
        name="unpack_grads",
    )(full, grads, post, vecs)


def head_shards(
    n_ctx,
    post_stream,
    sum_stream,
    cotangent,
    block_order,
    block_sequence,
    query_weight,
    key_weight,
    value_weight,
    output_weight,
    query_bias,
    value_bias,
    output_bias,
    attend_gain,
    attend_shift,
    expand_weight,
    expand_bias,
    shrink_weight,
    shrink_bias,
    middle_gain,
    middle_shift,
    final_gain,
    final_shift,
):
    x, summed, tangent = post_stream[0], sum_stream[0], cotangent[0]
    def across(values, stride):
        return lax.ppermute(values, "ctx", [(c, c ^ stride) for c in range(n_ctx)])

    vectors = [
        query_bias,
        value_bias,
        output_bias,
        attend_gain,
        attend_shift,
        shrink_bias,
        middle_gain,
        middle_shift,
        final_gain,
        final_shift,
        expand_bias,
    ]
    q, kv, w_other, order, seqs, vec, expand_add, wo_other, we_other, ws_other = (
        project_and_scatter(
            n_ctx,
            x,
            query_weight,
            key_weight,
            value_weight,
            block_order,
            block_sequence,
            (output_weight, expand_weight, shrink_weight),
            vectors,
        )
    )
    o, keep, lse, pairs = attend(order, seqs, q, kv)
    layer_output, sum_tan, entry, tan, vec_feed, stage_a, stage_b, kept = middle(
        n_ctx,
        o,
        x,
        summed,
        tangent,
        (output_weight, wo_other),
        (expand_weight, we_other),
        (shrink_weight, ws_other),
        expand_add,
        vec,
    )
    land_a, land_b = across(stage_a, 1), across(stage_b, 2)
    dq, dkv, layer_output, sum_tan = attend_back(
        pairs, q, tan, keep, lse, kv, (layer_output, sum_tan)
    )
    post_tangent, feed_sums, last_sums, vecs = finish(
        n_ctx,
        dq,
        dkv,
        kept,
        land_a,
        land_b,
        x,
        entry,
        query_weight,
        key_weight,
        value_weight,
        w_other,
        vec_feed,
    )
    (
        query_slope,
        key_slope,
        value_slope,
        output_slope,
        expand_slope,
        shrink_slope,
        post_tangent,
        query_drift,
        value_drift,
        output_drift,
        attend_stretch,
        attend_nudge,
        shrink_drift,
        middle_stretch,
        middle_nudge,
        final_stretch,
        final_nudge,
        expand_drift,
    ) = unpack_grads(shrink_weight.shape[0], feed_sums, last_sums, post_tangent, vecs)
    return (
        layer_output[None],
        post_tangent[None],
        sum_tan[None],
        query_slope,
        key_slope,
        value_slope,
        output_slope,
        query_drift[0],
        value_drift[0],
        output_drift[0],
        attend_stretch[0],
        attend_nudge[0],
        expand_slope,
        expand_drift[0],
        shrink_slope,
        shrink_drift[0],
        middle_stretch[0],
        middle_nudge[0],
        final_stretch[0],
        final_nudge[0],
    )


def solution(mesh):
    n_ctx, n_fsdp = mesh.shape["ctx"], mesh.shape["fsdp"]
    if n_fsdp == 2 and n_ctx == n_fsdp * H:
        body = functools.partial(head_shards, n_ctx)
    else:
        body = general_shards
    return jax.shard_map(
        body,
        mesh=mesh,
        in_specs=(
            P("fsdp", "ctx", None),
            P("fsdp", "ctx", None),
            P("fsdp", "ctx", None),
            P("fsdp", None),
            P("fsdp", None),
            P(None, "fsdp"),
            P(None, "fsdp"),
            P(None, "fsdp"),
            P("fsdp", None),
            P("fsdp"),
            P("fsdp"),
            P("fsdp"),
            P("fsdp"),
            P("fsdp"),
            P(None, "fsdp"),
            P("fsdp"),
            P("fsdp", None),
            P("fsdp"),
            P("fsdp"),
            P("fsdp"),
            P("fsdp"),
            P("fsdp"),
        ),
        out_specs=(
            P("fsdp", "ctx", None),
            P("fsdp", "ctx", None),
            P("fsdp", "ctx", None),
            P(None, "fsdp"),
            P(None, "fsdp"),
            P(None, "fsdp"),
            P("fsdp", None),
            P("fsdp"),
            P("fsdp"),
            P("fsdp"),
            P("fsdp"),
            P("fsdp"),
            P(None, "fsdp"),
            P("fsdp"),
            P("fsdp", None),
            P("fsdp"),
            P("fsdp"),
            P("fsdp"),
            P("fsdp"),
            P("fsdp"),
        ),
        check_vma=False,
    )
```
